32 devices in a mesh: items: 2 (over y), band: 16 (over z, x, core).
Axes of the slice: x: 2, y: 2, z: 4, core: 2. Of those that a mesh axis runs over, the one named last changes fastest.
Arguments:
- inputs: bfloat16 [2, 6, 1024, 768], P(None, 'items', 'band'), may hold values from -6 to 6
- counts: int32 [2, 6], P(None, 'items'), may hold values from 128 to 1024, as said below
- norm_gain1: float32 [768], replicated, may hold values from 0.5 to 1.5
- w_query: bfloat16 [768, 768], replicated, may hold values from -0.21875 to 0.21875
- w_key: bfloat16 [768, 768], replicated, may hold values from -0.21875 to 0.21875
- w_value: bfloat16 [768, 768], replicated, may hold values from -0.21875 to 0.21875
- w_out: bfloat16 [768, 768], replicated, may hold values from -6 to 6
- norm_gain2: float32 [768], replicated, may hold values from 0.5 to 1.5
- w_gate: bfloat16 [768, 2048], replicated, may hold values from -0.21875 to 0.21875
- w_up: bfloat16 [768, 2048], replicated, may hold values from -0.21875 to 0.21875
- w_down: bfloat16 [2048, 768], replicated, may hold values from -0.125 to 0.125
- cotangent: bfloat16 [2, 6, 1024, 768], P(None, 'items', 'band'), may hold values from -6 to 6
Outputs:
- outputs: bfloat16 [2, 6, 1024, 768], P(None, 'items', 'band')
- input_grad: bfloat16 [2, 6, 1024, 768], P(None, 'items', 'band')
- grad_gain1: float32 [768], replicated
- grad_query: float32 [768, 768], replicated
- grad_key: float32 [768, 768], replicated
- grad_value: float32 [768, 768], replicated
- grad_out: float32 [768, 768], replicated
- grad_gain2: float32 [768], replicated
- grad_gate: float32 [768, 2048], replicated
- grad_up: float32 [768, 2048], replicated
- grad_down: float32 [2048, 768], replicated
The draws below stay inside these ranges and needn't reach their ends.
Inputs may be any that keep to these rules, and one draw needn't show every extreme that they name: `counts`: the first item of every micro-batch has all 1024 patches valid; the last item of the last micro-batch has exactly 128.
All inputs are finite; a program needn't handle non-finite values.
Results may differ from the reference program's by a relative error of at most 0.02.
Values may be sent and summed in bfloat16 or wider, within the bound.
A program may use at most 256 MiB of HBM per device.

```python
import math
import jax
import jax.numpy as jnp
from jax import lax

HEADS = 12
HEAD_DIM = 64
D = 768
FF = 2048
MB = 2
LEN = 1024
SEQ = 6


def draw_counts(key, part):
    drawn = jax.random.randint(key, (MB, SEQ), LEN // 8, LEN + 1, dtype=jnp.int32)
    drawn = drawn.at[:, 0].set(LEN)
    drawn = drawn.at[MB - 1, SEQ - 1].set(LEN // 8)
    return drawn.astype(jnp.int32)


def level_of(rng, shape, shards, least, largest):
    level = 1.0
    for axis_at, parts in shards:
        heights = jax.random.uniform(jax.random.fold_in(jax.random.fold_in(rng, 6), axis_at), (parts,), jnp.float32, least / len(shards), largest / len(shards))
        level = level * jnp.repeat(jnp.exp(heights), shape[axis_at] // parts).reshape((-1,) + (1,) * (len(shape) - 1 - axis_at))
    return level


def normal_values(own_key, extent, scale, limit, cuts=(), held_as=jnp.bfloat16):
    values = scale * jax.random.normal(own_key, extent, jnp.float32)
    if cuts:
        values = values * level_of(own_key, extent, cuts, -0.22, 0.18)
    return jnp.clip(values, -limit, limit).astype(held_as)


def setup_inputs(seed: int = 0) -> dict:
    splits = jax.random.split(jax.random.key(seed), 13)
    return {
        "inputs": normal_values(splits[0], (MB, SEQ, LEN, D), 1.0, 6.0, ((1, 2), (2, 16))),
        "counts": draw_counts(jax.random.fold_in(splits[12], 71), 0),
        "norm_gain1": jnp.clip(1.0 + 0.1 * jax.random.normal(splits[2], (D,), jnp.float32), 0.5, 1.5),
        "w_query": normal_values(splits[3], (D, D), D ** -0.5, 0.21875),
        "w_key": normal_values(splits[4], (D, D), D ** -0.5, 0.21875),
        "w_value": normal_values(splits[5], (D, D), D ** -0.5, 0.21875),
        "w_out": normal_values(splits[6], (D, D), 1.0, 6.0),
        "norm_gain2": jnp.clip(1.0 + 0.1 * jax.random.normal(splits[7], (D,), jnp.float32), 0.5, 1.5),
        "w_gate": normal_values(splits[8], (D, FF), D ** -0.5, 0.21875),
        "w_up": normal_values(splits[9], (D, FF), D ** -0.5, 0.21875),
        "w_down": normal_values(splits[10], (FF, D), FF ** -0.5, 0.125),
        "cotangent": normal_values(splits[11], (MB, SEQ, LEN, D), 1.0, 6.0, ((1, 2), (2, 16))),
    }


@jax.custom_vjp
def low(v):
    return lax.optimization_barrier(v.astype(jnp.bfloat16)).astype(jnp.float32)

@jax.custom_vjp
def low_back(v):
    return v

def low_keep(v):
    return (low(v), None)

def low_pass(kept, grad):
    return (grad,)

def back_keep(v):
    return (v, None)

def back_low(kept, grad):
    return (low(grad),)
low.defvjp(low_keep, low_pass)
low_back.defvjp(back_keep, back_low)
EPS = 1e-06
HIGH = lax.Precision.HIGHEST

def exact(left, right):
    return jnp.dot(left, right, precision=HIGH)

def rms_scale(values, gain):
    return values * lax.rsqrt(lax.optimization_barrier(jnp.mean(values * values, axis=-1, keepdims=True)) + EPS) * gain

def layer(hidden, count, gain_one, wquery, wkey, wvalue, wout, gain_two, wgate, wupper, wdown):
    normed = low(rms_scale(hidden, gain_one))
    query = low_back(low(exact(normed, wquery))).reshape(LEN, HEADS, HEAD_DIM)
    key = low_back(low(exact(normed, wkey))).reshape(LEN, HEADS, HEAD_DIM)
    value = low_back(low(exact(normed, wvalue))).reshape(LEN, HEADS, HEAD_DIM)
    scale = 1.0 / math.sqrt(HEAD_DIM)
    logits = low_back(jnp.einsum('qhd,khd->hqk', query, key, precision=HIGH) * scale)
    live = jnp.arange(LEN, dtype=jnp.int32) < count
    logits = jnp.where(live[None, None, :], logits, -jnp.inf)
    prob = low(jax.nn.softmax(logits, axis=-1))
    attended = jnp.einsum('hqk,khd->qhd', prob, value, precision=HIGH).reshape(LEN, HEADS * HEAD_DIM)
    attended = low_back(low(attended))
    second = hidden + low_back(exact(attended, wout))
    normed_two = low(rms_scale(second, gain_two))
    gate = low_back(exact(normed_two, wgate))
    upper = low_back(exact(normed_two, wupper))
    mixed = low(jax.nn.gelu(gate, approximate=True) * upper)
    return second + low_back(exact(mixed, wdown))

def reference(inputs, counts, norm_gain1, w_query, w_key, w_value, w_out, norm_gain2, w_gate, w_up, w_down, cotangent):
    weights = tuple((w.astype(jnp.float32) for w in (norm_gain1, w_query, w_key, w_value, w_out, norm_gain2, w_gate, w_up, w_down)))
    flat_in = inputs.reshape(MB * SEQ, LEN, D)
    flat_counts = counts.reshape(MB * SEQ)
    flat_grad = cotangent.reshape(MB * SEQ, LEN, D)

    def visit(carry, item):
        block, count, grad_block = item

        def forward(hidden, *params):
            return layer(hidden, count, *params)
        result, pull = jax.vjp(forward, block.astype(jnp.float32), *weights)
        pulled = pull(grad_block.astype(jnp.float32))
        carry = tuple((total + part for total, part in zip(carry, pulled[1:])))
        return (carry, (result.astype(jnp.bfloat16), pulled[0].astype(jnp.bfloat16)))
    start = tuple((jnp.zeros(w.shape, jnp.float32) for w in weights))
    totals, (results, input_grads) = lax.scan(visit, start, (flat_in, flat_counts, flat_grad))
    outputs = results.reshape(MB, SEQ, LEN, D)
    input_grad = input_grads.reshape(MB, SEQ, LEN, D)
    return (outputs, input_grad, totals[0], totals[1], totals[2], totals[3], totals[4], totals[5], totals[6], totals[7], totals[8])
```

```python
import math

import jax
import jax.numpy as jnp
from jax import lax
from jax.experimental import pallas as pl
from jax.experimental.pallas import tpu as pltpu
from jax.sharding import PartitionSpec as P

HEADS = 12
HEAD_DIM = 64


EPS = 1e-06


def shortened(shard):

    def short(part):
        return part.astype(jnp.bfloat16) if part.dtype == jnp.float32 else part

    return jax.tree.map(short, shard)


def rms_scale(values, gain):
    return values * lax.rsqrt(jnp.mean(values * values, axis=-1, keepdims=True) + EPS) * gain


def gated(gate, upper):
    return jax.nn.gelu(gate, approximate=True) * upper


def outer(left, right):
    return lax.dot_general(
        left, right, (((0,), (0,)), ((), ())), preferred_element_type=jnp.float32
    )


def transposed(left, weight):
    return lax.dot_general(
        left, weight, (((1,), (1,)), ((), ())), preferred_element_type=jnp.float32
    )


def matmul(left, right):
    return jnp.dot(left, right, preferred_element_type=jnp.float32)


def scores(query, key, scale):
    return jnp.einsum("sqhd,skhd->shqk", query, key, preferred_element_type=jnp.float32) * scale


def per_device(
    inputs,
    counts,
    norm_gain1,
    w_query,
    w_key,
    w_value,
    w_out,
    norm_gain2,
    w_gate,
    w_up,
    w_down,
    cotangent,
):
    micro, seqs, band_rows, width = inputs.shape
    bands = lax.axis_size("band")
    length = band_rows * bands
    rows = seqs * band_rows
    heads = HEADS
    head_dim = HEAD_DIM
    scale = 1.0 / math.sqrt(head_dim)
    key_place = jnp.arange(length, dtype=jnp.int32)
    params = (norm_gain1, w_query, w_key, w_value, w_out, norm_gain2, w_gate, w_up, w_down)
    totals = [jnp.zeros(p.shape, jnp.float32) for p in params]
    results = []
    input_grads = []
    for number in range(micro):
        hidden = inputs[number].astype(jnp.float32).reshape(rows, width)
        lengths = counts[number]
        normed = rms_scale(hidden, norm_gain1).astype(jnp.bfloat16)
        query = matmul(normed, w_query).astype(jnp.bfloat16)
        key_local = matmul(normed, w_key).astype(jnp.bfloat16)
        value_local = matmul(normed, w_value).astype(jnp.bfloat16)
        query_four = query.reshape(seqs, band_rows, heads, head_dim)
        key_three = key_local.reshape(seqs, band_rows, width)
        value_three = value_local.reshape(seqs, band_rows, width)
        key_all, value_all = (
            lax.all_gather(key_three, "band", axis=1, tiled=True),
            lax.all_gather(value_three, "band", axis=1, tiled=True),
        )
        live = key_place[None, :] < lengths[:, None]
        key_four = key_all.reshape(seqs, length, heads, head_dim)
        value_four = value_all.reshape(seqs, length, heads, head_dim)
        logits = jnp.where(live[:, None, None, :], scores(query_four, key_four, scale), -jnp.inf)
        top = jnp.max(logits, axis=-1, keepdims=True)
        expo = jnp.exp(logits - top)
        summed = jnp.sum(expo, axis=-1, keepdims=True)
        log_total = top + jnp.log(summed)
        prob = (expo / summed).astype(jnp.bfloat16)
        attended = jnp.einsum(
            "shqk,skhd->sqhd", prob, value_four, preferred_element_type=jnp.float32
        )
        attended = attended.reshape(rows, width).astype(jnp.bfloat16)
        second = hidden + matmul(attended, w_out)
        normed_two = rms_scale(second, norm_gain2).astype(jnp.bfloat16)
        gate = matmul(normed_two, w_gate)
        upper = matmul(normed_two, w_up)
        mixed = gated(gate, upper).astype(jnp.bfloat16)
        results.append(
            (second + matmul(mixed, w_down)).astype(jnp.bfloat16).reshape(seqs, band_rows, width)
        )
        grad_rows = cotangent[number].reshape(rows, width)
        totals[8] = totals[8] + outer(mixed, grad_rows)
        d_mixed = transposed(grad_rows, w_down)
        pull_gate = jax.vjp(gated, gate, upper)[1]
        d_gate, d_upper = pull_gate(d_mixed)
        d_gate = d_gate.astype(jnp.bfloat16)
        d_upper = d_upper.astype(jnp.bfloat16)
        totals[6] = totals[6] + outer(normed_two, d_gate)
        totals[7] = totals[7] + outer(normed_two, d_upper)
        d_normed_two = transposed(d_gate, w_gate) + transposed(d_upper, w_up)
        pull_two = jax.vjp(rms_scale, second, norm_gain2)[1]
        d_second_norm, d_gain_two = pull_two(d_normed_two)
        totals[5] = totals[5] + d_gain_two
        d_second = grad_rows.astype(jnp.float32) + d_second_norm
        d_branch = d_second.astype(jnp.bfloat16)
        totals[4] = totals[4] + outer(attended, d_branch)
        d_attended = transposed(d_branch, w_out).astype(jnp.bfloat16)
        d_att_four = d_attended.reshape(seqs, band_rows, heads, head_dim)
        key_all, value_all = (
            lax.all_gather(key_three, "band", axis=1, tiled=True),
            lax.all_gather(value_three, "band", axis=1, tiled=True),
        )
        key_four = key_all.reshape(seqs, length, heads, head_dim)
        value_four = value_all.reshape(seqs, length, heads, head_dim)
        logits = jnp.where(live[:, None, None, :], scores(query_four, key_four, scale), -jnp.inf)
        prob_full = jnp.exp(logits - log_total)
        prob = prob_full.astype(jnp.bfloat16)
        d_prob = jnp.einsum(
            "sqhd,skhd->shqk", d_att_four, value_four, preferred_element_type=jnp.float32
        )
        delta = jnp.sum(d_prob * prob_full, axis=-1, keepdims=True)
        d_logits = (prob_full * (d_prob - delta)).astype(jnp.bfloat16)
        d_query = (
            jnp.einsum("shqk,skhd->sqhd", d_logits, key_four, preferred_element_type=jnp.float32)
            * scale
        )
        d_query = d_query.reshape(rows, width).astype(jnp.bfloat16)
        d_key_all = (
            jnp.einsum("shqk,sqhd->skhd", d_logits, query_four, preferred_element_type=jnp.float32)
            * scale
        )
        d_value_all = jnp.einsum(
            "shqk,sqhd->skhd", prob, d_att_four, preferred_element_type=jnp.float32
        )
        d_key_three, d_value_three = (
            lax.psum_scatter(
                d_key_all.reshape(seqs, length, width).astype(jnp.bfloat16),
                "band",
                scatter_dimension=1,
                tiled=True,
            ).astype(jnp.float32),
            lax.psum_scatter(
                d_value_all.reshape(seqs, length, width).astype(jnp.bfloat16),
                "band",
                scatter_dimension=1,
                tiled=True,
            ).astype(jnp.float32),
        )
        d_key = d_key_three.reshape(rows, width).astype(jnp.bfloat16)
        d_value = d_value_three.reshape(rows, width).astype(jnp.bfloat16)
        totals[1] = totals[1] + outer(normed, d_query)
        totals[2] = totals[2] + outer(normed, d_key)
        totals[3] = totals[3] + outer(normed, d_value)
        d_normed = (
            transposed(d_query, w_query) + transposed(d_key, w_key) + transposed(d_value, w_value)
        )
        pull_one = jax.vjp(rms_scale, hidden, norm_gain1)[1]
        d_hidden_norm, d_gain_one = pull_one(d_normed)
        totals[0] = totals[0] + d_gain_one
        input_grads.append(
            (d_second + d_hidden_norm).astype(jnp.bfloat16).reshape(seqs, band_rows, width)
        )
    shares = jax.tree.map(
        lambda part: part.astype(jnp.float32),
        lax.psum_scatter(shortened(tuple(totals)), "band", scatter_dimension=0, tiled=True),
    )
    summed_shares = jax.tree.map(
        lambda part: part.astype(jnp.float32), lax.psum(shortened(shares), "items")
    )
    whole = jax.tree.map(
        lambda part, own: part.astype(own.dtype),
        lax.all_gather(shortened(summed_shares), "band", axis=0, tiled=True),
        summed_shares,
    )
    return (jnp.stack(results), jnp.stack(input_grads)) + tuple(whole)


MESH_ID = pl.DeviceIdType.MESH
NEG = -1e30
BF = jnp.bfloat16
F32 = jnp.float32


def place():
    item = lax.axis_index("items")
    band = lax.axis_index("band")
    return item, band // 4, band % 4


def flip(value):
    return value + 1 - 2 * (value % 2)


def far(value):
    return (value + 2) % 4


def greet(peers):
    barrier = pltpu.get_barrier_semaphore()
    for peer in peers:
        pl.semaphore_signal(barrier, inc=1, device_id=peer, device_id_type=MESH_ID)
    pl.semaphore_wait(barrier, len(peers))


def remote(src, dst, send, recv, peer):
    return pltpu.make_async_remote_copy(
        src_ref=src, dst_ref=dst, send_sem=send, recv_sem=recv, device_id=peer, device_id_type=MESH_ID
    )


def params(number, vmem=40):
    return pltpu.CompilerParams(
        collective_id=number, has_side_effects=True, vmem_limit_bytes=vmem << 20
    )


ANY = pl.BlockSpec(memory_space=pl.ANY)
VMEM = pl.BlockSpec(memory_space=pltpu.VMEM)
SMEM = pl.BlockSpec(memory_space=pltpu.SMEM)


def gather_kernel(x_ref, out_ref, z_send, f_send, g_send, recv, own_sem):
    item, z, g = place()
    gc, gx = flip(g), far(g)
    gcx = far(gc)
    zs = (z, flip(z), far(z), far(flip(z)))
    core, across = (item, z * 4 + gc), (item, z * 4 + gx)
    greet([core, across] + [(item, s * 4 + g) for s in zs[1:]])

    def items_of(s):
        return (3 * (s // 2) + 2 * (s % 2), 3 * (s // 2) + 1)

    started = []
    for n, s in enumerate(zs[1:]):
        for ab in range(2):
            copy = remote(
                x_ref.at[items_of(s)[ab]],
                out_ref.at[ab, z * 4 + g],
                z_send.at[n, ab],
                recv.at[ab, z * 4 + g],
                (item, s * 4 + g),
            )
            copy.start()
            started.append(copy)
    local = []
    for ab in range(2):
        copy = pltpu.make_async_copy(
            x_ref.at[items_of(z)[ab]], out_ref.at[ab, z * 4 + g], own_sem.at[ab]
        )
        copy.start()
        local.append(copy)

    def arrived(ab, where):
        remote(
            out_ref.at[ab, where], out_ref.at[ab, where], z_send.at[0, 0], recv.at[ab, where], core
        ).wait_recv()

    for n, zz in enumerate(zs):
        for ab in range(2):
            where = zz * 4 + g
            if n > 0:
                arrived(ab, where)
            src = x_ref.at[items_of(z)[ab]] if n == 0 else out_ref.at[ab, where]
            for k, peer in enumerate((across, core)):
                copy = remote(
                    src, out_ref.at[ab, where], f_send.at[n, ab, k], recv.at[ab, where], peer
                )
                copy.start()
                started.append(copy)
    for n, zz in enumerate(zs):
        for ab in range(2):
            where = zz * 4 + gx
            arrived(ab, where)
            copy = remote(
                out_ref.at[ab, where],
                out_ref.at[ab, where],
                g_send.at[n, ab],
                recv.at[ab, where],
                core,
            )
            copy.start()
            started.append(copy)
    for n, zz in enumerate(zs):
        for ab in range(2):
            arrived(ab, zz * 4 + gc)
            arrived(ab, zz * 4 + gcx)
    for copy in local:
        copy.wait()
    for copy in started:
        copy.wait_send()


def gather_rows(x6):
    _, rows, width = x6.shape
    dma = pltpu.SemaphoreType.DMA
    return pl.pallas_call(
        gather_kernel,
        out_shape=jax.ShapeDtypeStruct((2, 16, rows, width), BF),
        in_specs=[ANY],
        out_specs=ANY,
        scratch_shapes=[dma((3, 2)), dma((4, 2, 2)), dma((4, 2)), dma((2, 16)), dma((2,))],
        compiler_params=params(1),
        name="gather_rows",
    )(x6)


def to_slots(item, z, g, src_ref, dst_ref, send, recv, own_sem):
    zs = (z, flip(z), far(z), far(flip(z)))
    p, r = z // 2, z % 2
    started = []
    for n, s in enumerate(zs[1:]):
        copy = remote(
            src_ref.at[3 * (s // 2) + 2 * (s % 2)],
            dst_ref.at[z],
            send.at[n],
            recv.at[z],
            (item, s * 4 + g),
        )
        copy.start()
        started.append(copy)
    copy = remote(
        src_ref.at[3 * (1 - p) + 1], dst_ref.at[4 + p], send.at[3], recv.at[4 + p], (item, far(z) * 4 + g)
    )
    copy.start()
    started.append(copy)
    local = [
        pltpu.make_async_copy(src_ref.at[3 * p + 2 * r], dst_ref.at[z], own_sem.at[0]),
        pltpu.make_async_copy(src_ref.at[3 * p + 1], dst_ref.at[4 + p], own_sem.at[1]),
    ]
    for copy in local:
        copy.start()

    def finish():
        for where in zs[1:] + (4 + (1 - p),):
            remote(
                dst_ref.at[where], dst_ref.at[where], send.at[0], recv.at[where], (item, far(z) * 4 + g)
            ).wait_recv()
        for copy in local:
            copy.wait()
        for copy in started:
            copy.wait_send()

    return finish


def from_slots(item, z, g, src_ref, dst_ref, send, recv, own_sem):
    zs = (z, flip(z), far(z), far(flip(z)))
    p, r = z // 2, z % 2
    mine = 3 * p + 2 * r
    started = []
    for n, s in enumerate(zs[1:]):
        copy = remote(src_ref.at[s], dst_ref.at[mine], send.at[n], recv.at[mine], (item, s * 4 + g))
        copy.start()
        started.append(copy)
    copy = remote(
        src_ref.at[4 + (1 - p)],
        dst_ref.at[3 * p + 1],
        send.at[3],
        recv.at[3 * p + 1],
        (item, far(z) * 4 + g),
    )
    copy.start()
    started.append(copy)
    local = [
        pltpu.make_async_copy(src_ref.at[z], dst_ref.at[mine], own_sem.at[0]),
        pltpu.make_async_copy(src_ref.at[4 + p], dst_ref.at[3 * p + 1], own_sem.at[1]),
    ]
    for copy in local:
        copy.start()

    def finish():
        for s in zs[1:]:
            where = 3 * (s // 2) + 2 * (s % 2)
            remote(
                dst_ref.at[where], dst_ref.at[where], send.at[0], recv.at[where], (item, far(z) * 4 + g)
            ).wait_recv()
        where = 3 * (1 - p) + 1
        remote(
            dst_ref.at[where], dst_ref.at[where], send.at[0], recv.at[where], (item, far(z) * 4 + g)
        ).wait_recv()
        for copy in local:
            copy.wait()
        for copy in started:
            copy.wait_send()

    return finish


def z_peers(item, z, g):
    return [(item, s * 4 + g) for s in (flip(z), far(z), far(flip(z)))]


def g_peers(item, z, g):
    return [(item, z * 4 + h) for h in (flip(g), far(g), far(flip(g)))]


def swap_heads(item, z, g, src_ref, dst_ref, send, recv, own_sem):
    started = []
    for n, h in enumerate((far(g), far(flip(g)), flip(g))):
        copy = remote(src_ref.at[h], dst_ref.at[g], send.at[n], recv.at[g], (item, z * 4 + h))
        copy.start()
        started.append(copy)
    local = pltpu.make_async_copy(src_ref.at[g], dst_ref.at[g], own_sem)
    local.start()

    def finish():
        for h in (flip(g), far(g), far(flip(g))):
            remote(
                dst_ref.at[h], dst_ref.at[h], send.at[0], recv.at[h], (item, z * 4 + h)
            ).wait_recv()
        local.wait()
        for copy in started:
            copy.wait_send()

    return finish


def swap_kernel(heads_ref, rows_ref, out_heads_ref, out_rows_ref, hs, hr, ho, zs, zr, zo):
    item, z, g = place()
    greet(z_peers(item, z, g) + g_peers(item, z, g))
    first = swap_heads(item, z, g, heads_ref, out_heads_ref, hs, hr, ho.at[0])
    second = to_slots(item, z, g, rows_ref, out_rows_ref, zs, zr, zo)
    first()
    second()


def swap_out(heads, rows):
    dma = pltpu.SemaphoreType.DMA
    return pl.pallas_call(
        swap_kernel,
        out_shape=(
            jax.ShapeDtypeStruct(heads.shape, heads.dtype),
            jax.ShapeDtypeStruct(rows.shape, rows.dtype),
        ),
        in_specs=[ANY, ANY],
        out_specs=(ANY, ANY),
        scratch_shapes=[dma((3,)), dma((4,)), dma((1,)), dma((4,)), dma((6,)), dma((2,))],
        compiler_params=params(2),
        name="swap_out",
    )(heads, rows)


def swap_back_kernel(heads_ref, out_heads_ref, hs, hr, ho):
    item, z, g = place()
    greet(g_peers(item, z, g))
    swap_heads(item, z, g, heads_ref, out_heads_ref, hs, hr, ho.at[0])()


def swap_back(heads):
    dma = pltpu.SemaphoreType.DMA
    return pl.pallas_call(
        swap_back_kernel,
        out_shape=jax.ShapeDtypeStruct(heads.shape, heads.dtype),
        in_specs=[ANY],
        out_specs=ANY,
        scratch_shapes=[dma((3,)), dma((4,)), dma((1,))],
        compiler_params=params(3),
        name="swap_back",
    )(heads)


def lanes_of(rows):
    return lax.broadcasted_iota(jnp.int32, (rows, 128), 1)


def nt(left, right):
    return lax.dot_general(left, right, (((1,), (1,)), ((), ())), preferred_element_type=F32)


def forward_kernel(
    scal_ref, x_ref, gain_ref, wc_ref,
    osend_ref, xn_ref, q_ref, k_ref, v_ref, kt_ref, o01_ref, o2_ref,
):
    r = scal_ref[2]
    lane = lanes_of(256)
    low = lane < 64

    @pl.loop(0, 8)
    def _(i):
        rows = pl.ds(pl.multiple_of(i * 256, 256), 256)
        h = x_ref[rows, :].astype(F32)
        inv = lax.rsqrt(jnp.mean(h * h, axis=-1, keepdims=True) + EPS)
        xn = (h * inv * gain_ref[...]).astype(BF)
        xn_ref[rows, :] = xn
        y = matmul(xn, wc_ref[:, 128:512])
        count = scal_ref[i // 4]
        at = lax.broadcasted_iota(jnp.int32, (256, 128), 0) + (i % 4) * 256
        bias = jnp.where(at < count, 0.0, NEG)
        one = jnp.where((lane % 64) < 4, 1.0, 0.0)
        k_aug = jnp.where(lane % 64 == 0, bias, one)
        k01, v01, kv2 = y[:, :128], y[:, 128:256], y[:, 256:]
        k_ref[0, rows, :] = jnp.where(low, k01, k_aug).astype(BF)
        k_ref[1, rows, :] = jnp.where(low, k_aug, k01).astype(BF)
        k_ref[2, rows, :] = jnp.where(low, kv2, k_aug).astype(BF)
        v_ref[0, rows, :] = jnp.where(low, v01, one).astype(BF)
        v_ref[1, rows, :] = jnp.where(low, one, v01).astype(BF)
        v_ref[2, rows, :] = jnp.where(low, one, kv2).astype(BF)

    for head in range(3):
        for ab in range(2):
            kt_ref[head, ab, :, :] = k_ref[head, ab * 1024 : (ab + 1) * 1024, :].T

    @pl.loop(0, 6)
    def _(t):
        off = jnp.where(t < 4, t, 4 + r + 2 * (t - 4)) * 256
        xq = xn_ref[pl.ds(pl.multiple_of(off, 256), 256), :]
        q01 = matmul(xq, wc_ref[:, 0:128]).astype(BF).astype(F32) * 0.125
        q2 = matmul(xq, wc_ref[:, 512:640]).astype(BF).astype(F32) * 0.125
        flag = jnp.where(lane % 64 == 0, 1.0, 0.0)
        qs = (jnp.where(low, q01, flag), jnp.where(low, flag, q01), jnp.where(low, q2, flag))
        at = pl.ds(pl.multiple_of(t * 256, 256), 256)
        ab = t // 4
        keys = pl.ds(pl.multiple_of(ab * 1024, 1024), 1024)
        outs = []
        for head in range(3):
            s = matmul(qs[head].astype(BF), kt_ref[head, ab])
            top = jnp.max(s, axis=1, keepdims=True)
            e = jnp.exp(s - top).astype(BF)
            o = matmul(e, v_ref[head, keys, :])
            total = o[:, 64:65] if head == 0 else o[:, 0:1]
            outs.append(o / total)
            lse = -(top + jnp.log(total))
            hi = lse.astype(BF).astype(F32)
            mid = (lse - hi).astype(BF).astype(F32)
            lo = lse - hi - mid
            part = lane % 64
            aug = jnp.where(part == 1, hi, jnp.where(part == 2, mid, jnp.where(part == 3, lo, flag)))
            data = low if head != 1 else jnp.logical_not(low)
            q_ref[head, at, :] = jnp.where(data, qs[head], aug).astype(BF)
        o01 = jnp.where(low, outs[0], outs[1])
        o2 = outs[2]
        o01_ref[at, :] = o01
        o2_ref[at, :] = o2
        for h in range(4):
            osend_ref[h, t, 0:64, :] = o01[h * 64 : h * 64 + 64].astype(BF)
            first = o2[h * 64 : h * 64 + 32]
            second = o2[h * 64 + 32 : h * 64 + 64]
            folded = jnp.where(low[:32], pltpu.roll(first, 64, 1), second)
            osend_ref[h, t, 64:96, :] = folded.astype(BF)


def forward_attention(scal, xall, gain, wc):
    s = jax.ShapeDtypeStruct
    return pl.pallas_call(
        forward_kernel,
        out_shape=(
            s((4, 6, 96, 128), BF), s((2048, 768), BF), s((3, 1536, 128), BF), s((3, 2048, 128), BF),
            s((3, 2048, 128), BF), s((3, 2, 128, 1024), BF), s((1536, 128), F32), s((1536, 128), F32),
        ),
        in_specs=[SMEM, VMEM, VMEM, VMEM],
        out_specs=(VMEM,) * 8,
        compiler_params=pltpu.CompilerParams(vmem_limit_bytes=50 << 20),
        name="forward_attention",
    )(scal, xall, gain, wc)


def backward_kernel(
    scal_ref, q_ref, k_ref, v_ref, kt_ref, o01_ref, o2_ref, do_ref, xn_ref, wc_ref,
    p_ref, gw_ref, dk_ref, dv_ref, d5_ref,
):
    r = scal_ref[2]
    lane = lanes_of(256)
    low = lane < 64
    part = lane % 64
    dk_ref[...] = jnp.zeros_like(dk_ref)
    dv_ref[...] = jnp.zeros_like(dv_ref)
    d5_ref[...] = jnp.zeros_like(d5_ref)

    def pieces(delta):
        neg = -delta
        hi = neg.astype(BF).astype(F32)
        mid = (neg - hi).astype(BF).astype(F32)
        lo = neg - hi - mid
        return jnp.where(part == 1, hi, jnp.where(part == 2, mid, jnp.where(part == 3, lo, 0.0)))

    @pl.loop(0, 6)
    def _(t):
        at = pl.ds(pl.multiple_of(t * 256, 256), 256)
        ab = t // 4
        keys = pl.ds(pl.multiple_of(ab * 1024, 1024), 1024)
        do01 = do_ref[:, t, 0:64, :].astype(F32).reshape(256, 128)
        folded = do_ref[:, t, 64:96, :].astype(F32)
        two = []
        for h in range(4):
            two.append(pltpu.roll(folded[h], 64, 1))
            two.append(folded[h])
        do2 = jnp.concatenate(two, axis=0)
        prod = do01 * o01_ref[at, :]
        prod2 = do2 * o2_ref[at, :]
        delta0 = jnp.sum(jnp.where(low, prod, 0.0), axis=1, keepdims=True)
        delta1 = jnp.sum(jnp.where(low, 0.0, prod), axis=1, keepdims=True)
        delta2 = jnp.sum(jnp.where(low, 0.0, prod2), axis=1, keepdims=True)
        dos = (
            jnp.where(low, do01, pieces(delta0)).astype(BF),
            jnp.where(low, pieces(delta1), do01).astype(BF),
            jnp.where(low, pieces(delta2), do2).astype(BF),
        )
        dqs = []
        for head in range(3):
            q = q_ref[head, at, :]
            prob = jnp.exp(nt(k_ref[head, keys, :], q))
            d_prob = nt(v_ref[head, keys, :], dos[head])
            d_log = (prob * d_prob).astype(BF)
            dv_ref[head, keys, :] += matmul(prob.astype(BF), dos[head])
            dk_ref[head, keys, :] += matmul(d_log, q)
            dqs.append(matmul(kt_ref[head, ab], d_log).T * 0.125)
        off = jnp.where(t < 4, t, 4 + r + 2 * (t - 4)) * 256
        rows = pl.ds(pl.multiple_of(off, 256), 256)
        d5_ref[rows, 0:128] = jnp.where(low, dqs[0], dqs[1]).astype(BF)
        d5_ref[rows, 512:640] = jnp.where(low, dqs[2], 0.0).astype(BF)

    @pl.loop(0, 8)
    def _(i):
        rows = pl.ds(pl.multiple_of(i * 256, 256), 256)
        d5_ref[rows, 128:256] = jnp.where(low, dk_ref[0, rows, :], dk_ref[1, rows, :]).astype(BF)
        d5_ref[rows, 256:384] = jnp.where(low, dv_ref[0, rows, :], dv_ref[1, rows, :]).astype(BF)
        d5_ref[rows, 384:512] = jnp.where(low, dk_ref[2, rows, :], dv_ref[2, rows, :]).astype(BF)
        d_xn = nt(d5_ref[rows, :], wc_ref[...]).astype(BF)
        for h in range(4):
            p_ref[h, i, :, :] = d_xn[h * 64 : h * 64 + 64]

    for c in range(5):
        cols = slice(c * 128, c * 128 + 128)
        gw_ref[:, cols] = outer(xn_ref[...], d5_ref[:, cols]).astype(BF)


def backward_attention(scal, q, k, v, kt, o01, o2, do, xn, wc):
    s = jax.ShapeDtypeStruct
    return pl.pallas_call(
        backward_kernel,
        out_shape=(s((4, 8, 64, 768), BF), s((768, 640), BF)),
        in_specs=[SMEM] + [VMEM] * 9,
        out_specs=(VMEM,) * 2,
        scratch_shapes=[
            pltpu.VMEM((3, 2048, 128), F32), pltpu.VMEM((3, 2048, 128), F32), pltpu.VMEM((2048, 640), BF),
        ],
        compiler_params=pltpu.CompilerParams(vmem_limit_bytes=56 << 20),
        name="backward_attention",
    )(scal, q, k, v, kt, o01, o2, do, xn, wc)


def reduce_kernel(
    p_ref, res_ref, out_ref, res_out_ref,
    rc_ref, sx_ref, rx_ref, t_ref, zb_ref, rz_ref,
    c_send, c_recv, x_send, x_recv, z_send, z_recv, rs_send, rs_recv, rs_own,
):
    item, z, g = place()
    gc, gx = flip(g), far(g)
    gcx = far(gc)
    r = z % 2
    core, across, pair = (item, z * 4 + gc), (item, z * 4 + gx), (item, flip(z) * 4 + g)
    greet([core, across] + z_peers(item, z, g))
    halves = ((1, slice(4, 8)), (0, slice(0, 4)))
    c_copies = {}
    for k, h in ((1, gcx), (0, gc)):
        for ab, cut in halves:
            c_copies[k, ab] = remote(
                p_ref.at[h, cut], rc_ref.at[k, cut], c_send.at[k, ab], c_recv.at[k, ab], core
            )
            c_copies[k, ab].start()
    done_rs = from_slots(item, z, g, res_ref, res_out_ref, rs_send, rs_recv, rs_own)
    x_copies = {}
    for ab, cut in halves:
        c_copies[1, ab].wait_recv()

        @pl.loop(0, 4)
        def _(j):
            n = ab * 4 + j
            sx_ref[n] = (p_ref[gx, n].astype(F32) + rc_ref[1, n].astype(F32)).astype(BF)

        x_copies[ab] = remote(sx_ref.at[cut], rx_ref.at[cut], x_send.at[ab], x_recv.at[ab], across)
        x_copies[ab].start()
    z_copy = None
    for ab, cut in halves:
        c_copies[0, ab].wait_recv()

        @pl.loop(0, 4)
        def _(j):
            n = ab * 4 + j
            t_ref[n] = p_ref[g, n].astype(F32) + rc_ref[0, n].astype(F32)

        x_copies[ab].wait_recv()
        if ab == 1:
            for q in range(2):
                n = 4 + (1 - r) + 2 * q
                zb_ref[q] = (t_ref[n] + rx_ref[n].astype(F32)).astype(BF)
            z_copy = remote(zb_ref, rz_ref, z_send.at[0], z_recv.at[0], pair)
            z_copy.start()
        else:

            @pl.loop(0, 4)
            def _(j):
                out_ref[j] = t_ref[j] + rx_ref[j].astype(F32)

    z_copy.wait_recv()
    for q in range(2):
        n = 4 + r + 2 * q
        out_ref[4 + q] = t_ref[n] + rx_ref[n].astype(F32) + rz_ref[q].astype(F32)
    done_rs()
    z_copy.wait_send()
    for copy in list(c_copies.values()) + list(x_copies.values()):
        copy.wait_send()


def reduce_rows(p, results):
    dma = pltpu.SemaphoreType.DMA
    s = jax.ShapeDtypeStruct
    rows, width = p.shape[2:]
    return pl.pallas_call(
        reduce_kernel,
        out_shape=(s((6, rows, width), F32), s(results.shape, results.dtype)),
        in_specs=[VMEM, ANY],
        out_specs=(VMEM, ANY),
        scratch_shapes=[
            pltpu.VMEM((2, 8, rows, width), BF), pltpu.VMEM((8, rows, width), BF), pltpu.VMEM((8, rows, width), BF),
            pltpu.VMEM((8, rows, width), F32), pltpu.VMEM((2, rows, width), BF), pltpu.VMEM((2, rows, width), BF),
            dma((2, 2)), dma((2, 2)), dma((2,)), dma((2,)), dma((1,)), dma((1,)), dma((4,)), dma((6,)), dma((2,)),
        ],
        compiler_params=params(4),
        name="reduce_rows",
    )(p, results)


def home_kernel(rows_ref, out_ref, send, recv, own):
    item, z, g = place()
    greet(z_peers(item, z, g))
    from_slots(item, z, g, rows_ref, out_ref, send, recv, own)()


def send_home(rows):
    dma = pltpu.SemaphoreType.DMA
    return pl.pallas_call(
        home_kernel,
        out_shape=jax.ShapeDtypeStruct(rows.shape, rows.dtype),
        in_specs=[ANY],
        out_specs=ANY,
        scratch_shapes=[dma((4,)), dma((6,)), dma((2,))],
        compiler_params=params(5),
        name="send_home",
    )(rows)


class Stream:
    def __init__(self, src, res, acc, first, rest, sems, order, coords, core):
        self.src, self.res, self.acc, self.first, self.rest = src, res, acc, first, rest
        self.send, self.recv, self.own, self.back, self.got, self.fwd, self.fgot = sems
        self.rows, self.half = acc.shape
        self.order = [coords[name] for name in order]
        bit, self.peer = core
        self.mine = pl.ds(pl.multiple_of(bit * self.half, 128), self.half)
        self.other = pl.ds(pl.multiple_of((1 - bit) * self.half, 128), self.half)
        self.base, self.size = [0], [self.rows]
        for bit, _ in self.order:
            self.size.append(self.size[-1] // 2)
            self.base.append(self.base[-1] + bit * self.size[-1])
        self.waits = []

    def go(self, copy):
        copy.start()
        self.waits.append(copy)
        return copy

    def part(self, base, size):
        return pl.ds(pl.multiple_of(base, 16), size)

    def spot(self, k):
        return self.rest.at[pl.ds(self.rows - 2 * self.size[k], self.size[k])]

    def open(self):
        self.local = pltpu.make_async_copy(self.src.at[:, self.mine], self.acc, self.own.at[0])
        self.local.start()
        self.pending = self.go(
            remote(self.src.at[:, self.other], self.first, self.send.at[0], self.recv.at[0], self.peer)
        )

    def add(self, base, size, other, at):
        step = 64 if size % 64 == 0 else 48

        @pl.loop(0, size // step)
        def _(n):
            rows = self.part(base + n * step, step)
            more = other[pl.ds(pl.multiple_of(at + n * step, 16), step), :]
            self.acc[rows, :] = (self.acc[rows, :].astype(F32) + more.astype(F32)).astype(BF)

    def fold(self, k):
        if k == 0:
            self.local.wait()
        self.pending.wait_recv()
        if k == 0:
            self.add(0, self.rows, self.first, 0)
        else:
            self.add(self.base[k], self.size[k], self.rest, self.rows - 2 * self.size[k])

    def push(self, k):
        bit, peer = self.order[k - 1]
        away = self.base[k - 1] + (1 - bit) * self.size[k]
        self.pending = self.go(
            remote(
                self.acc.at[self.part(away, self.size[k])],
                self.spot(k),
                self.send.at[k],
                self.recv.at[k],
                peer,
            )
        )

    def spread(self, k):
        deep = len(self.order)
        here = self.part(self.base[k], self.size[k])
        block = self.res.at[here, self.mine]
        if k == deep:
            src = self.acc.at[here]
            self.local = pltpu.make_async_copy(src, block, self.own.at[1])
            self.local.start()
            self.go(remote(src, block, self.fwd.at[0], self.fgot.at[0], self.peer))
        else:
            src = block
        _, peer = self.order[k - 1]
        self.go(remote(src, block, self.back.at[k - 1], self.got.at[k - 1], peer))

    def sibling(self, k):
        bit, _ = self.order[k - 1]
        return self.part(self.base[k - 1] + (1 - bit) * self.size[k], self.size[k])

    def collect(self, k):
        deep = len(self.order)
        block = self.res.at[self.sibling(k), self.mine]
        remote(block, block, self.back.at[k - 1], self.got.at[k - 1], self.peer).wait_recv()
        if k == deep:
            self.local.wait()
        self.go(remote(block, block, self.fwd.at[k], self.fgot.at[k], self.peer))

    def close(self):
        deep = len(self.order)
        for k in range(deep + 1):
            rows = self.part(self.base[deep], self.size[deep]) if k == 0 else self.sibling(k)
            block = self.res.at[rows, self.other]
            remote(block, block, self.fwd.at[k], self.fgot.at[k], self.peer).wait_recv()
        for copy in self.waits:
            copy.wait_send()


class Grouped(Stream):
    def __init__(self, src, res, acc, rest, sems, order, coords, core, group, across):
        super().__init__(src, res, acc, None, rest, sems, order, coords, core)
        self.group, self.gx, self.across = group, far(group), across

    def open(self):
        self.local = pltpu.make_async_copy(self.src, self.acc, self.own.at[0])
        self.local.start()

    def fold(self, k):
        if k == 0:
            self.local.wait()
            return
        super().fold(k)

    def spread(self, k):
        deep = len(self.order)
        here = self.part(self.base[k], self.size[k])
        _, peer = self.order[k - 1]
        if k == deep:
            src, block = self.acc.at[here], self.res.at[self.group, here]
            self.local = pltpu.make_async_copy(src, block, self.own.at[1])
            self.local.start()
            self.go(remote(src, block, self.fwd.at[0, 0], self.fgot.at[0, 0], self.peer))
            self.go(remote(src, block, self.back.at[deep, 0], self.got.at[deep, 0], self.across))
            self.go(remote(src, block, self.back.at[k - 1, 0], self.got.at[k - 1, 0], peer))
            theirs = self.res.at[self.gx, here]
            remote(
                theirs, theirs, self.back.at[deep, 0], self.got.at[deep, 0], self.across
            ).wait_recv()
            self.go(remote(theirs, theirs, self.fwd.at[0, 1], self.fgot.at[0, 1], self.peer))
            self.go(remote(theirs, theirs, self.back.at[k - 1, 1], self.got.at[k - 1, 1], peer))
            return
        for n, h in enumerate((self.group, self.gx)):
            block = self.res.at[h, here]
            self.go(remote(block, block, self.back.at[k - 1, n], self.got.at[k - 1, n], peer))

    def collect(self, k):
        deep = len(self.order)
        for n, h in enumerate((self.group, self.gx)):
            block = self.res.at[h, self.sibling(k)]
            remote(block, block, self.back.at[k - 1, n], self.got.at[k - 1, n], self.peer).wait_recv()
            self.go(remote(block, block, self.fwd.at[k, n], self.fgot.at[k, n], self.peer))
        if k == deep:
            self.local.wait()

    def close(self):
        deep = len(self.order)
        for k in range(deep + 1):
            rows = self.part(self.base[deep], self.size[deep]) if k == 0 else self.sibling(k)
            for n, h in enumerate((flip(self.group), far(flip(self.group)))):
                block = self.res.at[h, rows]
                remote(block, block, self.fwd.at[k, n], self.fgot.at[k, n], self.peer).wait_recv()
        for copy in self.waits:
            copy.wait_send()


ORDERS = (("x", "y", "zl", "zh"), ("y", "zl", "x", "zh"), ("zl", "x", "y", "zh"), ("y", "x", "zl", "zh"))
GROUP_ORDER = ("zl", "y", "zh")


def weights_kernel(*refs):
    take = iter(refs)
    srcs = [next(take) for _ in range(5)]
    gains = next(take)
    outs = [next(take) for _ in range(5)]
    gains_out = next(take)
    item, z, g = place()
    coords = {
        "x": (g // 2, (item, z * 4 + far(g))),
        "y": (item, (1 - item, z * 4 + g)),
        "zl": (z % 2, (item, flip(z) * 4 + g)),
        "zh": (z // 2, (item, far(z) * 4 + g)),
    }
    core = (g % 2, (item, z * 4 + flip(g)))
    greet([core[1]] + [peer for _, peer in coords.values()])
    streams = []
    for n in range(4):
        acc, first, rest = (next(take) for _ in range(3))
        sems = [next(take) for _ in range(7)]
        streams.append(Stream(srcs[n], outs[n], acc, first, rest, sems, ORDERS[n], coords, core))
    acc, rest = (next(take) for _ in range(2))
    sems = [next(take) for _ in range(7)]
    streams.append(
        Grouped(srcs[4], outs[4], acc, rest, sems, GROUP_ORDER, coords, core, g, coords["x"][1])
    )
    buf, got, gain_send, gain_recv = (next(take) for _ in range(4))
    for stream in streams:
        stream.open()
    buf[0] = gains[...]
    gain_peers = [core[1]] + [peer for _, peer in coords.values()]
    gain_waits = []

    def gain_step(k):
        if k > 0:
            gain_waits[k - 1].wait_recv()
            buf[k] = buf[k - 1] + got[k - 1]
        if k < 5:
            copy = remote(buf.at[k], got.at[k], gain_send.at[k], gain_recv.at[k], gain_peers[k])
            copy.start()
            gain_waits.append(copy)

    for k in range(5):
        gain_step(k)
        for stream in streams:
            deep = len(stream.order)
            if k <= deep:
                stream.fold(k)
                if k < deep:
                    stream.push(k + 1)
                else:
                    stream.spread(deep)
    gain_step(5)
    gains_out[...] = buf[5]
    for k in range(4, 0, -1):
        for stream in streams:
            deep = len(stream.order)
            if k <= deep:
                stream.collect(k)
                if k > 1:
                    stream.spread(k - 1)
    for stream in streams:
        stream.close()
    for copy in gain_waits:
        copy.wait_send()


def reduce_weights(arrays, qkv, gains):
    dma = pltpu.SemaphoreType.DMA
    s = jax.ShapeDtypeStruct
    shapes = tuple(s(a.shape, BF) for a in arrays) + (s((4,) + qkv.shape, BF), s(gains.shape, F32))
    scratch = []
    for a in arrays:
        rows, half = a.shape[0], a.shape[1] // 2
        scratch += [pltpu.VMEM((rows, half), BF)] * 3
        scratch += [dma((5,)), dma((5,)), dma((2,)), dma((4,)), dma((4,)), dma((5,)), dma((5,))]
    scratch += [pltpu.VMEM(qkv.shape, BF)] * 2
    scratch += [dma((4,)), dma((4,)), dma((2,)), dma((4, 2)), dma((4, 2)), dma((4, 2)), dma((4, 2))]
    scratch += [pltpu.VMEM((6,) + gains.shape, F32), pltpu.VMEM((5,) + gains.shape, F32), dma((5,)), dma((5,))]
    return pl.pallas_call(
        weights_kernel,
        out_shape=shapes,
        in_specs=[ANY] * 5 + [VMEM],
        out_specs=(ANY,) * 5 + (VMEM,),
        scratch_shapes=scratch,
        compiler_params=params(6, 50),
        name="reduce_weights",
    )(*arrays, qkv, gains)


def fast(
    inputs, counts, norm_gain1, w_query, w_key, w_value, w_out, norm_gain2, w_gate, w_up, w_down, cotangent
):
    micro, seqs, band_rows, width = inputs.shape
    _, z, g = place()
    p, r = z // 2, z % 2
    xall = gather_rows(inputs.reshape(6, band_rows, width))
    flat_counts = counts.reshape(6)
    scal = jnp.stack([flat_counts[3 * p + 2 * r], flat_counts[3 * p + 1], r]).astype(jnp.int32)

    def cut(weight):
        return lax.dynamic_slice(weight, (0, g * 192), (width, 192))

    wq, wk, wv = cut(w_query), cut(w_key), cut(w_value)
    wc = jnp.concatenate(
        [wq[:, :128], wk[:, :128], wv[:, :128], wk[:, 128:], wv[:, 128:], wq[:, 128:], jnp.zeros((width, 64), BF)],
        axis=1,
    )
    osend, xn, q, k, v, kt, o01, o2 = forward_attention(
        scal, xall.reshape(2048, width), norm_gain1.reshape(1, width), wc
    )
    orecv, dy6 = swap_out(osend, cotangent.reshape(6, band_rows, width))
    o_first = orecv[:, :, :64, :]
    o_last = orecv[:, :, 64:, :].reshape(4, 6, 32, 2, 64).transpose(0, 1, 3, 2, 4).reshape(4, 6, 64, 64)
    attended = jnp.concatenate([o_first, o_last], axis=-1).transpose(1, 2, 0, 3).reshape(384, width)
    rows_a = lax.dynamic_index_in_dim(xall[0].reshape(4, 4, 64, width), g, 1, keepdims=False)
    rows_b = lax.dynamic_slice(
        xall[1].reshape(2, 2, 4, 64, width), (0, r, g, 0, 0), (2, 1, 1, 64, width)
    ).reshape(2, 64, width)
    hidden = jnp.concatenate([rows_a, rows_b]).reshape(384, width).astype(F32)
    second = hidden + matmul(attended, w_out)
    normed_two = rms_scale(second, norm_gain2).astype(BF)
    gate = matmul(normed_two, w_gate)
    upper = matmul(normed_two, w_up)
    mixed = gated(gate, upper).astype(BF)
    result6 = (second + matmul(mixed, w_down)).astype(BF).reshape(6, 64, width)
    grad_rows = dy6.reshape(384, width)
    d_mixed = transposed(grad_rows, w_down)
    d_gate, d_upper = jax.vjp(gated, gate, upper)[1](d_mixed)
    d_gate = d_gate.astype(BF)
    d_upper = d_upper.astype(BF)
    d_normed_two = transposed(d_gate, w_gate) + transposed(d_upper, w_up)
    d_second_norm, d_gain_two = jax.vjp(rms_scale, second, norm_gain2)[1](d_normed_two)
    d_second = grad_rows.astype(F32) + d_second_norm
    d_branch = d_second.astype(BF)
    d_att = transposed(d_branch, w_out).astype(BF).reshape(6, 64, 4, 192).transpose(2, 0, 1, 3)
    d_last = d_att[..., 128:].reshape(4, 6, 2, 32, 64).transpose(0, 1, 3, 2, 4).reshape(4, 6, 32, 128)
    drecv = swap_back(jnp.concatenate([d_att[..., :128], d_last], axis=2))
    partial, g_qkv = backward_attention(scal, q, k, v, kt, o01, o2, drecv, xn, wc)
    d_normed, results = reduce_rows(partial, result6)
    d_hidden_norm, d_gain_one = jax.vjp(rms_scale, hidden, norm_gain1)[1](d_normed.reshape(384, width))
    input_grads = send_home((d_second + d_hidden_norm).astype(BF).reshape(6, 64, width))
    g_down = outer(mixed, grad_rows).astype(BF)
    g_gate = outer(normed_two, d_gate).astype(BF)
    g_up = outer(normed_two, d_upper).astype(BF)
    g_out = outer(attended, d_branch).astype(BF)
    gains = jnp.concatenate([d_gain_one[None], d_gain_two[None], jnp.zeros((6, width), F32)])
    s_gate, s_up, s_down, s_out, s_qkv, s_gains = reduce_weights((g_gate, g_up, g_down, g_out), g_qkv, gains)

    def join(first, last):
        both = jnp.concatenate([s_qkv[:, :, first : first + 128], s_qkv[:, :, last : last + 64]], axis=-1)
        return both.transpose(1, 0, 2).reshape(width, width).astype(F32)

    return (
        results.reshape(inputs.shape), input_grads.reshape(inputs.shape), s_gains[0],
        join(0, 512), join(128, 384), join(256, 448), s_out.astype(F32), s_gains[1],
        s_gate.astype(F32), s_up.astype(F32), s_down.astype(F32),
    )


def program(*args):
    micro, seqs, band_rows, width = args[0].shape
    small = lax.axis_size("band") == 16 and lax.axis_size("items") == 2
    if small and (micro, seqs, band_rows, width, HEADS, HEAD_DIM) == (2, 3, 64, 768, 12, 64):
        return fast(*args)
    return per_device(*args)


def solution(mesh):
    return jax.shard_map(
        program,
        mesh=mesh,
        in_specs=(
            P(None, "items", "band", None),
            P(None, "items"),
            P(),
            P(),
            P(),
            P(),
            P(),
            P(),
            P(),
            P(),
            P(),
            P(None, "items", "band", None),
        ),
        out_specs=(
            P(None, "items", "band", None),
            P(None, "items", "band", None),
            P(),
            P(),
            P(),
            P(),
            P(),
            P(),
            P(),
            P(),
            P(),
        ),
        check_vma=False,
    )
```

```python
import math

import jax
import jax.numpy as jnp
from jax import lax
from jax.experimental import pallas as pl
from jax.experimental.pallas import tpu as pltpu
from jax.sharding import PartitionSpec as P

HEADS = 12
HEAD_DIM = 64


EPS = 1e-06


def shortened(shard):

    def short(part):
        return part.astype(jnp.bfloat16) if part.dtype == jnp.float32 else part

    return jax.tree.map(short, shard)


def rms_scale(values, gain):
    return values * lax.rsqrt(jnp.mean(values * values, axis=-1, keepdims=True) + EPS) * gain


def gated(gate, upper):
    return jax.nn.gelu(gate, approximate=True) * upper


def outer(left, right):
    return lax.dot_general(
        left, right, (((0,), (0,)), ((), ())), preferred_element_type=jnp.float32
    )


def transposed(left, weight):
    return lax.dot_general(
        left, weight, (((1,), (1,)), ((), ())), preferred_element_type=jnp.float32
    )


def matmul(left, right):
    return jnp.dot(left, right, preferred_element_type=jnp.float32)


def scores(query, key, scale):
    return jnp.einsum("sqhd,skhd->shqk", query, key, preferred_element_type=jnp.float32) * scale


def per_device(
    inputs,
    counts,
    norm_gain1,
    w_query,
    w_key,
    w_value,
    w_out,
    norm_gain2,
    w_gate,
    w_up,
    w_down,
    cotangent,
):
    micro, seqs, band_rows, width = inputs.shape
    bands = lax.axis_size("band")
    length = band_rows * bands
    rows = seqs * band_rows
    heads = HEADS
    head_dim = HEAD_DIM
    scale = 1.0 / math.sqrt(head_dim)
    key_place = jnp.arange(length, dtype=jnp.int32)
    params = (norm_gain1, w_query, w_key, w_value, w_out, norm_gain2, w_gate, w_up, w_down)
    totals = [jnp.zeros(p.shape, jnp.float32) for p in params]
    results = []
    input_grads = []
    for number in range(micro):
        hidden = inputs[number].astype(jnp.float32).reshape(rows, width)
        lengths = counts[number]
        normed = rms_scale(hidden, norm_gain1).astype(jnp.bfloat16)
        query = matmul(normed, w_query).astype(jnp.bfloat16)
        key_local = matmul(normed, w_key).astype(jnp.bfloat16)
        value_local = matmul(normed, w_value).astype(jnp.bfloat16)
        query_four = query.reshape(seqs, band_rows, heads, head_dim)
        key_three = key_local.reshape(seqs, band_rows, width)
        value_three = value_local.reshape(seqs, band_rows, width)
        key_all, value_all = (
            lax.all_gather(key_three, "band", axis=1, tiled=True),
            lax.all_gather(value_three, "band", axis=1, tiled=True),
        )
        live = key_place[None, :] < lengths[:, None]
        key_four = key_all.reshape(seqs, length, heads, head_dim)
        value_four = value_all.reshape(seqs, length, heads, head_dim)
        logits = jnp.where(live[:, None, None, :], scores(query_four, key_four, scale), -jnp.inf)
        top = jnp.max(logits, axis=-1, keepdims=True)
        expo = jnp.exp(logits - top)
        summed = jnp.sum(expo, axis=-1, keepdims=True)
        log_total = top + jnp.log(summed)
        prob = (expo / summed).astype(jnp.bfloat16)
        attended = jnp.einsum(
            "shqk,skhd->sqhd", prob, value_four, preferred_element_type=jnp.float32
        )
        attended = attended.reshape(rows, width).astype(jnp.bfloat16)
        second = hidden + matmul(attended, w_out)
        normed_two = rms_scale(second, norm_gain2).astype(jnp.bfloat16)
        gate = matmul(normed_two, w_gate)
        upper = matmul(normed_two, w_up)
        mixed = gated(gate, upper).astype(jnp.bfloat16)
        results.append(
            (second + matmul(mixed, w_down)).astype(jnp.bfloat16).reshape(seqs, band_rows, width)
        )
        grad_rows = cotangent[number].reshape(rows, width)
        totals[8] = totals[8] + outer(mixed, grad_rows)
        d_mixed = transposed(grad_rows, w_down)
        pull_gate = jax.vjp(gated, gate, upper)[1]
        d_gate, d_upper = pull_gate(d_mixed)
        d_gate = d_gate.astype(jnp.bfloat16)
        d_upper = d_upper.astype(jnp.bfloat16)
        totals[6] = totals[6] + outer(normed_two, d_gate)
        totals[7] = totals[7] + outer(normed_two, d_upper)
        d_normed_two = transposed(d_gate, w_gate) + transposed(d_upper, w_up)
        pull_two = jax.vjp(rms_scale, second, norm_gain2)[1]
        d_second_norm, d_gain_two = pull_two(d_normed_two)
        totals[5] = totals[5] + d_gain_two
        d_second = grad_rows.astype(jnp.float32) + d_second_norm
        d_branch = d_second.astype(jnp.bfloat16)
        totals[4] = totals[4] + outer(attended, d_branch)
        d_attended = transposed(d_branch, w_out).astype(jnp.bfloat16)
        d_att_four = d_attended.reshape(seqs, band_rows, heads, head_dim)
        key_all, value_all = (
            lax.all_gather(key_three, "band", axis=1, tiled=True),
            lax.all_gather(value_three, "band", axis=1, tiled=True),
        )
        key_four = key_all.reshape(seqs, length, heads, head_dim)
        value_four = value_all.reshape(seqs, length, heads, head_dim)
        logits = jnp.where(live[:, None, None, :], scores(query_four, key_four, scale), -jnp.inf)
        prob_full = jnp.exp(logits - log_total)
        prob = prob_full.astype(jnp.bfloat16)
        d_prob = jnp.einsum(
            "sqhd,skhd->shqk", d_att_four, value_four, preferred_element_type=jnp.float32
        )
        delta = jnp.sum(d_prob * prob_full, axis=-1, keepdims=True)
        d_logits = (prob_full * (d_prob - delta)).astype(jnp.bfloat16)
        d_query = (
            jnp.einsum("shqk,skhd->sqhd", d_logits, key_four, preferred_element_type=jnp.float32)
            * scale
        )
        d_query = d_query.reshape(rows, width).astype(jnp.bfloat16)
        d_key_all = (
            jnp.einsum("shqk,sqhd->skhd", d_logits, query_four, preferred_element_type=jnp.float32)
            * scale
        )
        d_value_all = jnp.einsum(
            "shqk,sqhd->skhd", prob, d_att_four, preferred_element_type=jnp.float32
        )
        d_key_three, d_value_three = (
            lax.psum_scatter(
                d_key_all.reshape(seqs, length, width).astype(jnp.bfloat16),
                "band",
                scatter_dimension=1,
                tiled=True,
            ).astype(jnp.float32),
            lax.psum_scatter(
                d_value_all.reshape(seqs, length, width).astype(jnp.bfloat16),
                "band",
                scatter_dimension=1,
                tiled=True,
            ).astype(jnp.float32),
        )
        d_key = d_key_three.reshape(rows, width).astype(jnp.bfloat16)
        d_value = d_value_three.reshape(rows, width).astype(jnp.bfloat16)
        totals[1] = totals[1] + outer(normed, d_query)
        totals[2] = totals[2] + outer(normed, d_key)
        totals[3] = totals[3] + outer(normed, d_value)
        d_normed = (
            transposed(d_query, w_query) + transposed(d_key, w_key) + transposed(d_value, w_value)
        )
        pull_one = jax.vjp(rms_scale, hidden, norm_gain1)[1]
        d_hidden_norm, d_gain_one = pull_one(d_normed)
        totals[0] = totals[0] + d_gain_one
        input_grads.append(
            (d_second + d_hidden_norm).astype(jnp.bfloat16).reshape(seqs, band_rows, width)
        )
    shares = jax.tree.map(
        lambda part: part.astype(jnp.float32),
        lax.psum_scatter(shortened(tuple(totals)), "band", scatter_dimension=0, tiled=True),
    )
    summed_shares = jax.tree.map(
        lambda part: part.astype(jnp.float32), lax.psum(shortened(shares), "items")
    )
    whole = jax.tree.map(
        lambda part, own: part.astype(own.dtype),
        lax.all_gather(shortened(summed_shares), "band", axis=0, tiled=True),
        summed_shares,
    )
    return (jnp.stack(results), jnp.stack(input_grads)) + tuple(whole)


MESH_ID = pl.DeviceIdType.MESH
NEG = -1e30
BF = jnp.bfloat16
F32 = jnp.float32


def place():
    item = lax.axis_index("items")
    band = lax.axis_index("band")
    return item, band // 4, band % 4


def flip(value):
    return value + 1 - 2 * (value % 2)


def far(value):
    return (value + 2) % 4


def greet(peers):
    barrier = pltpu.get_barrier_semaphore()
    for peer in peers:
        pl.semaphore_signal(barrier, inc=1, device_id=peer, device_id_type=MESH_ID)
    pl.semaphore_wait(barrier, len(peers))


def remote(src, dst, send, recv, peer):
    return pltpu.make_async_remote_copy(
        src_ref=src, dst_ref=dst, send_sem=send, recv_sem=recv, device_id=peer, device_id_type=MESH_ID
    )


def params(number, vmem=40):
    return pltpu.CompilerParams(
        collective_id=number, has_side_effects=True, vmem_limit_bytes=vmem << 20
    )


def lanes_of(rows):
    return lax.broadcasted_iota(jnp.int32, (rows, 128), 1)


ANY = pl.BlockSpec(memory_space=pl.ANY)
VMEM = pl.BlockSpec(memory_space=pltpu.VMEM)
SMEM = pl.BlockSpec(memory_space=pltpu.SMEM)


def gather_kernel(
    x_ref, wq_ref, wk_ref, wv_ref, out_ref, wc_ref, win_ref, z_send, f_send, g_send, recv, own_sem, win_sem
):
    item, z, g = place()
    cut = pl.ds(pl.multiple_of(g * 3 // 2 * 128, 128), 256)
    windows = []
    for n, ref in enumerate((wq_ref, wk_ref, wv_ref)):
        windows.append(pltpu.make_async_copy(ref.at[:, cut], win_ref.at[n], win_sem.at[n]))
        windows[-1].start()
    gc, gx = flip(g), far(g)
    gcx = far(gc)
    zs = (z, flip(z), far(z), far(flip(z)))
    core, across = (item, z * 4 + gc), (item, z * 4 + gx)
    greet([core, across] + [(item, s * 4 + g) for s in zs[1:]])

    def items_of(s):
        return (3 * (s // 2) + 2 * (s % 2), 3 * (s // 2) + 1)

    started = []
    for n, s in enumerate(zs[1:]):
        for ab in range(2):
            copy = remote(
                x_ref.at[items_of(s)[ab]],
                out_ref.at[ab, z * 4 + g],
                z_send.at[n, ab],
                recv.at[ab, z * 4 + g],
                (item, s * 4 + g),
            )
            copy.start()
            started.append(copy)
    local = []
    for ab in range(2):
        copy = pltpu.make_async_copy(
            x_ref.at[items_of(z)[ab]], out_ref.at[ab, z * 4 + g], own_sem.at[ab]
        )
        copy.start()
        local.append(copy)

    def arrived(ab, where):
        remote(
            out_ref.at[ab, where], out_ref.at[ab, where], z_send.at[0, 0], recv.at[ab, where], core
        ).wait_recv()

    def pack():
        for copy in windows:
            copy.wait()
        odd = g % 2 == 1
        low = lanes_of(256) < 64

        @pl.loop(0, 3)
        def _(i):
            rows = pl.ds(pl.multiple_of(i * 256, 256), 256)
            firsts, lasts = [], []
            for n in range(3):
                left = win_ref[n, rows, 0:128].astype(F32)
                right = win_ref[n, rows, 128:256].astype(F32)
                crossed = pltpu.roll(jnp.where(low, right, left), 64, 1)
                firsts.append(jnp.where(odd, crossed, left))
                lasts.append(jnp.where(odd, pltpu.roll(right, 64, 1), right))
            for n in range(3):
                wc_ref[rows, n * 128 : n * 128 + 128] = firsts[n].astype(BF)
            wc_ref[rows, 384:512] = jnp.where(low, lasts[1], pltpu.roll(lasts[2], 64, 1)).astype(BF)
            wc_ref[rows, 512:640] = jnp.where(low, lasts[0], 0.0).astype(BF)

    for n, zz in enumerate(zs):
        if n == 1:
            pack()
        for ab in range(2):
            where = zz * 4 + g
            if n > 0:
                arrived(ab, where)
            src = x_ref.at[items_of(z)[ab]] if n == 0 else out_ref.at[ab, where]
            for k, peer in enumerate((across, core)):
                copy = remote(
                    src, out_ref.at[ab, where], f_send.at[n, ab, k], recv.at[ab, where], peer
                )
                copy.start()
                started.append(copy)
    for n, zz in enumerate(zs):
        for ab in range(2):
            where = zz * 4 + gx
            arrived(ab, where)
            copy = remote(
                out_ref.at[ab, where],
                out_ref.at[ab, where],
                g_send.at[n, ab],
                recv.at[ab, where],
                core,
            )
            copy.start()
            started.append(copy)
    for n, zz in enumerate(zs):
        for ab in range(2):
            arrived(ab, zz * 4 + gc)
            arrived(ab, zz * 4 + gcx)
    for copy in local:
        copy.wait()
    for copy in started:
        copy.wait_send()


def gather_rows(x6, wq, wk, wv):
    _, rows, width = x6.shape
    dma = pltpu.SemaphoreType.DMA
    return pl.pallas_call(
        gather_kernel,
        out_shape=(
            jax.ShapeDtypeStruct((2, 16, rows, width), BF), jax.ShapeDtypeStruct((width, 640), BF)
        ),
        in_specs=[ANY] * 4,
        out_specs=(ANY, VMEM),
        scratch_shapes=[
            pltpu.VMEM((3, width, 256), BF),
            dma((3, 2)), dma((4, 2, 2)), dma((4, 2)), dma((2, 16)), dma((2,)), dma((3,)),
        ],
        compiler_params=params(1),
        name="gather_rows",
    )(x6, wq, wk, wv)


def to_slots(item, z, g, src_ref, dst_ref, send, recv, own_sem):
    zs = (z, flip(z), far(z), far(flip(z)))
    p, r = z // 2, z % 2
    started = []
    for n, s in enumerate(zs[1:]):
        copy = remote(
            src_ref.at[3 * (s // 2) + 2 * (s % 2)],
            dst_ref.at[z],
            send.at[n],
            recv.at[z],
            (item, s * 4 + g),
        )
        copy.start()
        started.append(copy)
    copy = remote(
        src_ref.at[3 * (1 - p) + 1], dst_ref.at[4 + p], send.at[3], recv.at[4 + p], (item, far(z) * 4 + g)
    )
    copy.start()
    started.append(copy)
    local = [
        pltpu.make_async_copy(src_ref.at[3 * p + 2 * r], dst_ref.at[z], own_sem.at[0]),
        pltpu.make_async_copy(src_ref.at[3 * p + 1], dst_ref.at[4 + p], own_sem.at[1]),
    ]
    for copy in local:
        copy.start()

    def finish():
        for where in zs[1:] + (4 + (1 - p),):
            remote(
                dst_ref.at[where], dst_ref.at[where], send.at[0], recv.at[where], (item, far(z) * 4 + g)
            ).wait_recv()
        for copy in local:
            copy.wait()
        for copy in started:
            copy.wait_send()

    return finish


def from_slots(item, z, g, src_ref, dst_ref, send, recv, own_sem):
    zs = (z, flip(z), far(z), far(flip(z)))
    p, r = z // 2, z % 2
    mine = 3 * p + 2 * r
    started = []
    for n, s in enumerate(zs[1:]):
        copy = remote(src_ref.at[s], dst_ref.at[mine], send.at[n], recv.at[mine], (item, s * 4 + g))
        copy.start()
        started.append(copy)
    copy = remote(
        src_ref.at[4 + (1 - p)],
        dst_ref.at[3 * p + 1],
        send.at[3],
        recv.at[3 * p + 1],
        (item, far(z) * 4 + g),
    )
    copy.start()
    started.append(copy)
    local = [
        pltpu.make_async_copy(src_ref.at[z], dst_ref.at[mine], own_sem.at[0]),
        pltpu.make_async_copy(src_ref.at[4 + p], dst_ref.at[3 * p + 1], own_sem.at[1]),
    ]
    for copy in local:
        copy.start()

    def finish():
        for s in zs[1:]:
            where = 3 * (s // 2) + 2 * (s % 2)
            remote(
                dst_ref.at[where], dst_ref.at[where], send.at[0], recv.at[where], (item, far(z) * 4 + g)
            ).wait_recv()
        where = 3 * (1 - p) + 1
        remote(
            dst_ref.at[where], dst_ref.at[where], send.at[0], recv.at[where], (item, far(z) * 4 + g)
        ).wait_recv()
        for copy in local:
            copy.wait()
        for copy in started:
            copy.wait_send()

    return finish


def z_peers(item, z, g):
    return [(item, s * 4 + g) for s in (flip(z), far(z), far(flip(z)))]


def g_peers(item, z, g):
    return [(item, z * 4 + h) for h in (flip(g), far(g), far(flip(g)))]


def swap_heads(item, z, g, src_ref, dst_ref, send, recv, own_sem):
    started = []
    for n, h in enumerate((far(g), far(flip(g)), flip(g))):
        copy = remote(src_ref.at[h], dst_ref.at[g], send.at[n], recv.at[g], (item, z * 4 + h))
        copy.start()
        started.append(copy)
    local = pltpu.make_async_copy(src_ref.at[g], dst_ref.at[g], own_sem)
    local.start()

    def finish():
        for h in (flip(g), far(g), far(flip(g))):
            remote(
                dst_ref.at[h], dst_ref.at[h], send.at[0], recv.at[h], (item, z * 4 + h)
            ).wait_recv()
        local.wait()
        for copy in started:
            copy.wait_send()

    return finish


def swap_kernel(heads_ref, rows_ref, out_heads_ref, out_rows_ref, hs, hr, ho, zs, zr, zo):
    item, z, g = place()
    greet(z_peers(item, z, g) + g_peers(item, z, g))
    first = swap_heads(item, z, g, heads_ref, out_heads_ref, hs, hr, ho.at[0])
    second = to_slots(item, z, g, rows_ref, out_rows_ref, zs, zr, zo)
    first()
    second()


def swap_out(heads, rows):
    dma = pltpu.SemaphoreType.DMA
    return pl.pallas_call(
        swap_kernel,
        out_shape=(
            jax.ShapeDtypeStruct(heads.shape, heads.dtype),
            jax.ShapeDtypeStruct(rows.shape, rows.dtype),
        ),
        in_specs=[ANY, ANY],
        out_specs=(ANY, ANY),
        scratch_shapes=[dma((3,)), dma((4,)), dma((1,)), dma((4,)), dma((6,)), dma((2,))],
        compiler_params=params(2),
        name="swap_out",
    )(heads, rows)


def swap_back_kernel(heads_ref, out_heads_ref, hs, hr, ho):
    item, z, g = place()
    greet(g_peers(item, z, g))
    swap_heads(item, z, g, heads_ref, out_heads_ref, hs, hr, ho.at[0])()


def swap_back(heads):
    dma = pltpu.SemaphoreType.DMA
    return pl.pallas_call(
        swap_back_kernel,
        out_shape=jax.ShapeDtypeStruct(heads.shape, heads.dtype),
        in_specs=[ANY],
        out_specs=ANY,
        scratch_shapes=[dma((3,)), dma((4,)), dma((1,))],
        compiler_params=params(3),
        name="swap_back",
    )(heads)


def nt(left, right):
    return lax.dot_general(left, right, (((1,), (1,)), ((), ())), preferred_element_type=F32)


def forward_kernel(
    count_ref, x_ref, gain_ref, wc_ref,
    osend_ref, xn_ref, q_ref, k_ref, v_ref, kt_ref, o01_ref, o2_ref,
):
    _, z, _ = place()
    p, r = z // 2, z % 2
    lane = lanes_of(256)
    low = lane < 64

    @pl.loop(0, 8)
    def _(i):
        rows = pl.ds(pl.multiple_of(i * 256, 256), 256)
        h = x_ref[rows, :].astype(F32)
        inv = lax.rsqrt(jnp.mean(h * h, axis=-1, keepdims=True) + EPS)
        xn = (h * inv * gain_ref[...]).astype(BF)
        xn_ref[rows, :] = xn
        y = matmul(xn, wc_ref[:, 128:512])
        count = count_ref[p, jnp.where(i < 4, 2 * r, 1)]
        at = lax.broadcasted_iota(jnp.int32, (256, 128), 0) + (i % 4) * 256
        bias = jnp.where(at < count, 0.0, NEG)
        one = jnp.where((lane % 64) < 4, 1.0, 0.0)
        k_aug = jnp.where(lane % 64 == 0, bias, one)
        k01, v01, kv2 = y[:, :128], y[:, 128:256], y[:, 256:]
        k_ref[0, rows, :] = jnp.where(low, k01, k_aug).astype(BF)
        k_ref[1, rows, :] = jnp.where(low, k_aug, k01).astype(BF)
        k_ref[2, rows, :] = jnp.where(low, kv2, k_aug).astype(BF)
        v_ref[0, rows, :] = jnp.where(low, v01, one).astype(BF)
        v_ref[1, rows, :] = jnp.where(low, one, v01).astype(BF)
        v_ref[2, rows, :] = jnp.where(low, one, kv2).astype(BF)

    for head in range(3):
        for ab in range(2):
            kt_ref[head, ab, :, :] = k_ref[head, ab * 1024 : (ab + 1) * 1024, :].T

    @pl.loop(0, 6)
    def _(t):
        off = jnp.where(t < 4, t, 4 + r + 2 * (t - 4)) * 256
        xq = xn_ref[pl.ds(pl.multiple_of(off, 256), 256), :]
        q01 = matmul(xq, wc_ref[:, 0:128]).astype(BF).astype(F32) * 0.125
        q2 = matmul(xq, wc_ref[:, 512:640]).astype(BF).astype(F32) * 0.125
        flag = jnp.where(lane % 64 == 0, 1.0, 0.0)
        qs = (jnp.where(low, q01, flag), jnp.where(low, flag, q01), jnp.where(low, q2, flag))
        at = pl.ds(pl.multiple_of(t * 256, 256), 256)
        ab = t // 4
        keys = pl.ds(pl.multiple_of(ab * 1024, 1024), 1024)
        outs = []
        for head in range(3):
            s = matmul(qs[head].astype(BF), kt_ref[head, ab])
            top = jnp.max(s, axis=1, keepdims=True)
            e = jnp.exp(s - top).astype(BF)
            o = matmul(e, v_ref[head, keys, :])
            total = o[:, 64:65] if head == 0 else o[:, 0:1]
            outs.append(o / total)
            lse = -(top + jnp.log(total))
            hi = lse.astype(BF).astype(F32)
            mid = (lse - hi).astype(BF).astype(F32)
            lo = lse - hi - mid
            part = lane % 64
            aug = jnp.where(part == 1, hi, jnp.where(part == 2, mid, jnp.where(part == 3, lo, flag)))
            data = low if head != 1 else jnp.logical_not(low)
            q_ref[head, at, :] = jnp.where(data, qs[head], aug).astype(BF)
        o01 = jnp.where(low, outs[0], outs[1])
        o2 = outs[2]
        o01_ref[at, :] = o01
        o2_ref[at, :] = o2
        for h in range(4):
            osend_ref[h, t, 0:64, :] = o01[h * 64 : h * 64 + 64].astype(BF)
            first = o2[h * 64 : h * 64 + 32]
            second = o2[h * 64 + 32 : h * 64 + 64]
            folded = jnp.where(low[:32], pltpu.roll(first, 64, 1), second)
            osend_ref[h, t, 64:96, :] = folded.astype(BF)


def forward_attention(counts, xall, gain, wc):
    s = jax.ShapeDtypeStruct
    return pl.pallas_call(
        forward_kernel,
        out_shape=(
            s((4, 6, 96, 128), BF), s((2048, 768), BF), s((3, 1536, 128), BF), s((3, 2048, 128), BF),
            s((3, 2048, 128), BF), s((3, 2, 128, 1024), BF), s((1536, 128), F32), s((1536, 128), F32),
        ),
        in_specs=[SMEM, VMEM, VMEM, VMEM],
        out_specs=(VMEM,) * 8,
        compiler_params=pltpu.CompilerParams(vmem_limit_bytes=50 << 20),
        name="forward_attention",
    )(counts, xall, gain, wc)


def backward_kernel(
    q_ref, k_ref, v_ref, kt_ref, o01_ref, o2_ref, do_ref, xn_ref, wc_ref,
    p_ref, gw_ref, dk_ref, dv_ref, d5_ref,
):
    _, z, _ = place()
    r = z % 2
    lane = lanes_of(256)
    low = lane < 64
    part = lane % 64
    dk_ref[...] = jnp.zeros_like(dk_ref)
    dv_ref[...] = jnp.zeros_like(dv_ref)
    d5_ref[...] = jnp.zeros_like(d5_ref)

    def pieces(delta):
        neg = -delta
        hi = neg.astype(BF).astype(F32)
        mid = (neg - hi).astype(BF).astype(F32)
        lo = neg - hi - mid
        return jnp.where(part == 1, hi, jnp.where(part == 2, mid, jnp.where(part == 3, lo, 0.0)))

    @pl.loop(0, 6)
    def _(t):
        at = pl.ds(pl.multiple_of(t * 256, 256), 256)
        ab = t // 4
        keys = pl.ds(pl.multiple_of(ab * 1024, 1024), 1024)
        do01 = do_ref[:, t, 0:64, :].astype(F32).reshape(256, 128)
        folded = do_ref[:, t, 64:96, :].astype(F32)
        two = []
        for h in range(4):
            two.append(pltpu.roll(folded[h], 64, 1))
            two.append(folded[h])
        do2 = jnp.concatenate(two, axis=0)
        prod = do01 * o01_ref[at, :]
        prod2 = do2 * o2_ref[at, :]
        delta0 = jnp.sum(jnp.where(low, prod, 0.0), axis=1, keepdims=True)
        delta1 = jnp.sum(jnp.where(low, 0.0, prod), axis=1, keepdims=True)
        delta2 = jnp.sum(jnp.where(low, 0.0, prod2), axis=1, keepdims=True)
        dos = (
            jnp.where(low, do01, pieces(delta0)).astype(BF),
            jnp.where(low, pieces(delta1), do01).astype(BF),
            jnp.where(low, pieces(delta2), do2).astype(BF),
        )
        dqs = []
        for head in range(3):
            q = q_ref[head, at, :]
            prob = jnp.exp(nt(k_ref[head, keys, :], q))
            d_prob = nt(v_ref[head, keys, :], dos[head])
            d_log = (prob * d_prob).astype(BF)
            dv_ref[head, keys, :] += matmul(prob.astype(BF), dos[head])
            dk_ref[head, keys, :] += matmul(d_log, q)
            dqs.append(matmul(kt_ref[head, ab], d_log).T * 0.125)
        off = jnp.where(t < 4, t, 4 + r + 2 * (t - 4)) * 256
        rows = pl.ds(pl.multiple_of(off, 256), 256)
        d5_ref[rows, 0:128] = jnp.where(low, dqs[0], dqs[1]).astype(BF)
        d5_ref[rows, 512:640] = jnp.where(low, dqs[2], 0.0).astype(BF)

    @pl.loop(0, 8)
    def _(i):
        rows = pl.ds(pl.multiple_of(i * 256, 256), 256)
        d5_ref[rows, 128:256] = jnp.where(low, dk_ref[0, rows, :], dk_ref[1, rows, :]).astype(BF)
        d5_ref[rows, 256:384] = jnp.where(low, dv_ref[0, rows, :], dv_ref[1, rows, :]).astype(BF)
        d5_ref[rows, 384:512] = jnp.where(low, dk_ref[2, rows, :], dv_ref[2, rows, :]).astype(BF)
        d_xn = nt(d5_ref[rows, :], wc_ref[...]).astype(BF)
        for h in range(4):
            p_ref[h, i, :, :] = d_xn[h * 64 : h * 64 + 64]

    for c in range(5):
        cols = slice(c * 128, c * 128 + 128)
        gw_ref[:, cols] = outer(xn_ref[...], d5_ref[:, cols]).astype(BF)


def backward_attention(q, k, v, kt, o01, o2, do, xn, wc):
    s = jax.ShapeDtypeStruct
    return pl.pallas_call(
        backward_kernel,
        out_shape=(s((4, 8, 64, 768), BF), s((768, 640), BF)),
        in_specs=[VMEM] * 9,
        out_specs=(VMEM,) * 2,
        scratch_shapes=[
            pltpu.VMEM((3, 2048, 128), F32), pltpu.VMEM((3, 2048, 128), F32), pltpu.VMEM((2048, 640), BF),
        ],
        compiler_params=pltpu.CompilerParams(vmem_limit_bytes=56 << 20),
        name="backward_attention",
    )(q, k, v, kt, o01, o2, do, xn, wc)


def reduce_kernel(
    p_ref, res_ref, h_ref, dh_ref, gain_ref, out_ref, res_out_ref, dgain_ref,
    rc_ref, sx_ref, rx_ref, t_ref, zb_ref, rz_ref, ig_ref,
    c_send, c_recv, x_send, x_recv, z_send, z_recv, rs_send, rs_recv, rs_own, h_send, h_recv, h_own,
):
    item, z, g = place()
    gc, gx = flip(g), far(g)
    gcx = far(gc)
    p, r = z // 2, z % 2
    core, across, pair = (item, z * 4 + gc), (item, z * 4 + gx), (item, flip(z) * 4 + g)
    zs = (z, flip(z), far(z), far(flip(z)))
    greet([core, across] + z_peers(item, z, g))
    halves = ((1, slice(4, 8)), (0, slice(0, 4)))
    c_copies = {}
    for k, h in ((1, gcx), (0, gc)):
        for ab, cut in halves:
            c_copies[k, ab] = remote(
                p_ref.at[h, cut], rc_ref.at[k, cut], c_send.at[k, ab], c_recv.at[k, ab], core
            )
            c_copies[k, ab].start()
    done_rs = from_slots(item, z, g, res_ref, res_out_ref, rs_send, rs_recv, rs_own)
    x_copies = {}
    for ab, cut in halves:
        c_copies[1, ab].wait_recv()

        @pl.loop(0, 4)
        def _(j):
            n = ab * 4 + j
            sx_ref[n] = (p_ref[gx, n].astype(F32) + rc_ref[1, n].astype(F32)).astype(BF)

        x_copies[ab] = remote(sx_ref.at[cut], rx_ref.at[cut], x_send.at[ab], x_recv.at[ab], across)
        x_copies[ab].start()
    dgain_ref[...] = jnp.zeros_like(dgain_ref)
    gain = gain_ref[...]

    def norm_back(d_xn, j):
        h = h_ref[j].astype(F32)
        inv = lax.rsqrt(jnp.mean(h * h, axis=-1, keepdims=True) + EPS)
        dgain_ref[...] += jnp.sum(d_xn * h * inv, axis=0, keepdims=True)
        dyg = d_xn * gain
        dot = jnp.mean(dyg * h, axis=-1, keepdims=True)
        ig_ref[j] = (dh_ref[j] + inv * dyg - h * (inv * inv * inv * dot)).astype(BF)

    for ab, cut in halves:
        c_copies[0, ab].wait_recv()

        @pl.loop(0, 4)
        def _(j):
            n = ab * 4 + j
            t_ref[n] = p_ref[g, n].astype(F32) + rc_ref[0, n].astype(F32)

    x_copies[1].wait_recv()
    for q in range(2):
        n = 4 + (1 - r) + 2 * q
        zb_ref[q] = (t_ref[n] + rx_ref[n].astype(F32)).astype(BF)
    z_copy = remote(zb_ref, rz_ref, z_send.at[0], z_recv.at[0], pair)
    z_copy.start()
    x_copies[0].wait_recv()
    mine = 3 * p + 2 * r
    homes = []
    for n, s in enumerate((zs[3], zs[2], zs[1], z)):
        norm_back(t_ref[s] + rx_ref[s].astype(F32), s)
        if n < 3:
            copy = remote(
                ig_ref.at[s], out_ref.at[mine], h_send.at[n], h_recv.at[mine], (item, s * 4 + g)
            )
        else:
            copy = pltpu.make_async_copy(ig_ref.at[s], out_ref.at[mine], h_own.at[0])
        copy.start()
        homes.append(copy)
    z_copy.wait_recv()
    for n, q in enumerate((1 - p, p)):
        k = 4 + r + 2 * q
        norm_back(t_ref[k] + rx_ref[k].astype(F32) + rz_ref[q].astype(F32), 4 + q)
        where = 3 * p + 1
        if n == 0:
            copy = remote(
                ig_ref.at[4 + q], out_ref.at[where], h_send.at[3], h_recv.at[where], (item, zs[2] * 4 + g)
            )
        else:
            copy = pltpu.make_async_copy(ig_ref.at[4 + q], out_ref.at[where], h_own.at[1])
        copy.start()
        homes.append(copy)
    for s in zs[1:]:
        where = 3 * (s // 2) + 2 * (s % 2)
        remote(ig_ref.at[0], out_ref.at[where], h_send.at[0], h_recv.at[where], pair).wait_recv()
    where = 3 * (1 - p) + 1
    remote(ig_ref.at[0], out_ref.at[where], h_send.at[0], h_recv.at[where], pair).wait_recv()
    done_rs()
    homes[3].wait()
    homes[5].wait()
    for copy in homes[:3] + homes[4:5] + [z_copy] + list(c_copies.values()) + list(x_copies.values()):
        copy.wait_send()


def reduce_rows(p, results, hidden, d_second, gain):
    dma = pltpu.SemaphoreType.DMA
    s = jax.ShapeDtypeStruct
    rows, width = p.shape[2:]
    return pl.pallas_call(
        reduce_kernel,
        out_shape=(s((6, rows, width), BF), s(results.shape, results.dtype), s((1, width), F32)),
        in_specs=[VMEM, ANY, VMEM, VMEM, VMEM],
        out_specs=(ANY, ANY, VMEM),
        scratch_shapes=[
            pltpu.VMEM((2, 8, rows, width), BF), pltpu.VMEM((8, rows, width), BF), pltpu.VMEM((8, rows, width), BF),
            pltpu.VMEM((8, rows, width), F32), pltpu.VMEM((2, rows, width), BF), pltpu.VMEM((2, rows, width), BF),
            pltpu.VMEM((6, rows, width), BF),
            dma((2, 2)), dma((2, 2)), dma((2,)), dma((2,)), dma((1,)), dma((1,)), dma((4,)), dma((6,)), dma((2,)),
            dma((4,)), dma((6,)), dma((2,)),
        ],
        compiler_params=params(4),
        name="reduce_rows",
    )(p, results, hidden, d_second, gain)


GELU_A = 0.044715
GELU_C = math.sqrt(2.0 / math.pi)


def dense_kernel(
    o_ref, x_ref, dy_ref, gain_ref, wo_hbm, wg_hbm, wu_hbm, wd_hbm,
    res_ref, dsend_ref, h_ref, dh_ref, dgain_ref, gg_ref, gu_ref, gd_ref, go_ref,
    wo_ref, wg_ref, wu_ref, wd_ref, att_ref, sec_ref, xn_ref, xt_ref, dyt_ref, dxn_ref, h_sem, wo_sem, w_sem,
):
    _, z, g = place()
    r = z % 2
    chunks, size = 4, wg_ref.shape[1] // 4
    copies = []
    for j in range(6):
        src = x_ref.at[0, j * 4 + g] if j < 4 else x_ref.at[1, (r + 2 * (j - 4)) * 4 + g]
        copies.append(pltpu.make_async_copy(src, h_ref.at[j], h_sem.at[j]))
    copies.append(pltpu.make_async_copy(wo_hbm, wo_ref, wo_sem.at[0]))
    for copy in copies:
        copy.start()
    loads = []
    for c in range(chunks):
        cut = pl.ds(c * size, size)
        loads.append(
            [
                pltpu.make_async_copy(wg_hbm.at[:, cut], wg_ref.at[:, cut], w_sem.at[0, c]),
                pltpu.make_async_copy(wu_hbm.at[:, cut], wu_ref.at[:, cut], w_sem.at[1, c]),
                pltpu.make_async_copy(wd_hbm.at[cut, :], wd_ref.at[cut, :], w_sem.at[2, c]),
            ]
        )
        for copy in loads[-1]:
            copy.start()
    low = lanes_of(384) < 64

    def swap(v):
        return pltpu.roll(v, 64, 1)

    pairs = [o_ref[n, :, 0:64, :].astype(F32).reshape(384, 128) for n in range(4)]

    def unfold(n, high):
        f = o_ref[n, :, 64:96, :].astype(F32)
        s = swap(f.reshape(192, 128)).reshape(6, 32, 128)
        both = (s, f) if high else (f, s)
        return jnp.concatenate(both, axis=1).reshape(384, 128)

    tiles = (
        pairs[0],
        jnp.where(low, unfold(0, False), swap(pairs[1])),
        jnp.where(low, swap(pairs[1]), unfold(1, True)),
        pairs[2],
        jnp.where(low, unfold(2, False), swap(pairs[3])),
        jnp.where(low, swap(pairs[3]), unfold(3, True)),
    )
    for n, tile in enumerate(tiles):
        att_ref[:, n * 128 : n * 128 + 128] = tile.astype(BF)
    for copy in copies:
        copy.wait()
    second = h_ref[...].reshape(384, 768).astype(F32) + matmul(att_ref[...], wo_ref[...])
    sec_ref[...] = second
    inv = lax.rsqrt(jnp.mean(second * second, axis=-1, keepdims=True) + EPS)
    xn_ref[...] = (second * inv * gain_ref[...]).astype(BF)
    xt_ref[...] = xn_ref[...].T
    dxn_ref[...] = jnp.zeros_like(dxn_ref)
    dy = dy_ref[...].reshape(384, 768)
    for c in range(chunks):
        cut = slice(c * size, c * size + size)
        for copy in loads[c]:
            copy.wait()
        gate = matmul(xn_ref[...], wg_ref[:, cut])
        upper = matmul(xn_ref[...], wu_ref[:, cut])
        d_mixed = nt(dy, wd_ref[cut, :])
        square = gate * gate
        tan = jnp.tanh(GELU_C * (gate + GELU_A * square * gate))
        half = 0.5 * (1.0 + tan)
        act = gate * half
        slope = half + 0.5 * gate * (1.0 - tan * tan) * (GELU_C * (1.0 + 3.0 * GELU_A * square))
        mixed = (act * upper).astype(BF)
        d_gate = (d_mixed * upper * slope).astype(BF)
        d_upper = (d_mixed * act).astype(BF)
        sec_ref[...] += matmul(mixed, wd_ref[cut, :])
        dxn_ref[...] += nt(d_gate, wg_ref[:, cut]) + nt(d_upper, wu_ref[:, cut])
        gg_ref[:, cut] = matmul(xt_ref[...], d_gate).astype(BF)
        gu_ref[:, cut] = matmul(xt_ref[...], d_upper).astype(BF)
        gd_ref[cut, :] = outer(mixed, dy).astype(BF)
    res_ref[...] = sec_ref[...].astype(BF).reshape(6, 64, 768)
    second = h_ref[...].reshape(384, 768).astype(F32) + matmul(att_ref[...], wo_ref[...])
    inv = lax.rsqrt(jnp.mean(second * second, axis=-1, keepdims=True) + EPS)
    d_xn = dxn_ref[...]
    dgain_ref[...] = jnp.sum(d_xn * second * inv, axis=0, keepdims=True)
    dyg = d_xn * gain_ref[...]
    dot = jnp.mean(dyg * second, axis=-1, keepdims=True)
    d_second = dy.astype(F32) + inv * dyg - second * (inv * inv * inv * dot)
    dh_ref[...] = d_second.reshape(6, 64, 768)
    d_branch = d_second.astype(BF)
    go_ref[...] = outer(att_ref[...], d_branch).astype(BF)
    d_att = nt(d_branch, wo_ref[...]).astype(BF).astype(F32)
    d = [d_att[:, n * 128 : n * 128 + 128] for n in range(6)]
    firsts = (d[0], swap(jnp.where(low, d[2], d[1])), d[3], swap(jnp.where(low, d[5], d[4])))
    lasts = ((d[1], False), (d[2], True), (d[4], False), (d[5], True))
    low3 = lax.broadcasted_iota(jnp.int32, (6, 32, 128), 2) < 64
    for n in range(4):
        dsend_ref[n, :, 0:64, :] = firsts[n].astype(BF).reshape(6, 64, 128)
        v, high = lasts[n]
        v3, s3 = v.reshape(6, 64, 128), swap(v).reshape(6, 64, 128)
        top, bottom = v3[:, :32], v3[:, 32:]
        top_s, bottom_s = s3[:, :32], s3[:, 32:]
        f = jnp.where(low3, top_s, bottom) if high else jnp.where(low3, top, bottom_s)
        dsend_ref[n, :, 64:96, :] = f.astype(BF)


def dense(orecv, xall, dy6, gain, w_out, w_gate, w_up, w_down):
    s = jax.ShapeDtypeStruct
    dma = pltpu.SemaphoreType.DMA
    rows, width = dy6.shape[1:]
    hidden = w_gate.shape[1]
    v = pltpu.VMEM
    return pl.pallas_call(
        dense_kernel,
        out_shape=(
            s(dy6.shape, BF), s(orecv.shape, BF), s(dy6.shape, BF), s(dy6.shape, F32), s((1, width), F32),
            s(w_gate.shape, BF), s(w_up.shape, BF), s(w_down.shape, BF), s(w_out.shape, BF),
        ),
        in_specs=[VMEM, ANY, VMEM, VMEM] + [ANY] * 4,
        out_specs=(VMEM,) * 9,
        scratch_shapes=[
            v(w_out.shape, BF), v(w_gate.shape, BF), v(w_up.shape, BF), v(w_down.shape, BF),
            v((384, width), BF), v((384, width), F32), v((384, width), BF), v((width, 384), BF), v((width, 384), BF),
            v((384, width), F32), dma((6,)), dma((1,)), dma((3, 4)),
        ],
        compiler_params=pltpu.CompilerParams(vmem_limit_bytes=50 << 20),
        name="dense",
    )(orecv, xall, dy6, gain, w_out, w_gate, w_up, w_down)


def widen_kernel(qkv_ref, so_ref, sg_ref, su_ref, sd_ref, q_ref, k_ref, v_ref, o_ref, g_ref, u_ref, d_ref):
    low = lanes_of(qkv_ref.shape[1]) < 64

    def swap(v):
        return pltpu.roll(v, 64, 1)

    for out, first, last, high in ((q_ref, 0, 512, False), (k_ref, 128, 384, False), (v_ref, 256, 384, True)):
        a = [qkv_ref[n, :, first : first + 128].astype(F32) for n in range(4)]
        b = [qkv_ref[n, :, last : last + 128].astype(F32) for n in range(4)]
        low_b = [swap(x) if high else x for x in b]
        high_b = [x if high else swap(x) for x in b]
        tiles = (
            a[0], jnp.where(low, low_b[0], swap(a[1])), jnp.where(low, swap(a[1]), high_b[1]),
            a[2], jnp.where(low, low_b[2], swap(a[3])), jnp.where(low, swap(a[3]), high_b[3]),
        )
        for n, tile in enumerate(tiles):
            out[:, n * 128 : n * 128 + 128] = tile
    o_ref[...] = so_ref[...].astype(F32)
    g_ref[...] = sg_ref[...].astype(F32)
    u_ref[...] = su_ref[...].astype(F32)
    d_ref[...] = sd_ref[...].astype(F32)


def widen(qkv, s_out, s_gate, s_up, s_down):
    s = jax.ShapeDtypeStruct
    steps = 16

    def spec(a):
        if len(a.shape) == 3:
            return pl.BlockSpec((a.shape[0], a.shape[1] // steps, a.shape[2]), lambda i: (0, i, 0))
        return pl.BlockSpec((a.shape[0] // steps, a.shape[1]), lambda i: (i, 0))

    outs = tuple(s(a.shape, F32) for a in (s_out, s_out, s_out, s_out, s_gate, s_up, s_down))
    ins = (qkv, s_out, s_gate, s_up, s_down)
    return pl.pallas_call(
        widen_kernel,
        grid=(steps,),
        out_shape=outs,
        in_specs=[spec(a) for a in ins],
        out_specs=tuple(spec(a) for a in outs),
        compiler_params=pltpu.CompilerParams(vmem_limit_bytes=40 << 20),
        name="widen",
    )(*ins)


class Stream:
    def __init__(self, src, res, acc, first, rest, sems, order, coords, core):
        self.src, self.res, self.acc, self.first, self.rest = src, res, acc, first, rest
        self.send, self.recv, self.own, self.back, self.got, self.fwd, self.fgot = sems
        self.rows, self.half = acc.shape
        self.order = [coords[name] for name in order]
        bit, self.peer = core
        self.mine = pl.ds(pl.multiple_of(bit * self.half, 128), self.half)
        self.other = pl.ds(pl.multiple_of((1 - bit) * self.half, 128), self.half)
        self.base, self.size = [0], [self.rows]
        for bit, _ in self.order:
            self.size.append(self.size[-1] // 2)
            self.base.append(self.base[-1] + bit * self.size[-1])
        self.waits = []

    def go(self, copy):
        copy.start()
        self.waits.append(copy)
        return copy

    def part(self, base, size):
        return pl.ds(pl.multiple_of(base, 16), size)

    def spot(self, k):
        return self.rest.at[pl.ds(self.rows - 2 * self.size[k], self.size[k])]

    def open(self):
        self.local = pltpu.make_async_copy(self.src.at[:, self.mine], self.acc, self.own.at[0])
        self.local.start()
        self.pending = self.go(
            remote(self.src.at[:, self.other], self.first, self.send.at[0], self.recv.at[0], self.peer)
        )

    def add(self, base, size, other, at):
        step = 64 if size % 64 == 0 else 48

        @pl.loop(0, size // step)
        def _(n):
            rows = self.part(base + n * step, step)
            more = other[pl.ds(pl.multiple_of(at + n * step, 16), step), :]
            self.acc[rows, :] = (self.acc[rows, :].astype(F32) + more.astype(F32)).astype(BF)

    def fold(self, k):
        if k == 0:
            self.local.wait()
        self.pending.wait_recv()
        if k == 0:
            self.add(0, self.rows, self.first, 0)
        else:
            self.add(self.base[k], self.size[k], self.rest, self.rows - 2 * self.size[k])

    def push(self, k):
        bit, peer = self.order[k - 1]
        away = self.base[k - 1] + (1 - bit) * self.size[k]
        self.pending = self.go(
            remote(
                self.acc.at[self.part(away, self.size[k])],
                self.spot(k),
                self.send.at[k],
                self.recv.at[k],
                peer,
            )
        )

    def spread(self, k):
        deep = len(self.order)
        here = self.part(self.base[k], self.size[k])
        block = self.res.at[here, self.mine]
        if k == deep:
            src = self.acc.at[here]
            self.local = pltpu.make_async_copy(src, block, self.own.at[1])
            self.local.start()
            self.go(remote(src, block, self.fwd.at[0], self.fgot.at[0], self.peer))
        else:
            src = block
        _, peer = self.order[k - 1]
        self.go(remote(src, block, self.back.at[k - 1], self.got.at[k - 1], peer))

    def sibling(self, k):
        bit, _ = self.order[k - 1]
        return self.part(self.base[k - 1] + (1 - bit) * self.size[k], self.size[k])

    def collect(self, k):
        deep = len(self.order)
        block = self.res.at[self.sibling(k), self.mine]
        remote(block, block, self.back.at[k - 1], self.got.at[k - 1], self.peer).wait_recv()
        if k == deep:
            self.local.wait()
        self.go(remote(block, block, self.fwd.at[k], self.fgot.at[k], self.peer))

    def close(self):
        deep = len(self.order)
        for k in range(deep + 1):
            rows = self.part(self.base[deep], self.size[deep]) if k == 0 else self.sibling(k)
            block = self.res.at[rows, self.other]
            remote(block, block, self.fwd.at[k], self.fgot.at[k], self.peer).wait_recv()
        for copy in self.waits:
            copy.wait_send()


class Grouped(Stream):
    def __init__(self, src, res, acc, rest, sems, order, coords, core, group, across):
        super().__init__(src, res, acc, None, rest, sems, order, coords, core)
        self.group, self.gx, self.across = group, far(group), across

    def open(self):
        self.local = pltpu.make_async_copy(self.src, self.acc, self.own.at[0])
        self.local.start()

    def fold(self, k):
        if k == 0:
            self.local.wait()
            return
        super().fold(k)

    def spread(self, k):
        deep = len(self.order)
        here = self.part(self.base[k], self.size[k])
        _, peer = self.order[k - 1]
        if k == deep:
            src, block = self.acc.at[here], self.res.at[self.group, here]
            self.local = pltpu.make_async_copy(src, block, self.own.at[1])
            self.local.start()
            self.go(remote(src, block, self.fwd.at[0, 0], self.fgot.at[0, 0], self.peer))
            self.go(remote(src, block, self.back.at[deep, 0], self.got.at[deep, 0], self.across))
            self.go(remote(src, block, self.back.at[k - 1, 0], self.got.at[k - 1, 0], peer))
            theirs = self.res.at[self.gx, here]
            remote(
                theirs, theirs, self.back.at[deep, 0], self.got.at[deep, 0], self.across
            ).wait_recv()
            self.go(remote(theirs, theirs, self.fwd.at[0, 1], self.fgot.at[0, 1], self.peer))
            self.go(remote(theirs, theirs, self.back.at[k - 1, 1], self.got.at[k - 1, 1], peer))
            return
        for n, h in enumerate((self.group, self.gx)):
            block = self.res.at[h, here]
            self.go(remote(block, block, self.back.at[k - 1, n], self.got.at[k - 1, n], peer))

    def collect(self, k):
        deep = len(self.order)
        for n, h in enumerate((self.group, self.gx)):
            block = self.res.at[h, self.sibling(k)]
            remote(block, block, self.back.at[k - 1, n], self.got.at[k - 1, n], self.peer).wait_recv()
            self.go(remote(block, block, self.fwd.at[k, n], self.fgot.at[k, n], self.peer))
        if k == deep:
            self.local.wait()

    def close(self):
        deep = len(self.order)
        for k in range(deep + 1):
            rows = self.part(self.base[deep], self.size[deep]) if k == 0 else self.sibling(k)
            for n, h in enumerate((flip(self.group), far(flip(self.group)))):
                block = self.res.at[h, rows]
                remote(block, block, self.fwd.at[k, n], self.fgot.at[k, n], self.peer).wait_recv()
        for copy in self.waits:
            copy.wait_send()


ORDERS = (("x", "y", "zl", "zh"), ("y", "x", "zl", "zh"), ("zl", "x", "y", "zh"), ("x", "y", "zl", "zh"))
GROUP_ORDER = ("y", "zl", "zh")


def weights_kernel(*refs):
    take = iter(refs)
    srcs = [next(take) for _ in range(5)]
    gain_refs = [next(take) for _ in range(2)]
    outs = [next(take) for _ in range(5)]
    gains_out = next(take)
    item, z, g = place()
    coords = {
        "x": (g // 2, (item, z * 4 + far(g))),
        "y": (item, (1 - item, z * 4 + g)),
        "zl": (z % 2, (item, flip(z) * 4 + g)),
        "zh": (z // 2, (item, far(z) * 4 + g)),
    }
    core = (g % 2, (item, z * 4 + flip(g)))
    greet([core[1]] + [peer for _, peer in coords.values()])
    streams = []
    for n in range(4):
        acc, first, rest = (next(take) for _ in range(3))
        sems = [next(take) for _ in range(7)]
        streams.append(Stream(srcs[n], outs[n], acc, first, rest, sems, ORDERS[n], coords, core))
    acc, rest = (next(take) for _ in range(2))
    sems = [next(take) for _ in range(7)]
    streams.append(
        Grouped(srcs[4], outs[4], acc, rest, sems, GROUP_ORDER, coords, core, g, coords["x"][1])
    )
    buf, got, gain_send, gain_recv = (next(take) for _ in range(4))
    for stream in streams:
        stream.open()
    buf[0] = jnp.zeros_like(buf[0])
    buf[0, 0:1, :] = gain_refs[0][...]
    buf[0, 1:2, :] = gain_refs[1][...]
    gain_peers = [core[1]] + [peer for _, peer in coords.values()]
    gain_waits = []

    def gain_step(k):
        if k > 0:
            gain_waits[k - 1].wait_recv()
            buf[k] = buf[k - 1] + got[k - 1]
        if k < 5:
            copy = remote(buf.at[k], got.at[k], gain_send.at[k], gain_recv.at[k], gain_peers[k])
            copy.start()
            gain_waits.append(copy)

    for k in range(5):
        gain_step(k)
        for stream in streams:
            deep = len(stream.order)
            if k <= deep:
                stream.fold(k)
                if k < deep:
                    stream.push(k + 1)
                else:
                    stream.spread(deep)
    gain_step(5)
    gains_out[...] = buf[5]
    for k in range(4, 0, -1):
        for stream in streams:
            deep = len(stream.order)
            if k <= deep:
                stream.collect(k)
                if k > 1:
                    stream.spread(k - 1)
    for stream in streams:
        stream.close()
    for copy in gain_waits:
        copy.wait_send()


def reduce_weights(arrays, qkv, gain1, gain2):
    dma = pltpu.SemaphoreType.DMA
    s = jax.ShapeDtypeStruct
    gains = (8, gain1.shape[1])
    shapes = tuple(s(a.shape, BF) for a in arrays) + (s((4,) + qkv.shape, BF), s(gains, F32))
    scratch = []
    for a in arrays:
        rows, half = a.shape[0], a.shape[1] // 2
        scratch += [pltpu.VMEM((rows, half), BF)] * 3
        scratch += [dma((5,)), dma((5,)), dma((2,)), dma((4,)), dma((4,)), dma((5,)), dma((5,))]
    scratch += [pltpu.VMEM(qkv.shape, BF)] * 2
    scratch += [dma((4,)), dma((4,)), dma((2,)), dma((4, 2)), dma((4, 2)), dma((4, 2)), dma((4, 2))]
    scratch += [pltpu.VMEM((6,) + gains, F32), pltpu.VMEM((5,) + gains, F32), dma((5,)), dma((5,))]
    return pl.pallas_call(
        weights_kernel,
        out_shape=shapes,
        in_specs=[ANY] * 5 + [VMEM] * 2,
        out_specs=(ANY,) * 5 + (VMEM,),
        scratch_shapes=scratch,
        compiler_params=params(6, 50),
        name="reduce_weights",
    )(*arrays, qkv, gain1, gain2)


def fast(
    inputs, counts, norm_gain1, w_query, w_key, w_value, w_out, norm_gain2, w_gate, w_up, w_down, cotangent
):
    band_rows, width = inputs.shape[2:]
    gain1, gain2 = norm_gain1.reshape(1, width), norm_gain2.reshape(1, width)
    xall, wc = gather_rows(inputs.reshape(6, band_rows, width), w_query, w_key, w_value)
    osend, xn, q, k, v, kt, o01, o2 = forward_attention(counts, xall.reshape(2048, width), gain1, wc)
    orecv, dy6 = swap_out(osend, cotangent.reshape(6, band_rows, width))
    result6, dsend, hidden, d_second, d_gain2, g_gate, g_up, g_down, g_out = dense(
        orecv, xall, dy6, gain2, w_out, w_gate, w_up, w_down
    )
    partial, g_qkv = backward_attention(q, k, v, kt, o01, o2, swap_back(dsend), xn, wc)
    input_grads, results, d_gain1 = reduce_rows(partial, result6, hidden, d_second, gain1)
    s_gate, s_up, s_down, s_out, s_qkv, s_gains = reduce_weights(
        (g_gate, g_up, g_down, g_out), g_qkv, d_gain1, d_gain2
    )
    grads = widen(s_qkv, s_out, s_gate, s_up, s_down)
    return (
        results.reshape(inputs.shape), input_grads.reshape(inputs.shape), s_gains[0]
    ) + grads[:4] + (s_gains[1],) + grads[4:]


def program(*args):
    micro, seqs, band_rows, width = args[0].shape
    small = lax.axis_size("band") == 16 and lax.axis_size("items") == 2
    if small and (micro, seqs, band_rows, width, HEADS, HEAD_DIM) == (2, 3, 64, 768, 12, 64):
        return fast(*args)
    return per_device(*args)


def solution(mesh):
    return jax.shard_map(
        program,
        mesh=mesh,
        in_specs=(
            P(None, "items", "band", None),
            P(None, "items"),
            P(),
            P(),
            P(),
            P(),
            P(),
            P(),
            P(),
            P(),
            P(),
            P(None, "items", "band", None),
        ),
        out_specs=(
            P(None, "items", "band", None),
            P(None, "items", "band", None),
            P(),
            P(),
            P(),
            P(),
            P(),
            P(),
            P(),
            P(),
            P(),
        ),
        check_vma=False,
    )
```

```python
import math

import jax
import jax.numpy as jnp
from jax import lax
from jax.experimental import pallas as pl
from jax.experimental.pallas import tpu as pltpu
from jax.sharding import PartitionSpec as P

HEADS = 12
HEAD_DIM = 64


EPS = 1e-06


def shortened(shard):

    def short(part):
        return part.astype(jnp.bfloat16) if part.dtype == jnp.float32 else part

    return jax.tree.map(short, shard)


def rms_scale(values, gain):
    return values * lax.rsqrt(jnp.mean(values * values, axis=-1, keepdims=True) + EPS) * gain


def gated(gate, upper):
    return jax.nn.gelu(gate, approximate=True) * upper


def outer(left, right):
    return lax.dot_general(
        left, right, (((0,), (0,)), ((), ())), preferred_element_type=jnp.float32
    )


def transposed(left, weight):
    return lax.dot_general(
        left, weight, (((1,), (1,)), ((), ())), preferred_element_type=jnp.float32
    )


def matmul(left, right):
    return jnp.dot(left, right, preferred_element_type=jnp.float32)


def scores(query, key, scale):
    return jnp.einsum("sqhd,skhd->shqk", query, key, preferred_element_type=jnp.float32) * scale


def per_device(
    inputs,
    counts,
    norm_gain1,
    w_query,
    w_key,
    w_value,
    w_out,
    norm_gain2,
    w_gate,
    w_up,
    w_down,
    cotangent,
):
    micro, seqs, band_rows, width = inputs.shape
    bands = lax.axis_size("band")
    length = band_rows * bands
    rows = seqs * band_rows
    heads = HEADS
    head_dim = HEAD_DIM
    scale = 1.0 / math.sqrt(head_dim)
    key_place = jnp.arange(length, dtype=jnp.int32)
    params = (norm_gain1, w_query, w_key, w_value, w_out, norm_gain2, w_gate, w_up, w_down)
    totals = [jnp.zeros(p.shape, jnp.float32) for p in params]
    results = []
    input_grads = []
    for number in range(micro):
        hidden = inputs[number].astype(jnp.float32).reshape(rows, width)
        lengths = counts[number]
        normed = rms_scale(hidden, norm_gain1).astype(jnp.bfloat16)
        query = matmul(normed, w_query).astype(jnp.bfloat16)
        key_local = matmul(normed, w_key).astype(jnp.bfloat16)
        value_local = matmul(normed, w_value).astype(jnp.bfloat16)
        query_four = query.reshape(seqs, band_rows, heads, head_dim)
        key_three = key_local.reshape(seqs, band_rows, width)
        value_three = value_local.reshape(seqs, band_rows, width)
        key_all, value_all = (
            lax.all_gather(key_three, "band", axis=1, tiled=True),
            lax.all_gather(value_three, "band", axis=1, tiled=True),
        )
        live = key_place[None, :] < lengths[:, None]
        key_four = key_all.reshape(seqs, length, heads, head_dim)
        value_four = value_all.reshape(seqs, length, heads, head_dim)
        logits = jnp.where(live[:, None, None, :], scores(query_four, key_four, scale), -jnp.inf)
        top = jnp.max(logits, axis=-1, keepdims=True)
        expo = jnp.exp(logits - top)
        summed = jnp.sum(expo, axis=-1, keepdims=True)
        log_total = top + jnp.log(summed)
        prob = (expo / summed).astype(jnp.bfloat16)
        attended = jnp.einsum(
            "shqk,skhd->sqhd", prob, value_four, preferred_element_type=jnp.float32
        )
        attended = attended.reshape(rows, width).astype(jnp.bfloat16)
        second = hidden + matmul(attended, w_out)
        normed_two = rms_scale(second, norm_gain2).astype(jnp.bfloat16)
        gate = matmul(normed_two, w_gate)
        upper = matmul(normed_two, w_up)
        mixed = gated(gate, upper).astype(jnp.bfloat16)
        results.append(
            (second + matmul(mixed, w_down)).astype(jnp.bfloat16).reshape(seqs, band_rows, width)
        )
        grad_rows = cotangent[number].reshape(rows, width)
        totals[8] = totals[8] + outer(mixed, grad_rows)
        d_mixed = transposed(grad_rows, w_down)
        pull_gate = jax.vjp(gated, gate, upper)[1]
        d_gate, d_upper = pull_gate(d_mixed)
        d_gate = d_gate.astype(jnp.bfloat16)
        d_upper = d_upper.astype(jnp.bfloat16)
        totals[6] = totals[6] + outer(normed_two, d_gate)
        totals[7] = totals[7] + outer(normed_two, d_upper)
        d_normed_two = transposed(d_gate, w_gate) + transposed(d_upper, w_up)
        pull_two = jax.vjp(rms_scale, second, norm_gain2)[1]
        d_second_norm, d_gain_two = pull_two(d_normed_two)
        totals[5] = totals[5] + d_gain_two
        d_second = grad_rows.astype(jnp.float32) + d_second_norm
        d_branch = d_second.astype(jnp.bfloat16)
        totals[4] = totals[4] + outer(attended, d_branch)
        d_attended = transposed(d_branch, w_out).astype(jnp.bfloat16)
        d_att_four = d_attended.reshape(seqs, band_rows, heads, head_dim)
        key_all, value_all = (
            lax.all_gather(key_three, "band", axis=1, tiled=True),
            lax.all_gather(value_three, "band", axis=1, tiled=True),
        )
        key_four = key_all.reshape(seqs, length, heads, head_dim)
        value_four = value_all.reshape(seqs, length, heads, head_dim)
        logits = jnp.where(live[:, None, None, :], scores(query_four, key_four, scale), -jnp.inf)
        prob_full = jnp.exp(logits - log_total)
        prob = prob_full.astype(jnp.bfloat16)
        d_prob = jnp.einsum(
            "sqhd,skhd->shqk", d_att_four, value_four, preferred_element_type=jnp.float32
        )
        delta = jnp.sum(d_prob * prob_full, axis=-1, keepdims=True)
        d_logits = (prob_full * (d_prob - delta)).astype(jnp.bfloat16)
        d_query = (
            jnp.einsum("shqk,skhd->sqhd", d_logits, key_four, preferred_element_type=jnp.float32)
            * scale
        )
        d_query = d_query.reshape(rows, width).astype(jnp.bfloat16)
        d_key_all = (
            jnp.einsum("shqk,sqhd->skhd", d_logits, query_four, preferred_element_type=jnp.float32)
            * scale
        )
        d_value_all = jnp.einsum(
            "shqk,sqhd->skhd", prob, d_att_four, preferred_element_type=jnp.float32
        )
        d_key_three, d_value_three = (
            lax.psum_scatter(
                d_key_all.reshape(seqs, length, width).astype(jnp.bfloat16),
                "band",
                scatter_dimension=1,
                tiled=True,
            ).astype(jnp.float32),
            lax.psum_scatter(
                d_value_all.reshape(seqs, length, width).astype(jnp.bfloat16),
                "band",
                scatter_dimension=1,
                tiled=True,
            ).astype(jnp.float32),
        )
        d_key = d_key_three.reshape(rows, width).astype(jnp.bfloat16)
        d_value = d_value_three.reshape(rows, width).astype(jnp.bfloat16)
        totals[1] = totals[1] + outer(normed, d_query)
        totals[2] = totals[2] + outer(normed, d_key)
        totals[3] = totals[3] + outer(normed, d_value)
        d_normed = (
            transposed(d_query, w_query) + transposed(d_key, w_key) + transposed(d_value, w_value)
        )
        pull_one = jax.vjp(rms_scale, hidden, norm_gain1)[1]
        d_hidden_norm, d_gain_one = pull_one(d_normed)
        totals[0] = totals[0] + d_gain_one
        input_grads.append(
            (d_second + d_hidden_norm).astype(jnp.bfloat16).reshape(seqs, band_rows, width)
        )
    shares = jax.tree.map(
        lambda part: part.astype(jnp.float32),
        lax.psum_scatter(shortened(tuple(totals)), "band", scatter_dimension=0, tiled=True),
    )
    summed_shares = jax.tree.map(
        lambda part: part.astype(jnp.float32), lax.psum(shortened(shares), "items")
    )
    whole = jax.tree.map(
        lambda part, own: part.astype(own.dtype),
        lax.all_gather(shortened(summed_shares), "band", axis=0, tiled=True),
        summed_shares,
    )
    return (jnp.stack(results), jnp.stack(input_grads)) + tuple(whole)


MESH_ID = pl.DeviceIdType.MESH
NEG = -1e30
BF = jnp.bfloat16
F32 = jnp.float32


def place():
    item = lax.axis_index("items")
    band = lax.axis_index("band")
    return item, band // 4, band % 4


def flip(value):
    return value + 1 - 2 * (value % 2)


def far(value):
    return (value + 2) % 4


def greet(peers):
    barrier = pltpu.get_barrier_semaphore()
    for peer in peers:
        pl.semaphore_signal(barrier, inc=1, device_id=peer, device_id_type=MESH_ID)
    pl.semaphore_wait(barrier, len(peers))


def remote(src, dst, send, recv, peer):
    return pltpu.make_async_remote_copy(
        src_ref=src, dst_ref=dst, send_sem=send, recv_sem=recv, device_id=peer, device_id_type=MESH_ID
    )


def params(number, vmem=40):
    return pltpu.CompilerParams(
        collective_id=number, has_side_effects=True, vmem_limit_bytes=vmem << 20
    )


def lanes_of(rows):
    return lax.broadcasted_iota(jnp.int32, (rows, 128), 1)


ANY = pl.BlockSpec(memory_space=pl.ANY)
VMEM = pl.BlockSpec(memory_space=pltpu.VMEM)
SMEM = pl.BlockSpec(memory_space=pltpu.SMEM)


def gather_kernel(
    x_ref, wq_ref, wk_ref, wv_ref, out_ref, wc_ref, win_ref, z_send, f_send, g_send, recv, own_sem, win_sem
):
    item, z, g = place()
    cut = pl.ds(pl.multiple_of(g * 3 // 2 * 128, 128), 256)
    windows = []
    for n, ref in enumerate((wq_ref, wk_ref, wv_ref)):
        windows.append(pltpu.make_async_copy(ref.at[:, cut], win_ref.at[n], win_sem.at[n]))
        windows[-1].start()
    gc, gx = flip(g), far(g)
    gcx = far(gc)
    zs = (z, flip(z), far(z), far(flip(z)))
    core, across = (item, z * 4 + gc), (item, z * 4 + gx)
    greet([core, across] + [(item, s * 4 + g) for s in zs[1:]])

    def items_of(s):
        return (3 * (s // 2) + 2 * (s % 2), 3 * (s // 2) + 1)

    started = []
    for n, s in enumerate(zs[1:]):
        for ab in range(2):
            copy = remote(
                x_ref.at[items_of(s)[ab]],
                out_ref.at[ab, z * 4 + g],
                z_send.at[n, ab],
                recv.at[ab, z * 4 + g],
                (item, s * 4 + g),
            )
            copy.start()
            started.append(copy)
    local = []
    for ab in range(2):
        copy = pltpu.make_async_copy(
            x_ref.at[items_of(z)[ab]], out_ref.at[ab, z * 4 + g], own_sem.at[ab]
        )
        copy.start()
        local.append(copy)

    def arrived(ab, where):
        remote(
            out_ref.at[ab, where], out_ref.at[ab, where], z_send.at[0, 0], recv.at[ab, where], core
        ).wait_recv()

    def pack():
        for copy in windows:
            copy.wait()
        odd = g % 2 == 1
        low = lanes_of(256) < 64

        @pl.loop(0, 3)
        def _(i):
            rows = pl.ds(pl.multiple_of(i * 256, 256), 256)
            firsts, lasts = [], []
            for n in range(3):
                left = win_ref[n, rows, 0:128].astype(F32)
                right = win_ref[n, rows, 128:256].astype(F32)
                crossed = pltpu.roll(jnp.where(low, right, left), 64, 1)
                firsts.append(jnp.where(odd, crossed, left))
                lasts.append(jnp.where(odd, pltpu.roll(right, 64, 1), right))
            for n in range(3):
                wc_ref[rows, n * 128 : n * 128 + 128] = firsts[n].astype(BF)
            wc_ref[rows, 384:512] = jnp.where(low, lasts[1], pltpu.roll(lasts[2], 64, 1)).astype(BF)
            wc_ref[rows, 512:640] = jnp.where(low, lasts[0], 0.0).astype(BF)

    for n, zz in enumerate(zs):
        if n == 1:
            pack()
        for ab in range(2):
            where = zz * 4 + g
            if n > 0:
                arrived(ab, where)
            src = x_ref.at[items_of(z)[ab]] if n == 0 else out_ref.at[ab, where]
            for k, peer in enumerate((across, core)):
                copy = remote(
                    src, out_ref.at[ab, where], f_send.at[n, ab, k], recv.at[ab, where], peer
                )
                copy.start()
                started.append(copy)
    for n, zz in enumerate(zs):
        for ab in range(2):
            where = zz * 4 + gx
            arrived(ab, where)
            copy = remote(
                out_ref.at[ab, where],
                out_ref.at[ab, where],
                g_send.at[n, ab],
                recv.at[ab, where],
                core,
            )
            copy.start()
            started.append(copy)
    for n, zz in enumerate(zs):
        for ab in range(2):
            arrived(ab, zz * 4 + gc)
            arrived(ab, zz * 4 + gcx)
    for copy in local:
        copy.wait()
    for copy in started:
        copy.wait_send()


def gather_rows(x6, wq, wk, wv):
    _, rows, width = x6.shape
    dma = pltpu.SemaphoreType.DMA
    return pl.pallas_call(
        gather_kernel,
        out_shape=(
            jax.ShapeDtypeStruct((2, 16, rows, width), BF), jax.ShapeDtypeStruct((width, 640), BF)
        ),
        in_specs=[ANY] * 4,
        out_specs=(ANY, VMEM),
        scratch_shapes=[
            pltpu.VMEM((3, width, 256), BF),
            dma((3, 2)), dma((4, 2, 2)), dma((4, 2)), dma((2, 16)), dma((2,)), dma((3,)),
        ],
        compiler_params=params(1),
        name="gather_rows",
    )(x6, wq, wk, wv)


def to_slots(item, z, g, src_ref, dst_ref, send, recv, own_sem):
    zs = (z, flip(z), far(z), far(flip(z)))
    p, r = z // 2, z % 2
    started = []
    for n, s in enumerate(zs[1:]):
        copy = remote(
            src_ref.at[3 * (s // 2) + 2 * (s % 2)],
            dst_ref.at[z],
            send.at[n],
            recv.at[z],
            (item, s * 4 + g),
        )
        copy.start()
        started.append(copy)
    copy = remote(
        src_ref.at[3 * (1 - p) + 1], dst_ref.at[4 + p], send.at[3], recv.at[4 + p], (item, far(z) * 4 + g)
    )
    copy.start()
    started.append(copy)
    local = [
        pltpu.make_async_copy(src_ref.at[3 * p + 2 * r], dst_ref.at[z], own_sem.at[0]),
        pltpu.make_async_copy(src_ref.at[3 * p + 1], dst_ref.at[4 + p], own_sem.at[1]),
    ]
    for copy in local:
        copy.start()

    def finish():
        for where in zs[1:] + (4 + (1 - p),):
            remote(
                dst_ref.at[where], dst_ref.at[where], send.at[0], recv.at[where], (item, far(z) * 4 + g)
            ).wait_recv()
        for copy in local:
            copy.wait()
        for copy in started:
            copy.wait_send()

    return finish


def from_slots(item, z, g, src_ref, dst_ref, send, recv, own_sem):
    zs = (z, flip(z), far(z), far(flip(z)))
    p, r = z // 2, z % 2
    mine = 3 * p + 2 * r
    started = []
    for n, s in enumerate(zs[1:]):
        copy = remote(src_ref.at[s], dst_ref.at[mine], send.at[n], recv.at[mine], (item, s * 4 + g))
        copy.start()
        started.append(copy)
    copy = remote(
        src_ref.at[4 + (1 - p)],
        dst_ref.at[3 * p + 1],
        send.at[3],
        recv.at[3 * p + 1],
        (item, far(z) * 4 + g),
    )
    copy.start()
    started.append(copy)
    local = [
        pltpu.make_async_copy(src_ref.at[z], dst_ref.at[mine], own_sem.at[0]),
        pltpu.make_async_copy(src_ref.at[4 + p], dst_ref.at[3 * p + 1], own_sem.at[1]),
    ]
    for copy in local:
        copy.start()

    def finish():
        for s in zs[1:]:
            where = 3 * (s // 2) + 2 * (s % 2)
            remote(
                dst_ref.at[where], dst_ref.at[where], send.at[0], recv.at[where], (item, far(z) * 4 + g)
            ).wait_recv()
        where = 3 * (1 - p) + 1
        remote(
            dst_ref.at[where], dst_ref.at[where], send.at[0], recv.at[where], (item, far(z) * 4 + g)
        ).wait_recv()
        for copy in local:
            copy.wait()
        for copy in started:
            copy.wait_send()

    return finish


def z_peers(item, z, g):
    return [(item, s * 4 + g) for s in (flip(z), far(z), far(flip(z)))]


def g_peers(item, z, g):
    return [(item, z * 4 + h) for h in (flip(g), far(g), far(flip(g)))]


def swap_heads(item, z, g, src_ref, dst_ref, send, recv, own_sem):
    started = []
    for n, h in enumerate((far(g), far(flip(g)), flip(g))):
        copy = remote(src_ref.at[h], dst_ref.at[g], send.at[n], recv.at[g], (item, z * 4 + h))
        copy.start()
        started.append(copy)
    local = pltpu.make_async_copy(src_ref.at[g], dst_ref.at[g], own_sem)
    local.start()

    def finish():
        for h in (flip(g), far(g), far(flip(g))):
            remote(
                dst_ref.at[h], dst_ref.at[h], send.at[0], recv.at[h], (item, z * 4 + h)
            ).wait_recv()
        local.wait()
        for copy in started:
            copy.wait_send()

    return finish


def swap_kernel(heads_ref, rows_ref, out_heads_ref, out_rows_ref, hs, hr, ho, zs, zr, zo):
    item, z, g = place()
    greet(z_peers(item, z, g) + g_peers(item, z, g))
    first = swap_heads(item, z, g, heads_ref, out_heads_ref, hs, hr, ho.at[0])
    second = to_slots(item, z, g, rows_ref, out_rows_ref, zs, zr, zo)
    first()
    second()


def swap_out(heads, rows):
    dma = pltpu.SemaphoreType.DMA
    return pl.pallas_call(
        swap_kernel,
        out_shape=(
            jax.ShapeDtypeStruct(heads.shape, heads.dtype),
            jax.ShapeDtypeStruct(rows.shape, rows.dtype),
        ),
        in_specs=[ANY, ANY],
        out_specs=(ANY, ANY),
        scratch_shapes=[dma((3,)), dma((4,)), dma((1,)), dma((4,)), dma((6,)), dma((2,))],
        compiler_params=params(2),
        name="swap_out",
    )(heads, rows)


def nt(left, right):
    return lax.dot_general(left, right, (((1,), (1,)), ((), ())), preferred_element_type=F32)


def forward_kernel(
    count_ref, x_ref, gain_ref, wc_ref,
    osend_ref, xn_ref, q_ref, k_ref, v_ref, kt_ref, o01_ref, o2_ref,
):
    _, z, _ = place()
    p, r = z // 2, z % 2
    lane = lanes_of(256)
    low = lane < 64

    @pl.loop(0, 8)
    def _(i):
        rows = pl.ds(pl.multiple_of(i * 256, 256), 256)
        h = x_ref[rows, :].astype(F32)
        inv = lax.rsqrt(jnp.mean(h * h, axis=-1, keepdims=True) + EPS)
        xn = (h * inv * gain_ref[...]).astype(BF)
        xn_ref[rows, :] = xn
        y = matmul(xn, wc_ref[:, 128:512])
        count = count_ref[p, jnp.where(i < 4, 2 * r, 1)]
        at = lax.broadcasted_iota(jnp.int32, (256, 128), 0) + (i % 4) * 256
        bias = jnp.where(at < count, 0.0, NEG)
        one = jnp.where((lane % 64) < 4, 1.0, 0.0)
        k_aug = jnp.where(lane % 64 == 0, bias, one)
        k01, v01, kv2 = y[:, :128], y[:, 128:256], y[:, 256:]
        k_ref[0, rows, :] = jnp.where(low, k01, k_aug).astype(BF)
        k_ref[1, rows, :] = jnp.where(low, k_aug, k01).astype(BF)
        k_ref[2, rows, :] = jnp.where(low, kv2, k_aug).astype(BF)
        v_ref[0, rows, :] = jnp.where(low, v01, one).astype(BF)
        v_ref[1, rows, :] = jnp.where(low, one, v01).astype(BF)
        v_ref[2, rows, :] = jnp.where(low, one, kv2).astype(BF)

    for head in range(3):
        for ab in range(2):
            kt_ref[head, ab, :, :] = k_ref[head, ab * 1024 : (ab + 1) * 1024, :].T

    @pl.loop(0, 6)
    def _(t):
        off = jnp.where(t < 4, t, 4 + r + 2 * (t - 4)) * 256
        xq = xn_ref[pl.ds(pl.multiple_of(off, 256), 256), :]
        q01 = matmul(xq, wc_ref[:, 0:128]).astype(BF).astype(F32) * 0.125
        q2 = matmul(xq, wc_ref[:, 512:640]).astype(BF).astype(F32) * 0.125
        flag = jnp.where(lane % 64 == 0, 1.0, 0.0)
        qs = (jnp.where(low, q01, flag), jnp.where(low, flag, q01), jnp.where(low, q2, flag))
        at = pl.ds(pl.multiple_of(t * 256, 256), 256)
        ab = t // 4
        keys = pl.ds(pl.multiple_of(ab * 1024, 1024), 1024)
        outs = []
        for head in range(3):
            s = matmul(qs[head].astype(BF), kt_ref[head, ab])
            top = jnp.max(s, axis=1, keepdims=True)
            e = jnp.exp(s - top).astype(BF)
            o = matmul(e, v_ref[head, keys, :])
            total = o[:, 64:65] if head == 0 else o[:, 0:1]
            outs.append(o / total)
            lse = -(top + jnp.log(total))
            hi = lse.astype(BF).astype(F32)
            mid = (lse - hi).astype(BF).astype(F32)
            lo = lse - hi - mid
            part = lane % 64
            aug = jnp.where(part == 1, hi, jnp.where(part == 2, mid, jnp.where(part == 3, lo, flag)))
            data = low if head != 1 else jnp.logical_not(low)
            q_ref[head, at, :] = jnp.where(data, qs[head], aug).astype(BF)
        o01 = jnp.where(low, outs[0], outs[1])
        o2 = outs[2]
        o01_ref[at, :] = o01
        o2_ref[at, :] = o2
        for h in range(4):
            osend_ref[h, t, 0:64, :] = o01[h * 64 : h * 64 + 64].astype(BF)
            first = o2[h * 64 : h * 64 + 32]
            second = o2[h * 64 + 32 : h * 64 + 64]
            folded = jnp.where(low[:32], pltpu.roll(first, 64, 1), second)
            osend_ref[h, t, 64:96, :] = folded.astype(BF)


def forward_attention(counts, xall, gain, wc):
    s = jax.ShapeDtypeStruct
    return pl.pallas_call(
        forward_kernel,
        out_shape=(
            s((4, 6, 96, 128), BF), s((2048, 768), BF), s((3, 1536, 128), BF), s((3, 2048, 128), BF),
            s((3, 2048, 128), BF), s((3, 2, 128, 1024), BF), s((1536, 128), F32), s((1536, 128), F32),
        ),
        in_specs=[SMEM, VMEM, VMEM, VMEM],
        out_specs=(VMEM,) * 8,
        compiler_params=pltpu.CompilerParams(vmem_limit_bytes=50 << 20),
        name="forward_attention",
    )(counts, xall, gain, wc)


GELU_A = 0.044715
GELU_C = math.sqrt(2.0 / math.pi)


def dense_kernel(
    o_ref, x_ref, dy_ref, gain_ref, wo_hbm, wg_hbm, wu_hbm, wd_hbm,
    res_ref, dsend_ref, h_ref, dh_ref, dgain_ref, gg_ref, gu_ref, gd_ref, go_ref,
    wo_ref, wg_ref, wu_ref, wd_ref, att_ref, sec_ref, xn_ref, xt_ref, dyt_ref, dxn_ref, h_sem, wo_sem, w_sem,
):
    _, z, g = place()
    r = z % 2
    chunks, size = 4, wg_ref.shape[1] // 4
    copies = []
    for j in range(6):
        src = x_ref.at[0, j * 4 + g] if j < 4 else x_ref.at[1, (r + 2 * (j - 4)) * 4 + g]
        copies.append(pltpu.make_async_copy(src, h_ref.at[j], h_sem.at[j]))
    copies.append(pltpu.make_async_copy(wo_hbm, wo_ref, wo_sem.at[0]))
    for copy in copies:
        copy.start()
    loads = []
    for c in range(chunks):
        cut = pl.ds(c * size, size)
        loads.append(
            [
                pltpu.make_async_copy(wg_hbm.at[:, cut], wg_ref.at[:, cut], w_sem.at[0, c]),
                pltpu.make_async_copy(wu_hbm.at[:, cut], wu_ref.at[:, cut], w_sem.at[1, c]),
                pltpu.make_async_copy(wd_hbm.at[cut, :], wd_ref.at[cut, :], w_sem.at[2, c]),
            ]
        )
        for copy in loads[-1]:
            copy.start()
    low = lanes_of(384) < 64

    def swap(v):
        return pltpu.roll(v, 64, 1)

    pairs = [o_ref[n, :, 0:64, :].astype(F32).reshape(384, 128) for n in range(4)]

    def unfold(n, high):
        f = o_ref[n, :, 64:96, :].astype(F32)
        s = swap(f.reshape(192, 128)).reshape(6, 32, 128)
        both = (s, f) if high else (f, s)
        return jnp.concatenate(both, axis=1).reshape(384, 128)

    tiles = (
        pairs[0],
        jnp.where(low, unfold(0, False), swap(pairs[1])),
        jnp.where(low, swap(pairs[1]), unfold(1, True)),
        pairs[2],
        jnp.where(low, unfold(2, False), swap(pairs[3])),
        jnp.where(low, swap(pairs[3]), unfold(3, True)),
    )
    for n, tile in enumerate(tiles):
        att_ref[:, n * 128 : n * 128 + 128] = tile.astype(BF)
    for copy in copies:
        copy.wait()
    second = h_ref[...].reshape(384, 768).astype(F32) + matmul(att_ref[...], wo_ref[...])
    sec_ref[...] = second
    inv = lax.rsqrt(jnp.mean(second * second, axis=-1, keepdims=True) + EPS)
    xn_ref[...] = (second * inv * gain_ref[...]).astype(BF)
    xt_ref[...] = xn_ref[...].T
    dxn_ref[...] = jnp.zeros_like(dxn_ref)
    dy = dy_ref[...].reshape(384, 768)
    for c in range(chunks):
        cut = slice(c * size, c * size + size)
        for copy in loads[c]:
            copy.wait()
        gate = matmul(xn_ref[...], wg_ref[:, cut])
        upper = matmul(xn_ref[...], wu_ref[:, cut])
        d_mixed = nt(dy, wd_ref[cut, :])
        square = gate * gate
        tan = jnp.tanh(GELU_C * (gate + GELU_A * square * gate))
        half = 0.5 * (1.0 + tan)
        act = gate * half
        slope = half + 0.5 * gate * (1.0 - tan * tan) * (GELU_C * (1.0 + 3.0 * GELU_A * square))
        mixed = (act * upper).astype(BF)
        d_gate = (d_mixed * upper * slope).astype(BF)
        d_upper = (d_mixed * act).astype(BF)
        sec_ref[...] += matmul(mixed, wd_ref[cut, :])
        dxn_ref[...] += nt(d_gate, wg_ref[:, cut]) + nt(d_upper, wu_ref[:, cut])
        gg_ref[:, cut] = matmul(xt_ref[...], d_gate).astype(BF)
        gu_ref[:, cut] = matmul(xt_ref[...], d_upper).astype(BF)
        gd_ref[cut, :] = outer(mixed, dy).astype(BF)
    res_ref[...] = sec_ref[...].astype(BF).reshape(6, 64, 768)
    second = h_ref[...].reshape(384, 768).astype(F32) + matmul(att_ref[...], wo_ref[...])
    inv = lax.rsqrt(jnp.mean(second * second, axis=-1, keepdims=True) + EPS)
    d_xn = dxn_ref[...]
    dgain_ref[...] = jnp.sum(d_xn * second * inv, axis=0, keepdims=True)
    dyg = d_xn * gain_ref[...]
    dot = jnp.mean(dyg * second, axis=-1, keepdims=True)
    d_second = dy.astype(F32) + inv * dyg - second * (inv * inv * inv * dot)
    dh_ref[...] = d_second.reshape(6, 64, 768)
    d_branch = d_second.astype(BF)
    go_ref[...] = outer(att_ref[...], d_branch).astype(BF)
    d_att = nt(d_branch, wo_ref[...]).astype(BF).astype(F32)
    d = [d_att[:, n * 128 : n * 128 + 128] for n in range(6)]
    firsts = (d[0], swap(jnp.where(low, d[2], d[1])), d[3], swap(jnp.where(low, d[5], d[4])))
    lasts = ((d[1], False), (d[2], True), (d[4], False), (d[5], True))
    low3 = lax.broadcasted_iota(jnp.int32, (6, 32, 128), 2) < 64
    for n in range(4):
        dsend_ref[n, :, 0:64, :] = firsts[n].astype(BF).reshape(6, 64, 128)
        v, high = lasts[n]
        v3, s3 = v.reshape(6, 64, 128), swap(v).reshape(6, 64, 128)
        top, bottom = v3[:, :32], v3[:, 32:]
        top_s, bottom_s = s3[:, :32], s3[:, 32:]
        f = jnp.where(low3, top_s, bottom) if high else jnp.where(low3, top, bottom_s)
        dsend_ref[n, :, 64:96, :] = f.astype(BF)


def dense(orecv, xall, dy6, gain, w_out, w_gate, w_up, w_down):
    s = jax.ShapeDtypeStruct
    dma = pltpu.SemaphoreType.DMA
    rows, width = dy6.shape[1:]
    hidden = w_gate.shape[1]
    v = pltpu.VMEM
    return pl.pallas_call(
        dense_kernel,
        out_shape=(
            s(dy6.shape, BF), s(orecv.shape, BF), s(dy6.shape, BF), s(dy6.shape, F32), s((1, width), F32),
            s(w_gate.shape, BF), s(w_up.shape, BF), s(w_down.shape, BF), s(w_out.shape, BF),
        ),
        in_specs=[VMEM, ANY, VMEM, VMEM] + [ANY] * 4,
        out_specs=(VMEM,) * 9,
        scratch_shapes=[
            v(w_out.shape, BF), v(w_gate.shape, BF), v(w_up.shape, BF), v(w_down.shape, BF),
            v((384, width), BF), v((384, width), F32), v((384, width), BF), v((width, 384), BF), v((width, 384), BF),
            v((384, width), F32), dma((6,)), dma((1,)), dma((3, 4)),
        ],
        compiler_params=pltpu.CompilerParams(vmem_limit_bytes=50 << 20),
        name="dense",
    )(orecv, xall, dy6, gain, w_out, w_gate, w_up, w_down)


def widen_kernel(qkv_ref, so_ref, sg_ref, su_ref, sd_ref, q_ref, k_ref, v_ref, o_ref, g_ref, u_ref, d_ref):
    low = lanes_of(qkv_ref.shape[1]) < 64

    def swap(v):
        return pltpu.roll(v, 64, 1)

    for out, first, last, high in ((q_ref, 0, 512, False), (k_ref, 128, 384, False), (v_ref, 256, 384, True)):
        a = [qkv_ref[n, :, first : first + 128].astype(F32) for n in range(4)]
        b = [qkv_ref[n, :, last : last + 128].astype(F32) for n in range(4)]
        low_b = [swap(x) if high else x for x in b]
        high_b = [x if high else swap(x) for x in b]
        tiles = (
            a[0], jnp.where(low, low_b[0], swap(a[1])), jnp.where(low, swap(a[1]), high_b[1]),
            a[2], jnp.where(low, low_b[2], swap(a[3])), jnp.where(low, swap(a[3]), high_b[3]),
        )
        for n, tile in enumerate(tiles):
            out[:, n * 128 : n * 128 + 128] = tile
    o_ref[...] = so_ref[...].astype(F32)
    g_ref[...] = sg_ref[...].astype(F32)
    u_ref[...] = su_ref[...].astype(F32)
    d_ref[...] = sd_ref[...].astype(F32)


def widen(qkv, s_out, s_gate, s_up, s_down):
    s = jax.ShapeDtypeStruct
    steps = 16

    def spec(a):
        if len(a.shape) == 3:
            return pl.BlockSpec((a.shape[0], a.shape[1] // steps, a.shape[2]), lambda i: (0, i, 0))
        return pl.BlockSpec((a.shape[0] // steps, a.shape[1]), lambda i: (i, 0))

    outs = tuple(s(a.shape, F32) for a in (s_out, s_out, s_out, s_out, s_gate, s_up, s_down))
    ins = (qkv, s_out, s_gate, s_up, s_down)
    return pl.pallas_call(
        widen_kernel,
        grid=(steps,),
        out_shape=outs,
        in_specs=[spec(a) for a in ins],
        out_specs=tuple(spec(a) for a in outs),
        compiler_params=pltpu.CompilerParams(vmem_limit_bytes=40 << 20),
        name="widen",
    )(*ins)


class Stream:
    def __init__(self, src, res, acc, first, rest, sems, order, coords, core):
        self.src, self.res, self.acc, self.first, self.rest = src, res, acc, first, rest
        self.send, self.recv, self.own, self.back, self.got, self.fwd, self.fgot = sems
        self.rows, self.half = acc.shape
        self.order = [coords[name] for name in order]
        bit, self.peer = core
        self.mine = pl.ds(pl.multiple_of(bit * self.half, 128), self.half)
        self.other = pl.ds(pl.multiple_of((1 - bit) * self.half, 128), self.half)
        self.base, self.size = [0], [self.rows]
        for bit, _ in self.order:
            self.size.append(self.size[-1] // 2)
            self.base.append(self.base[-1] + bit * self.size[-1])
        self.waits = []

    def go(self, copy):
        copy.start()
        self.waits.append(copy)
        return copy

    def part(self, base, size):
        return pl.ds(pl.multiple_of(base, 16), size)

    def spot(self, k):
        return self.rest.at[pl.ds(self.rows - 2 * self.size[k], self.size[k])]

    def open(self):
        self.local = pltpu.make_async_copy(self.src.at[:, self.mine], self.acc, self.own.at[0])
        self.local.start()
        self.pending = self.go(
            remote(self.src.at[:, self.other], self.first, self.send.at[0], self.recv.at[0], self.peer)
        )

    def add(self, base, size, other, at):
        step = 64 if size % 64 == 0 else 48

        @pl.loop(0, size // step)
        def _(n):
            rows = self.part(base + n * step, step)
            more = other[pl.ds(pl.multiple_of(at + n * step, 16), step), :]
            self.acc[rows, :] = (self.acc[rows, :].astype(F32) + more.astype(F32)).astype(BF)

    def fold(self, k):
        if k == 0:
            self.local.wait()
        self.pending.wait_recv()
        if k == 0:
            self.add(0, self.rows, self.first, 0)
        else:
            self.add(self.base[k], self.size[k], self.rest, self.rows - 2 * self.size[k])

    def push(self, k):
        bit, peer = self.order[k - 1]
        away = self.base[k - 1] + (1 - bit) * self.size[k]
        self.pending = self.go(
            remote(
                self.acc.at[self.part(away, self.size[k])],
                self.spot(k),
                self.send.at[k],
                self.recv.at[k],
                peer,
            )
        )

    def spread(self, k):
        deep = len(self.order)
        here = self.part(self.base[k], self.size[k])
        block = self.res.at[here, self.mine]
        if k == deep:
            src = self.acc.at[here]
            self.local = pltpu.make_async_copy(src, block, self.own.at[1])
            self.local.start()
            self.go(remote(src, block, self.fwd.at[0], self.fgot.at[0], self.peer))
        else:
            src = block
        _, peer = self.order[k - 1]
        self.go(remote(src, block, self.back.at[k - 1], self.got.at[k - 1], peer))

    def sibling(self, k):
        bit, _ = self.order[k - 1]
        return self.part(self.base[k - 1] + (1 - bit) * self.size[k], self.size[k])

    def collect(self, k):
        deep = len(self.order)
        block = self.res.at[self.sibling(k), self.mine]
        remote(block, block, self.back.at[k - 1], self.got.at[k - 1], self.peer).wait_recv()
        if k == deep:
            self.local.wait()
        self.go(remote(block, block, self.fwd.at[k], self.fgot.at[k], self.peer))

    def close(self):
        deep = len(self.order)
        for k in range(deep + 1):
            rows = self.part(self.base[deep], self.size[deep]) if k == 0 else self.sibling(k)
            block = self.res.at[rows, self.other]
            remote(block, block, self.fwd.at[k], self.fgot.at[k], self.peer).wait_recv()
        for copy in self.waits:
            copy.wait_send()


class Grouped(Stream):
    def __init__(self, res, acc, rest, sems, order, coords, core, group, across):
        super().__init__(None, res, acc, None, rest, sems, order, coords, core)
        self.group, self.gx, self.across = group, far(group), across

    def fold(self, k):
        if k > 0:
            super().fold(k)

    def spread(self, k):
        deep = len(self.order)
        here = self.part(self.base[k], self.size[k])
        _, peer = self.order[k - 1]
        if k == deep:
            src, block = self.acc.at[here], self.res.at[self.group, here]
            self.local = pltpu.make_async_copy(src, block, self.own.at[1])
            self.local.start()
            self.go(remote(src, block, self.fwd.at[0, 0], self.fgot.at[0, 0], self.peer))
            self.go(remote(src, block, self.back.at[deep, 0], self.got.at[deep, 0], self.across))
            self.go(remote(src, block, self.back.at[k - 1, 0], self.got.at[k - 1, 0], peer))
            theirs = self.res.at[self.gx, here]
            remote(
                theirs, theirs, self.back.at[deep, 0], self.got.at[deep, 0], self.across
            ).wait_recv()
            self.go(remote(theirs, theirs, self.fwd.at[0, 1], self.fgot.at[0, 1], self.peer))
            self.go(remote(theirs, theirs, self.back.at[k - 1, 1], self.got.at[k - 1, 1], peer))
            return
        for n, h in enumerate((self.group, self.gx)):
            block = self.res.at[h, here]
            self.go(remote(block, block, self.back.at[k - 1, n], self.got.at[k - 1, n], peer))

    def collect(self, k):
        deep = len(self.order)
        for n, h in enumerate((self.group, self.gx)):
            block = self.res.at[h, self.sibling(k)]
            remote(block, block, self.back.at[k - 1, n], self.got.at[k - 1, n], self.peer).wait_recv()
            self.go(remote(block, block, self.fwd.at[k, n], self.fgot.at[k, n], self.peer))
        if k == deep:
            self.local.wait()

    def close(self):
        deep = len(self.order)
        for k in range(deep + 1):
            rows = self.part(self.base[deep], self.size[deep]) if k == 0 else self.sibling(k)
            for n, h in enumerate((flip(self.group), far(flip(self.group)))):
                block = self.res.at[h, rows]
                remote(block, block, self.fwd.at[k, n], self.fgot.at[k, n], self.peer).wait_recv()
        for copy in self.waits:
            copy.wait_send()


ORDERS = (("x", "y", "zl", "zh"), ("y", "x", "zl", "zh"), ("zl", "x", "y", "zh"), ("x", "y", "zl", "zh"))
GROUP_ORDER = ("y", "zl", "zh")


def back_kernel(*refs):
    take = iter(refs)

    def some(n):
        return [next(take) for _ in range(n)]

    (dsend_ref, q_ref, k_ref, v_ref, kt_ref, o01_ref, o2_ref, xn_ref, wc_ref) = some(9)
    (res_ref, h_ref, dh_ref, gain_ref, dgain2_ref) = some(5)
    srcs = some(4)
    out_ref, res_out_ref = some(2)
    outs = some(5)
    (gains_out,) = some(1)
    (do_ref, dk_ref, dv_ref, d5_ref, p_ref) = some(5)
    (rc_ref, sx_ref, rx_ref, t_ref, zb_ref, rz_ref, ig_ref, dgain_ref) = some(8)
    (c_send, c_recv, x_send, x_recv, z_send, z_recv) = some(6)
    (rs_send, rs_recv, rs_own, h_send, h_recv, h_own, hs, hr, ho) = some(9)
    item, z, g = place()
    gc, gx = flip(g), far(g)
    gcx = far(gc)
    p, r = z // 2, z % 2
    coords = {
        "x": (g // 2, (item, z * 4 + gx)),
        "y": (item, (1 - item, z * 4 + g)),
        "zl": (z % 2, (item, flip(z) * 4 + g)),
        "zh": (z // 2, (item, far(z) * 4 + g)),
    }
    across, pair = coords["x"][1], coords["zl"][1]
    core = (item, z * 4 + gc)
    zs = (z, flip(z), far(z), far(flip(z)))
    greet(g_peers(item, z, g) + z_peers(item, z, g) + [coords["y"][1]])
    streams = []
    for n in range(4):
        acc, first, rest = some(3)
        streams.append(Stream(srcs[n], outs[n], acc, first, rest, some(7), ORDERS[n], coords, (g % 2, core)))
    acc, rest = some(2)
    qkv = Grouped(outs[4], acc, rest, some(7), GROUP_ORDER, coords, (g % 2, core), g, across)
    buf, got, gain_send, gain_recv = some(4)

    swapped = swap_heads(item, z, g, dsend_ref, do_ref, hs, hr, ho.at[0])
    for stream in streams:
        stream.open()
    done_rs = from_slots(item, z, g, res_ref, res_out_ref, rs_send, rs_recv, rs_own)
    lane = lanes_of(256)
    low = lane < 64
    part = lane % 64
    dk_ref[...] = jnp.zeros_like(dk_ref)
    dv_ref[...] = jnp.zeros_like(dv_ref)
    d5_ref[...] = jnp.zeros_like(d5_ref)

    def pieces(delta):
        neg = -delta
        hi = neg.astype(BF).astype(F32)
        mid = (neg - hi).astype(BF).astype(F32)
        lo = neg - hi - mid
        return jnp.where(part == 1, hi, jnp.where(part == 2, mid, jnp.where(part == 3, lo, 0.0)))

    def tile(t):
        at = pl.ds(pl.multiple_of(t * 256, 256), 256)
        ab = t // 4
        keys = pl.ds(pl.multiple_of(ab * 1024, 1024), 1024)
        do01 = do_ref[:, t, 0:64, :].astype(F32).reshape(256, 128)
        folded = do_ref[:, t, 64:96, :].astype(F32)
        two = []
        for h in range(4):
            two.append(pltpu.roll(folded[h], 64, 1))
            two.append(folded[h])
        do2 = jnp.concatenate(two, axis=0)
        prod = do01 * o01_ref[at, :]
        prod2 = do2 * o2_ref[at, :]
        delta0 = jnp.sum(jnp.where(low, prod, 0.0), axis=1, keepdims=True)
        delta1 = jnp.sum(jnp.where(low, 0.0, prod), axis=1, keepdims=True)
        delta2 = jnp.sum(jnp.where(low, 0.0, prod2), axis=1, keepdims=True)
        dos = (
            jnp.where(low, do01, pieces(delta0)).astype(BF),
            jnp.where(low, pieces(delta1), do01).astype(BF),
            jnp.where(low, pieces(delta2), do2).astype(BF),
        )
        dqs = []
        for head in range(3):
            q = q_ref[head, at, :]
            prob = jnp.exp(nt(k_ref[head, keys, :], q))
            d_prob = nt(v_ref[head, keys, :], dos[head])
            d_log = (prob * d_prob).astype(BF)
            dv_ref[head, keys, :] += matmul(prob.astype(BF), dos[head])
            dk_ref[head, keys, :] += matmul(d_log, q)
            dqs.append(matmul(kt_ref[head, ab], d_log).T * 0.125)
        off = jnp.where(t < 4, t, 4 + r + 2 * (t - 4)) * 256
        rows = pl.ds(pl.multiple_of(off, 256), 256)
        d5_ref[rows, 0:128] = jnp.where(low, dqs[0], dqs[1]).astype(BF)
        d5_ref[rows, 512:640] = jnp.where(low, dqs[2], 0.0).astype(BF)

    def step(k):
        for stream in streams:
            stream.fold(k)
            if k < 4:
                stream.push(k + 1)
            else:
                stream.spread(4)

    swapped()
    pl.loop(0, SPLIT)(tile)
    step(0)
    pl.loop(SPLIT, 6)(tile)
    step(1)

    @pl.loop(0, 8)
    def _(i):
        rows = pl.ds(pl.multiple_of(i * 256, 256), 256)
        d5_ref[rows, 128:256] = jnp.where(low, dk_ref[0, rows, :], dk_ref[1, rows, :]).astype(BF)
        d5_ref[rows, 256:384] = jnp.where(low, dv_ref[0, rows, :], dv_ref[1, rows, :]).astype(BF)
        d5_ref[rows, 384:512] = jnp.where(low, dk_ref[2, rows, :], dv_ref[2, rows, :]).astype(BF)
        d_xn = nt(d5_ref[rows, :], wc_ref[...]).astype(BF)
        for h in range(4):
            p_ref[h, i, :, :] = d_xn[h * 64 : h * 64 + 64]

    halves = ((1, slice(4, 8)), (0, slice(0, 4)))
    c_copies = {}
    for k, h in ((1, gcx), (0, gc)):
        for ab, cut in halves:
            c_copies[k, ab] = remote(
                p_ref.at[h, cut], rc_ref.at[k, cut], c_send.at[k, ab], c_recv.at[k, ab], core
            )
            c_copies[k, ab].start()
    for c in range(5):
        cols = slice(c * 128, c * 128 + 128)
        acc[:, cols] = outer(xn_ref[...], d5_ref[:, cols]).astype(BF)
    x_copies = {}
    for ab, cut in halves:
        c_copies[1, ab].wait_recv()

        @pl.loop(0, 4)
        def _(j):
            n = ab * 4 + j
            sx_ref[n] = (p_ref[gx, n].astype(F32) + rc_ref[1, n].astype(F32)).astype(BF)

        x_copies[ab] = remote(sx_ref.at[cut], rx_ref.at[cut], x_send.at[ab], x_recv.at[ab], across)
        x_copies[ab].start()
    qkv.push(1)
    step(2)
    dgain_ref[...] = jnp.zeros_like(dgain_ref)
    gain = gain_ref[...]

    def norm_back(d_xn, j):
        h = h_ref[j].astype(F32)
        inv = lax.rsqrt(jnp.mean(h * h, axis=-1, keepdims=True) + EPS)
        dgain_ref[...] += jnp.sum(d_xn * h * inv, axis=0, keepdims=True)
        dyg = d_xn * gain
        dot = jnp.mean(dyg * h, axis=-1, keepdims=True)
        ig_ref[j] = (dh_ref[j] + inv * dyg - h * (inv * inv * inv * dot)).astype(BF)

    for ab, cut in halves:
        c_copies[0, ab].wait_recv()

        @pl.loop(0, 4)
        def _(j):
            n = ab * 4 + j
            t_ref[n] = p_ref[g, n].astype(F32) + rc_ref[0, n].astype(F32)

    step(3)
    x_copies[1].wait_recv()
    for q in range(2):
        n = 4 + (1 - r) + 2 * q
        zb_ref[q] = (t_ref[n] + rx_ref[n].astype(F32)).astype(BF)
    z_copy = remote(zb_ref, rz_ref, z_send.at[0], z_recv.at[0], pair)
    z_copy.start()
    qkv.fold(1)
    qkv.push(2)
    x_copies[0].wait_recv()
    mine = 3 * p + 2 * r
    homes = []
    for n, s in enumerate((zs[3], zs[2], zs[1], z)):
        norm_back(t_ref[s] + rx_ref[s].astype(F32), s)
        if n < 3:
            copy = remote(
                ig_ref.at[s], out_ref.at[mine], h_send.at[n], h_recv.at[mine], (item, s * 4 + g)
            )
        else:
            copy = pltpu.make_async_copy(ig_ref.at[s], out_ref.at[mine], h_own.at[0])
        copy.start()
        homes.append(copy)
    step(4)
    qkv.fold(2)
    qkv.push(3)
    z_copy.wait_recv()
    for n, q in enumerate((1 - p, p)):
        k = 4 + r + 2 * q
        norm_back(t_ref[k] + rx_ref[k].astype(F32) + rz_ref[q].astype(F32), 4 + q)
        where = 3 * p + 1
        if n == 0:
            copy = remote(
                ig_ref.at[4 + q], out_ref.at[where], h_send.at[3], h_recv.at[where], (item, zs[2] * 4 + g)
            )
        else:
            copy = pltpu.make_async_copy(ig_ref.at[4 + q], out_ref.at[where], h_own.at[1])
        copy.start()
        homes.append(copy)

    buf[0] = jnp.zeros_like(buf[0])
    buf[0, 0:1, :] = dgain_ref[...]
    buf[0, 1:2, :] = dgain2_ref[...]
    gain_peers = [core] + [peer for _, peer in coords.values()]
    gain_waits = []

    def gain_step(k):
        if k > 0:
            gain_waits[k - 1].wait_recv()
            buf[k] = buf[k - 1] + got[k - 1]
        if k < 5:
            copy = remote(buf.at[k], got.at[k], gain_send.at[k], gain_recv.at[k], gain_peers[k])
            copy.start()
            gain_waits.append(copy)

    gain_step(0)
    qkv.fold(3)
    qkv.spread(3)
    streams.append(qkv)
    for k in range(4, 0, -1):
        for stream in streams:
            if k <= len(stream.order):
                stream.collect(k)
                if k > 1:
                    stream.spread(k - 1)
        gain_step(5 - k)
    gain_step(5)
    gains_out[...] = buf[5]
    for s in zs[1:]:
        where = 3 * (s // 2) + 2 * (s % 2)
        remote(ig_ref.at[0], out_ref.at[where], h_send.at[0], h_recv.at[where], pair).wait_recv()
    where = 3 * (1 - p) + 1
    remote(ig_ref.at[0], out_ref.at[where], h_send.at[0], h_recv.at[where], pair).wait_recv()
    done_rs()
    homes[3].wait()
    homes[5].wait()
    for stream in streams:
        stream.close()
    for copy in homes[:3] + homes[4:5] + [z_copy] + list(c_copies.values()) + list(x_copies.values()) + gain_waits:
        copy.wait_send()


SPLIT = 2


def back(dsend, saved, xn, wc, results, hidden, d_second, gain1, d_gain2, arrays):
    dma = pltpu.SemaphoreType.DMA
    s = jax.ShapeDtypeStruct
    v = pltpu.VMEM
    _, rows, width = results.shape
    gains = (8, width)
    group = (width, 640)
    outs = (s(results.shape, BF), s(results.shape, BF)) + tuple(s(a.shape, BF) for a in arrays)
    outs += (s((4,) + group, BF), s(gains, F32))
    scratch = [
        v(dsend.shape, BF), v((3, 2048, 128), F32), v((3, 2048, 128), F32), v((2048, 640), BF), v((4, 8, rows, width), BF),
        v((2, 8, rows, width), BF), v((8, rows, width), BF), v((8, rows, width), BF),
        v((8, rows, width), F32), v((2, rows, width), BF), v((2, rows, width), BF), v((6, rows, width), BF),
        v((1, width), F32),
        dma((2, 2)), dma((2, 2)), dma((2,)), dma((2,)), dma((1,)), dma((1,)), dma((4,)), dma((6,)), dma((2,)),
        dma((4,)), dma((6,)), dma((2,)), dma((3,)), dma((4,)), dma((1,)),
    ]
    for a in arrays:
        scratch += [v((a.shape[0], a.shape[1] // 2), BF)] * 3
        scratch += [dma((5,)), dma((5,)), dma((2,)), dma((4,)), dma((4,)), dma((5,)), dma((5,))]
    scratch += [v(group, BF)] * 2
    scratch += [dma((4,)), dma((4,)), dma((2,)), dma((4, 2)), dma((4, 2)), dma((4, 2)), dma((4, 2))]
    scratch += [v((6,) + gains, F32), v((5,) + gains, F32), dma((5,)), dma((5,))]
    return pl.pallas_call(
        back_kernel,
        out_shape=outs,
        in_specs=[ANY] + [VMEM] * 8 + [ANY] + [VMEM] * 4 + [ANY] * 4,
        out_specs=(ANY,) * 7 + (VMEM,),
        scratch_shapes=scratch,
        compiler_params=params(3, 62),
        name="back",
    )(dsend, *saved, xn, wc, results, hidden, d_second, gain1, d_gain2, *arrays)


def fast(
    inputs, counts, norm_gain1, w_query, w_key, w_value, w_out, norm_gain2, w_gate, w_up, w_down, cotangent
):
    band_rows, width = inputs.shape[2:]
    gain1, gain2 = norm_gain1.reshape(1, width), norm_gain2.reshape(1, width)
    xall, wc = gather_rows(inputs.reshape(6, band_rows, width), w_query, w_key, w_value)
    osend, xn, q, k, v, kt, o01, o2 = forward_attention(counts, xall.reshape(2048, width), gain1, wc)
    orecv, dy6 = swap_out(osend, cotangent.reshape(6, band_rows, width))
    result6, dsend, hidden, d_second, d_gain2, g_gate, g_up, g_down, g_out = dense(
        orecv, xall, dy6, gain2, w_out, w_gate, w_up, w_down
    )
    input_grads, results, s_gate, s_up, s_down, s_out, s_qkv, s_gains = back(
        dsend, (q, k, v, kt, o01, o2), xn, wc, result6, hidden, d_second, gain1, d_gain2,
        (g_gate, g_up, g_down, g_out),
    )
    grads = widen(s_qkv, s_out, s_gate, s_up, s_down)
    return (
        results.reshape(inputs.shape), input_grads.reshape(inputs.shape), s_gains[0]
    ) + grads[:4] + (s_gains[1],) + grads[4:]


def program(*args):
    micro, seqs, band_rows, width = args[0].shape
    small = lax.axis_size("band") == 16 and lax.axis_size("items") == 2
    if small and (micro, seqs, band_rows, width, HEADS, HEAD_DIM) == (2, 3, 64, 768, 12, 64):
        return fast(*args)
    return per_device(*args)


def solution(mesh):
    return jax.shard_map(
        program,
        mesh=mesh,
        in_specs=(
            P(None, "items", "band", None),
            P(None, "items"),
            P(),
            P(),
            P(),
            P(),
            P(),
            P(),
            P(),
            P(),
            P(),
            P(None, "items", "band", None),
        ),
        out_specs=(
            P(None, "items", "band", None),
            P(None, "items", "band", None),
            P(),
            P(),
            P(),
            P(),
            P(),
            P(),
            P(),
            P(),
            P(),
        ),
        check_vma=False,
    )
```

```python
import math

import jax
import jax.numpy as jnp
from jax import lax
from jax.experimental import pallas as pl
from jax.experimental.pallas import tpu as pltpu
from jax.sharding import PartitionSpec as P

HEADS = 12
HEAD_DIM = 64


EPS = 1e-06


def shortened(shard):

    def short(part):
        return part.astype(jnp.bfloat16) if part.dtype == jnp.float32 else part

    return jax.tree.map(short, shard)


def rms_scale(values, gain):
    return values * lax.rsqrt(jnp.mean(values * values, axis=-1, keepdims=True) + EPS) * gain


def gated(gate, upper):
    return jax.nn.gelu(gate, approximate=True) * upper


def outer(left, right):
    return lax.dot_general(
        left, right, (((0,), (0,)), ((), ())), preferred_element_type=jnp.float32
    )


def transposed(left, weight):
    return lax.dot_general(
        left, weight, (((1,), (1,)), ((), ())), preferred_element_type=jnp.float32
    )


def matmul(left, right):
    return jnp.dot(left, right, preferred_element_type=jnp.float32)


def scores(query, key, scale):
    return jnp.einsum("sqhd,skhd->shqk", query, key, preferred_element_type=jnp.float32) * scale


def per_device(
    inputs,
    counts,
    norm_gain1,
    w_query,
    w_key,
    w_value,
    w_out,
    norm_gain2,
    w_gate,
    w_up,
    w_down,
    cotangent,
):
    micro, seqs, band_rows, width = inputs.shape
    bands = lax.axis_size("band")
    length = band_rows * bands
    rows = seqs * band_rows
    heads = HEADS
    head_dim = HEAD_DIM
    scale = 1.0 / math.sqrt(head_dim)
    key_place = jnp.arange(length, dtype=jnp.int32)
    params = (norm_gain1, w_query, w_key, w_value, w_out, norm_gain2, w_gate, w_up, w_down)
    totals = [jnp.zeros(p.shape, jnp.float32) for p in params]
    results = []
    input_grads = []
    for number in range(micro):
        hidden = inputs[number].astype(jnp.float32).reshape(rows, width)
        lengths = counts[number]
        normed = rms_scale(hidden, norm_gain1).astype(jnp.bfloat16)
        query = matmul(normed, w_query).astype(jnp.bfloat16)
        key_local = matmul(normed, w_key).astype(jnp.bfloat16)
        value_local = matmul(normed, w_value).astype(jnp.bfloat16)
        query_four = query.reshape(seqs, band_rows, heads, head_dim)
        key_three = key_local.reshape(seqs, band_rows, width)
        value_three = value_local.reshape(seqs, band_rows, width)
        key_all, value_all = (
            lax.all_gather(key_three, "band", axis=1, tiled=True),
            lax.all_gather(value_three, "band", axis=1, tiled=True),
        )
        live = key_place[None, :] < lengths[:, None]
        key_four = key_all.reshape(seqs, length, heads, head_dim)
        value_four = value_all.reshape(seqs, length, heads, head_dim)
        logits = jnp.where(live[:, None, None, :], scores(query_four, key_four, scale), -jnp.inf)
        top = jnp.max(logits, axis=-1, keepdims=True)
        expo = jnp.exp(logits - top)
        summed = jnp.sum(expo, axis=-1, keepdims=True)
        log_total = top + jnp.log(summed)
        prob = (expo / summed).astype(jnp.bfloat16)
        attended = jnp.einsum(
            "shqk,skhd->sqhd", prob, value_four, preferred_element_type=jnp.float32
        )
        attended = attended.reshape(rows, width).astype(jnp.bfloat16)
        second = hidden + matmul(attended, w_out)
        normed_two = rms_scale(second, norm_gain2).astype(jnp.bfloat16)
        gate = matmul(normed_two, w_gate)
        upper = matmul(normed_two, w_up)
        mixed = gated(gate, upper).astype(jnp.bfloat16)
        results.append(
            (second + matmul(mixed, w_down)).astype(jnp.bfloat16).reshape(seqs, band_rows, width)
        )
        grad_rows = cotangent[number].reshape(rows, width)
        totals[8] = totals[8] + outer(mixed, grad_rows)
        d_mixed = transposed(grad_rows, w_down)
        pull_gate = jax.vjp(gated, gate, upper)[1]
        d_gate, d_upper = pull_gate(d_mixed)
        d_gate = d_gate.astype(jnp.bfloat16)
        d_upper = d_upper.astype(jnp.bfloat16)
        totals[6] = totals[6] + outer(normed_two, d_gate)
        totals[7] = totals[7] + outer(normed_two, d_upper)
        d_normed_two = transposed(d_gate, w_gate) + transposed(d_upper, w_up)
        pull_two = jax.vjp(rms_scale, second, norm_gain2)[1]
        d_second_norm, d_gain_two = pull_two(d_normed_two)
        totals[5] = totals[5] + d_gain_two
        d_second = grad_rows.astype(jnp.float32) + d_second_norm
        d_branch = d_second.astype(jnp.bfloat16)
        totals[4] = totals[4] + outer(attended, d_branch)
        d_attended = transposed(d_branch, w_out).astype(jnp.bfloat16)
        d_att_four = d_attended.reshape(seqs, band_rows, heads, head_dim)
        key_all, value_all = (
            lax.all_gather(key_three, "band", axis=1, tiled=True),
            lax.all_gather(value_three, "band", axis=1, tiled=True),
        )
        key_four = key_all.reshape(seqs, length, heads, head_dim)
        value_four = value_all.reshape(seqs, length, heads, head_dim)
        logits = jnp.where(live[:, None, None, :], scores(query_four, key_four, scale), -jnp.inf)
        prob_full = jnp.exp(logits - log_total)
        prob = prob_full.astype(jnp.bfloat16)
        d_prob = jnp.einsum(
            "sqhd,skhd->shqk", d_att_four, value_four, preferred_element_type=jnp.float32
        )
        delta = jnp.sum(d_prob * prob_full, axis=-1, keepdims=True)
        d_logits = (prob_full * (d_prob - delta)).astype(jnp.bfloat16)
        d_query = (
            jnp.einsum("shqk,skhd->sqhd", d_logits, key_four, preferred_element_type=jnp.float32)
            * scale
        )
        d_query = d_query.reshape(rows, width).astype(jnp.bfloat16)
        d_key_all = (
            jnp.einsum("shqk,sqhd->skhd", d_logits, query_four, preferred_element_type=jnp.float32)
            * scale
        )
        d_value_all = jnp.einsum(
            "shqk,sqhd->skhd", prob, d_att_four, preferred_element_type=jnp.float32
        )
        d_key_three, d_value_three = (
            lax.psum_scatter(
                d_key_all.reshape(seqs, length, width).astype(jnp.bfloat16),
                "band",
                scatter_dimension=1,
                tiled=True,
            ).astype(jnp.float32),
            lax.psum_scatter(
                d_value_all.reshape(seqs, length, width).astype(jnp.bfloat16),
                "band",
                scatter_dimension=1,
                tiled=True,
            ).astype(jnp.float32),
        )
        d_key = d_key_three.reshape(rows, width).astype(jnp.bfloat16)
        d_value = d_value_three.reshape(rows, width).astype(jnp.bfloat16)
        totals[1] = totals[1] + outer(normed, d_query)
        totals[2] = totals[2] + outer(normed, d_key)
        totals[3] = totals[3] + outer(normed, d_value)
        d_normed = (
            transposed(d_query, w_query) + transposed(d_key, w_key) + transposed(d_value, w_value)
        )
        pull_one = jax.vjp(rms_scale, hidden, norm_gain1)[1]
        d_hidden_norm, d_gain_one = pull_one(d_normed)
        totals[0] = totals[0] + d_gain_one
        input_grads.append(
            (d_second + d_hidden_norm).astype(jnp.bfloat16).reshape(seqs, band_rows, width)
        )
    shares = jax.tree.map(
        lambda part: part.astype(jnp.float32),
        lax.psum_scatter(shortened(tuple(totals)), "band", scatter_dimension=0, tiled=True),
    )
    summed_shares = jax.tree.map(
        lambda part: part.astype(jnp.float32), lax.psum(shortened(shares), "items")
    )
    whole = jax.tree.map(
        lambda part, own: part.astype(own.dtype),
        lax.all_gather(shortened(summed_shares), "band", axis=0, tiled=True),
        summed_shares,
    )
    return (jnp.stack(results), jnp.stack(input_grads)) + tuple(whole)


MESH_ID = pl.DeviceIdType.MESH
NEG = -1e30
BF = jnp.bfloat16
F32 = jnp.float32


def place():
    item = lax.axis_index("items")
    band = lax.axis_index("band")
    return item, band // 4, band % 4


def flip(value):
    return value + 1 - 2 * (value % 2)


def far(value):
    return (value + 2) % 4


def greet(peers):
    barrier = pltpu.get_barrier_semaphore()
    for peer in peers:
        pl.semaphore_signal(barrier, inc=1, device_id=peer, device_id_type=MESH_ID)
    pl.semaphore_wait(barrier, len(peers))


def remote(src, dst, send, recv, peer):
    return pltpu.make_async_remote_copy(
        src_ref=src, dst_ref=dst, send_sem=send, recv_sem=recv, device_id=peer, device_id_type=MESH_ID
    )


def params(number, vmem=62):
    return pltpu.CompilerParams(
        collective_id=number, has_side_effects=True, vmem_limit_bytes=vmem << 20
    )


def whole(value, unit):
    return value if isinstance(value, int) else pl.multiple_of(value, unit)


def lanes_of(rows):
    return lax.broadcasted_iota(jnp.int32, (rows, 128), 1)


ANY = pl.BlockSpec(memory_space=pl.ANY)
VMEM = pl.BlockSpec(memory_space=pltpu.VMEM)
SMEM = pl.BlockSpec(memory_space=pltpu.SMEM)


def gather_kernel(
    x_ref, wq_ref, wk_ref, wv_ref, out_ref, wc_ref, win_ref, z_send, f_send, g_send, recv, own_sem, win_sem
):
    item, z, g = place()
    cut = pl.ds(pl.multiple_of(g * 3 // 2 * 128, 128), 256)
    windows = []
    for n, ref in enumerate((wq_ref, wk_ref, wv_ref)):
        windows.append(pltpu.make_async_copy(ref.at[:, cut], win_ref.at[n], win_sem.at[n]))
        windows[-1].start()
    gc, gx = flip(g), far(g)
    gcx = far(gc)
    zs = (z, flip(z), far(z), far(flip(z)))
    core, across = (item, z * 4 + gc), (item, z * 4 + gx)
    greet([core, across] + [(item, s * 4 + g) for s in zs[1:]])

    def items_of(s):
        return (3 * (s // 2) + 2 * (s % 2), 3 * (s // 2) + 1)

    started = []
    for n, s in enumerate(zs[1:]):
        for ab in range(2):
            copy = remote(
                x_ref.at[items_of(s)[ab]],
                out_ref.at[ab, z * 4 + g],
                z_send.at[n, ab],
                recv.at[ab, z * 4 + g],
                (item, s * 4 + g),
            )
            copy.start()
            started.append(copy)
    local = []
    for ab in range(2):
        copy = pltpu.make_async_copy(
            x_ref.at[items_of(z)[ab]], out_ref.at[ab, z * 4 + g], own_sem.at[ab]
        )
        copy.start()
        local.append(copy)

    def arrived(ab, where):
        remote(
            out_ref.at[ab, where], out_ref.at[ab, where], z_send.at[0, 0], recv.at[ab, where], core
        ).wait_recv()

    def pack():
        for copy in windows:
            copy.wait()
        odd = g % 2 == 1
        low = lanes_of(256) < 64

        @pl.loop(0, 3)
        def _(i):
            rows = pl.ds(pl.multiple_of(i * 256, 256), 256)
            firsts, lasts = [], []
            for n in range(3):
                left = win_ref[n, rows, 0:128].astype(F32)
                right = win_ref[n, rows, 128:256].astype(F32)
                crossed = pltpu.roll(jnp.where(low, right, left), 64, 1)
                firsts.append(jnp.where(odd, crossed, left))
                lasts.append(jnp.where(odd, pltpu.roll(right, 64, 1), right))
            for n in range(3):
                wc_ref[rows, n * 128 : n * 128 + 128] = firsts[n].astype(BF)
            wc_ref[rows, 384:512] = jnp.where(low, lasts[1], pltpu.roll(lasts[2], 64, 1)).astype(BF)
            wc_ref[rows, 512:640] = jnp.where(low, lasts[0], 0.0).astype(BF)

    for n, zz in enumerate(zs):
        if n == 1:
            pack()
        for ab in range(2):
            where = zz * 4 + g
            if n > 0:
                arrived(ab, where)
            src = x_ref.at[items_of(z)[ab]] if n == 0 else out_ref.at[ab, where]
            for k, peer in enumerate((across, core)):
                copy = remote(
                    src, out_ref.at[ab, where], f_send.at[n, ab, k], recv.at[ab, where], peer
                )
                copy.start()
                started.append(copy)
    for n, zz in enumerate(zs):
        for ab in range(2):
            where = zz * 4 + gx
            arrived(ab, where)
            copy = remote(
                out_ref.at[ab, where],
                out_ref.at[ab, where],
                g_send.at[n, ab],
                recv.at[ab, where],
                core,
            )
            copy.start()
            started.append(copy)
    for n, zz in enumerate(zs):
        for ab in range(2):
            arrived(ab, zz * 4 + gc)
            arrived(ab, zz * 4 + gcx)
    for copy in local:
        copy.wait()
    for copy in started:
        copy.wait_send()


def gather_rows(x6, wq, wk, wv):
    _, rows, width = x6.shape
    dma = pltpu.SemaphoreType.DMA
    return pl.pallas_call(
        gather_kernel,
        out_shape=(
            jax.ShapeDtypeStruct((2, 16, rows, width), BF), jax.ShapeDtypeStruct((width, 640), BF)
        ),
        in_specs=[ANY] * 4,
        out_specs=(ANY, VMEM),
        scratch_shapes=[
            pltpu.VMEM((3, width, 256), BF),
            dma((3, 2)), dma((4, 2, 2)), dma((4, 2)), dma((2, 16)), dma((2,)), dma((3,)),
        ],
        compiler_params=params(1),
        name="gather_rows",
    )(x6, wq, wk, wv)


def to_slots(item, z, g, src_ref, dst_ref, send, recv, own_sem):
    zs = (z, flip(z), far(z), far(flip(z)))
    p, r = z // 2, z % 2
    started = []
    for n, s in enumerate(zs[1:]):
        copy = remote(
            src_ref.at[3 * (s // 2) + 2 * (s % 2)],
            dst_ref.at[z],
            send.at[n],
            recv.at[z],
            (item, s * 4 + g),
        )
        copy.start()
        started.append(copy)
    copy = remote(
        src_ref.at[3 * (1 - p) + 1], dst_ref.at[4 + p], send.at[3], recv.at[4 + p], (item, far(z) * 4 + g)
    )
    copy.start()
    started.append(copy)
    local = [
        pltpu.make_async_copy(src_ref.at[3 * p + 2 * r], dst_ref.at[z], own_sem.at[0]),
        pltpu.make_async_copy(src_ref.at[3 * p + 1], dst_ref.at[4 + p], own_sem.at[1]),
    ]
    for copy in local:
        copy.start()

    def finish():
        for where in zs[1:] + (4 + (1 - p),):
            remote(
                dst_ref.at[where], dst_ref.at[where], send.at[0], recv.at[where], (item, far(z) * 4 + g)
            ).wait_recv()
        for copy in local:
            copy.wait()
        for copy in started:
            copy.wait_send()

    return finish


def from_slots(item, z, g, src_ref, dst_ref, send, recv, own_sem):
    zs = (z, flip(z), far(z), far(flip(z)))
    p, r = z // 2, z % 2
    mine = 3 * p + 2 * r
    started = []
    for n, s in enumerate(zs[1:]):
        copy = remote(src_ref.at[s], dst_ref.at[mine], send.at[n], recv.at[mine], (item, s * 4 + g))
        copy.start()
        started.append(copy)
    copy = remote(
        src_ref.at[4 + (1 - p)],
        dst_ref.at[3 * p + 1],
        send.at[3],
        recv.at[3 * p + 1],
        (item, far(z) * 4 + g),
    )
    copy.start()
    started.append(copy)
    local = [
        pltpu.make_async_copy(src_ref.at[z], dst_ref.at[mine], own_sem.at[0]),
        pltpu.make_async_copy(src_ref.at[4 + p], dst_ref.at[3 * p + 1], own_sem.at[1]),
    ]
    for copy in local:
        copy.start()

    def finish():
        for s in zs[1:]:
            where = 3 * (s // 2) + 2 * (s % 2)
            remote(
                dst_ref.at[where], dst_ref.at[where], send.at[0], recv.at[where], (item, far(z) * 4 + g)
            ).wait_recv()
        where = 3 * (1 - p) + 1
        remote(
            dst_ref.at[where], dst_ref.at[where], send.at[0], recv.at[where], (item, far(z) * 4 + g)
        ).wait_recv()
        for copy in local:
            copy.wait()
        for copy in started:
            copy.wait_send()

    return finish


def z_peers(item, z, g):
    return [(item, s * 4 + g) for s in (flip(z), far(z), far(flip(z)))]


def g_peers(item, z, g):
    return [(item, z * 4 + h) for h in (flip(g), far(g), far(flip(g)))]


def swap_heads(item, z, g, src_ref, dst_ref, send, recv, own_sem):
    started = []
    for n, h in enumerate((far(g), far(flip(g)), flip(g))):
        copy = remote(src_ref.at[h], dst_ref.at[g], send.at[n], recv.at[g], (item, z * 4 + h))
        copy.start()
        started.append(copy)
    local = pltpu.make_async_copy(src_ref.at[g], dst_ref.at[g], own_sem)
    local.start()

    def finish():
        for h in (flip(g), far(g), far(flip(g))):
            remote(
                dst_ref.at[h], dst_ref.at[h], send.at[0], recv.at[h], (item, z * 4 + h)
            ).wait_recv()
        local.wait()
        for copy in started:
            copy.wait_send()

    return finish


def swap_kernel(heads_ref, rows_ref, out_heads_ref, out_rows_ref, hs, hr, ho, zs, zr, zo):
    item, z, g = place()
    greet(z_peers(item, z, g) + g_peers(item, z, g))
    first = swap_heads(item, z, g, heads_ref, out_heads_ref, hs, hr, ho.at[0])
    second = to_slots(item, z, g, rows_ref, out_rows_ref, zs, zr, zo)
    first()
    second()


def swap_out(heads, rows):
    dma = pltpu.SemaphoreType.DMA
    return pl.pallas_call(
        swap_kernel,
        out_shape=(
            jax.ShapeDtypeStruct(heads.shape, heads.dtype),
            jax.ShapeDtypeStruct(rows.shape, rows.dtype),
        ),
        in_specs=[ANY, ANY],
        out_specs=(ANY, ANY),
        scratch_shapes=[dma((3,)), dma((4,)), dma((1,)), dma((4,)), dma((6,)), dma((2,))],
        compiler_params=params(2),
        name="swap_out",
    )(heads, rows)


def nt(left, right):
    return lax.dot_general(left, right, (((1,), (1,)), ((), ())), preferred_element_type=F32)


def forward_kernel(
    count_ref, x_ref, gain_ref, wc_ref,
    osend_ref, xn_ref, q_ref, k_ref, v_ref, kt_ref, o01_ref, o2_ref,
):
    _, z, _ = place()
    p, r = z // 2, z % 2
    lane = lanes_of(256)
    low = lane < 64

    @pl.loop(0, 8)
    def _(i):
        rows = pl.ds(pl.multiple_of(i * 256, 256), 256)
        h = x_ref[rows, :].astype(F32)
        inv = lax.rsqrt(jnp.mean(h * h, axis=-1, keepdims=True) + EPS)
        xn = (h * inv * gain_ref[...]).astype(BF)
        xn_ref[rows, :] = xn
        y = matmul(xn, wc_ref[:, 128:512])
        count = count_ref[p, jnp.where(i < 4, 2 * r, 1)]
        at = lax.broadcasted_iota(jnp.int32, (256, 128), 0) + (i % 4) * 256
        bias = jnp.where(at < count, 0.0, NEG)
        one = jnp.where((lane % 64) < 4, 1.0, 0.0)
        k_aug = jnp.where(lane % 64 == 0, bias, one)
        k01, v01, kv2 = y[:, :128], y[:, 128:256], y[:, 256:]
        k_ref[0, rows, :] = jnp.where(low, k01, k_aug).astype(BF)
        k_ref[1, rows, :] = jnp.where(low, k_aug, k01).astype(BF)
        k_ref[2, rows, :] = jnp.where(low, kv2, k_aug).astype(BF)
        v_ref[0, rows, :] = jnp.where(low, v01, one).astype(BF)
        v_ref[1, rows, :] = jnp.where(low, one, v01).astype(BF)
        v_ref[2, rows, :] = jnp.where(low, one, kv2).astype(BF)

    for head in range(3):
        for ab in range(2):
            kt_ref[head, ab, :, :] = k_ref[head, ab * 1024 : (ab + 1) * 1024, :].T

    @pl.loop(0, 6)
    def _(t):
        off = jnp.where(t < 4, t, 4 + r + 2 * (t - 4)) * 256
        xq = xn_ref[pl.ds(pl.multiple_of(off, 256), 256), :]
        q01 = matmul(xq, wc_ref[:, 0:128]).astype(BF).astype(F32) * 0.125
        q2 = matmul(xq, wc_ref[:, 512:640]).astype(BF).astype(F32) * 0.125
        flag = jnp.where(lane % 64 == 0, 1.0, 0.0)
        qs = (jnp.where(low, q01, flag), jnp.where(low, flag, q01), jnp.where(low, q2, flag))
        at = pl.ds(pl.multiple_of(t * 256, 256), 256)
        ab = t // 4
        keys = pl.ds(pl.multiple_of(ab * 1024, 1024), 1024)
        outs = []
        for head in range(3):
            s = matmul(qs[head].astype(BF), kt_ref[head, ab])
            top = jnp.max(s, axis=1, keepdims=True)
            e = jnp.exp(s - top).astype(BF)
            o = matmul(e, v_ref[head, keys, :])
            total = o[:, 64:65] if head == 0 else o[:, 0:1]
            outs.append(o / total)
            lse = -(top + jnp.log(total))
            hi = lse.astype(BF).astype(F32)
            mid = (lse - hi).astype(BF).astype(F32)
            lo = lse - hi - mid
            part = lane % 64
            aug = jnp.where(part == 1, hi, jnp.where(part == 2, mid, jnp.where(part == 3, lo, flag)))
            data = low if head != 1 else jnp.logical_not(low)
            q_ref[head, at, :] = jnp.where(data, qs[head], aug).astype(BF)
        o01 = jnp.where(low, outs[0], outs[1])
        o2 = outs[2]
        o01_ref[at, :] = o01
        o2_ref[at, :] = o2
        for h in range(4):
            osend_ref[h, t, 0:64, :] = o01[h * 64 : h * 64 + 64].astype(BF)
            first = o2[h * 64 : h * 64 + 32]
            second = o2[h * 64 + 32 : h * 64 + 64]
            folded = jnp.where(low[:32], pltpu.roll(first, 64, 1), second)
            osend_ref[h, t, 64:96, :] = folded.astype(BF)


def forward_attention(counts, xall, gain, wc):
    s = jax.ShapeDtypeStruct
    return pl.pallas_call(
        forward_kernel,
        out_shape=(
            s((4, 6, 96, 128), BF), s((2048, 768), BF), s((3, 1536, 128), BF), s((3, 2048, 128), BF),
            s((3, 2048, 128), BF), s((3, 2, 128, 1024), BF), s((1536, 128), F32), s((1536, 128), F32),
        ),
        in_specs=[SMEM, VMEM, VMEM, VMEM],
        out_specs=(VMEM,) * 8,
        compiler_params=pltpu.CompilerParams(vmem_limit_bytes=62 << 20),
        name="forward_attention",
    )(counts, xall, gain, wc)


GELU_A = 0.044715
GELU_C = math.sqrt(2.0 / math.pi)


def dense_kernel(
    o_ref, x_ref, dy_ref, gain_ref, wo_hbm, wg_hbm, wu_hbm, wd_hbm,
    res_ref, dsend_ref, h_ref, dh_ref, dgain_ref, gg_ref, gu_ref, gd_ref, go_ref,
    wo_ref, wg_ref, wu_ref, wd_ref, att_ref, sec_ref, xn_ref, xt_ref, dyt_ref, dxn_ref, h_sem, wo_sem, w_sem,
):
    _, z, g = place()
    r = z % 2
    chunks, size = 4, wg_ref.shape[1] // 4
    copies = []
    for j in range(6):
        src = x_ref.at[0, j * 4 + g] if j < 4 else x_ref.at[1, (r + 2 * (j - 4)) * 4 + g]
        copies.append(pltpu.make_async_copy(src, h_ref.at[j], h_sem.at[j]))
    copies.append(pltpu.make_async_copy(wo_hbm, wo_ref, wo_sem.at[0]))
    for copy in copies:
        copy.start()
    loads = []
    for c in range(chunks):
        cut = pl.ds(c * size, size)
        loads.append(
            [
                pltpu.make_async_copy(wg_hbm.at[:, cut], wg_ref.at[:, cut], w_sem.at[0, c]),
                pltpu.make_async_copy(wu_hbm.at[:, cut], wu_ref.at[:, cut], w_sem.at[1, c]),
                pltpu.make_async_copy(wd_hbm.at[cut, :], wd_ref.at[cut, :], w_sem.at[2, c]),
            ]
        )
        for copy in loads[-1]:
            copy.start()
    low = lanes_of(384) < 64

    def swap(v):
        return pltpu.roll(v, 64, 1)

    pairs = [o_ref[n, :, 0:64, :].astype(F32).reshape(384, 128) for n in range(4)]

    def unfold(n, high):
        f = o_ref[n, :, 64:96, :].astype(F32)
        s = swap(f.reshape(192, 128)).reshape(6, 32, 128)
        both = (s, f) if high else (f, s)
        return jnp.concatenate(both, axis=1).reshape(384, 128)

    tiles = (
        pairs[0],
        jnp.where(low, unfold(0, False), swap(pairs[1])),
        jnp.where(low, swap(pairs[1]), unfold(1, True)),
        pairs[2],
        jnp.where(low, unfold(2, False), swap(pairs[3])),
        jnp.where(low, swap(pairs[3]), unfold(3, True)),
    )
    for n, tile in enumerate(tiles):
        att_ref[:, n * 128 : n * 128 + 128] = tile.astype(BF)
    for copy in copies:
        copy.wait()
    second = h_ref[...].reshape(384, 768).astype(F32) + matmul(att_ref[...], wo_ref[...])
    sec_ref[...] = second
    inv = lax.rsqrt(jnp.mean(second * second, axis=-1, keepdims=True) + EPS)
    xn_ref[...] = (second * inv * gain_ref[...]).astype(BF)
    xt_ref[...] = xn_ref[...].T
    dxn_ref[...] = jnp.zeros_like(dxn_ref)
    dy = dy_ref[...].reshape(384, 768)
    for c in range(chunks):
        cut = slice(c * size, c * size + size)
        for copy in loads[c]:
            copy.wait()
        gate = matmul(xn_ref[...], wg_ref[:, cut])
        upper = matmul(xn_ref[...], wu_ref[:, cut])
        d_mixed = nt(dy, wd_ref[cut, :])
        square = gate * gate
        tan = jnp.tanh(GELU_C * (gate + GELU_A * square * gate))
        half = 0.5 * (1.0 + tan)
        act = gate * half
        slope = half + 0.5 * gate * (1.0 - tan * tan) * (GELU_C * (1.0 + 3.0 * GELU_A * square))
        mixed = (act * upper).astype(BF)
        d_gate = (d_mixed * upper * slope).astype(BF)
        d_upper = (d_mixed * act).astype(BF)
        sec_ref[...] += matmul(mixed, wd_ref[cut, :])
        dxn_ref[...] += nt(d_gate, wg_ref[:, cut]) + nt(d_upper, wu_ref[:, cut])
        gg_ref[:, cut] = matmul(xt_ref[...], d_gate).astype(BF)
        gu_ref[:, cut] = matmul(xt_ref[...], d_upper).astype(BF)
        gd_ref[cut, :] = outer(mixed, dy).astype(BF)
    res_ref[...] = sec_ref[...].astype(BF).reshape(6, 64, 768)
    second = h_ref[...].reshape(384, 768).astype(F32) + matmul(att_ref[...], wo_ref[...])
    inv = lax.rsqrt(jnp.mean(second * second, axis=-1, keepdims=True) + EPS)
    d_xn = dxn_ref[...]
    dgain_ref[...] = jnp.sum(d_xn * second * inv, axis=0, keepdims=True)
    dyg = d_xn * gain_ref[...]
    dot = jnp.mean(dyg * second, axis=-1, keepdims=True)
    d_second = dy.astype(F32) + inv * dyg - second * (inv * inv * inv * dot)
    dh_ref[...] = d_second.reshape(6, 64, 768)
    d_branch = d_second.astype(BF)
    go_ref[...] = outer(att_ref[...], d_branch).astype(BF)
    d_att = nt(d_branch, wo_ref[...]).astype(BF).astype(F32)
    d = [d_att[:, n * 128 : n * 128 + 128] for n in range(6)]
    firsts = (d[0], swap(jnp.where(low, d[2], d[1])), d[3], swap(jnp.where(low, d[5], d[4])))
    lasts = ((d[1], False), (d[2], True), (d[4], False), (d[5], True))
    low3 = lax.broadcasted_iota(jnp.int32, (6, 32, 128), 2) < 64
    for n in range(4):
        dsend_ref[n, :, 0:64, :] = firsts[n].astype(BF).reshape(6, 64, 128)
        v, high = lasts[n]
        v3, s3 = v.reshape(6, 64, 128), swap(v).reshape(6, 64, 128)
        top, bottom = v3[:, :32], v3[:, 32:]
        top_s, bottom_s = s3[:, :32], s3[:, 32:]
        f = jnp.where(low3, top_s, bottom) if high else jnp.where(low3, top, bottom_s)
        dsend_ref[n, :, 64:96, :] = f.astype(BF)


def dense(orecv, xall, dy6, gain, w_out, w_gate, w_up, w_down):
    s = jax.ShapeDtypeStruct
    dma = pltpu.SemaphoreType.DMA
    rows, width = dy6.shape[1:]
    hidden = w_gate.shape[1]
    v = pltpu.VMEM
    return pl.pallas_call(
        dense_kernel,
        out_shape=(
            s(dy6.shape, BF), s(orecv.shape, BF), s(dy6.shape, BF), s(dy6.shape, F32), s((1, width), F32),
            s(w_gate.shape, BF), s(w_up.shape, BF), s(w_down.shape, BF), s(w_out.shape, BF),
        ),
        in_specs=[VMEM, ANY, VMEM, VMEM] + [ANY] * 4,
        out_specs=(VMEM,) * 9,
        scratch_shapes=[
            v(w_out.shape, BF), v(w_gate.shape, BF), v(w_up.shape, BF), v(w_down.shape, BF),
            v((384, width), BF), v((384, width), F32), v((384, width), BF), v((width, 384), BF), v((width, 384), BF),
            v((384, width), F32), dma((6,)), dma((1,)), dma((3, 4)),
        ],
        compiler_params=pltpu.CompilerParams(vmem_limit_bytes=62 << 20),
        name="dense",
    )(orecv, xall, dy6, gain, w_out, w_gate, w_up, w_down)


def widen_kernel(qkv_ref, so_ref, sg_ref, su_ref, sd_ref, q_ref, k_ref, v_ref, o_ref, g_ref, u_ref, d_ref):
    low = lanes_of(qkv_ref.shape[1]) < 64

    def swap(v):
        return pltpu.roll(v, 64, 1)

    for out, first, last, high in ((q_ref, 0, 512, False), (k_ref, 128, 384, False), (v_ref, 256, 384, True)):
        a = [qkv_ref[n, :, first : first + 128].astype(F32) for n in range(4)]
        b = [qkv_ref[n, :, last : last + 128].astype(F32) for n in range(4)]
        low_b = [swap(x) if high else x for x in b]
        high_b = [x if high else swap(x) for x in b]
        tiles = (
            a[0], jnp.where(low, low_b[0], swap(a[1])), jnp.where(low, swap(a[1]), high_b[1]),
            a[2], jnp.where(low, low_b[2], swap(a[3])), jnp.where(low, swap(a[3]), high_b[3]),
        )
        for n, tile in enumerate(tiles):
            out[:, n * 128 : n * 128 + 128] = tile
    o_ref[...] = so_ref[...].astype(F32)
    g_ref[...] = sg_ref[...].astype(F32)
    u_ref[...] = su_ref[...].astype(F32)
    d_ref[...] = sd_ref[...].astype(F32)


def widen(qkv, s_out, s_gate, s_up, s_down):
    s = jax.ShapeDtypeStruct
    steps = 16

    def spec(a):
        if len(a.shape) == 3:
            return pl.BlockSpec((a.shape[0], a.shape[1] // steps, a.shape[2]), lambda i: (0, i, 0))
        return pl.BlockSpec((a.shape[0] // steps, a.shape[1]), lambda i: (i, 0))

    outs = tuple(s(a.shape, F32) for a in (s_out, s_out, s_out, s_out, s_gate, s_up, s_down))
    ins = (qkv, s_out, s_gate, s_up, s_down)
    return pl.pallas_call(
        widen_kernel,
        grid=(steps,),
        out_shape=outs,
        in_specs=[spec(a) for a in ins],
        out_specs=tuple(spec(a) for a in outs),
        compiler_params=pltpu.CompilerParams(vmem_limit_bytes=62 << 20),
        name="widen",
    )(*ins)


class Stream:
    def __init__(self, src, res, acc, first, rest, sems, order, coords, core, cut):
        self.src, self.res, self.acc, self.first, self.rest = src, res, acc, first, rest
        self.send, self.recv, self.own, self.back, self.got, self.fwd, self.fgot = sems
        row, col, half = cut
        self.rows, self.wide = acc.shape
        self.row = row
        self.order = [coords[name] for name in order]
        self.deep = len(order)
        bit, self.peer = core
        if half:
            self.mine = pl.ds(pl.multiple_of(bit * half + col, 128), self.wide)
            self.other = pl.ds(pl.multiple_of((1 - bit) * half + col, 128), self.wide)
        else:
            self.mine = pl.ds(col, self.wide)
        self.base, self.size = [0], [self.rows]
        for bit, _ in self.order:
            self.size.append(self.size[-1] // 2)
            self.base.append(self.base[-1] + bit * self.size[-1])

    def part(self, base, size):
        return pl.ds(whole(base, 16), size)

    def at(self, base, size, mine=True):
        cols = self.mine if mine else self.other
        return self.res.at[pl.ds(whole(self.row + base, 16), size), cols]

    def sibling(self, k):
        return self.base[k - 1] + (1 - self.order[k - 1][0]) * self.size[k]

    def own_in(self):
        rows = pl.ds(self.row, self.rows)
        return pltpu.make_async_copy(self.src.at[rows, self.mine], self.acc, self.own.at[0])

    def own_out(self):
        here = self.base[self.deep], self.size[self.deep]
        return pltpu.make_async_copy(self.acc.at[self.part(*here)], self.at(*here), self.own.at[1])

    def c_push(self, k):
        if k == 0:
            src = self.src.at[pl.ds(self.row, self.rows), self.other]
            return remote(src, self.first, self.send.at[0], self.recv.at[0], self.peer)
        return remote(
            self.acc.at[self.part(self.sibling(k), self.size[k])],
            self.rest.at[pl.ds(self.rows - 2 * self.size[k], self.size[k])],
            self.send.at[k],
            self.recv.at[k],
            self.order[k - 1][1],
        )

    def c_back(self, k):
        here = self.base[k], self.size[k]
        src = self.acc.at[self.part(*here)] if k == self.deep else self.at(*here)
        return remote(
            src, self.at(*here), self.back.at[k - 1], self.got.at[k - 1], self.order[k - 1][1]
        )

    def c_forward(self, k):
        if k == 0:
            here = self.base[self.deep], self.size[self.deep]
            src = self.acc.at[self.part(*here)]
        else:
            here = self.sibling(k), self.size[k]
            src = self.at(*here)
        return remote(src, self.at(*here), self.fwd.at[k], self.fgot.at[k], self.peer)

    def open(self):
        self.own_in().start()
        self.c_push(0).start()

    def fold(self, k):
        if k == 0:
            self.own_in().wait()
        self.c_push(k).wait_recv()
        base, size = self.base[k], self.size[k]
        other, at = (self.first, 0) if k == 0 else (self.rest, self.rows - 2 * size)
        step = 64 if size % 64 == 0 else 48

        @pl.loop(0, size // step)
        def _(n):
            rows = self.part(base + n * step, step)
            more = other[pl.ds(pl.multiple_of(at + n * step, 16), step), :]
            self.acc[rows, :] = (self.acc[rows, :].astype(F32) + more.astype(F32)).astype(BF)

        if k < self.deep:
            self.c_push(k + 1).start()
        else:
            self.c_back(k).start()
            self.c_forward(0).start()
            self.own_out().start()

    def collect(self, k):
        here = self.sibling(k), self.size[k]
        block = self.at(*here)
        remote(block, block, self.back.at[k - 1], self.got.at[k - 1], self.peer).wait_recv()
        if k == self.deep:
            self.own_out().wait()
        if k > 1:
            self.c_back(k - 1).start()
        self.c_forward(k).start()

    def close(self):
        for k in range(self.deep + 1):
            if k == 0:
                here = self.base[self.deep], self.size[self.deep]
            else:
                here = self.sibling(k), self.size[k]
            block = self.at(*here, mine=False)
            remote(block, block, self.fwd.at[k], self.fgot.at[k], self.peer).wait_recv()
            self.c_push(k).wait_send()
            self.c_forward(k).wait_send()
            if k > 0:
                self.c_back(k).wait_send()


class Grouped(Stream):
    def __init__(self, res, acc, rest, sems, order, coords, core, cut, group, across):
        super().__init__(None, res, acc, None, rest, sems, order, coords, core, cut)
        self.group, self.gx, self.across = group, far(group), across

    def at(self, base, size, n=0):
        h = (self.group, self.gx, flip(self.group), far(flip(self.group)))[n]
        return self.res.at[h, self.part(base, size), self.mine]

    def c_across(self):
        here = self.base[self.deep], self.size[self.deep]
        return remote(
            self.acc.at[self.part(*here)],
            self.at(*here),
            self.back.at[self.deep, 0],
            self.got.at[self.deep, 0],
            self.across,
        )

    def c_back(self, k, n):
        here = self.base[k], self.size[k]
        own = k == self.deep and n == 0
        src = self.acc.at[self.part(*here)] if own else self.at(*here, n)
        return remote(
            src, self.at(*here, n), self.back.at[k - 1, n], self.got.at[k - 1, n], self.order[k - 1][1]
        )

    def c_forward(self, k, n):
        if k == 0:
            here = self.base[self.deep], self.size[self.deep]
            src = self.acc.at[self.part(*here)] if n == 0 else self.at(*here, n)
        else:
            here = self.sibling(k), self.size[k]
            src = self.at(*here, n)
        return remote(src, self.at(*here, n), self.fwd.at[k, n], self.fgot.at[k, n], self.peer)

    def fold(self, k):
        if k == 0:
            self.c_push(1).start()
            return
        if k < self.deep:
            super().fold(k)
            return
        self.c_push(k).wait_recv()
        base, size = self.base[k], self.size[k]
        rows = self.part(base, size)
        more = self.rest[pl.ds(self.rows - 2 * size, size), :]
        self.acc[rows, :] = (self.acc[rows, :].astype(F32) + more.astype(F32)).astype(BF)
        self.c_across().start()
        self.c_back(k, 0).start()
        self.c_forward(0, 0).start()
        self.own_out().start()

    def extend(self):
        self.c_across().wait_recv()
        self.c_back(self.deep, 1).start()
        self.c_forward(0, 1).start()

    def collect(self, k):
        here = self.sibling(k), self.size[k]
        if k == self.deep:
            self.own_out().wait()
        for n in range(2):
            block = self.at(*here, n)
            remote(block, block, self.back.at[k - 1, n], self.got.at[k - 1, n], self.peer).wait_recv()
            if k > 1:
                if n == 1:
                    self.c_back(k - 1, 0).start()
                    self.c_back(k - 1, 1).start()
            self.c_forward(k, n).start()

    def close(self):
        self.c_across().wait_send()
        for k in range(self.deep + 1):
            if k == 0:
                here = self.base[self.deep], self.size[self.deep]
            else:
                here = self.sibling(k), self.size[k]
                self.c_push(k).wait_send()
            for n in range(2):
                block = self.at(*here, 2 + n)
                remote(block, block, self.fwd.at[k, n], self.fgot.at[k, n], self.peer).wait_recv()
                self.c_forward(k, n).wait_send()
                if k > 0:
                    self.c_back(k, n).wait_send()


PIECES = {
    "U1": (1, 0, 512, 768, 512, 1024, ("x", "y", "zl", "zh")),
    "G1": (0, 0, 512, 768, 512, 1024, ("zh", "x", "y", "zl")),
    "O": (3, 0, 0, 768, 384, 384, ("x", "y", "zl", "zh")),
    "U0": (1, 0, 0, 768, 512, 1024, ("zl", "x", "y", "zh")),
    "D0": (2, 0, 0, 1024, 384, 384, ("y", "x", "zl", "zh")),
    "G0": (0, 0, 0, 768, 512, 1024, ("x", "y", "zl", "zh")),
    "D1": (2, 1024, 0, 1024, 384, 384, ("x", "y", "zl", "zh")),
}
GROUPS = {
    "qA": (0, 256, ("y", "zl", "zh")),
    "qB": (256, 384, ("y", "zl", "zh")),
}
PLAN = (
    "fU1.0", "fG1.0", "fO.0", "swap", "res", "tile.0.2", "fU0.0", "fD0.0", "fG0.0", "fD1.0",
    "fU1.1", "tile.2.4", "fO.1", "tile.4.6", "fD0.1", "fU1.2", "fG1.1", "fU0.1", "fG0.1", "dxn",
    "fO.2", "gw", "xsB", "fU1.3", "fD1.1", "xsA", "fG0.2", "fqA.0", "fqB.0", "fO.3",
    "tB", "tA", "fD0.2", "fU1.4", "fG0.3", "fG1.2", "fD1.2", "fO.4", "fD0.3", "gU1.4",
    "fU0.2", "fqA.1", "fG0.4", "fD1.3", "gO.4", "fqB.1", "fD0.4", "gU1.3", "zB", "fG1.3",
    "fqA.2", "fU0.3", "gG0.4", "fD1.4", "gO.3", "gU1.2", "nA", "fqB.2", "gD0.4", "gO.2",
    "nB", "fG1.4", "gain.0", "gU1.1", "fqA.3", "gain.1", "fU0.4", "gG0.3", "gD1.4", "gO.1",
    "eqA", "gain.2", "gG0.2", "gain.3", "gG0.1", "fqB.3", "gD0.3", "gG1.4", "eqB", "gU0.4",
    "gD1.3", "gG1.3", "gD0.2", "gain.4", "gU0.3", "gqA.3", "gG1.2", "gD1.2", "gain.5", "gqB.3",
    "gU0.2", "gqA.2", "gD0.1", "gD1.1", "gqA.1", "gqB.2", "gG1.1", "gU0.1", "gqB.1",
)


def back_kernel(*refs):
    take = iter(refs)

    def some(n):
        return [next(take) for _ in range(n)]

    (dsend_ref,) = some(1)
    loads_hbm = some(10)
    gain_ref, dgain2_ref = some(2)
    (res_ref,) = some(1)
    srcs = some(4)
    out_ref, res_out_ref = some(2)
    outs = some(5)
    (gains_out,) = some(1)
    loads_vmem = some(10)
    q_ref, k_ref, v_ref, kt_ref, o01_ref, o2_ref, xn_ref, wc_ref, h_ref, dh_ref = loads_vmem
    (load_sem,) = some(1)
    (do_ref, dk_ref, dv_ref, d5_ref, p_ref) = some(5)
    (rc_ref, sx_ref, rx_ref, t_ref, zb_ref, rz_ref, ig_ref, dgain_ref) = some(8)
    (c_send, c_recv, x_send, x_recv, z_send, z_recv) = some(6)
    (rs_send, rs_recv, rs_own, h_send, h_recv, h_own, hs, hr, ho) = some(9)
    item, z, g = place()
    gc, gx = flip(g), far(g)
    gcx = far(gc)
    p, r = z // 2, z % 2
    coords = {
        "x": (g // 2, (item, z * 4 + gx)),
        "y": (item, (1 - item, z * 4 + g)),
        "zl": (z % 2, (item, flip(z) * 4 + g)),
        "zh": (z // 2, (item, far(z) * 4 + g)),
    }
    across, pair = coords["x"][1], coords["zl"][1]
    core = (item, z * 4 + gc)
    zs = (z, flip(z), far(z), far(flip(z)))
    streams = {}
    for name, (n, row, col, _, _, half, order) in PIECES.items():
        acc, first, rest = some(3)
        streams[name] = Stream(
            srcs[n], outs[n], acc, first, rest, some(7), order, coords, (g % 2, core), (row, col, half)
        )
    (gw_ref,) = some(1)
    for name, (col, wide, order) in GROUPS.items():
        (rest,) = some(1)
        acc = gw_ref.at[:, pl.ds(col, wide)]
        streams[name] = Grouped(
            outs[4], acc, rest, some(7), order, coords, (g % 2, core), (0, col, 0), g, across
        )
    buf, got, gain_send, gain_recv = some(4)

    greet(g_peers(item, z, g) + z_peers(item, z, g) + [coords["y"][1]])
    swapped = swap_heads(item, z, g, dsend_ref, do_ref, hs, hr, ho.at[0])
    for name in PIECES:
        streams[name].open()
    loads = [
        pltpu.make_async_copy(a, b, load_sem.at[n]) for n, (a, b) in enumerate(zip(loads_hbm, loads_vmem))
    ]
    for copy in loads:
        copy.start()
    lane = lanes_of(256)
    low = lane < 64
    part = lane % 64
    dk_ref[...] = jnp.zeros_like(dk_ref)
    dv_ref[...] = jnp.zeros_like(dv_ref)
    d5_ref[...] = jnp.zeros_like(d5_ref)
    dgain_ref[...] = jnp.zeros_like(dgain_ref)

    def pieces(delta):
        neg = -delta
        hi = neg.astype(BF).astype(F32)
        mid = (neg - hi).astype(BF).astype(F32)
        lo = neg - hi - mid
        return jnp.where(part == 1, hi, jnp.where(part == 2, mid, jnp.where(part == 3, lo, 0.0)))

    def tile(t):
        at = pl.ds(pl.multiple_of(t * 256, 256), 256)
        ab = t // 4
        keys = pl.ds(pl.multiple_of(ab * 1024, 1024), 1024)
        do01 = do_ref[:, t, 0:64, :].astype(F32).reshape(256, 128)
        folded = do_ref[:, t, 64:96, :].astype(F32)
        two = []
        for h in range(4):
            two.append(pltpu.roll(folded[h], 64, 1))
            two.append(folded[h])
        do2 = jnp.concatenate(two, axis=0)
        prod = do01 * o01_ref[at, :]
        prod2 = do2 * o2_ref[at, :]
        delta0 = jnp.sum(jnp.where(low, prod, 0.0), axis=1, keepdims=True)
        delta1 = jnp.sum(jnp.where(low, 0.0, prod), axis=1, keepdims=True)
        delta2 = jnp.sum(jnp.where(low, 0.0, prod2), axis=1, keepdims=True)
        dos = (
            jnp.where(low, do01, pieces(delta0)).astype(BF),
            jnp.where(low, pieces(delta1), do01).astype(BF),
            jnp.where(low, pieces(delta2), do2).astype(BF),
        )
        dqs = []
        for head in range(3):
            q = q_ref[head, at, :]
            prob = jnp.exp(nt(k_ref[head, keys, :], q))
            d_prob = nt(v_ref[head, keys, :], dos[head])
            d_log = (prob * d_prob).astype(BF)
            dv_ref[head, keys, :] += matmul(prob.astype(BF), dos[head])
            dk_ref[head, keys, :] += matmul(d_log, q)
            dqs.append(matmul(kt_ref[head, ab], d_log).T * 0.125)
        off = jnp.where(t < 4, t, 4 + r + 2 * (t - 4)) * 256
        rows = pl.ds(pl.multiple_of(off, 256), 256)
        d5_ref[rows, 0:128] = jnp.where(low, dqs[0], dqs[1]).astype(BF)
        d5_ref[rows, 512:640] = jnp.where(low, dqs[2], 0.0).astype(BF)

    halves = ((0, slice(0, 4)), (1, slice(4, 8)))
    away = (gc, gcx)

    def c_copy(k, ab):
        cut = halves[ab][1]
        return remote(p_ref.at[away[k], cut], rc_ref.at[k, cut], c_send.at[k, ab], c_recv.at[k, ab], core)

    def x_copy(ab):
        cut = halves[ab][1]
        return remote(sx_ref.at[cut], rx_ref.at[cut], x_send.at[ab], x_recv.at[ab], across)

    z_copy = remote(zb_ref, rz_ref, z_send.at[0], z_recv.at[0], pair)
    mine = 3 * p + 2 * r

    def home(n):
        if n < 4:
            s = (zs[3], zs[2], zs[1], z)[n]
            src, dst = ig_ref.at[s], out_ref.at[mine]
        else:
            s = z if n == 5 else zs[2]
            src, dst = ig_ref.at[4 + (1 - p if n == 4 else p)], out_ref.at[3 * p + 1]
        if n in (3, 5):
            return pltpu.make_async_copy(src, dst, h_own.at[n // 4])
        where = mine if n < 4 else 3 * p + 1
        return remote(src, dst, h_send.at[min(n, 3)], h_recv.at[where], (item, s * 4 + g))

    gain = gain_ref[...]

    def norm_back(d_xn, j):
        h = h_ref[j].astype(F32)
        inv = lax.rsqrt(jnp.mean(h * h, axis=-1, keepdims=True) + EPS)
        dgain_ref[...] += jnp.sum(d_xn * h * inv, axis=0, keepdims=True)
        dyg = d_xn * gain
        dot = jnp.mean(dyg * h, axis=-1, keepdims=True)
        ig_ref[j] = (dh_ref[j] + inv * dyg - h * (inv * inv * inv * dot)).astype(BF)

    def run_swap():
        for copy in loads:
            copy.wait()
        swapped()

    def run_dxn():
        @pl.loop(0, 8)
        def _(i):
            rows = pl.ds(pl.multiple_of(i * 256, 256), 256)
            d5_ref[rows, 128:256] = jnp.where(low, dk_ref[0, rows, :], dk_ref[1, rows, :]).astype(BF)
            d5_ref[rows, 256:384] = jnp.where(low, dv_ref[0, rows, :], dv_ref[1, rows, :]).astype(BF)
            d5_ref[rows, 384:512] = jnp.where(low, dk_ref[2, rows, :], dv_ref[2, rows, :]).astype(BF)
            d_xn = nt(d5_ref[rows, :], wc_ref[...]).astype(BF)
            for h in range(4):
                p_ref[h, i, :, :] = d_xn[h * 64 : h * 64 + 64]

        for k in (1, 0):
            for ab in (1, 0):
                c_copy(k, ab).start()

    def run_gw():
        for c in range(5):
            cols = slice(c * 128, c * 128 + 128)
            gw_ref[:, cols] = outer(xn_ref[...], d5_ref[:, cols]).astype(BF)

    def run_xs(ab):
        c_copy(1, ab).wait_recv()

        @pl.loop(0, 4)
        def _(j):
            n = ab * 4 + j
            sx_ref[n] = (p_ref[gx, n].astype(F32) + rc_ref[1, n].astype(F32)).astype(BF)

        x_copy(ab).start()

    def run_t(ab):
        c_copy(0, ab).wait_recv()

        @pl.loop(0, 4)
        def _(j):
            n = ab * 4 + j
            t_ref[n] = p_ref[g, n].astype(F32) + rc_ref[0, n].astype(F32)

    def run_z():
        x_copy(1).wait_recv()
        for q in range(2):
            n = 4 + (1 - r) + 2 * q
            zb_ref[q] = (t_ref[n] + rx_ref[n].astype(F32)).astype(BF)
        z_copy.start()

    def run_na():
        x_copy(0).wait_recv()
        for n, s in enumerate((zs[3], zs[2], zs[1], z)):
            norm_back(t_ref[s] + rx_ref[s].astype(F32), s)
            home(n).start()

    def run_nb():
        z_copy.wait_recv()
        for n, q in enumerate((1 - p, p)):
            k = 4 + r + 2 * q
            norm_back(t_ref[k] + rx_ref[k].astype(F32) + rz_ref[q].astype(F32), 4 + q)
            home(4 + n).start()

    gain_peers = [core] + [peer for _, peer in coords.values()]

    def gain_copy(k):
        return remote(buf.at[k], got.at[k], gain_send.at[k], gain_recv.at[k], gain_peers[k])

    def run_gain(k):
        if k == 0:
            buf[0] = jnp.zeros_like(buf[0])
            buf[0, 0:1, :] = dgain_ref[...]
            buf[0, 1:2, :] = dgain2_ref[...]
        else:
            gain_copy(k - 1).wait_recv()
            buf[k] = buf[k - 1] + got[k - 1]
        if k < 5:
            gain_copy(k).start()
        else:
            gains_out[...] = buf[5]

    done_rs = []

    def run_res():
        done_rs.append(from_slots(item, z, g, res_ref, res_out_ref, rs_send, rs_recv, rs_own))

    single = {
        "swap": run_swap, "dxn": run_dxn, "gw": run_gw, "xsB": lambda: run_xs(1), "xsA": lambda: run_xs(0),
        "tB": lambda: run_t(1), "tA": lambda: run_t(0), "zB": run_z, "nA": run_na, "nB": run_nb, "res": run_res,
    }

    def emit(task):
        if task in single:
            single[task]()
            return
        head, _, k = task.partition(".")
        if head == "tile":
            first, _, last = k.partition(".")
            pl.loop(int(first), int(last))(tile)
            return
        if head == "gain":
            run_gain(int(k))
        elif head[0] == "f":
            streams[head[1:]].fold(int(k))
        elif head[0] == "g":
            streams[head[1:]].collect(int(k))
        else:
            streams[head[1:]].extend()

    for task in PLAN:
        emit(task)

    for s in zs[1:]:
        where = 3 * (s // 2) + 2 * (s % 2)
        remote(ig_ref.at[0], out_ref.at[where], h_send.at[0], h_recv.at[where], pair).wait_recv()
    where = 3 * (1 - p) + 1
    remote(ig_ref.at[0], out_ref.at[where], h_send.at[0], h_recv.at[where], pair).wait_recv()
    done_rs[0]()
    home(3).wait()
    home(5).wait()
    for stream in streams.values():
        stream.close()
    for n in (0, 1, 2, 4):
        home(n).wait_send()
    z_copy.wait_send()
    for ab in range(2):
        x_copy(ab).wait_send()
        for k in range(2):
            c_copy(k, ab).wait_send()
    for k in range(5):
        gain_copy(k).wait_send()


def back(dsend, loads, results, gain1, d_gain2, arrays):
    dma = pltpu.SemaphoreType.DMA
    s = jax.ShapeDtypeStruct
    v = pltpu.VMEM
    _, rows, width = results.shape
    gains = (8, width)
    group = (width, 640)
    outs = (s(results.shape, BF), s(results.shape, BF)) + tuple(s(a.shape, BF) for a in arrays)
    outs += (s((4,) + group, BF), s(gains, F32))
    scratch = [v(a.shape, a.dtype) for a in loads] + [dma((len(loads),))]
    scratch += [
        v(dsend.shape, BF), v((3, 2048, 128), F32), v((3, 2048, 128), F32), v((2048, 640), BF), v((4, 8, rows, width), BF),
        v((2, 8, rows, width), BF), v((8, rows, width), BF), v((8, rows, width), BF),
        v((8, rows, width), F32), v((2, rows, width), BF), v((2, rows, width), BF), v((6, rows, width), BF),
        v((1, width), F32),
        dma((2, 2)), dma((2, 2)), dma((2,)), dma((2,)), dma((1,)), dma((1,)), dma((4,)), dma((6,)), dma((2,)),
        dma((4,)), dma((6,)), dma((2,)), dma((3,)), dma((4,)), dma((1,)),
    ]
    for _, _, _, high, wide, _, _ in PIECES.values():
        scratch += [v((high, wide), BF)] * 3
        scratch += [dma((5,)), dma((5,)), dma((2,)), dma((4,)), dma((4,)), dma((5,)), dma((5,))]
    scratch += [v(group, BF)]
    for _, wide, _ in GROUPS.values():
        scratch += [v((width, wide), BF)]
        scratch += [dma((4,)), dma((4,)), dma((2,)), dma((4, 2)), dma((4, 2)), dma((4, 2)), dma((4, 2))]
    scratch += [v((6,) + gains, F32), v((5,) + gains, F32), dma((5,)), dma((5,))]
    return pl.pallas_call(
        back_kernel,
        out_shape=outs,
        in_specs=[ANY] * (1 + len(loads)) + [VMEM] * 2 + [ANY] * 5,
        out_specs=(ANY,) * 7 + (VMEM,),
        scratch_shapes=scratch,
        compiler_params=params(3, 62),
        name="back",
    )(dsend, *loads, gain1, d_gain2, results, *arrays)


def fast(
    inputs, counts, norm_gain1, w_query, w_key, w_value, w_out, norm_gain2, w_gate, w_up, w_down, cotangent
):
    band_rows, width = inputs.shape[2:]
    gain1, gain2 = norm_gain1.reshape(1, width), norm_gain2.reshape(1, width)
    xall, wc = gather_rows(inputs.reshape(6, band_rows, width), w_query, w_key, w_value)
    osend, xn, q, k, v, kt, o01, o2 = forward_attention(counts, xall.reshape(2048, width), gain1, wc)
    orecv, dy6 = swap_out(osend, cotangent.reshape(6, band_rows, width))
    result6, dsend, hidden, d_second, d_gain2, g_gate, g_up, g_down, g_out = dense(
        orecv, xall, dy6, gain2, w_out, w_gate, w_up, w_down
    )
    input_grads, results, s_gate, s_up, s_down, s_out, s_qkv, s_gains = back(
        dsend, (q, k, v, kt, o01, o2, xn, wc, hidden, d_second), result6, gain1, d_gain2,
        (g_gate, g_up, g_down, g_out),
    )
    grads = widen(s_qkv, s_out, s_gate, s_up, s_down)
    return (
        results.reshape(inputs.shape), input_grads.reshape(inputs.shape), s_gains[0]
    ) + grads[:4] + (s_gains[1],) + grads[4:]


def program(*args):
    micro, seqs, band_rows, width = args[0].shape
    small = lax.axis_size("band") == 16 and lax.axis_size("items") == 2
    if small and (micro, seqs, band_rows, width, HEADS, HEAD_DIM) == (2, 3, 64, 768, 12, 64):
        return fast(*args)
    return per_device(*args)


def solution(mesh):
    return jax.shard_map(
        program,
        mesh=mesh,
        in_specs=(
            P(None, "items", "band", None),
            P(None, "items"),
            P(),
            P(),
            P(),
            P(),
            P(),
            P(),
            P(),
            P(),
            P(),
            P(None, "items", "band", None),
        ),
        out_specs=(
            P(None, "items", "band", None),
            P(None, "items", "band", None),
            P(),
            P(),
            P(),
            P(),
            P(),
            P(),
            P(),
            P(),
            P(),
        ),
        check_vma=False,
    )
```

```python
import math

import jax
import jax.numpy as jnp
from jax import lax
from jax.experimental import pallas as pl
from jax.experimental.pallas import tpu as pltpu
from jax.sharding import PartitionSpec as P

HEADS = 12
HEAD_DIM = 64


EPS = 1e-06


def shortened(shard):

    def short(part):
        return part.astype(jnp.bfloat16) if part.dtype == jnp.float32 else part

    return jax.tree.map(short, shard)


def rms_scale(values, gain):
    return values * lax.rsqrt(jnp.mean(values * values, axis=-1, keepdims=True) + EPS) * gain


def gated(gate, upper):
    return jax.nn.gelu(gate, approximate=True) * upper


def outer(left, right):
    return lax.dot_general(
        left, right, (((0,), (0,)), ((), ())), preferred_element_type=jnp.float32
    )


def transposed(left, weight):
    return lax.dot_general(
        left, weight, (((1,), (1,)), ((), ())), preferred_element_type=jnp.float32
    )


def matmul(left, right):
    return jnp.dot(left, right, preferred_element_type=jnp.float32)


def scores(query, key, scale):
    return jnp.einsum("sqhd,skhd->shqk", query, key, preferred_element_type=jnp.float32) * scale


def per_device(
    inputs,
    counts,
    norm_gain1,
    w_query,
    w_key,
    w_value,
    w_out,
    norm_gain2,
    w_gate,
    w_up,
    w_down,
    cotangent,
):
    micro, seqs, band_rows, width = inputs.shape
    bands = lax.axis_size("band")
    length = band_rows * bands
    rows = seqs * band_rows
    heads = HEADS
    head_dim = HEAD_DIM
    scale = 1.0 / math.sqrt(head_dim)
    key_place = jnp.arange(length, dtype=jnp.int32)
    params = (norm_gain1, w_query, w_key, w_value, w_out, norm_gain2, w_gate, w_up, w_down)
    totals = [jnp.zeros(p.shape, jnp.float32) for p in params]
    results = []
    input_grads = []
    for number in range(micro):
        hidden = inputs[number].astype(jnp.float32).reshape(rows, width)
        lengths = counts[number]
        normed = rms_scale(hidden, norm_gain1).astype(jnp.bfloat16)
        query = matmul(normed, w_query).astype(jnp.bfloat16)
        key_local = matmul(normed, w_key).astype(jnp.bfloat16)
        value_local = matmul(normed, w_value).astype(jnp.bfloat16)
        query_four = query.reshape(seqs, band_rows, heads, head_dim)
        key_three = key_local.reshape(seqs, band_rows, width)
        value_three = value_local.reshape(seqs, band_rows, width)
        key_all, value_all = (
            lax.all_gather(key_three, "band", axis=1, tiled=True),
            lax.all_gather(value_three, "band", axis=1, tiled=True),
        )
        live = key_place[None, :] < lengths[:, None]
        key_four = key_all.reshape(seqs, length, heads, head_dim)
        value_four = value_all.reshape(seqs, length, heads, head_dim)
        logits = jnp.where(live[:, None, None, :], scores(query_four, key_four, scale), -jnp.inf)
        top = jnp.max(logits, axis=-1, keepdims=True)
        expo = jnp.exp(logits - top)
        summed = jnp.sum(expo, axis=-1, keepdims=True)
        log_total = top + jnp.log(summed)
        prob = (expo / summed).astype(jnp.bfloat16)
        attended = jnp.einsum(
            "shqk,skhd->sqhd", prob, value_four, preferred_element_type=jnp.float32
        )
        attended = attended.reshape(rows, width).astype(jnp.bfloat16)
        second = hidden + matmul(attended, w_out)
        normed_two = rms_scale(second, norm_gain2).astype(jnp.bfloat16)
        gate = matmul(normed_two, w_gate)
        upper = matmul(normed_two, w_up)
        mixed = gated(gate, upper).astype(jnp.bfloat16)
        results.append(
            (second + matmul(mixed, w_down)).astype(jnp.bfloat16).reshape(seqs, band_rows, width)
        )
        grad_rows = cotangent[number].reshape(rows, width)
        totals[8] = totals[8] + outer(mixed, grad_rows)
        d_mixed = transposed(grad_rows, w_down)
        pull_gate = jax.vjp(gated, gate, upper)[1]
        d_gate, d_upper = pull_gate(d_mixed)
        d_gate = d_gate.astype(jnp.bfloat16)
        d_upper = d_upper.astype(jnp.bfloat16)
        totals[6] = totals[6] + outer(normed_two, d_gate)
        totals[7] = totals[7] + outer(normed_two, d_upper)
        d_normed_two = transposed(d_gate, w_gate) + transposed(d_upper, w_up)
        pull_two = jax.vjp(rms_scale, second, norm_gain2)[1]
        d_second_norm, d_gain_two = pull_two(d_normed_two)
        totals[5] = totals[5] + d_gain_two
        d_second = grad_rows.astype(jnp.float32) + d_second_norm
        d_branch = d_second.astype(jnp.bfloat16)
        totals[4] = totals[4] + outer(attended, d_branch)
        d_attended = transposed(d_branch, w_out).astype(jnp.bfloat16)
        d_att_four = d_attended.reshape(seqs, band_rows, heads, head_dim)
        key_all, value_all = (
            lax.all_gather(key_three, "band", axis=1, tiled=True),
            lax.all_gather(value_three, "band", axis=1, tiled=True),
        )
        key_four = key_all.reshape(seqs, length, heads, head_dim)
        value_four = value_all.reshape(seqs, length, heads, head_dim)
        logits = jnp.where(live[:, None, None, :], scores(query_four, key_four, scale), -jnp.inf)
        prob_full = jnp.exp(logits - log_total)
        prob = prob_full.astype(jnp.bfloat16)
        d_prob = jnp.einsum(
            "sqhd,skhd->shqk", d_att_four, value_four, preferred_element_type=jnp.float32
        )
        delta = jnp.sum(d_prob * prob_full, axis=-1, keepdims=True)
        d_logits = (prob_full * (d_prob - delta)).astype(jnp.bfloat16)
        d_query = (
            jnp.einsum("shqk,skhd->sqhd", d_logits, key_four, preferred_element_type=jnp.float32)
            * scale
        )
        d_query = d_query.reshape(rows, width).astype(jnp.bfloat16)
        d_key_all = (
            jnp.einsum("shqk,sqhd->skhd", d_logits, query_four, preferred_element_type=jnp.float32)
            * scale
        )
        d_value_all = jnp.einsum(
            "shqk,sqhd->skhd", prob, d_att_four, preferred_element_type=jnp.float32
        )
        d_key_three, d_value_three = (
            lax.psum_scatter(
                d_key_all.reshape(seqs, length, width).astype(jnp.bfloat16),
                "band",
                scatter_dimension=1,
                tiled=True,
            ).astype(jnp.float32),
            lax.psum_scatter(
                d_value_all.reshape(seqs, length, width).astype(jnp.bfloat16),
                "band",
                scatter_dimension=1,
                tiled=True,
            ).astype(jnp.float32),
        )
        d_key = d_key_three.reshape(rows, width).astype(jnp.bfloat16)
        d_value = d_value_three.reshape(rows, width).astype(jnp.bfloat16)
        totals[1] = totals[1] + outer(normed, d_query)
        totals[2] = totals[2] + outer(normed, d_key)
        totals[3] = totals[3] + outer(normed, d_value)
        d_normed = (
            transposed(d_query, w_query) + transposed(d_key, w_key) + transposed(d_value, w_value)
        )
        pull_one = jax.vjp(rms_scale, hidden, norm_gain1)[1]
        d_hidden_norm, d_gain_one = pull_one(d_normed)
        totals[0] = totals[0] + d_gain_one
        input_grads.append(
            (d_second + d_hidden_norm).astype(jnp.bfloat16).reshape(seqs, band_rows, width)
        )
    shares = jax.tree.map(
        lambda part: part.astype(jnp.float32),
        lax.psum_scatter(shortened(tuple(totals)), "band", scatter_dimension=0, tiled=True),
    )
    summed_shares = jax.tree.map(
        lambda part: part.astype(jnp.float32), lax.psum(shortened(shares), "items")
    )
    whole = jax.tree.map(
        lambda part, own: part.astype(own.dtype),
        lax.all_gather(shortened(summed_shares), "band", axis=0, tiled=True),
        summed_shares,
    )
    return (jnp.stack(results), jnp.stack(input_grads)) + tuple(whole)


MESH_ID = pl.DeviceIdType.MESH
NEG = -1e30
BF = jnp.bfloat16
F32 = jnp.float32


def place():
    item = lax.axis_index("items")
    band = lax.axis_index("band")
    return item, band // 4, band % 4


def flip(value):
    return value + 1 - 2 * (value % 2)


def far(value):
    return (value + 2) % 4


def greet(peers):
    barrier = pltpu.get_barrier_semaphore()
    for peer in peers:
        pl.semaphore_signal(barrier, inc=1, device_id=peer, device_id_type=MESH_ID)
    pl.semaphore_wait(barrier, len(peers))


def remote(src, dst, send, recv, peer):
    return pltpu.make_async_remote_copy(
        src_ref=src, dst_ref=dst, send_sem=send, recv_sem=recv, device_id=peer, device_id_type=MESH_ID
    )


def params(number, vmem=62):
    return pltpu.CompilerParams(
        collective_id=number, has_side_effects=True, vmem_limit_bytes=vmem << 20
    )


def whole(value, unit):
    return value if isinstance(value, int) else pl.multiple_of(value, unit)


def lanes_of(rows):
    return lax.broadcasted_iota(jnp.int32, (rows, 128), 1)


ANY = pl.BlockSpec(memory_space=pl.ANY)
VMEM = pl.BlockSpec(memory_space=pltpu.VMEM)
SMEM = pl.BlockSpec(memory_space=pltpu.SMEM)


class Moves:
    def __init__(self):
        self.remotes, self.locals, self.arrivals = [], [], []

    def start(self):
        for make in self.remotes + self.locals:
            make().start()

    def finish(self):
        for make in self.arrivals:
            make().wait_recv()
        for make in self.locals:
            make().wait()
        for make in self.remotes:
            make().wait_send()


def to_slots(item, z, g, src_ref, dst_ref, send, recv, own_sem):
    zs = (z, flip(z), far(z), far(flip(z)))
    p, r = z // 2, z % 2
    moves = Moves()

    def out(n):
        if n < 3:
            s = zs[n + 1]
            src, where = src_ref.at[3 * (s // 2) + 2 * (s % 2)], z
        else:
            s = far(z)
            src, where = src_ref.at[3 * (1 - p) + 1], 4 + p
        return remote(src, dst_ref.at[where], send.at[n], recv.at[where], (item, s * 4 + g))

    def came(where):
        block = dst_ref.at[where]
        return remote(block, block, send.at[0], recv.at[where], (item, far(z) * 4 + g))

    moves.remotes = [lambda n=n: out(n) for n in range(4)]
    moves.locals = [
        lambda: pltpu.make_async_copy(src_ref.at[3 * p + 2 * r], dst_ref.at[z], own_sem.at[0]),
        lambda: pltpu.make_async_copy(src_ref.at[3 * p + 1], dst_ref.at[4 + p], own_sem.at[1]),
    ]
    moves.arrivals = [lambda w=w: came(w) for w in zs[1:] + (4 + (1 - p),)]
    return moves


def from_slots(item, z, g, src_ref, dst_ref, send, recv, own_sem):
    zs = (z, flip(z), far(z), far(flip(z)))
    p, r = z // 2, z % 2
    mine = 3 * p + 2 * r
    moves = Moves()

    def out(n):
        s = zs[n + 1] if n < 3 else far(z)
        src, where = (src_ref.at[s], mine) if n < 3 else (src_ref.at[4 + (1 - p)], 3 * p + 1)
        return remote(src, dst_ref.at[where], send.at[n], recv.at[where], (item, s * 4 + g))

    def came(where):
        block = dst_ref.at[where]
        return remote(block, block, send.at[0], recv.at[where], (item, far(z) * 4 + g))

    moves.remotes = [lambda n=n: out(n) for n in range(4)]
    moves.locals = [
        lambda: pltpu.make_async_copy(src_ref.at[z], dst_ref.at[mine], own_sem.at[0]),
        lambda: pltpu.make_async_copy(src_ref.at[4 + p], dst_ref.at[3 * p + 1], own_sem.at[1]),
    ]
    theirs = [3 * (s // 2) + 2 * (s % 2) for s in zs[1:]] + [3 * (1 - p) + 1]
    moves.arrivals = [lambda w=w: came(w) for w in theirs]
    return moves


def z_peers(item, z, g):
    return [(item, s * 4 + g) for s in (flip(z), far(z), far(flip(z)))]


def g_peers(item, z, g):
    return [(item, z * 4 + h) for h in (flip(g), far(g), far(flip(g)))]


def swap_heads(item, z, g, src_ref, dst_ref, send, recv, own_sem):
    moves = Moves()

    def out(n, h):
        return remote(src_ref.at[h], dst_ref.at[g], send.at[n], recv.at[g], (item, z * 4 + h))

    def came(h):
        return remote(dst_ref.at[h], dst_ref.at[h], send.at[0], recv.at[h], (item, z * 4 + h))

    moves.remotes = [lambda n=n, h=h: out(n, h) for n, h in enumerate((far(g), far(flip(g)), flip(g)))]
    moves.locals = [lambda: pltpu.make_async_copy(src_ref.at[g], dst_ref.at[g], own_sem)]
    moves.arrivals = [lambda h=h: came(h) for h in (flip(g), far(g), far(flip(g)))]
    return moves


def nt(left, right):
    return lax.dot_general(left, right, (((1,), (1,)), ((), ())), preferred_element_type=F32)


def front_kernel(
    x_ref, cot_ref, count_ref, gain_ref, wq_ref, wk_ref, wv_ref,
    orecv_ref, dy_ref, hid_ref, q_out, k_out, v_out, kt_out, o01_out, o2_out, xn_out, wc_out,
    xall_ref, win_ref, wc_ref, xn_ref, q_ref, k_ref, v_ref, kt_ref, o01_ref, o2_ref, osend_ref,
    z_send, f_send, g_send, recv, own_sem, win_sem, o_send, o_recv, o_own, cot_send, cot_recv, cot_own,
    half_sem, tile_sem, last_sem,
):
    item, z, g = place()
    p, r = z // 2, z % 2
    gc, gx = flip(g), far(g)
    gcx = far(gc)
    zs = (z, flip(z), far(z), far(flip(z)))
    core, across = (item, z * 4 + gc), (item, z * 4 + gx)
    lane = lanes_of(256)
    low = lane < 64
    greet(g_peers(item, z, g) + z_peers(item, z, g))

    def items_of(s):
        return (3 * (s // 2) + 2 * (s % 2), 3 * (s // 2) + 1)

    started = []

    def go(make):
        make().start()
        started.append(make)

    def forward(n, ab):
        def make(k, peer):
            where = zs[n] * 4 + g
            src = x_ref.at[items_of(z)[ab]] if n == 0 else xall_ref.at[ab, where]
            return remote(src, xall_ref.at[ab, where], f_send.at[n, ab, k], recv.at[ab, where], peer)

        go(lambda: make(0, across))
        go(lambda: make(1, core))

    def arrived(ab, where):
        block = xall_ref.at[ab, where]
        remote(block, block, z_send.at[0, 0], recv.at[ab, where], core).wait_recv()

    def send_z(ab):
        for n, s in enumerate(zs[1:]):
            go(
                lambda n=n, s=s: remote(
                    x_ref.at[items_of(s)[ab]],
                    xall_ref.at[ab, z * 4 + g],
                    z_send.at[n, ab],
                    recv.at[ab, z * 4 + g],
                    (item, s * 4 + g),
                )
            )

    send_z(0)
    forward(0, 0)
    send_z(1)
    forward(0, 1)
    cut = pl.ds(pl.multiple_of(g * 3 // 2 * 128, 128), 256)
    windows = []
    for n, ref in enumerate((wq_ref, wk_ref, wv_ref)):
        windows.append(pltpu.make_async_copy(ref.at[:, cut], win_ref.at[n], win_sem.at[n]))

    def own_copy(ab):
        return pltpu.make_async_copy(x_ref.at[items_of(z)[ab]], xall_ref.at[ab, z * 4 + g], own_sem.at[ab])

    for copy in windows + [own_copy(0), own_copy(1)]:
        copy.start()
    for copy in windows:
        copy.wait()
    odd = g % 2 == 1

    @pl.loop(0, 3)
    def _(i):
        rows = pl.ds(pl.multiple_of(i * 256, 256), 256)
        firsts, lasts = [], []
        for n in range(3):
            left = win_ref[n, rows, 0:128].astype(F32)
            right = win_ref[n, rows, 128:256].astype(F32)
            crossed = pltpu.roll(jnp.where(low, right, left), 64, 1)
            firsts.append(jnp.where(odd, crossed, left))
            lasts.append(jnp.where(odd, pltpu.roll(right, 64, 1), right))
        for n in range(3):
            wc_ref[rows, n * 128 : n * 128 + 128] = firsts[n].astype(BF)
        wc_ref[rows, 384:512] = jnp.where(low, lasts[1], pltpu.roll(lasts[2], 64, 1)).astype(BF)
        wc_ref[rows, 512:640] = jnp.where(low, lasts[0], 0.0).astype(BF)

    def forward_z(ab):
        for n in range(1, 4):
            arrived(ab, zs[n] * 4 + g)
            forward(n, ab)

    def forward_x(ab):
        def make(n):
            where = zs[n] * 4 + gx
            block = xall_ref.at[ab, where]
            return remote(block, block, g_send.at[n, ab], recv.at[ab, where], core)

        for n in range(4):
            arrived(ab, zs[n] * 4 + gx)
            go(lambda n=n: make(n))

    def project(ab):
        own_copy(ab).wait()
        for n in range(4):
            for h in (gc, gcx):
                arrived(ab, zs[n] * 4 + h)

        @pl.loop(0, 4)
        def _(i):
            rows = pl.ds(pl.multiple_of(ab * 1024 + i * 256, 256), 256)
            h = xall_ref[ab, pl.ds(i * 4, 4)].reshape(256, 768).astype(F32)
            inv = lax.rsqrt(jnp.mean(h * h, axis=-1, keepdims=True) + EPS)
            xn = (h * inv * gain_ref[...]).astype(BF)
            xn_ref[rows, :] = xn
            y = matmul(xn, wc_ref[:, 128:512])
            count = count_ref[p, (2 * r if ab == 0 else 1)]
            at = lax.broadcasted_iota(jnp.int32, (256, 128), 0) + i * 256
            bias = jnp.where(at < count, 0.0, NEG)
            one = jnp.where((lane % 64) < 4, 1.0, 0.0)
            k_aug = jnp.where(lane % 64 == 0, bias, one)
            k01, v01, kv2 = y[:, :128], y[:, 128:256], y[:, 256:]
            k_ref[0, rows, :] = jnp.where(low, k01, k_aug).astype(BF)
            k_ref[1, rows, :] = jnp.where(low, k_aug, k01).astype(BF)
            k_ref[2, rows, :] = jnp.where(low, kv2, k_aug).astype(BF)
            v_ref[0, rows, :] = jnp.where(low, v01, one).astype(BF)
            v_ref[1, rows, :] = jnp.where(low, one, v01).astype(BF)
            v_ref[2, rows, :] = jnp.where(low, one, kv2).astype(BF)

        for head in range(3):
            kt_ref[head, ab, :, :] = k_ref[head, ab * 1024 : (ab + 1) * 1024, :].T
        def make(n):
            rows = pl.ds(ab * 1024, 1024)
            a, b = (
                (k_ref.at[:, rows], k_out.at[:, rows]), (v_ref.at[:, rows], v_out.at[:, rows]),
                (kt_ref.at[:, ab], kt_out.at[:, ab]), (xn_ref.at[rows], xn_out.at[rows]),
            )[n]
            return pltpu.make_async_copy(a, b, half_sem.at[ab, n])

        keep([lambda n=n: make(n) for n in range(4)])

    def tile(t):
        off = jnp.where(t < 4, t, 4 + r + 2 * (t - 4)) * 256
        xq = xn_ref[pl.ds(pl.multiple_of(off, 256), 256), :]
        q01 = matmul(xq, wc_ref[:, 0:128]).astype(BF).astype(F32) * 0.125
        q2 = matmul(xq, wc_ref[:, 512:640]).astype(BF).astype(F32) * 0.125
        flag = jnp.where(lane % 64 == 0, 1.0, 0.0)
        qs = (jnp.where(low, q01, flag), jnp.where(low, flag, q01), jnp.where(low, q2, flag))
        at = pl.ds(pl.multiple_of(t * 256, 256), 256)
        ab = t // 4
        keys = pl.ds(pl.multiple_of(ab * 1024, 1024), 1024)
        outs = []
        for head in range(3):
            s = matmul(qs[head].astype(BF), kt_ref[head, ab])
            top = jnp.max(s, axis=1, keepdims=True)
            e = jnp.exp(s - top).astype(BF)
            o = matmul(e, v_ref[head, keys, :])
            total = o[:, 64:65] if head == 0 else o[:, 0:1]
            outs.append(o / total)
            lse = -(top + jnp.log(total))
            hi = lse.astype(BF).astype(F32)
            mid = (lse - hi).astype(BF).astype(F32)
            lo = lse - hi - mid
            part = lane % 64
            aug = jnp.where(part == 1, hi, jnp.where(part == 2, mid, jnp.where(part == 3, lo, flag)))
            data = low if head != 1 else jnp.logical_not(low)
            q_ref[head, at, :] = jnp.where(data, qs[head], aug).astype(BF)
        o01 = jnp.where(low, outs[0], outs[1])
        o2 = outs[2]
        o01_ref[at, :] = o01
        o2_ref[at, :] = o2
        for h in range(4):
            osend_ref[h, t, 0:64, :] = o01[h * 64 : h * 64 + 64].astype(BF)
            first = o2[h * 64 : h * 64 + 32]
            second = o2[h * 64 + 32 : h * 64 + 64]
            folded = jnp.where(low[:32], pltpu.roll(first, 64, 1), second)
            osend_ref[h, t, 64:96, :] = folded.astype(BF)

    saved = []

    def keep(makes):
        for make in makes:
            make().start()
            saved.append(make)

    def o_copy(t, k):
        h = (gx, gcx, gc)[k]
        return remote(
            osend_ref.at[h, t], orecv_ref.at[g, t], o_send.at[t, k], o_recv.at[g, t], (item, z * 4 + h)
        )

    def tile_copy(t, k):
        rows = pl.ds(whole(t * 256, 256), 256)
        a, b = (
            (q_ref.at[:, rows], q_out.at[:, rows]), (o01_ref.at[rows], o01_out.at[rows]),
            (o2_ref.at[rows], o2_out.at[rows]), (osend_ref.at[g, t], orecv_ref.at[g, t]),
        )[k]
        return pltpu.make_async_copy(a, b, tile_sem.at[t, k])

    def block_copy(j):
        src = xall_ref.at[0, j * 4 + g] if j < 4 else xall_ref.at[1, (r + 2 * (j - 4)) * 4 + g]
        return pltpu.make_async_copy(src, hid_ref.at[j], last_sem.at[j])

    moved = to_slots(item, z, g, cot_ref, dy_ref, cot_send, cot_recv, cot_own)
    forward_z(0)
    forward_x(0)
    keep([lambda: pltpu.make_async_copy(wc_ref, wc_out, last_sem.at[6])])
    project(0)
    forward_z(1)

    @pl.loop(0, 6)
    def _(t):
        tile(t)
        for k in range(3):
            o_copy(t, k).start()
        for k in range(4):
            tile_copy(t, k).start()

        @pl.when(t == 1)
        def _():
            forward_x(1)
            moved.start()

        @pl.when(t == 3)
        def _():
            project(1)
            keep([lambda j=j: block_copy(j) for j in range(6)])

    for t in range(6):
        for h in (gx, gcx, gc):
            block = orecv_ref.at[h, t]
            remote(block, block, o_send.at[0, 0], o_recv.at[h, t], core).wait_recv()
        for k in range(4):
            tile_copy(t, k).wait()
        for k in range(3):
            o_copy(t, k).wait_send()
    moved.finish()
    for make in saved:
        make().wait()
    for make in started:
        make().wait_send()


def front(x6, cot6, counts, gain, wq, wk, wv):
    s = jax.ShapeDtypeStruct
    dma = pltpu.SemaphoreType.DMA
    v = pltpu.VMEM
    _, rows, width = x6.shape
    kept = (
        s((3, 1536, 128), BF), s((3, 2048, 128), BF), s((3, 2048, 128), BF), s((3, 2, 128, 1024), BF),
        s((1536, 128), F32), s((1536, 128), F32), s((2048, width), BF), s((width, 640), BF),
    )
    q, k, vv, kt, o01, o2, xn, wc = [v(a.shape, a.dtype) for a in kept]
    heads = (4, 6, 96, 128)
    return pl.pallas_call(
        front_kernel,
        out_shape=(s(heads, BF), s(x6.shape, BF), s(x6.shape, BF)) + kept,
        in_specs=[ANY, ANY, SMEM, VMEM, ANY, ANY, ANY],
        out_specs=(ANY,) * 11,
        scratch_shapes=[
            v((2, 16, rows, width), BF), v((3, width, 256), BF), wc, xn, q, k, vv, kt, o01, o2, v(heads, BF),
            dma((3, 2)), dma((4, 2, 2)), dma((4, 2)), dma((2, 16)), dma((2,)), dma((3,)),
            dma((6, 3)), dma((4, 6)), dma((1,)), dma((4,)), dma((6,)), dma((2,)), dma((2, 4)), dma((6, 4)), dma((7,)),
        ],
        compiler_params=params(1),
        name="front",
    )(x6, cot6, counts, gain, wq, wk, wv)


GELU_A = 0.044715
GELU_C = math.sqrt(2.0 / math.pi)


def dense_kernel(
    o_ref, x_ref, dy_ref, gain_ref, wo_hbm, wg_hbm, wu_hbm, wd_hbm,
    res_ref, dsend_ref, dh_ref, dgain_ref, gg_ref, gu_ref, gd_ref, go_ref,
    h_ref, wo_ref, wg_ref, wu_ref, wd_ref, att_ref, sec_ref, xn_ref, xt_ref, dyt_ref, dxn_ref, h_sem, wo_sem, w_sem,
):
    chunks, size = 4, wg_ref.shape[1] // 4
    copies = []
    for j in range(6):
        copies.append(pltpu.make_async_copy(x_ref.at[j], h_ref.at[j], h_sem.at[j]))
    copies.append(pltpu.make_async_copy(wo_hbm, wo_ref, wo_sem.at[0]))
    for copy in copies:
        copy.start()
    loads = []
    for c in range(chunks):
        cut = pl.ds(c * size, size)
        loads.append(
            [
                pltpu.make_async_copy(wg_hbm.at[:, cut], wg_ref.at[:, cut], w_sem.at[0, c]),
                pltpu.make_async_copy(wu_hbm.at[:, cut], wu_ref.at[:, cut], w_sem.at[1, c]),
                pltpu.make_async_copy(wd_hbm.at[cut, :], wd_ref.at[cut, :], w_sem.at[2, c]),
            ]
        )
        for copy in loads[-1]:
            copy.start()
    low = lanes_of(384) < 64

    def swap(v):
        return pltpu.roll(v, 64, 1)

    pairs = [o_ref[n, :, 0:64, :].astype(F32).reshape(384, 128) for n in range(4)]

    def unfold(n, high):
        f = o_ref[n, :, 64:96, :].astype(F32)
        s = swap(f.reshape(192, 128)).reshape(6, 32, 128)
        both = (s, f) if high else (f, s)
        return jnp.concatenate(both, axis=1).reshape(384, 128)

    tiles = (
        pairs[0],
        jnp.where(low, unfold(0, False), swap(pairs[1])),
        jnp.where(low, swap(pairs[1]), unfold(1, True)),
        pairs[2],
        jnp.where(low, unfold(2, False), swap(pairs[3])),
        jnp.where(low, swap(pairs[3]), unfold(3, True)),
    )
    for n, tile in enumerate(tiles):
        att_ref[:, n * 128 : n * 128 + 128] = tile.astype(BF)
    for copy in copies:
        copy.wait()
    second = h_ref[...].reshape(384, 768).astype(F32) + matmul(att_ref[...], wo_ref[...])
    sec_ref[...] = second
    inv = lax.rsqrt(jnp.mean(second * second, axis=-1, keepdims=True) + EPS)
    xn_ref[...] = (second * inv * gain_ref[...]).astype(BF)
    xt_ref[...] = xn_ref[...].T
    dxn_ref[...] = jnp.zeros_like(dxn_ref)
    dy = dy_ref[...].reshape(384, 768)
    for c in range(chunks):
        cut = slice(c * size, c * size + size)
        for copy in loads[c]:
            copy.wait()
        gate = matmul(xn_ref[...], wg_ref[:, cut])
        upper = matmul(xn_ref[...], wu_ref[:, cut])
        d_mixed = nt(dy, wd_ref[cut, :])
        square = gate * gate
        tan = jnp.tanh(GELU_C * (gate + GELU_A * square * gate))
        half = 0.5 * (1.0 + tan)
        act = gate * half
        slope = half + 0.5 * gate * (1.0 - tan * tan) * (GELU_C * (1.0 + 3.0 * GELU_A * square))
        mixed = (act * upper).astype(BF)
        d_gate = (d_mixed * upper * slope).astype(BF)
        d_upper = (d_mixed * act).astype(BF)
        sec_ref[...] += matmul(mixed, wd_ref[cut, :])
        dxn_ref[...] += nt(d_gate, wg_ref[:, cut]) + nt(d_upper, wu_ref[:, cut])
        gg_ref[:, cut] = matmul(xt_ref[...], d_gate).astype(BF)
        gu_ref[:, cut] = matmul(xt_ref[...], d_upper).astype(BF)
        gd_ref[cut, :] = outer(mixed, dy).astype(BF)
    res_ref[...] = sec_ref[...].astype(BF).reshape(6, 64, 768)
    second = h_ref[...].reshape(384, 768).astype(F32) + matmul(att_ref[...], wo_ref[...])
    inv = lax.rsqrt(jnp.mean(second * second, axis=-1, keepdims=True) + EPS)
    d_xn = dxn_ref[...]
    dgain_ref[...] = jnp.sum(d_xn * second * inv, axis=0, keepdims=True)
    dyg = d_xn * gain_ref[...]
    dot = jnp.mean(dyg * second, axis=-1, keepdims=True)
    d_second = dy.astype(F32) + inv * dyg - second * (inv * inv * inv * dot)
    dh_ref[...] = d_second.reshape(6, 64, 768)
    d_branch = d_second.astype(BF)
    go_ref[...] = outer(att_ref[...], d_branch).astype(BF)
    d_att = nt(d_branch, wo_ref[...]).astype(BF).astype(F32)
    d = [d_att[:, n * 128 : n * 128 + 128] for n in range(6)]
    firsts = (d[0], swap(jnp.where(low, d[2], d[1])), d[3], swap(jnp.where(low, d[5], d[4])))
    lasts = ((d[1], False), (d[2], True), (d[4], False), (d[5], True))
    low3 = lax.broadcasted_iota(jnp.int32, (6, 32, 128), 2) < 64
    for n in range(4):
        dsend_ref[n, :, 0:64, :] = firsts[n].astype(BF).reshape(6, 64, 128)
        v, high = lasts[n]
        v3, s3 = v.reshape(6, 64, 128), swap(v).reshape(6, 64, 128)
        top, bottom = v3[:, :32], v3[:, 32:]
        top_s, bottom_s = s3[:, :32], s3[:, 32:]
        f = jnp.where(low3, top_s, bottom) if high else jnp.where(low3, top, bottom_s)
        dsend_ref[n, :, 64:96, :] = f.astype(BF)


def dense(orecv, xall, dy6, gain, w_out, w_gate, w_up, w_down):
    s = jax.ShapeDtypeStruct
    dma = pltpu.SemaphoreType.DMA
    rows, width = dy6.shape[1:]
    hidden = w_gate.shape[1]
    v = pltpu.VMEM
    return pl.pallas_call(
        dense_kernel,
        out_shape=(
            s(dy6.shape, BF), s(orecv.shape, BF), s(dy6.shape, F32), s((1, width), F32),
            s(w_gate.shape, BF), s(w_up.shape, BF), s(w_down.shape, BF), s(w_out.shape, BF),
        ),
        in_specs=[VMEM, ANY, VMEM, VMEM] + [ANY] * 4,
        out_specs=(VMEM,) * 8,
        scratch_shapes=[
            v(dy6.shape, BF), v(w_out.shape, BF), v(w_gate.shape, BF), v(w_up.shape, BF), v(w_down.shape, BF),
            v((384, width), BF), v((384, width), F32), v((384, width), BF), v((width, 384), BF), v((width, 384), BF),
            v((384, width), F32), dma((6,)), dma((1,)), dma((3, 4)),
        ],
        compiler_params=pltpu.CompilerParams(vmem_limit_bytes=62 << 20),
        name="dense",
    )(orecv, xall, dy6, gain, w_out, w_gate, w_up, w_down)


def widen_kernel(qkv_ref, so_ref, sg_ref, su_ref, sd_ref, q_ref, k_ref, v_ref, o_ref, g_ref, u_ref, d_ref):
    low = lanes_of(qkv_ref.shape[1]) < 64

    def swap(v):
        return pltpu.roll(v, 64, 1)

    for out, first, last, high in ((q_ref, 0, 512, False), (k_ref, 128, 384, False), (v_ref, 256, 384, True)):
        a = [qkv_ref[n, :, first : first + 128].astype(F32) for n in range(4)]
        b = [qkv_ref[n, :, last : last + 128].astype(F32) for n in range(4)]
        low_b = [swap(x) if high else x for x in b]
        high_b = [x if high else swap(x) for x in b]
        tiles = (
            a[0], jnp.where(low, low_b[0], swap(a[1])), jnp.where(low, swap(a[1]), high_b[1]),
            a[2], jnp.where(low, low_b[2], swap(a[3])), jnp.where(low, swap(a[3]), high_b[3]),
        )
        for n, tile in enumerate(tiles):
            out[:, n * 128 : n * 128 + 128] = tile
    o_ref[...] = so_ref[...].astype(F32)
    g_ref[...] = sg_ref[...].astype(F32)
    u_ref[...] = su_ref[...].astype(F32)
    d_ref[...] = sd_ref[...].astype(F32)


def widen(qkv, s_out, s_gate, s_up, s_down):
    s = jax.ShapeDtypeStruct
    steps = 16

    def spec(a):
        if len(a.shape) == 3:
            return pl.BlockSpec((a.shape[0], a.shape[1] // steps, a.shape[2]), lambda i: (0, i, 0))
        return pl.BlockSpec((a.shape[0] // steps, a.shape[1]), lambda i: (i, 0))

    outs = tuple(s(a.shape, F32) for a in (s_out, s_out, s_out, s_out, s_gate, s_up, s_down))
    ins = (qkv, s_out, s_gate, s_up, s_down)
    return pl.pallas_call(
        widen_kernel,
        grid=(steps,),
        out_shape=outs,
        in_specs=[spec(a) for a in ins],
        out_specs=tuple(spec(a) for a in outs),
        compiler_params=pltpu.CompilerParams(vmem_limit_bytes=62 << 20),
        name="widen",
    )(*ins)


class Stream:
    def __init__(self, src, res, acc, first, rest, sems, order, coords, core, cut):
        self.src, self.res, self.acc, self.first, self.rest = src, res, acc, first, rest
        self.send, self.recv, self.own, self.back, self.got, self.fwd, self.fgot = sems
        row, col, half = cut
        self.rows, self.wide = acc.shape
        self.row = row
        self.order = [coords[name] for name in order]
        self.deep = len(order)
        bit, self.peer = core
        if half:
            self.mine = pl.ds(pl.multiple_of(bit * half + col, 128), self.wide)
            self.other = pl.ds(pl.multiple_of((1 - bit) * half + col, 128), self.wide)
        else:
            self.mine = pl.ds(col, self.wide)
        self.base, self.size = [0], [self.rows]
        for bit, _ in self.order:
            self.size.append(self.size[-1] // 2)
            self.base.append(self.base[-1] + bit * self.size[-1])

    def part(self, base, size):
        return pl.ds(whole(base, 16), size)

    def at(self, base, size, mine=True):
        cols = self.mine if mine else self.other
        return self.res.at[pl.ds(whole(self.row + base, 16), size), cols]

    def sibling(self, k):
        return self.base[k - 1] + (1 - self.order[k - 1][0]) * self.size[k]

    def own_in(self):
        rows = pl.ds(self.row, self.rows)
        return pltpu.make_async_copy(self.src.at[rows, self.mine], self.acc, self.own.at[0])

    def own_out(self):
        here = self.base[self.deep], self.size[self.deep]
        return pltpu.make_async_copy(self.acc.at[self.part(*here)], self.at(*here), self.own.at[1])

    def c_push(self, k):
        if k == 0:
            src = self.src.at[pl.ds(self.row, self.rows), self.other]
            return remote(src, self.first, self.send.at[0], self.recv.at[0], self.peer)
        return remote(
            self.acc.at[self.part(self.sibling(k), self.size[k])],
            self.rest.at[pl.ds(self.rows - 2 * self.size[k], self.size[k])],
            self.send.at[k],
            self.recv.at[k],
            self.order[k - 1][1],
        )

    def c_back(self, k):
        here = self.base[k], self.size[k]
        src = self.acc.at[self.part(*here)] if k == self.deep else self.at(*here)
        return remote(
            src, self.at(*here), self.back.at[k - 1], self.got.at[k - 1], self.order[k - 1][1]
        )

    def c_forward(self, k):
        if k == 0:
            here = self.base[self.deep], self.size[self.deep]
            src = self.acc.at[self.part(*here)]
        else:
            here = self.sibling(k), self.size[k]
            src = self.at(*here)
        return remote(src, self.at(*here), self.fwd.at[k], self.fgot.at[k], self.peer)

    def open(self):
        self.own_in().start()
        self.c_push(0).start()

    def fold(self, k):
        if k == 0:
            self.own_in().wait()
        self.c_push(k).wait_recv()
        base, size = self.base[k], self.size[k]
        other, at = (self.first, 0) if k == 0 else (self.rest, self.rows - 2 * size)
        step = 64 if size % 64 == 0 else 48

        @pl.loop(0, size // step)
        def _(n):
            rows = self.part(base + n * step, step)
            more = other[pl.ds(pl.multiple_of(at + n * step, 16), step), :]
            self.acc[rows, :] = (self.acc[rows, :].astype(F32) + more.astype(F32)).astype(BF)

        if k < self.deep:
            self.c_push(k + 1).start()
        else:
            self.c_back(k).start()
            self.c_forward(0).start()
            self.own_out().start()

    def collect(self, k):
        here = self.sibling(k), self.size[k]
        block = self.at(*here)
        remote(block, block, self.back.at[k - 1], self.got.at[k - 1], self.peer).wait_recv()
        if k == self.deep:
            self.own_out().wait()
        if k > 1:
            self.c_back(k - 1).start()
        self.c_forward(k).start()

    def close(self):
        for k in range(self.deep + 1):
            if k == 0:
                here = self.base[self.deep], self.size[self.deep]
            else:
                here = self.sibling(k), self.size[k]
            block = self.at(*here, mine=False)
            remote(block, block, self.fwd.at[k], self.fgot.at[k], self.peer).wait_recv()
            self.c_push(k).wait_send()
            self.c_forward(k).wait_send()
            if k > 0:
                self.c_back(k).wait_send()


class Grouped(Stream):
    def __init__(self, res, acc, rest, sems, order, coords, core, cut, group, across):
        super().__init__(None, res, acc, None, rest, sems, order, coords, core, cut)
        self.group, self.gx, self.across = group, far(group), across

    def at(self, base, size, n=0):
        h = (self.group, self.gx, flip(self.group), far(flip(self.group)))[n]
        return self.res.at[h, self.part(base, size), self.mine]

    def c_across(self):
        here = self.base[self.deep], self.size[self.deep]
        return remote(
            self.acc.at[self.part(*here)],
            self.at(*here),
            self.back.at[self.deep, 0],
            self.got.at[self.deep, 0],
            self.across,
        )

    def c_back(self, k, n):
        here = self.base[k], self.size[k]
        own = k == self.deep and n == 0
        src = self.acc.at[self.part(*here)] if own else self.at(*here, n)
        return remote(
            src, self.at(*here, n), self.back.at[k - 1, n], self.got.at[k - 1, n], self.order[k - 1][1]
        )

    def c_forward(self, k, n):
        if k == 0:
            here = self.base[self.deep], self.size[self.deep]
            src = self.acc.at[self.part(*here)] if n == 0 else self.at(*here, n)
        else:
            here = self.sibling(k), self.size[k]
            src = self.at(*here, n)
        return remote(src, self.at(*here, n), self.fwd.at[k, n], self.fgot.at[k, n], self.peer)

    def fold(self, k):
        if k == 0:
            self.c_push(1).start()
            return
        if k < self.deep:
            super().fold(k)
            return
        self.c_push(k).wait_recv()
        base, size = self.base[k], self.size[k]
        rows = self.part(base, size)
        more = self.rest[pl.ds(self.rows - 2 * size, size), :]
        self.acc[rows, :] = (self.acc[rows, :].astype(F32) + more.astype(F32)).astype(BF)
        self.c_across().start()
        self.c_back(k, 0).start()
        self.c_forward(0, 0).start()
        self.own_out().start()

    def extend(self):
        self.c_across().wait_recv()
        self.c_back(self.deep, 1).start()
        self.c_forward(0, 1).start()

    def collect(self, k):
        here = self.sibling(k), self.size[k]
        if k == self.deep:
            self.own_out().wait()
        for n in range(2):
            block = self.at(*here, n)
            remote(block, block, self.back.at[k - 1, n], self.got.at[k - 1, n], self.peer).wait_recv()
            if k > 1:
                if n == 1:
                    self.c_back(k - 1, 0).start()
                    self.c_back(k - 1, 1).start()
            self.c_forward(k, n).start()

    def close(self):
        self.c_across().wait_send()
        for k in range(self.deep + 1):
            if k == 0:
                here = self.base[self.deep], self.size[self.deep]
            else:
                here = self.sibling(k), self.size[k]
                self.c_push(k).wait_send()
            for n in range(2):
                block = self.at(*here, 2 + n)
                remote(block, block, self.fwd.at[k, n], self.fgot.at[k, n], self.peer).wait_recv()
                self.c_forward(k, n).wait_send()
                if k > 0:
                    self.c_back(k, n).wait_send()


PIECES = {
    "U1": (1, 0, 512, 768, 512, 1024, ("x", "y", "zl", "zh")),
    "G1": (0, 0, 512, 768, 512, 1024, ("zh", "x", "y", "zl")),
    "O": (3, 0, 0, 768, 384, 384, ("x", "y", "zl", "zh")),
    "U0": (1, 0, 0, 768, 512, 1024, ("zl", "x", "y", "zh")),
    "D0": (2, 0, 0, 1024, 384, 384, ("y", "x", "zl", "zh")),
    "G0": (0, 0, 0, 768, 512, 1024, ("x", "y", "zl", "zh")),
    "D1": (2, 1024, 0, 1024, 384, 384, ("x", "y", "zl", "zh")),
}
GROUPS = {
    "qA": (0, 256, ("y", "zl", "zh")),
    "qB": (256, 384, ("y", "zl", "zh")),
}
PLAN = (
    "fU1.0", "fG1.0", "fO.0", "swap", "res", "tile", "fU0.0", "fD0.0", "tile", "fG0.0",
    "fD1.0", "fU1.1", "tile", "tile", "fO.1", "fD0.1", "tile", "fU1.2", "tile", "fO.2",
    "fG1.1", "fU0.1", "fG0.1", "fU1.3", "dxn", "fO.3", "gw", "xsB", "fU1.4", "fD1.1",
    "xsA", "fG0.2", "fqA.0", "fqB.0", "fO.4", "tB", "tA", "fD0.2", "gU1.4", "fG0.3",
    "fG1.2", "fD1.2", "gO.4", "fD0.3", "fU0.2", "gU1.3", "fqA.1", "fG0.4", "fD1.3", "gO.3",
    "fqB.1", "fD0.4", "fqA.2", "zB", "fG1.3", "gG0.4", "fU0.3", "fD1.4", "fqB.2", "gU1.2",
    "gD0.4", "nA", "gO.2", "fqA.3", "nB", "fG1.4", "gain.0", "gG0.3", "gain.1", "gU1.1",
    "fU0.4", "gD1.4", "gG0.2", "fqB.3", "gO.1", "gD0.3", "eqA", "gain.2", "gain.3", "gG0.1",
    "eqB", "gD0.2", "gG1.4", "gU0.4", "gD1.3", "gain.4", "gqA.3", "gD0.1", "gain.5", "gG1.3",
    "gU0.3", "gqB.3", "gqA.2", "gD1.2", "gG1.2", "gU0.2", "gqB.2", "gqA.1", "gD1.1", "gqB.1",
    "gG1.1", "gU0.1",
)


def back_kernel(*refs):
    take = iter(refs)

    def some(n):
        return [next(take) for _ in range(n)]

    (dsend_ref,) = some(1)
    loads_hbm = some(10)
    gain_ref, dgain2_ref = some(2)
    (res_ref,) = some(1)
    srcs = some(4)
    out_ref, res_out_ref = some(2)
    outs = some(5)
    (gains_out,) = some(1)
    loads_vmem = some(10)
    q_ref, k_ref, v_ref, kt_ref, o01_ref, o2_ref, xn_ref, wc_ref, h_ref, dh_ref = loads_vmem
    (load_sem,) = some(1)
    (do_ref, dk_ref, dv_ref, d5_ref, p_ref) = some(5)
    (rc_ref, sx_ref, rx_ref, t_ref, zb_ref, rz_ref, ig_ref, dgain_ref) = some(8)
    (c_send, c_recv, x_send, x_recv, z_send, z_recv) = some(6)
    (rs_send, rs_recv, rs_own, h_send, h_recv, h_own, hs, hr, ho) = some(9)
    item, z, g = place()
    gc, gx = flip(g), far(g)
    gcx = far(gc)
    p, r = z // 2, z % 2
    coords = {
        "x": (g // 2, (item, z * 4 + gx)),
        "y": (item, (1 - item, z * 4 + g)),
        "zl": (z % 2, (item, flip(z) * 4 + g)),
        "zh": (z // 2, (item, far(z) * 4 + g)),
    }
    across, pair = coords["x"][1], coords["zl"][1]
    core = (item, z * 4 + gc)
    zs = (z, flip(z), far(z), far(flip(z)))
    streams = {}
    for name, (n, row, col, _, _, half, order) in PIECES.items():
        acc, first, rest = some(3)
        streams[name] = Stream(
            srcs[n], outs[n], acc, first, rest, some(7), order, coords, (g % 2, core), (row, col, half)
        )
    (gw_ref,) = some(1)
    for name, (col, wide, order) in GROUPS.items():
        (rest,) = some(1)
        acc = gw_ref.at[:, pl.ds(col, wide)]
        streams[name] = Grouped(
            outs[4], acc, rest, some(7), order, coords, (g % 2, core), (0, col, 0), g, across
        )
    buf, got, gain_send, gain_recv = some(4)

    greet(g_peers(item, z, g) + z_peers(item, z, g) + [coords["y"][1]])
    swapped = swap_heads(item, z, g, dsend_ref, do_ref, hs, hr, ho.at[0])
    swapped.start()
    for name in PIECES:
        streams[name].open()
    loads = [
        pltpu.make_async_copy(a, b, load_sem.at[n]) for n, (a, b) in enumerate(zip(loads_hbm, loads_vmem))
    ]
    for copy in loads:
        copy.start()
    lane = lanes_of(256)
    low = lane < 64
    part = lane % 64
    dk_ref[...] = jnp.zeros_like(dk_ref)
    dv_ref[...] = jnp.zeros_like(dv_ref)
    d5_ref[...] = jnp.zeros_like(d5_ref)
    dgain_ref[...] = jnp.zeros_like(dgain_ref)

    def pieces(delta):
        neg = -delta
        hi = neg.astype(BF).astype(F32)
        mid = (neg - hi).astype(BF).astype(F32)
        lo = neg - hi - mid
        return jnp.where(part == 1, hi, jnp.where(part == 2, mid, jnp.where(part == 3, lo, 0.0)))

    def tile(t):
        at = pl.ds(pl.multiple_of(t * 256, 256), 256)
        ab = t // 4
        keys = pl.ds(pl.multiple_of(ab * 1024, 1024), 1024)
        do01 = do_ref[:, t, 0:64, :].astype(F32).reshape(256, 128)
        folded = do_ref[:, t, 64:96, :].astype(F32)
        two = []
        for h in range(4):
            two.append(pltpu.roll(folded[h], 64, 1))
            two.append(folded[h])
        do2 = jnp.concatenate(two, axis=0)
        prod = do01 * o01_ref[at, :]
        prod2 = do2 * o2_ref[at, :]
        delta0 = jnp.sum(jnp.where(low, prod, 0.0), axis=1, keepdims=True)
        delta1 = jnp.sum(jnp.where(low, 0.0, prod), axis=1, keepdims=True)
        delta2 = jnp.sum(jnp.where(low, 0.0, prod2), axis=1, keepdims=True)
        dos = (
            jnp.where(low, do01, pieces(delta0)).astype(BF),
            jnp.where(low, pieces(delta1), do01).astype(BF),
            jnp.where(low, pieces(delta2), do2).astype(BF),
        )
        dqs = []
        for head in range(3):
            q = q_ref[head, at, :]
            prob = jnp.exp(nt(k_ref[head, keys, :], q))
            d_prob = nt(v_ref[head, keys, :], dos[head])
            d_log = (prob * d_prob).astype(BF)
            dv_ref[head, keys, :] += matmul(prob.astype(BF), dos[head])
            dk_ref[head, keys, :] += matmul(d_log, q)
            dqs.append(matmul(kt_ref[head, ab], d_log).T * 0.125)
        off = jnp.where(t < 4, t, 4 + r + 2 * (t - 4)) * 256
        rows = pl.ds(pl.multiple_of(off, 256), 256)
        d5_ref[rows, 0:128] = jnp.where(low, dqs[0], dqs[1]).astype(BF)
        d5_ref[rows, 512:640] = jnp.where(low, dqs[2], 0.0).astype(BF)

    halves = ((0, slice(0, 4)), (1, slice(4, 8)))
    away = (gc, gcx)

    def c_copy(k, ab):
        cut = halves[ab][1]
        return remote(p_ref.at[away[k], cut], rc_ref.at[k, cut], c_send.at[k, ab], c_recv.at[k, ab], core)

    def x_copy(ab):
        cut = halves[ab][1]
        return remote(sx_ref.at[cut], rx_ref.at[cut], x_send.at[ab], x_recv.at[ab], across)

    z_copy = remote(zb_ref, rz_ref, z_send.at[0], z_recv.at[0], pair)
    mine = 3 * p + 2 * r

    def home(n):
        if n < 4:
            s = (zs[3], zs[2], zs[1], z)[n]
            src, dst = ig_ref.at[s], out_ref.at[mine]
        else:
            s = z if n == 5 else zs[2]
            src, dst = ig_ref.at[4 + (1 - p if n == 4 else p)], out_ref.at[3 * p + 1]
        if n in (3, 5):
            return pltpu.make_async_copy(src, dst, h_own.at[n // 4])
        where = mine if n < 4 else 3 * p + 1
        return remote(src, dst, h_send.at[min(n, 3)], h_recv.at[where], (item, s * 4 + g))

    gain = gain_ref[...]

    def norm_back(d_xn, j):
        h = h_ref[j].astype(F32)
        inv = lax.rsqrt(jnp.mean(h * h, axis=-1, keepdims=True) + EPS)
        dgain_ref[...] += jnp.sum(d_xn * h * inv, axis=0, keepdims=True)
        dyg = d_xn * gain
        dot = jnp.mean(dyg * h, axis=-1, keepdims=True)
        ig_ref[j] = (dh_ref[j] + inv * dyg - h * (inv * inv * inv * dot)).astype(BF)

    def run_swap():
        for copy in loads:
            copy.wait()
        swapped.finish()

    def run_dxn():
        @pl.loop(0, 8)
        def _(i):
            rows = pl.ds(pl.multiple_of(i * 256, 256), 256)
            d5_ref[rows, 128:256] = jnp.where(low, dk_ref[0, rows, :], dk_ref[1, rows, :]).astype(BF)
            d5_ref[rows, 256:384] = jnp.where(low, dv_ref[0, rows, :], dv_ref[1, rows, :]).astype(BF)
            d5_ref[rows, 384:512] = jnp.where(low, dk_ref[2, rows, :], dv_ref[2, rows, :]).astype(BF)
            d_xn = nt(d5_ref[rows, :], wc_ref[...]).astype(BF)
            for h in range(4):
                p_ref[h, i, :, :] = d_xn[h * 64 : h * 64 + 64]

        for k in (1, 0):
            for ab in (1, 0):
                c_copy(k, ab).start()

    def run_gw():
        for c in range(5):
            cols = slice(c * 128, c * 128 + 128)
            gw_ref[:, cols] = outer(xn_ref[...], d5_ref[:, cols]).astype(BF)

    def run_xs(ab):
        c_copy(1, ab).wait_recv()

        @pl.loop(0, 4)
        def _(j):
            n = ab * 4 + j
            sx_ref[n] = (p_ref[gx, n].astype(F32) + rc_ref[1, n].astype(F32)).astype(BF)

        x_copy(ab).start()

    def run_t(ab):
        c_copy(0, ab).wait_recv()

        @pl.loop(0, 4)
        def _(j):
            n = ab * 4 + j
            t_ref[n] = p_ref[g, n].astype(F32) + rc_ref[0, n].astype(F32)

    def run_z():
        x_copy(1).wait_recv()
        for q in range(2):
            n = 4 + (1 - r) + 2 * q
            zb_ref[q] = (t_ref[n] + rx_ref[n].astype(F32)).astype(BF)
        z_copy.start()

    def run_na():
        x_copy(0).wait_recv()
        for n, s in enumerate((zs[3], zs[2], zs[1], z)):
            norm_back(t_ref[s] + rx_ref[s].astype(F32), s)
            home(n).start()

    def run_nb():
        z_copy.wait_recv()
        for n, q in enumerate((1 - p, p)):
            k = 4 + r + 2 * q
            norm_back(t_ref[k] + rx_ref[k].astype(F32) + rz_ref[q].astype(F32), 4 + q)
            home(4 + n).start()

    gain_peers = [core] + [peer for _, peer in coords.values()]

    def gain_copy(k):
        return remote(buf.at[k], got.at[k], gain_send.at[k], gain_recv.at[k], gain_peers[k])

    def run_gain(k):
        if k == 0:
            buf[0] = jnp.zeros_like(buf[0])
            buf[0, 0:1, :] = dgain_ref[...]
            buf[0, 1:2, :] = dgain2_ref[...]
        else:
            gain_copy(k - 1).wait_recv()
            buf[k] = buf[k - 1] + got[k - 1]
        if k < 5:
            gain_copy(k).start()
        else:
            gains_out[...] = buf[5]

    homes = from_slots(item, z, g, res_ref, res_out_ref, rs_send, rs_recv, rs_own)

    single = {
        "swap": run_swap, "dxn": run_dxn, "gw": run_gw, "xsB": lambda: run_xs(1), "xsA": lambda: run_xs(0),
        "tB": lambda: run_t(1), "tA": lambda: run_t(0), "zB": run_z, "nA": run_na, "nB": run_nb, "res": homes.start,
    }

    def emit(task):
        if task in single:
            single[task]()
            return
        head, _, k = task.partition(".")
        if head == "gain":
            run_gain(int(k))
        elif head[0] == "f":
            streams[head[1:]].fold(int(k))
        elif head[0] == "g":
            streams[head[1:]].collect(int(k))
        else:
            streams[head[1:]].extend()

    tiles = [n for n, task in enumerate(PLAN) if task == "tile"]
    for task in PLAN[: tiles[0]]:
        emit(task)

    @pl.loop(0, 6)
    def _(t):
        tile(t)
        for n in range(5):
            tasks = PLAN[tiles[n] + 1 : tiles[n + 1]]
            if tasks:

                @pl.when(t == n)
                def _():
                    for task in tasks:
                        emit(task)

    for task in PLAN[tiles[5] + 1 :]:
        emit(task)

    for s in zs[1:]:
        where = 3 * (s // 2) + 2 * (s % 2)
        remote(ig_ref.at[0], out_ref.at[where], h_send.at[0], h_recv.at[where], pair).wait_recv()
    where = 3 * (1 - p) + 1
    remote(ig_ref.at[0], out_ref.at[where], h_send.at[0], h_recv.at[where], pair).wait_recv()
    homes.finish()
    home(3).wait()
    home(5).wait()
    for stream in streams.values():
        stream.close()
    for n in (0, 1, 2, 4):
        home(n).wait_send()
    z_copy.wait_send()
    for ab in range(2):
        x_copy(ab).wait_send()
        for k in range(2):
            c_copy(k, ab).wait_send()
    for k in range(5):
        gain_copy(k).wait_send()


def back(dsend, loads, results, gain1, d_gain2, arrays):
    dma = pltpu.SemaphoreType.DMA
    s = jax.ShapeDtypeStruct
    v = pltpu.VMEM
    _, rows, width = results.shape
    gains = (8, width)
    group = (width, 640)
    outs = (s(results.shape, BF), s(results.shape, BF)) + tuple(s(a.shape, BF) for a in arrays)
    outs += (s((4,) + group, BF), s(gains, F32))
    scratch = [v(a.shape, a.dtype) for a in loads] + [dma((len(loads),))]
    scratch += [
        v(dsend.shape, BF), v((3, 2048, 128), F32), v((3, 2048, 128), F32), v((2048, 640), BF), v((4, 8, rows, width), BF),
        v((2, 8, rows, width), BF), v((8, rows, width), BF), v((8, rows, width), BF),
        v((8, rows, width), F32), v((2, rows, width), BF), v((2, rows, width), BF), v((6, rows, width), BF),
        v((1, width), F32),
        dma((2, 2)), dma((2, 2)), dma((2,)), dma((2,)), dma((1,)), dma((1,)), dma((4,)), dma((6,)), dma((2,)),
        dma((4,)), dma((6,)), dma((2,)), dma((3,)), dma((4,)), dma((1,)),
    ]
    for _, _, _, high, wide, _, _ in PIECES.values():
        scratch += [v((high, wide), BF)] * 3
        scratch += [dma((5,)), dma((5,)), dma((2,)), dma((4,)), dma((4,)), dma((5,)), dma((5,))]
    scratch += [v(group, BF)]
    for _, wide, _ in GROUPS.values():
        scratch += [v((width, wide), BF)]
        scratch += [dma((4,)), dma((4,)), dma((2,)), dma((4, 2)), dma((4, 2)), dma((4, 2)), dma((4, 2))]
    scratch += [v((6,) + gains, F32), v((5,) + gains, F32), dma((5,)), dma((5,))]
    return pl.pallas_call(
        back_kernel,
        out_shape=outs,
        in_specs=[ANY] * (1 + len(loads)) + [VMEM] * 2 + [ANY] * 5,
        out_specs=(ANY,) * 7 + (VMEM,),
        scratch_shapes=scratch,
        compiler_params=params(3, 62),
        name="back",
    )(dsend, *loads, gain1, d_gain2, results, *arrays)


def fast(
    inputs, counts, norm_gain1, w_query, w_key, w_value, w_out, norm_gain2, w_gate, w_up, w_down, cotangent
):
    band_rows, width = inputs.shape[2:]
    gain1, gain2 = norm_gain1.reshape(1, width), norm_gain2.reshape(1, width)
    orecv, dy6, hidden, q, k, v, kt, o01, o2, xn, wc = front(
        inputs.reshape(6, band_rows, width), cotangent.reshape(6, band_rows, width), counts, gain1,
        w_query, w_key, w_value,
    )
    result6, dsend, d_second, d_gain2, g_gate, g_up, g_down, g_out = dense(
        orecv, hidden, dy6, gain2, w_out, w_gate, w_up, w_down
    )
    input_grads, results, s_gate, s_up, s_down, s_out, s_qkv, s_gains = back(
        dsend, (q, k, v, kt, o01, o2, xn, wc, hidden, d_second), result6, gain1, d_gain2,
        (g_gate, g_up, g_down, g_out),
    )
    grads = widen(s_qkv, s_out, s_gate, s_up, s_down)
    return (
        results.reshape(inputs.shape), input_grads.reshape(inputs.shape), s_gains[0]
    ) + grads[:4] + (s_gains[1],) + grads[4:]


def program(*args):
    micro, seqs, band_rows, width = args[0].shape
    small = lax.axis_size("band") == 16 and lax.axis_size("items") == 2
    if small and (micro, seqs, band_rows, width, HEADS, HEAD_DIM) == (2, 3, 64, 768, 12, 64):
        return fast(*args)
    return per_device(*args)


def solution(mesh):
    return jax.shard_map(
        program,
        mesh=mesh,
        in_specs=(
            P(None, "items", "band", None),
            P(None, "items"),
            P(),
            P(),
            P(),
            P(),
            P(),
            P(),
            P(),
            P(),
            P(),
            P(None, "items", "band", None),
        ),
        out_specs=(
            P(None, "items", "band", None),
            P(None, "items", "band", None),
            P(),
            P(),
            P(),
            P(),
            P(),
            P(),
            P(),
            P(),
            P(),
        ),
        check_vma=False,
    )
```

```python
import functools
import math

import jax
import jax.numpy as jnp
from jax import lax
from jax.experimental import pallas as pl
from jax.experimental.pallas import tpu as pltpu
from jax.sharding import PartitionSpec as P

HEADS = 12
HEAD_DIM = 64


EPS = 1e-06


def shortened(shard):

    def short(part):
        return part.astype(jnp.bfloat16) if part.dtype == jnp.float32 else part

    return jax.tree.map(short, shard)


def rms_scale(values, gain):
    return values * lax.rsqrt(jnp.mean(values * values, axis=-1, keepdims=True) + EPS) * gain


def gated(gate, upper):
    return jax.nn.gelu(gate, approximate=True) * upper


def outer(left, right):
    return lax.dot_general(
        left, right, (((0,), (0,)), ((), ())), preferred_element_type=jnp.float32
    )


def transposed(left, weight):
    return lax.dot_general(
        left, weight, (((1,), (1,)), ((), ())), preferred_element_type=jnp.float32
    )


def matmul(left, right):
    return jnp.dot(left, right, preferred_element_type=jnp.float32)


def scores(query, key, scale):
    return jnp.einsum("sqhd,skhd->shqk", query, key, preferred_element_type=jnp.float32) * scale


def per_device(
    inputs,
    counts,
    norm_gain1,
    w_query,
    w_key,
    w_value,
    w_out,
    norm_gain2,
    w_gate,
    w_up,
    w_down,
    cotangent,
):
    micro, seqs, band_rows, width = inputs.shape
    bands = lax.axis_size("band")
    length = band_rows * bands
    rows = seqs * band_rows
    heads = HEADS
    head_dim = HEAD_DIM
    scale = 1.0 / math.sqrt(head_dim)
    key_place = jnp.arange(length, dtype=jnp.int32)
    params = (norm_gain1, w_query, w_key, w_value, w_out, norm_gain2, w_gate, w_up, w_down)
    totals = [jnp.zeros(p.shape, jnp.float32) for p in params]
    results = []
    input_grads = []
    for number in range(micro):
        hidden = inputs[number].astype(jnp.float32).reshape(rows, width)
        lengths = counts[number]
        normed = rms_scale(hidden, norm_gain1).astype(jnp.bfloat16)
        query = matmul(normed, w_query).astype(jnp.bfloat16)
        key_local = matmul(normed, w_key).astype(jnp.bfloat16)
        value_local = matmul(normed, w_value).astype(jnp.bfloat16)
        query_four = query.reshape(seqs, band_rows, heads, head_dim)
        key_three = key_local.reshape(seqs, band_rows, width)
        value_three = value_local.reshape(seqs, band_rows, width)
        key_all, value_all = (
            lax.all_gather(key_three, "band", axis=1, tiled=True),
            lax.all_gather(value_three, "band", axis=1, tiled=True),
        )
        live = key_place[None, :] < lengths[:, None]
        key_four = key_all.reshape(seqs, length, heads, head_dim)
        value_four = value_all.reshape(seqs, length, heads, head_dim)
        logits = jnp.where(live[:, None, None, :], scores(query_four, key_four, scale), -jnp.inf)
        top = jnp.max(logits, axis=-1, keepdims=True)
        expo = jnp.exp(logits - top)
        summed = jnp.sum(expo, axis=-1, keepdims=True)
        log_total = top + jnp.log(summed)
        prob = (expo / summed).astype(jnp.bfloat16)
        attended = jnp.einsum(
            "shqk,skhd->sqhd", prob, value_four, preferred_element_type=jnp.float32
        )
        attended = attended.reshape(rows, width).astype(jnp.bfloat16)
        second = hidden + matmul(attended, w_out)
        normed_two = rms_scale(second, norm_gain2).astype(jnp.bfloat16)
        gate = matmul(normed_two, w_gate)
        upper = matmul(normed_two, w_up)
        mixed = gated(gate, upper).astype(jnp.bfloat16)
        results.append(
            (second + matmul(mixed, w_down)).astype(jnp.bfloat16).reshape(seqs, band_rows, width)
        )
        grad_rows = cotangent[number].reshape(rows, width)
        totals[8] = totals[8] + outer(mixed, grad_rows)
        d_mixed = transposed(grad_rows, w_down)
        pull_gate = jax.vjp(gated, gate, upper)[1]
        d_gate, d_upper = pull_gate(d_mixed)
        d_gate = d_gate.astype(jnp.bfloat16)
        d_upper = d_upper.astype(jnp.bfloat16)
        totals[6] = totals[6] + outer(normed_two, d_gate)
        totals[7] = totals[7] + outer(normed_two, d_upper)
        d_normed_two = transposed(d_gate, w_gate) + transposed(d_upper, w_up)
        pull_two = jax.vjp(rms_scale, second, norm_gain2)[1]
        d_second_norm, d_gain_two = pull_two(d_normed_two)
        totals[5] = totals[5] + d_gain_two
        d_second = grad_rows.astype(jnp.float32) + d_second_norm
        d_branch = d_second.astype(jnp.bfloat16)
        totals[4] = totals[4] + outer(attended, d_branch)
        d_attended = transposed(d_branch, w_out).astype(jnp.bfloat16)
        d_att_four = d_attended.reshape(seqs, band_rows, heads, head_dim)
        key_all, value_all = (
            lax.all_gather(key_three, "band", axis=1, tiled=True),
            lax.all_gather(value_three, "band", axis=1, tiled=True),
        )
        key_four = key_all.reshape(seqs, length, heads, head_dim)
        value_four = value_all.reshape(seqs, length, heads, head_dim)
        logits = jnp.where(live[:, None, None, :], scores(query_four, key_four, scale), -jnp.inf)
        prob_full = jnp.exp(logits - log_total)
        prob = prob_full.astype(jnp.bfloat16)
        d_prob = jnp.einsum(
            "sqhd,skhd->shqk", d_att_four, value_four, preferred_element_type=jnp.float32
        )
        delta = jnp.sum(d_prob * prob_full, axis=-1, keepdims=True)
        d_logits = (prob_full * (d_prob - delta)).astype(jnp.bfloat16)
        d_query = (
            jnp.einsum("shqk,skhd->sqhd", d_logits, key_four, preferred_element_type=jnp.float32)
            * scale
        )
        d_query = d_query.reshape(rows, width).astype(jnp.bfloat16)
        d_key_all = (
            jnp.einsum("shqk,sqhd->skhd", d_logits, query_four, preferred_element_type=jnp.float32)
            * scale
        )
        d_value_all = jnp.einsum(
            "shqk,sqhd->skhd", prob, d_att_four, preferred_element_type=jnp.float32
        )
        d_key_three, d_value_three = (
            lax.psum_scatter(
                d_key_all.reshape(seqs, length, width).astype(jnp.bfloat16),
                "band",
                scatter_dimension=1,
                tiled=True,
            ).astype(jnp.float32),
            lax.psum_scatter(
                d_value_all.reshape(seqs, length, width).astype(jnp.bfloat16),
                "band",
                scatter_dimension=1,
                tiled=True,
            ).astype(jnp.float32),
        )
        d_key = d_key_three.reshape(rows, width).astype(jnp.bfloat16)
        d_value = d_value_three.reshape(rows, width).astype(jnp.bfloat16)
        totals[1] = totals[1] + outer(normed, d_query)
        totals[2] = totals[2] + outer(normed, d_key)
        totals[3] = totals[3] + outer(normed, d_value)
        d_normed = (
            transposed(d_query, w_query) + transposed(d_key, w_key) + transposed(d_value, w_value)
        )
        pull_one = jax.vjp(rms_scale, hidden, norm_gain1)[1]
        d_hidden_norm, d_gain_one = pull_one(d_normed)
        totals[0] = totals[0] + d_gain_one
        input_grads.append(
            (d_second + d_hidden_norm).astype(jnp.bfloat16).reshape(seqs, band_rows, width)
        )
    shares = jax.tree.map(
        lambda part: part.astype(jnp.float32),
        lax.psum_scatter(shortened(tuple(totals)), "band", scatter_dimension=0, tiled=True),
    )
    summed_shares = jax.tree.map(
        lambda part: part.astype(jnp.float32), lax.psum(shortened(shares), "items")
    )
    whole = jax.tree.map(
        lambda part, own: part.astype(own.dtype),
        lax.all_gather(shortened(summed_shares), "band", axis=0, tiled=True),
        summed_shares,
    )
    return (jnp.stack(results), jnp.stack(input_grads)) + tuple(whole)


MESH_ID = pl.DeviceIdType.MESH
NEG = -1e30
BF = jnp.bfloat16
F32 = jnp.float32


def place():
    item = lax.axis_index("items")
    band = lax.axis_index("band")
    return item, band // 4, band % 4


def flip(value):
    return value + 1 - 2 * (value % 2)


def far(value):
    return (value + 2) % 4


def greet(peers):
    barrier = pltpu.get_barrier_semaphore()
    for peer in peers:
        pl.semaphore_signal(barrier, inc=1, device_id=peer, device_id_type=MESH_ID)
    pl.semaphore_wait(barrier, len(peers))


def remote(src, dst, send, recv, peer):
    return pltpu.make_async_remote_copy(
        src_ref=src, dst_ref=dst, send_sem=send, recv_sem=recv, device_id=peer, device_id_type=MESH_ID
    )


def params(number, vmem=62):
    return pltpu.CompilerParams(
        collective_id=number, has_side_effects=True, vmem_limit_bytes=vmem << 20
    )


def whole(value, unit):
    return value if isinstance(value, int) else pl.multiple_of(value, unit)


def lanes_of(rows):
    return lax.broadcasted_iota(jnp.int32, (rows, 128), 1)


ANY = pl.BlockSpec(memory_space=pl.ANY)
VMEM = pl.BlockSpec(memory_space=pltpu.VMEM)
SMEM = pl.BlockSpec(memory_space=pltpu.SMEM)


class Moves:
    def __init__(self):
        self.remotes, self.locals, self.arrivals = [], [], []

    def start(self):
        for make in self.remotes + self.locals:
            make().start()

    def finish(self):
        for make in self.arrivals:
            make().wait_recv()
        for make in self.locals:
            make().wait()
        for make in self.remotes:
            make().wait_send()


def to_slots(item, z, g, src_ref, dst_ref, send, recv, own_sem):
    zs = (z, flip(z), far(z), far(flip(z)))
    p, r = z // 2, z % 2
    moves = Moves()

    def out(n):
        if n < 3:
            s = zs[n + 1]
            src, where = src_ref.at[3 * (s // 2) + 2 * (s % 2)], z
        else:
            s = far(z)
            src, where = src_ref.at[3 * (1 - p) + 1], 4 + p
        return remote(src, dst_ref.at[where], send.at[n], recv.at[where], (item, s * 4 + g))

    def came(where):
        block = dst_ref.at[where]
        return remote(block, block, send.at[0], recv.at[where], (item, far(z) * 4 + g))

    moves.remotes = [lambda n=n: out(n) for n in range(4)]
    moves.locals = [
        lambda: pltpu.make_async_copy(src_ref.at[3 * p + 2 * r], dst_ref.at[z], own_sem.at[0]),
        lambda: pltpu.make_async_copy(src_ref.at[3 * p + 1], dst_ref.at[4 + p], own_sem.at[1]),
    ]
    moves.arrivals = [lambda w=w: came(w) for w in zs[1:] + (4 + (1 - p),)]
    return moves


def from_slots(item, z, g, src_ref, dst_ref, send, recv, own_sem):
    zs = (z, flip(z), far(z), far(flip(z)))
    p, r = z // 2, z % 2
    mine = 3 * p + 2 * r
    moves = Moves()

    def out(n):
        s = zs[n + 1] if n < 3 else far(z)
        src, where = (src_ref.at[s], mine) if n < 3 else (src_ref.at[4 + (1 - p)], 3 * p + 1)
        return remote(src, dst_ref.at[where], send.at[n], recv.at[where], (item, s * 4 + g))

    def came(where):
        block = dst_ref.at[where]
        return remote(block, block, send.at[0], recv.at[where], (item, far(z) * 4 + g))

    moves.remotes = [lambda n=n: out(n) for n in range(4)]
    moves.locals = [
        lambda: pltpu.make_async_copy(src_ref.at[z], dst_ref.at[mine], own_sem.at[0]),
        lambda: pltpu.make_async_copy(src_ref.at[4 + p], dst_ref.at[3 * p + 1], own_sem.at[1]),
    ]
    theirs = [3 * (s // 2) + 2 * (s % 2) for s in zs[1:]] + [3 * (1 - p) + 1]
    moves.arrivals = [lambda w=w: came(w) for w in theirs]
    return moves


def z_peers(item, z, g):
    return [(item, s * 4 + g) for s in (flip(z), far(z), far(flip(z)))]


def g_peers(item, z, g):
    return [(item, z * 4 + h) for h in (flip(g), far(g), far(flip(g)))]


def swap_heads(item, z, g, src_ref, dst_ref, send, recv, own_sem):
    moves = Moves()

    def out(n, h):
        return remote(src_ref.at[h], dst_ref.at[g], send.at[n], recv.at[g], (item, z * 4 + h))

    def came(h):
        return remote(dst_ref.at[h], dst_ref.at[h], send.at[0], recv.at[h], (item, z * 4 + h))

    moves.remotes = [lambda n=n, h=h: out(n, h) for n, h in enumerate((far(g), far(flip(g)), flip(g)))]
    moves.locals = [lambda: pltpu.make_async_copy(src_ref.at[g], dst_ref.at[g], own_sem)]
    moves.arrivals = [lambda h=h: came(h) for h in (flip(g), far(g), far(flip(g)))]
    return moves


def nt(left, right):
    return lax.dot_general(left, right, (((1,), (1,)), ((), ())), preferred_element_type=F32)


def front_kernel(
    x_ref, cot_ref, count_ref, gain_ref, wq_ref, wk_ref, wv_ref,
    orecv_ref, dy_ref, hid_ref, q_out, k_out, v_out, kt_out, o01_out, o2_out, xn_out, wc_out,
    xall_ref, win_ref, wc_ref, xn_ref, q_ref, k_ref, v_ref, kt_ref, o01_ref, o2_ref, osend_ref,
    z_send, f_send, g_send, recv, own_sem, win_sem, o_send, o_recv, o_own, cot_send, cot_recv, cot_own,
    half_sem, tile_sem, last_sem,
):
    item, z, g = place()
    p, r = z // 2, z % 2
    gc, gx = flip(g), far(g)
    gcx = far(gc)
    zs = (z, flip(z), far(z), far(flip(z)))
    core, across = (item, z * 4 + gc), (item, z * 4 + gx)
    lane = lanes_of(256)
    low = lane < 64
    greet(g_peers(item, z, g) + z_peers(item, z, g))

    def items_of(s):
        return (3 * (s // 2) + 2 * (s % 2), 3 * (s // 2) + 1)

    started = []

    def go(make):
        make().start()
        started.append(make)

    def forward(n, ab):
        def make(k, peer):
            where = zs[n] * 4 + g
            src = x_ref.at[items_of(z)[ab]] if n == 0 else xall_ref.at[ab, where]
            return remote(src, xall_ref.at[ab, where], f_send.at[n, ab, k], recv.at[ab, where], peer)

        go(lambda: make(0, across))
        go(lambda: make(1, core))

    def arrived(ab, where):
        block = xall_ref.at[ab, where]
        remote(block, block, z_send.at[0, 0], recv.at[ab, where], core).wait_recv()

    def send_z(ab):
        for n, s in enumerate(zs[1:]):
            go(
                lambda n=n, s=s: remote(
                    x_ref.at[items_of(s)[ab]],
                    xall_ref.at[ab, z * 4 + g],
                    z_send.at[n, ab],
                    recv.at[ab, z * 4 + g],
                    (item, s * 4 + g),
                )
            )

    send_z(0)
    forward(0, 0)
    send_z(1)
    forward(0, 1)
    cut = pl.ds(pl.multiple_of(g * 3 // 2 * 128, 128), 256)
    windows = []
    for n, ref in enumerate((wq_ref, wk_ref, wv_ref)):
        windows.append(pltpu.make_async_copy(ref.at[:, cut], win_ref.at[n], win_sem.at[n]))

    def own_copy(ab):
        return pltpu.make_async_copy(x_ref.at[items_of(z)[ab]], xall_ref.at[ab, z * 4 + g], own_sem.at[ab])

    for copy in windows + [own_copy(0), own_copy(1)]:
        copy.start()
    for copy in windows:
        copy.wait()
    odd = g % 2 == 1

    @pl.loop(0, 3)
    def _(i):
        rows = pl.ds(pl.multiple_of(i * 256, 256), 256)
        firsts, lasts = [], []
        for n in range(3):
            left = win_ref[n, rows, 0:128].astype(F32)
            right = win_ref[n, rows, 128:256].astype(F32)
            crossed = pltpu.roll(jnp.where(low, right, left), 64, 1)
            firsts.append(jnp.where(odd, crossed, left))
            lasts.append(jnp.where(odd, pltpu.roll(right, 64, 1), right))
        for n in range(3):
            wc_ref[rows, n * 128 : n * 128 + 128] = firsts[n].astype(BF)
        wc_ref[rows, 384:512] = jnp.where(low, lasts[1], pltpu.roll(lasts[2], 64, 1)).astype(BF)
        wc_ref[rows, 512:640] = jnp.where(low, lasts[0], 0.0).astype(BF)

    def forward_z(ab, n):
        arrived(ab, zs[n] * 4 + g)
        forward(n, ab)

    def forward_x(ab, n):
        def make():
            where = zs[n] * 4 + gx
            block = xall_ref.at[ab, where]
            return remote(block, block, g_send.at[n, ab], recv.at[ab, where], core)

        arrived(ab, zs[n] * 4 + gx)
        go(make)

    def project(ab, n):
        zz = zs[n]
        if n == 0:
            own_copy(ab).wait()
        for h in (gc, gcx):
            arrived(ab, zz * 4 + h)
        rows = pl.ds(pl.multiple_of(ab * 1024 + zz * 256, 256), 256)
        h = xall_ref[ab, pl.ds(zz * 4, 4)].reshape(256, 768).astype(F32)
        inv = lax.rsqrt(jnp.mean(h * h, axis=-1, keepdims=True) + EPS)
        xn = (h * inv * gain_ref[...].reshape(1, 768)).astype(BF)
        xn_ref[rows, :] = xn
        y = matmul(xn, wc_ref[:, 128:512])
        count = count_ref[p, (2 * r if ab == 0 else 1)]
        at = lax.broadcasted_iota(jnp.int32, (256, 128), 0) + zz * 256
        bias = jnp.where(at < count, 0.0, NEG)
        one = jnp.where((lane % 64) < 4, 1.0, 0.0)
        k_aug = jnp.where(lane % 64 == 0, bias, one)
        k01, v01, kv2 = y[:, :128], y[:, 128:256], y[:, 256:]
        keys = (jnp.where(low, k01, k_aug), jnp.where(low, k_aug, k01), jnp.where(low, kv2, k_aug))
        cols = pl.ds(pl.multiple_of(zz * 256, 256), 256)
        for head in range(3):
            key = keys[head].astype(BF)
            k_ref[head, rows, :] = key
            kt_ref[head, ab, :, cols] = key.T
        v_ref[0, rows, :] = jnp.where(low, v01, one).astype(BF)
        v_ref[1, rows, :] = jnp.where(low, one, v01).astype(BF)
        v_ref[2, rows, :] = jnp.where(low, one, kv2).astype(BF)

    def half_copy(ab, n):
        rows = pl.ds(ab * 1024, 1024)
        a, b = (
            (k_ref.at[:, rows], k_out.at[:, rows]), (v_ref.at[:, rows], v_out.at[:, rows]),
            (kt_ref.at[:, ab], kt_out.at[:, ab]), (xn_ref.at[rows], xn_out.at[rows]),
        )[n]
        return pltpu.make_async_copy(a, b, half_sem.at[ab, n])

    def tile(t):
        off = jnp.where(t < 4, t, 4 + r + 2 * (t - 4)) * 256
        xq = xn_ref[pl.ds(pl.multiple_of(off, 256), 256), :]
        q01 = matmul(xq, wc_ref[:, 0:128]).astype(BF).astype(F32) * 0.125
        q2 = matmul(xq, wc_ref[:, 512:640]).astype(BF).astype(F32) * 0.125
        flag = jnp.where(lane % 64 == 0, 1.0, 0.0)
        qs = (jnp.where(low, q01, flag), jnp.where(low, flag, q01), jnp.where(low, q2, flag))
        at = pl.ds(pl.multiple_of(t * 256, 256), 256)
        ab = t // 4
        keys = pl.ds(pl.multiple_of(ab * 1024, 1024), 1024)
        outs = []
        for head in range(3):
            s = matmul(qs[head].astype(BF), kt_ref[head, ab])
            top = jnp.max(s, axis=1, keepdims=True)
            e = jnp.exp(s - top).astype(BF)
            o = matmul(e, v_ref[head, keys, :])
            total = o[:, 64:65] if head == 0 else o[:, 0:1]
            outs.append(o / total)
            lse = -(top + jnp.log(total))
            hi = lse.astype(BF).astype(F32)
            mid = (lse - hi).astype(BF).astype(F32)
            lo = lse - hi - mid
            part = lane % 64
            aug = jnp.where(part == 1, hi, jnp.where(part == 2, mid, jnp.where(part == 3, lo, flag)))
            data = low if head != 1 else jnp.logical_not(low)
            q_ref[head, at, :] = jnp.where(data, qs[head], aug).astype(BF)
        o01 = jnp.where(low, outs[0], outs[1])
        o2 = outs[2]
        o01_ref[at, :] = o01
        o2_ref[at, :] = o2
        for h in range(4):
            osend_ref[h, t, 0:64, :] = o01[h * 64 : h * 64 + 64].astype(BF)
            first = o2[h * 64 : h * 64 + 32]
            second = o2[h * 64 + 32 : h * 64 + 64]
            folded = jnp.where(low[:32], pltpu.roll(first, 64, 1), second)
            osend_ref[h, t, 64:96, :] = folded.astype(BF)

    saved = []

    def keep(makes):
        for make in makes:
            make().start()
            saved.append(make)

    def o_copy(t, k):
        h = (gx, gcx, gc)[k]
        return remote(
            osend_ref.at[h, t], orecv_ref.at[g, t], o_send.at[t, k], o_recv.at[g, t], (item, z * 4 + h)
        )

    def tile_copy(t, k):
        rows = pl.ds(whole(t * 256, 256), 256)
        a, b = (
            (q_ref.at[:, rows], q_out.at[:, rows]), (o01_ref.at[rows], o01_out.at[rows]),
            (o2_ref.at[rows], o2_out.at[rows]), (osend_ref.at[g, t], orecv_ref.at[g, t]),
        )[k]
        return pltpu.make_async_copy(a, b, tile_sem.at[t, k])

    def block_copy(j):
        src = xall_ref.at[0, j * 4 + g] if j < 4 else xall_ref.at[1, (r + 2 * (j - 4)) * 4 + g]
        return pltpu.make_async_copy(src, hid_ref.at[j], last_sem.at[j])

    moved = to_slots(item, z, g, cot_ref, dy_ref, cot_send, cot_recv, cot_own)
    keep([lambda: pltpu.make_async_copy(wc_ref, wc_out, last_sem.at[6])])
    forward_z(0, 1)
    forward_x(0, 0)
    project(0, 0)
    forward_z(0, 2)
    forward_x(0, 1)
    project(0, 1)
    forward_z(0, 3)
    forward_z(1, 1)
    forward_x(0, 2)
    project(0, 2)
    forward_x(0, 3)
    forward_x(1, 0)
    project(0, 3)
    keep([lambda n=n: half_copy(0, n) for n in range(4)])
    forward_z(1, 2)

    @pl.loop(0, 6)
    def _(t):
        tile(t)
        for k in range(3):
            o_copy(t, k).start()
        for k in range(4):
            tile_copy(t, k).start()

        @pl.when(t == 0)
        def _():
            forward_z(1, 3)
            moved.start()
            forward_x(1, 1)

        @pl.when(t == 1)
        def _():
            project(1, 0)
            project(1, 1)

        @pl.when(t == 2)
        def _():
            forward_x(1, 2)
            project(1, 2)

        @pl.when(t == 3)
        def _():
            forward_x(1, 3)
            project(1, 3)
            keep([lambda n=n: half_copy(1, n) for n in range(4)])
            keep([lambda j=j: block_copy(j) for j in range(6)])

    for t in range(6):
        for h in (gx, gcx, gc):
            block = orecv_ref.at[h, t]
            remote(block, block, o_send.at[0, 0], o_recv.at[h, t], core).wait_recv()
        for k in range(4):
            tile_copy(t, k).wait()
        for k in range(3):
            o_copy(t, k).wait_send()
    moved.finish()
    for make in saved:
        make().wait()
    for make in started:
        make().wait_send()


def front(x6, cot6, counts, gain, wq, wk, wv):
    s = jax.ShapeDtypeStruct
    dma = pltpu.SemaphoreType.DMA
    v = pltpu.VMEM
    _, rows, width = x6.shape
    kept = (
        s((3, 1536, 128), BF), s((3, 2048, 128), BF), s((3, 2048, 128), BF), s((3, 2, 128, 1024), BF),
        s((1536, 128), F32), s((1536, 128), F32), s((2048, width), BF), s((width, 640), BF),
    )
    q, k, vv, kt, o01, o2, xn, wc = [v(a.shape, a.dtype) for a in kept]
    heads = (4, 6, 96, 128)
    return pl.pallas_call(
        front_kernel,
        out_shape=(s(heads, BF), s(x6.shape, BF), s(x6.shape, BF)) + kept,
        in_specs=[ANY, ANY, SMEM, VMEM, ANY, ANY, ANY],
        out_specs=(ANY,) * 11,
        scratch_shapes=[
            v((2, 16, rows, width), BF), v((3, width, 256), BF), wc, xn, q, k, vv, kt, o01, o2, v(heads, BF),
            dma((3, 2)), dma((4, 2, 2)), dma((4, 2)), dma((2, 16)), dma((2,)), dma((3,)),
            dma((6, 3)), dma((4, 6)), dma((1,)), dma((4,)), dma((6,)), dma((2,)), dma((2, 4)), dma((6, 4)), dma((7,)),
        ],
        compiler_params=params(1),
        name="front",
    )(x6, cot6, counts, gain, wq, wk, wv)


GELU_A = 0.044715
GELU_C = math.sqrt(2.0 / math.pi)


def widen_kernel(
    qkv_ref, so_ref, sg_ref, su_ref, sd_ref, gains_ref, first_ref, second_ref,
    q_ref, k_ref, v_ref, o_ref, g_ref, u_ref, d_ref, gain1_ref, gain2_ref, first_out, second_out,
):
    first_out[...] = first_ref[...]
    second_out[...] = second_ref[...]

    @pl.when(pl.program_id(0) == 0)
    def _():
        gain1_ref[...] = gains_ref[0, :]
        gain2_ref[...] = gains_ref[1, :]

    low = lanes_of(qkv_ref.shape[1]) < 64

    def swap(v):
        return pltpu.roll(v, 64, 1)

    for out, first, last, high in ((q_ref, 0, 512, False), (k_ref, 128, 384, False), (v_ref, 256, 384, True)):
        a = [qkv_ref[n, :, first : first + 128].astype(F32) for n in range(4)]
        b = [qkv_ref[n, :, last : last + 128].astype(F32) for n in range(4)]
        low_b = [swap(x) if high else x for x in b]
        high_b = [x if high else swap(x) for x in b]
        tiles = (
            a[0], jnp.where(low, low_b[0], swap(a[1])), jnp.where(low, swap(a[1]), high_b[1]),
            a[2], jnp.where(low, low_b[2], swap(a[3])), jnp.where(low, swap(a[3]), high_b[3]),
        )
        for n, tile in enumerate(tiles):
            out[:, n * 128 : n * 128 + 128] = tile
    o_ref[...] = so_ref[...].astype(F32)
    g_ref[...] = sg_ref[...].astype(F32)
    u_ref[...] = su_ref[...].astype(F32)
    d_ref[...] = sd_ref[...].astype(F32)

def widen(qkv, s_out, s_gate, s_up, s_down, gains, first, second):
    s = jax.ShapeDtypeStruct
    steps = 4

    def spec(a):
        if len(a.shape) == 3:
            return pl.BlockSpec((a.shape[0], a.shape[1] // steps, a.shape[2]), lambda i: (0, i, 0))
        return pl.BlockSpec((a.shape[0] // steps, a.shape[1]), lambda i: (i, 0))

    outs = tuple(s(a.shape, F32) for a in (s_out, s_out, s_out, s_out, s_gate, s_up, s_down))
    ins = (qkv, s_out, s_gate, s_up, s_down)
    width = gains.shape[1]
    vector = pl.BlockSpec((width,), lambda i: (0,))
    moved = (s(first.shape, first.dtype), s(second.shape, second.dtype))
    return pl.pallas_call(
        widen_kernel,
        grid=(steps,),
        out_shape=outs + (s((width,), F32),) * 2 + moved,
        in_specs=[spec(a) for a in ins] + [pl.BlockSpec(gains.shape, lambda i: (0, 0)), spec(first), spec(second)],
        out_specs=tuple(spec(a) for a in outs) + (vector, vector, spec(first), spec(second)),
        compiler_params=pltpu.CompilerParams(vmem_limit_bytes=62 << 20),
        name="widen",
    )(*ins, gains, first, second)


class Stream:
    def __init__(self, spare, res, acc, first, rest, sems, order, coords, core, cut):
        self.spare, self.res, self.acc, self.first, self.rest = spare, res, acc, first, rest
        self.send, self.recv, self.own, self.back, self.got, self.fwd, self.fgot = sems
        row, col, half = cut
        self.rows, self.wide = acc.shape
        self.row = row
        self.order = [coords[name] for name in order]
        self.deep = len(order)
        bit, self.peer = core
        if half:
            self.mine = pl.ds(pl.multiple_of(bit * half + col, 128), self.wide)
            self.other = pl.ds(pl.multiple_of((1 - bit) * half + col, 128), self.wide)
        else:
            self.mine = pl.ds(col, self.wide)
        self.base, self.size = [0], [self.rows]
        for bit, _ in self.order:
            self.size.append(self.size[-1] // 2)
            self.base.append(self.base[-1] + bit * self.size[-1])

    def part(self, base, size):
        return pl.ds(whole(base, 16), size)

    def at(self, base, size, mine=True):
        cols = self.mine if mine else self.other
        return self.res.at[pl.ds(whole(self.row + base, 16), size), cols]

    def sibling(self, k):
        return self.base[k - 1] + (1 - self.order[k - 1][0]) * self.size[k]

    def own_out(self):
        here = self.base[self.deep], self.size[self.deep]
        return pltpu.make_async_copy(self.acc.at[self.part(*here)], self.at(*here), self.own.at[1])

    def c_push(self, k):
        if k == 0:
            return remote(self.spare, self.first, self.send.at[0], self.recv.at[0], self.peer)
        return remote(
            self.acc.at[self.part(self.sibling(k), self.size[k])],
            self.rest.at[pl.ds(self.rows - 2 * self.size[k], self.size[k])],
            self.send.at[k],
            self.recv.at[k],
            self.order[k - 1][1],
        )

    def c_back(self, k):
        here = self.base[k], self.size[k]
        src = self.acc.at[self.part(*here)] if k == self.deep else self.at(*here)
        return remote(
            src, self.at(*here), self.back.at[k - 1], self.got.at[k - 1], self.order[k - 1][1]
        )

    def c_forward(self, k):
        if k == 0:
            here = self.base[self.deep], self.size[self.deep]
            src = self.acc.at[self.part(*here)]
        else:
            here = self.sibling(k), self.size[k]
            src = self.at(*here)
        return remote(src, self.at(*here), self.fwd.at[k], self.fgot.at[k], self.peer)

    def open(self):
        self.c_push(0).start()

    def fold(self, k):
        self.c_push(k).wait_recv()
        base, size = self.base[k], self.size[k]
        other, at = (self.first, 0) if k == 0 else (self.rest, self.rows - 2 * size)
        step = 64 if size % 64 == 0 else 48

        @pl.loop(0, size // step)
        def _(n):
            rows = self.part(base + n * step, step)
            more = other[pl.ds(pl.multiple_of(at + n * step, 16), step), :]
            self.acc[rows, :] = (self.acc[rows, :].astype(F32) + more.astype(F32)).astype(BF)

        if k < self.deep:
            self.c_push(k + 1).start()
        else:
            self.c_back(k).start()
            self.c_forward(0).start()
            self.own_out().start()

    def collect(self, k):
        here = self.sibling(k), self.size[k]
        block = self.at(*here)
        remote(block, block, self.back.at[k - 1], self.got.at[k - 1], self.peer).wait_recv()
        if k == self.deep:
            self.own_out().wait()
        if k > 1:
            self.c_back(k - 1).start()
        self.c_forward(k).start()

    def close(self):
        for k in range(self.deep + 1):
            if k == 0:
                here = self.base[self.deep], self.size[self.deep]
            else:
                here = self.sibling(k), self.size[k]
            block = self.at(*here, mine=False)
            remote(block, block, self.fwd.at[k], self.fgot.at[k], self.peer).wait_recv()
            self.c_push(k).wait_send()
            self.c_forward(k).wait_send()
            if k > 0:
                self.c_back(k).wait_send()


class Grouped(Stream):
    def __init__(self, res, acc, rest, sems, order, coords, core, cut, group, across):
        super().__init__(None, res, acc, None, rest, sems, order, coords, core, cut)
        self.group, self.gx, self.across = group, far(group), across

    def at(self, base, size, n=0):
        h = (self.group, self.gx, flip(self.group), far(flip(self.group)))[n]
        return self.res.at[h, self.part(base, size), self.mine]

    def c_across(self):
        here = self.base[self.deep], self.size[self.deep]
        return remote(
            self.acc.at[self.part(*here)],
            self.at(*here),
            self.back.at[self.deep, 0],
            self.got.at[self.deep, 0],
            self.across,
        )

    def c_back(self, k, n):
        here = self.base[k], self.size[k]
        own = k == self.deep and n == 0
        src = self.acc.at[self.part(*here)] if own else self.at(*here, n)
        return remote(
            src, self.at(*here, n), self.back.at[k - 1, n], self.got.at[k - 1, n], self.order[k - 1][1]
        )

    def c_forward(self, k, n):
        if k == 0:
            here = self.base[self.deep], self.size[self.deep]
            src = self.acc.at[self.part(*here)] if n == 0 else self.at(*here, n)
        else:
            here = self.sibling(k), self.size[k]
            src = self.at(*here, n)
        return remote(src, self.at(*here, n), self.fwd.at[k, n], self.fgot.at[k, n], self.peer)

    def fold(self, k):
        if k == 0:
            self.c_push(1).start()
            return
        if k < self.deep:
            super().fold(k)
            return
        self.c_push(k).wait_recv()
        base, size = self.base[k], self.size[k]
        rows = self.part(base, size)
        more = self.rest[pl.ds(self.rows - 2 * size, size), :]
        self.acc[rows, :] = (self.acc[rows, :].astype(F32) + more.astype(F32)).astype(BF)
        self.c_across().start()
        self.c_back(k, 0).start()
        self.c_forward(0, 0).start()
        self.own_out().start()

    def extend(self):
        self.c_across().wait_recv()
        self.c_back(self.deep, 1).start()
        self.c_forward(0, 1).start()

    def collect(self, k):
        here = self.sibling(k), self.size[k]
        if k == self.deep:
            self.own_out().wait()
        for n in range(2):
            block = self.at(*here, n)
            remote(block, block, self.back.at[k - 1, n], self.got.at[k - 1, n], self.peer).wait_recv()
            if k > 1:
                if n == 1:
                    self.c_back(k - 1, 0).start()
                    self.c_back(k - 1, 1).start()
            self.c_forward(k, n).start()

    def close(self):
        self.c_across().wait_send()
        for k in range(self.deep + 1):
            if k == 0:
                here = self.base[self.deep], self.size[self.deep]
            else:
                here = self.sibling(k), self.size[k]
                self.c_push(k).wait_send()
            for n in range(2):
                block = self.at(*here, 2 + n)
                remote(block, block, self.fwd.at[k, n], self.fgot.at[k, n], self.peer).wait_recv()
                self.c_forward(k, n).wait_send()
                if k > 0:
                    self.c_back(k, n).wait_send()


PIECES = {
    "D1": (2, 1, 1024, 0, 1024, 384, 384, ("zl", "x", "y", "zh")),
    "U1": (1, 1, 0, 1024, 768, 512, 512, ("zl", "x", "y", "zh")),
    "G0": (0, 0, 0, 0, 768, 512, 512, ("x", "y", "zh", "zl")),
    "G1": (0, 1, 0, 1024, 768, 512, 512, ("x", "y", "zh", "zl")),
    "O": (3, 0, 0, 0, 768, 384, 384, ("x", "zl", "y", "zh")),
    "U0": (1, 0, 0, 0, 768, 512, 512, ("y", "x", "zl", "zh")),
    "D0": (2, 0, 0, 0, 1024, 384, 384, ("y", "x", "zl", "zh")),
}
GROUPS = {
    "qA": (0, 256, ("y", "zh", "zl")),
    "qB": (256, 384, ("y", "zl", "zh")),
}
PLAN = (
    "ff", "ff", "open.G0", "open.U0", "open.D0", "ff", "ff", "fG0.0", "fU0.0", "open.D1",
    "open.U1", "open.G1", "fD0.0", "res", "open.O", "fD1.0", "fU1.0", "fG1.0", "fO.0", "fG0.1",
    "fU0.1", "swap", "tile", "tile", "fD0.1", "tile", "fD1.1", "fG0.2", "tile", "fG1.1",
    "tile", "tile", "fO.1", "fU1.1", "dxn", "fG1.2", "fU0.2", "gw", "end", "xsB",
    "fO.2", "fG0.3", "xsA", "fqB.0", "fD0.2", "tB", "fqA.0", "tA", "fG1.3", "fU0.3",
    "fD1.2", "fG0.4", "fO.3", "fD0.3", "fU1.2", "gG0.4", "fqB.1", "fO.4", "fD0.4", "fqA.1",
    "zB", "fD1.3", "gG0.3", "fU0.4", "fqB.2", "fU1.3", "gO.4", "gD0.4", "gG0.2", "nA",
    "gO.3", "fqA.2", "nB", "gain.0", "gain.1", "gU0.4", "fD1.4", "gG0.1", "gain.2", "fqB.3",
    "gain.3", "fU1.4", "gD0.3", "eqB", "gD0.2", "fG1.4", "gO.2", "fqA.3", "gU0.3", "gD0.1",
    "gain.4", "gO.1", "gD1.4", "eqA", "gU1.4", "gD1.3", "gU0.2", "gG1.4", "gU1.3", "gain.5",
    "gqB.3", "gqA.3", "gD1.2", "gG1.3", "gU1.2", "gU0.1", "gqB.2", "gG1.2", "gqA.2", "gD1.1",
    "gG1.1", "gqB.1", "gU1.1", "gqA.1",
)


def back_kernel(*refs):
    take = iter(refs)

    def some(n):
        return [next(take) for _ in range(n)]

    dense_hbm = some(7)
    gain2_ref, gain_ref = some(2)
    loads_hbm = some(8)
    out_ref, res_out_ref = some(2)
    outs = some(5)
    (gains_out,) = some(1)
    h_ref, dh_ref, res_ref, dsend_ref, dgain2_ref = some(5)
    both = some(4)
    dense_sem, w_sem, load_sem = some(3)
    (do_ref, p_ref) = some(2)
    (rc_ref, sx_ref, rx_ref, t_ref, zb_ref, rz_ref, ig_ref, dgain_ref) = some(8)
    (c_send, c_recv, x_send, x_recv, z_send, z_recv) = some(6)
    (rs_send, rs_recv, rs_own, h_send, h_recv, h_own, hs, hr, ho) = some(9)
    item, z, g = place()
    gc, gx = flip(g), far(g)
    gcx = far(gc)
    p, r = z // 2, z % 2
    side = g % 2
    coords = {
        "x": (g // 2, (item, z * 4 + gx)),
        "y": (item, (1 - item, z * 4 + g)),
        "zl": (z % 2, (item, flip(z) * 4 + g)),
        "zh": (z // 2, (item, far(z) * 4 + g)),
    }
    across, pair = coords["x"][1], coords["zl"][1]
    core = (item, z * 4 + gc)
    zs = (z, flip(z), far(z), far(flip(z)))
    streams = {}
    for name, (n, m, row, col, _, _, half, order) in PIECES.items():
        first, rest = some(2)
        streams[name] = Stream(
            both[n].at[m, 1 - side], outs[n], both[n].at[m, side], first, rest, some(7), order, coords,
            (side, core), (row, col, half),
        )
    (gw_ref,) = some(1)
    for name, (col, wide, order) in GROUPS.items():
        (rest,) = some(1)
        acc = gw_ref.at[:, pl.ds(col, wide)]
        streams[name] = Grouped(
            outs[4], acc, rest, some(7), order, coords, (side, core), (0, col, 0), g, across
        )
    buf, got, gain_send, gain_recv = some(4)

    greet(g_peers(item, z, g) + z_peers(item, z, g) + [coords["y"][1]])
    swapped = swap_heads(item, z, g, dsend_ref, do_ref, hs, hr, ho.at[0])
    lane = lanes_of(256)
    low = lane < 64
    part = lane % 64

    def dense(emit, wo_ref, wg_ref, wu_ref, wd_ref, o_ref, dy_ref, att_ref, sec_ref, xn_ref, xt_ref, dxn_ref):
        o_hbm, h_hbm, dy_hbm, wo_hbm, wg_hbm, wu_hbm, wd_hbm = dense_hbm
        size = 512
        pairs = ((o_hbm, o_ref), (h_hbm, h_ref), (wo_hbm, wo_ref), (dy_hbm, dy_ref))
        copies = [pltpu.make_async_copy(a, b, dense_sem.at[n]) for n, (a, b) in enumerate(pairs)]
        for copy in copies:
            copy.start()

        def load(c, n):
            cut = pl.ds(whole(c * size, size), size)
            a, b = ((wg_hbm, wg_ref), (wu_hbm, wu_ref), (wd_hbm, wd_ref))[n]
            a, b = (a.at[:, cut], b.at[:, cut]) if n < 2 else (a.at[cut, :], b.at[cut, :])
            return pltpu.make_async_copy(a, b, w_sem.at[n, c])

        for c in range(4):
            for n in range(3):
                load(c, n).start()
        low = lanes_of(384) < 64

        def swap(v):
            return pltpu.roll(v, 64, 1)

        copies[0].wait()
        pairs = [o_ref[n, :, 0:64, :].astype(F32).reshape(384, 128) for n in range(4)]

        def unfold(n, high):
            f = o_ref[n, :, 64:96, :].astype(F32)
            s = swap(f.reshape(192, 128)).reshape(6, 32, 128)
            two = (s, f) if high else (f, s)
            return jnp.concatenate(two, axis=1).reshape(384, 128)

        tiles = (
            pairs[0],
            jnp.where(low, unfold(0, False), swap(pairs[1])),
            jnp.where(low, swap(pairs[1]), unfold(1, True)),
            pairs[2],
            jnp.where(low, unfold(2, False), swap(pairs[3])),
            jnp.where(low, swap(pairs[3]), unfold(3, True)),
        )
        for n, v in enumerate(tiles):
            att_ref[:, n * 128 : n * 128 + 128] = v.astype(BF)
        for copy in copies[1:]:
            copy.wait()
        second = h_ref[...].reshape(384, 768).astype(F32) + matmul(att_ref[...], wo_ref[...])
        sec_ref[...] = second
        dh_ref[...] = second.reshape(6, 64, 768)
        inv = lax.rsqrt(jnp.mean(second * second, axis=-1, keepdims=True) + EPS)
        xn_ref[...] = (second * inv * gain2_ref[...].reshape(1, 768)).astype(BF)
        xt_ref[...] = xn_ref[...].T
        dxn_ref[...] = jnp.zeros_like(dxn_ref)

        def chunk(c):
            cut = pl.ds(pl.multiple_of(c * size, size), size)
            for n in range(3):
                load(c, n).wait()
            dy = dy_ref[...].reshape(384, 768)
            gate = matmul(xn_ref[...], wg_ref[:, cut])
            upper = matmul(xn_ref[...], wu_ref[:, cut])
            d_mixed = nt(dy, wd_ref[cut, :])
            square = gate * gate
            tan = jnp.tanh(GELU_C * (gate + GELU_A * square * gate))
            half = 0.5 * (1.0 + tan)
            act = gate * half
            slope = half + 0.5 * gate * (1.0 - tan * tan) * (GELU_C * (1.0 + 3.0 * GELU_A * square))
            mixed = (act * upper).astype(BF)
            d_gate = (d_mixed * upper * slope).astype(BF)
            d_upper = (d_mixed * act).astype(BF)
            m, i = c // 2, c % 2
            both[0][m, i] = matmul(xt_ref[...], d_gate).astype(BF)
            both[1][m, i] = matmul(xt_ref[...], d_upper).astype(BF)
            down = outer(mixed, dy).astype(BF)
            rows = pl.ds(pl.multiple_of(i * size, size), size)
            both[2][m, 0, rows, :] = down[:, :384]
            both[2][m, 1, rows, :] = down[:, 384:]
            sec_ref[...] += matmul(mixed, wd_ref[cut, :])
            dxn_ref[...] += nt(d_gate, wg_ref[:, cut]) + nt(d_upper, wu_ref[:, cut])

        run_loop("ff", 4, chunk, emit)
        res_ref[...] = sec_ref[...].astype(BF).reshape(6, 64, 768)
        second = dh_ref[...].reshape(384, 768)
        inv = lax.rsqrt(jnp.mean(second * second, axis=-1, keepdims=True) + EPS)
        d_xn = dxn_ref[...]
        dgain2_ref[...] = jnp.sum(d_xn * second * inv, axis=0, keepdims=True)
        dyg = d_xn * gain2_ref[...].reshape(1, 768)
        dot = jnp.mean(dyg * second, axis=-1, keepdims=True)
        dy = dy_ref[...].reshape(384, 768)
        d_second = dy.astype(F32) + inv * dyg - second * (inv * inv * inv * dot)
        dh_ref[...] = d_second.reshape(6, 64, 768)
        d_branch = d_second.astype(BF)
        d_att = nt(d_branch, wo_ref[...]).astype(BF).astype(F32)
        d = [d_att[:, n * 128 : n * 128 + 128] for n in range(6)]
        firsts = (d[0], swap(jnp.where(low, d[2], d[1])), d[3], swap(jnp.where(low, d[5], d[4])))
        lasts = ((d[1], False), (d[2], True), (d[4], False), (d[5], True))
        low3 = lax.broadcasted_iota(jnp.int32, (6, 32, 128), 2) < 64
        for n in range(4):
            dsend_ref[n, :, 0:64, :] = firsts[n].astype(BF).reshape(6, 64, 128)
            v, high = lasts[n]
            v3, s3 = v.reshape(6, 64, 128), swap(v).reshape(6, 64, 128)
            top, bottom = v3[:, :32], v3[:, 32:]
            top_s, bottom_s = s3[:, :32], s3[:, 32:]
            f = jnp.where(low3, top_s, bottom) if high else jnp.where(low3, top, bottom_s)
            dsend_ref[n, :, 64:96, :] = f.astype(BF)
        swapped.start()
        g_out = outer(att_ref[...], d_branch).astype(BF)
        both[3][0, 0] = g_out[:, :384]
        both[3][0, 1] = g_out[:, 384:]

    def pieces(delta):
        neg = -delta
        hi = neg.astype(BF).astype(F32)
        mid = (neg - hi).astype(BF).astype(F32)
        lo = neg - hi - mid
        return jnp.where(part == 1, hi, jnp.where(part == 2, mid, jnp.where(part == 3, lo, 0.0)))

    loads = {}

    def tile(t):
        q_ref, k_ref, v_ref, kt_ref, o01_ref, o2_ref = (loads[n] for n in range(6))
        dk_ref, dv_ref, d5_ref = (loads[n] for n in ("dk", "dv", "d5"))
        at = pl.ds(pl.multiple_of(t * 256, 256), 256)
        ab = t // 4
        keys = pl.ds(pl.multiple_of(ab * 1024, 1024), 1024)
        do01 = do_ref[:, t, 0:64, :].astype(F32).reshape(256, 128)
        folded = do_ref[:, t, 64:96, :].astype(F32)
        two = []
        for h in range(4):
            two.append(pltpu.roll(folded[h], 64, 1))
            two.append(folded[h])
        do2 = jnp.concatenate(two, axis=0)
        prod = do01 * o01_ref[at, :]
        prod2 = do2 * o2_ref[at, :]
        delta0 = jnp.sum(jnp.where(low, prod, 0.0), axis=1, keepdims=True)
        delta1 = jnp.sum(jnp.where(low, 0.0, prod), axis=1, keepdims=True)
        delta2 = jnp.sum(jnp.where(low, 0.0, prod2), axis=1, keepdims=True)
        dos = (
            jnp.where(low, do01, pieces(delta0)).astype(BF),
            jnp.where(low, pieces(delta1), do01).astype(BF),
            jnp.where(low, pieces(delta2), do2).astype(BF),
        )
        dqs = []
        for head in range(3):
            q = q_ref[head, at, :]
            prob = jnp.exp(nt(k_ref[head, keys, :], q))
            d_prob = nt(v_ref[head, keys, :], dos[head])
            d_log = (prob * d_prob).astype(BF)
            dv_ref[head, keys, :] += matmul(prob.astype(BF), dos[head])
            dk_ref[head, keys, :] += matmul(d_log, q)
            dqs.append(matmul(kt_ref[head, ab], d_log).T * 0.125)
        off = jnp.where(t < 4, t, 4 + r + 2 * (t - 4)) * 256
        rows = pl.ds(pl.multiple_of(off, 256), 256)
        d5_ref[rows, 0:128] = jnp.where(low, dqs[0], dqs[1]).astype(BF)
        d5_ref[rows, 512:640] = jnp.where(low, dqs[2], 0.0).astype(BF)

    halves = ((0, slice(0, 4)), (1, slice(4, 8)))
    away = (gc, gcx)

    def c_copy(k, ab):
        cut = halves[ab][1]
        return remote(p_ref.at[away[k], cut], rc_ref.at[k, cut], c_send.at[k, ab], c_recv.at[k, ab], core)

    def x_copy(ab):
        cut = halves[ab][1]
        return remote(sx_ref.at[cut], rx_ref.at[cut], x_send.at[ab], x_recv.at[ab], across)

    z_copy = remote(zb_ref, rz_ref, z_send.at[0], z_recv.at[0], pair)
    mine = 3 * p + 2 * r

    def home(n):
        if n < 4:
            s = (zs[3], zs[2], zs[1], z)[n]
            src, dst = ig_ref.at[s], out_ref.at[mine]
        else:
            s = z if n == 5 else zs[2]
            src, dst = ig_ref.at[4 + (1 - p if n == 4 else p)], out_ref.at[3 * p + 1]
        if n in (3, 5):
            return pltpu.make_async_copy(src, dst, h_own.at[n // 4])
        where = mine if n < 4 else 3 * p + 1
        return remote(src, dst, h_send.at[min(n, 3)], h_recv.at[where], (item, s * 4 + g))

    gain = gain_ref[...].reshape(1, 768)

    def norm_back(d_xn, j):
        h = h_ref[j].astype(F32)
        inv = lax.rsqrt(jnp.mean(h * h, axis=-1, keepdims=True) + EPS)
        dgain_ref[...] += jnp.sum(d_xn * h * inv, axis=0, keepdims=True)
        dyg = d_xn * gain
        dot = jnp.mean(dyg * h, axis=-1, keepdims=True)
        ig_ref[j] = (dh_ref[j] + inv * dyg - h * (inv * inv * inv * dot)).astype(BF)

    def load_copy(n):
        return pltpu.make_async_copy(loads_hbm[n], loads[n], load_sem.at[n])

    def run_swap():
        for n in range(8):
            load_copy(n).wait()
        swapped.finish()

    def run_dxn():
        wc_ref, dk_ref, dv_ref, d5_ref = (loads[n] for n in (7, "dk", "dv", "d5"))

        @pl.loop(0, 8)
        def _(i):
            rows = pl.ds(pl.multiple_of(i * 256, 256), 256)
            d5_ref[rows, 128:256] = jnp.where(low, dk_ref[0, rows, :], dk_ref[1, rows, :]).astype(BF)
            d5_ref[rows, 256:384] = jnp.where(low, dv_ref[0, rows, :], dv_ref[1, rows, :]).astype(BF)
            d5_ref[rows, 384:512] = jnp.where(low, dk_ref[2, rows, :], dv_ref[2, rows, :]).astype(BF)
            d_xn = nt(d5_ref[rows, :], wc_ref[...]).astype(BF)
            for h in range(4):
                p_ref[h, i, :, :] = d_xn[h * 64 : h * 64 + 64]

        for k in (1, 0):
            for ab in (1, 0):
                c_copy(k, ab).start()

    def run_gw():
        for c in range(5):
            cols = slice(c * 128, c * 128 + 128)
            gw_ref[:, cols] = outer(loads[6][...], loads["d5"][:, cols]).astype(BF)

    def run_xs(ab):
        c_copy(1, ab).wait_recv()

        @pl.loop(0, 4)
        def _(j):
            n = ab * 4 + j
            sx_ref[n] = (p_ref[gx, n].astype(F32) + rc_ref[1, n].astype(F32)).astype(BF)

        x_copy(ab).start()

    def run_t(ab):
        c_copy(0, ab).wait_recv()

        @pl.loop(0, 4)
        def _(j):
            n = ab * 4 + j
            t_ref[n] = p_ref[g, n].astype(F32) + rc_ref[0, n].astype(F32)

    def run_z():
        x_copy(1).wait_recv()
        for q in range(2):
            n = 4 + (1 - r) + 2 * q
            zb_ref[q] = (t_ref[n] + rx_ref[n].astype(F32)).astype(BF)
        z_copy.start()

    def run_na():
        x_copy(0).wait_recv()
        for n, s in enumerate((zs[3], zs[2], zs[1], z)):
            norm_back(t_ref[s] + rx_ref[s].astype(F32), s)
            home(n).start()

    def run_nb():
        z_copy.wait_recv()
        for n, q in enumerate((1 - p, p)):
            k = 4 + r + 2 * q
            norm_back(t_ref[k] + rx_ref[k].astype(F32) + rz_ref[q].astype(F32), 4 + q)
            home(4 + n).start()

    gain_peers = [core] + [peer for _, peer in coords.values()]

    def gain_copy(k):
        return remote(buf.at[k], got.at[k], gain_send.at[k], gain_recv.at[k], gain_peers[k])

    def run_gain(k):
        if k == 0:
            buf[0] = jnp.zeros_like(buf[0])
            buf[0, 0:1, :] = dgain_ref[...]
            buf[0, 1:2, :] = dgain2_ref[...]
        else:
            gain_copy(k - 1).wait_recv()
            buf[k] = buf[k - 1] + got[k - 1]
        if k < 5:
            gain_copy(k).start()
        else:
            gains_out[...] = buf[5]

    homes = from_slots(item, z, g, res_ref, res_out_ref, rs_send, rs_recv, rs_own)

    single = {
        "swap": run_swap, "dxn": run_dxn, "gw": run_gw, "xsB": lambda: run_xs(1), "xsA": lambda: run_xs(0),
        "tB": lambda: run_t(1), "tA": lambda: run_t(0), "zB": run_z, "nA": run_na, "nB": run_nb, "res": homes.start,
    }

    def emit(task):
        if task in single:
            single[task]()
            return
        head, _, k = task.partition(".")
        if head == "gain":
            run_gain(int(k))
        elif head[0] == "f":
            streams[head[1:]].fold(int(k))
        elif head == "open":
            streams[k].open()
        elif head[0] == "g":
            streams[head[1:]].collect(int(k))
        else:
            streams[head[1:]].extend()

    def run_loop(name, count, body, emit):
        at = [n for n, task in enumerate(PLAN) if task == name]

        @pl.loop(0, count)
        def _(t):
            body(t)
            for n in range(count - 1):
                tasks = PLAN[at[n] + 1 : at[n + 1]]
                if tasks:

                    @pl.when(t == n)
                    def _():
                        for task in tasks:
                            emit(task)

    def emit_between(first, last):
        start = 0 if first is None else len(PLAN) - PLAN[::-1].index(first)
        stop = len(PLAN) if last is None else PLAN.index(last)
        for task in PLAN[start:stop]:
            emit(task)

    shape = (6, 64, 768)
    width, hidden = dense_hbm[4].shape
    v = pltpu.VMEM
    pl.run_scoped(
        functools.partial(dense, emit),
        v((width, width), BF), v((width, hidden), BF), v((width, hidden), BF), v((hidden, width), BF),
        v(dense_hbm[0].shape, BF), v(shape, BF), v((384, width), BF), v((384, width), F32), v((384, width), BF),
        v((width, 384), BF), v((384, width), F32),
    )

    def attend(*scoped):
        loads.update(enumerate(scoped[:8]))
        loads.update(zip(("dk", "dv", "d5"), scoped[8:]))
        for n in range(8):
            load_copy(n).start()
        for n in ("dk", "dv", "d5"):
            loads[n][...] = jnp.zeros_like(loads[n])
        dgain_ref[...] = jnp.zeros_like(dgain_ref)
        emit_between("ff", "tile")
        run_loop("tile", 6, tile, emit)
        emit_between("tile", "end")

    pl.run_scoped(
        attend,
        *[v(ref.shape, ref.dtype) for ref in loads_hbm],
        v((3, 2048, 128), F32), v((3, 2048, 128), F32), v((2048, 640), BF),
    )
    emit_between("end", None)

    for s in zs[1:]:
        where = 3 * (s // 2) + 2 * (s % 2)
        remote(ig_ref.at[0], out_ref.at[where], h_send.at[0], h_recv.at[where], pair).wait_recv()
    where = 3 * (1 - p) + 1
    remote(ig_ref.at[0], out_ref.at[where], h_send.at[0], h_recv.at[where], pair).wait_recv()
    homes.finish()
    home(3).wait()
    home(5).wait()
    for stream in streams.values():
        stream.close()
    for n in (0, 1, 2, 4):
        home(n).wait_send()
    z_copy.wait_send()
    for ab in range(2):
        x_copy(ab).wait_send()
        for k in range(2):
            c_copy(k, ab).wait_send()
    for k in range(5):
        gain_copy(k).wait_send()


def back(dense, gain2, gain1, loads, rows_shape):
    dma = pltpu.SemaphoreType.DMA
    s = jax.ShapeDtypeStruct
    v = pltpu.VMEM
    _, rows, width = rows_shape
    heads = dense[0].shape
    gains = (8, width)
    group = (width, 640)
    w_out, w_gate, w_up, w_down = dense[3:]
    outs = (s(rows_shape, BF), s(rows_shape, BF)) + tuple(s(a.shape, BF) for a in (w_gate, w_up, w_down, w_out))
    outs += (s((4,) + group, BF), s(gains, F32))
    scratch = [
        v(rows_shape, BF), v(rows_shape, F32), v(rows_shape, BF), v(heads, BF), v((1, width), F32),
        v((2, 2, width, 512), BF), v((2, 2, width, 512), BF), v((2, 2, 1024, width // 2), BF), v((1, 2, width, width // 2), BF),
        dma((4,)), dma((3, 4)), dma((8,)),
        v(heads, BF), v((4, 8, rows, width), BF),
        v((2, 8, rows, width), BF), v((8, rows, width), BF), v((8, rows, width), BF),
        v((8, rows, width), F32), v((2, rows, width), BF), v((2, rows, width), BF), v((6, rows, width), BF),
        v((1, width), F32),
        dma((2, 2)), dma((2, 2)), dma((2,)), dma((2,)), dma((1,)), dma((1,)), dma((4,)), dma((6,)), dma((2,)),
        dma((4,)), dma((6,)), dma((2,)), dma((3,)), dma((4,)), dma((1,)),
    ]
    for _, _, _, _, high, wide, _, _ in PIECES.values():
        scratch += [v((high, wide), BF)] * 2
        scratch += [dma((5,)), dma((5,)), dma((2,)), dma((4,)), dma((4,)), dma((5,)), dma((5,))]
    scratch += [v(group, BF)]
    for _, wide, _ in GROUPS.values():
        scratch += [v((width, wide), BF)]
        scratch += [dma((4,)), dma((4,)), dma((2,)), dma((4, 2)), dma((4, 2)), dma((4, 2)), dma((4, 2))]
    scratch += [v((6,) + gains, F32), v((5,) + gains, F32), dma((5,)), dma((5,))]
    return pl.pallas_call(
        back_kernel,
        out_shape=outs,
        in_specs=[ANY] * 7 + [VMEM] * 2 + [ANY] * 8,
        out_specs=(ANY,) * 7 + (VMEM,),
        scratch_shapes=scratch,
        compiler_params=params(3, 63),
        name="back",
    )(*dense, gain2, gain1, *loads)


def fast(
    inputs, counts, norm_gain1, w_query, w_key, w_value, w_out, norm_gain2, w_gate, w_up, w_down, cotangent
):
    band_rows, width = inputs.shape[2:]
    orecv, dy6, hidden, q, k, v, kt, o01, o2, xn, wc = front(
        inputs.reshape(6, band_rows, width), cotangent.reshape(6, band_rows, width), counts, norm_gain1,
        w_query, w_key, w_value,
    )
    input_grads, results, s_gate, s_up, s_down, s_out, s_qkv, s_gains = back(
        (orecv, hidden, dy6, w_out, w_gate, w_up, w_down), norm_gain2, norm_gain1, (q, k, v, kt, o01, o2, xn, wc), hidden.shape
    )
    *grads, gain1, gain2, results, input_grads = widen(
        s_qkv, s_out, s_gate, s_up, s_down, s_gains, results, input_grads
    )
    return (
        results.reshape(inputs.shape), input_grads.reshape(inputs.shape), gain1, *grads[:4], gain2, *grads[4:]
    )


def program(*args):
    micro, seqs, band_rows, width = args[0].shape
    small = lax.axis_size("band") == 16 and lax.axis_size("items") == 2
    if small and (micro, seqs, band_rows, width, HEADS, HEAD_DIM) == (2, 3, 64, 768, 12, 64):
        return fast(*args)
    return per_device(*args)


def solution(mesh):
    return jax.shard_map(
        program,
        mesh=mesh,
        in_specs=(
            P(None, "items", "band", None),
            P(None, "items"),
            P(),
            P(),
            P(),
            P(),
            P(),
            P(),
            P(),
            P(),
            P(),
            P(None, "items", "band", None),
        ),
        out_specs=(
            P(None, "items", "band", None),
            P(None, "items", "band", None),
            P(),
            P(),
            P(),
            P(),
            P(),
            P(),
            P(),
            P(),
            P(),
        ),
        check_vma=False,
    )
```

```python
import functools
import math

import jax
import jax.numpy as jnp
from jax import lax
from jax.experimental import pallas as pl
from jax.experimental.pallas import tpu as pltpu
from jax.sharding import PartitionSpec as P

HEADS = 12
HEAD_DIM = 64


EPS = 1e-06


def shortened(shard):

    def short(part):
        return part.astype(jnp.bfloat16) if part.dtype == jnp.float32 else part

    return jax.tree.map(short, shard)


def rms_scale(values, gain):
    return values * lax.rsqrt(jnp.mean(values * values, axis=-1, keepdims=True) + EPS) * gain


def gated(gate, upper):
    return jax.nn.gelu(gate, approximate=True) * upper


def outer(left, right):
    return lax.dot_general(
        left, right, (((0,), (0,)), ((), ())), preferred_element_type=jnp.float32
    )


def transposed(left, weight):
    return lax.dot_general(
        left, weight, (((1,), (1,)), ((), ())), preferred_element_type=jnp.float32
    )


def matmul(left, right):
    return jnp.dot(left, right, preferred_element_type=jnp.float32)


def scores(query, key, scale):
    return jnp.einsum("sqhd,skhd->shqk", query, key, preferred_element_type=jnp.float32) * scale


def per_device(
    inputs,
    counts,
    norm_gain1,
    w_query,
    w_key,
    w_value,
    w_out,
    norm_gain2,
    w_gate,
    w_up,
    w_down,
    cotangent,
):
    micro, seqs, band_rows, width = inputs.shape
    bands = lax.axis_size("band")
    length = band_rows * bands
    rows = seqs * band_rows
    heads = HEADS
    head_dim = HEAD_DIM
    scale = 1.0 / math.sqrt(head_dim)
    key_place = jnp.arange(length, dtype=jnp.int32)
    params = (norm_gain1, w_query, w_key, w_value, w_out, norm_gain2, w_gate, w_up, w_down)
    totals = [jnp.zeros(p.shape, jnp.float32) for p in params]
    results = []
    input_grads = []
    for number in range(micro):
        hidden = inputs[number].astype(jnp.float32).reshape(rows, width)
        lengths = counts[number]
        normed = rms_scale(hidden, norm_gain1).astype(jnp.bfloat16)
        query = matmul(normed, w_query).astype(jnp.bfloat16)
        key_local = matmul(normed, w_key).astype(jnp.bfloat16)
        value_local = matmul(normed, w_value).astype(jnp.bfloat16)
        query_four = query.reshape(seqs, band_rows, heads, head_dim)
        key_three = key_local.reshape(seqs, band_rows, width)
        value_three = value_local.reshape(seqs, band_rows, width)
        key_all, value_all = (
            lax.all_gather(key_three, "band", axis=1, tiled=True),
            lax.all_gather(value_three, "band", axis=1, tiled=True),
        )
        live = key_place[None, :] < lengths[:, None]
        key_four = key_all.reshape(seqs, length, heads, head_dim)
        value_four = value_all.reshape(seqs, length, heads, head_dim)
        logits = jnp.where(live[:, None, None, :], scores(query_four, key_four, scale), -jnp.inf)
        top = jnp.max(logits, axis=-1, keepdims=True)
        expo = jnp.exp(logits - top)
        summed = jnp.sum(expo, axis=-1, keepdims=True)
        log_total = top + jnp.log(summed)
        prob = (expo / summed).astype(jnp.bfloat16)
        attended = jnp.einsum(
            "shqk,skhd->sqhd", prob, value_four, preferred_element_type=jnp.float32
        )
        attended = attended.reshape(rows, width).astype(jnp.bfloat16)
        second = hidden + matmul(attended, w_out)
        normed_two = rms_scale(second, norm_gain2).astype(jnp.bfloat16)
        gate = matmul(normed_two, w_gate)
        upper = matmul(normed_two, w_up)
        mixed = gated(gate, upper).astype(jnp.bfloat16)
        results.append(
            (second + matmul(mixed, w_down)).astype(jnp.bfloat16).reshape(seqs, band_rows, width)
        )
        grad_rows = cotangent[number].reshape(rows, width)
        totals[8] = totals[8] + outer(mixed, grad_rows)
        d_mixed = transposed(grad_rows, w_down)
        pull_gate = jax.vjp(gated, gate, upper)[1]
        d_gate, d_upper = pull_gate(d_mixed)
        d_gate = d_gate.astype(jnp.bfloat16)
        d_upper = d_upper.astype(jnp.bfloat16)
        totals[6] = totals[6] + outer(normed_two, d_gate)
        totals[7] = totals[7] + outer(normed_two, d_upper)
        d_normed_two = transposed(d_gate, w_gate) + transposed(d_upper, w_up)
        pull_two = jax.vjp(rms_scale, second, norm_gain2)[1]
        d_second_norm, d_gain_two = pull_two(d_normed_two)
        totals[5] = totals[5] + d_gain_two
        d_second = grad_rows.astype(jnp.float32) + d_second_norm
        d_branch = d_second.astype(jnp.bfloat16)
        totals[4] = totals[4] + outer(attended, d_branch)
        d_attended = transposed(d_branch, w_out).astype(jnp.bfloat16)
        d_att_four = d_attended.reshape(seqs, band_rows, heads, head_dim)
        key_all, value_all = (
            lax.all_gather(key_three, "band", axis=1, tiled=True),
            lax.all_gather(value_three, "band", axis=1, tiled=True),
        )
        key_four = key_all.reshape(seqs, length, heads, head_dim)
        value_four = value_all.reshape(seqs, length, heads, head_dim)
        logits = jnp.where(live[:, None, None, :], scores(query_four, key_four, scale), -jnp.inf)
        prob_full = jnp.exp(logits - log_total)
        prob = prob_full.astype(jnp.bfloat16)
        d_prob = jnp.einsum(
            "sqhd,skhd->shqk", d_att_four, value_four, preferred_element_type=jnp.float32
        )
        delta = jnp.sum(d_prob * prob_full, axis=-1, keepdims=True)
        d_logits = (prob_full * (d_prob - delta)).astype(jnp.bfloat16)
        d_query = (
            jnp.einsum("shqk,skhd->sqhd", d_logits, key_four, preferred_element_type=jnp.float32)
            * scale
        )
        d_query = d_query.reshape(rows, width).astype(jnp.bfloat16)
        d_key_all = (
            jnp.einsum("shqk,sqhd->skhd", d_logits, query_four, preferred_element_type=jnp.float32)
            * scale
        )
        d_value_all = jnp.einsum(
            "shqk,sqhd->skhd", prob, d_att_four, preferred_element_type=jnp.float32
        )
        d_key_three, d_value_three = (
            lax.psum_scatter(
                d_key_all.reshape(seqs, length, width).astype(jnp.bfloat16),
                "band",
                scatter_dimension=1,
                tiled=True,
            ).astype(jnp.float32),
            lax.psum_scatter(
                d_value_all.reshape(seqs, length, width).astype(jnp.bfloat16),
                "band",
                scatter_dimension=1,
                tiled=True,
            ).astype(jnp.float32),
        )
        d_key = d_key_three.reshape(rows, width).astype(jnp.bfloat16)
        d_value = d_value_three.reshape(rows, width).astype(jnp.bfloat16)
        totals[1] = totals[1] + outer(normed, d_query)
        totals[2] = totals[2] + outer(normed, d_key)
        totals[3] = totals[3] + outer(normed, d_value)
        d_normed = (
            transposed(d_query, w_query) + transposed(d_key, w_key) + transposed(d_value, w_value)
        )
        pull_one = jax.vjp(rms_scale, hidden, norm_gain1)[1]
        d_hidden_norm, d_gain_one = pull_one(d_normed)
        totals[0] = totals[0] + d_gain_one
        input_grads.append(
            (d_second + d_hidden_norm).astype(jnp.bfloat16).reshape(seqs, band_rows, width)
        )
    shares = jax.tree.map(
        lambda part: part.astype(jnp.float32),
        lax.psum_scatter(shortened(tuple(totals)), "band", scatter_dimension=0, tiled=True),
    )
    summed_shares = jax.tree.map(
        lambda part: part.astype(jnp.float32), lax.psum(shortened(shares), "items")
    )
    whole = jax.tree.map(
        lambda part, own: part.astype(own.dtype),
        lax.all_gather(shortened(summed_shares), "band", axis=0, tiled=True),
        summed_shares,
    )
    return (jnp.stack(results), jnp.stack(input_grads)) + tuple(whole)


MESH_ID = pl.DeviceIdType.MESH
NEG = -1e30
BF = jnp.bfloat16
F32 = jnp.float32


def place():
    item = lax.axis_index("items")
    band = lax.axis_index("band")
    return item, band // 4, band % 4


def flip(value):
    return value + 1 - 2 * (value % 2)


def far(value):
    return (value + 2) % 4


def greet(peers):
    barrier = pltpu.get_barrier_semaphore()
    for peer in peers:
        pl.semaphore_signal(barrier, inc=1, device_id=peer, device_id_type=MESH_ID)
    pl.semaphore_wait(barrier, len(peers))


def remote(src, dst, send, recv, peer):
    return pltpu.make_async_remote_copy(
        src_ref=src, dst_ref=dst, send_sem=send, recv_sem=recv, device_id=peer, device_id_type=MESH_ID
    )


def params(number, vmem=62):
    return pltpu.CompilerParams(
        collective_id=number, has_side_effects=True, vmem_limit_bytes=vmem << 20
    )


def whole(value, unit):
    return value if isinstance(value, int) else pl.multiple_of(value, unit)


def lanes_of(rows):
    return lax.broadcasted_iota(jnp.int32, (rows, 128), 1)


ANY = pl.BlockSpec(memory_space=pl.ANY)
VMEM = pl.BlockSpec(memory_space=pltpu.VMEM)
SMEM = pl.BlockSpec(memory_space=pltpu.SMEM)


class Moves:
    def __init__(self):
        self.remotes, self.locals, self.arrivals = [], [], []

    def start(self):
        for make in self.remotes + self.locals:
            make().start()

    def finish(self):
        for make in self.arrivals:
            make().wait_recv()
        for make in self.locals:
            make().wait()
        for make in self.remotes:
            make().wait_send()


def to_slots(item, z, g, src_ref, dst_ref, send, recv, own_sem):
    zs = (z, flip(z), far(z), far(flip(z)))
    p, r = z // 2, z % 2
    moves = Moves()

    def out(n):
        if n < 3:
            s = zs[n + 1]
            src, where = src_ref.at[3 * (s // 2) + 2 * (s % 2)], z
        else:
            s = far(z)
            src, where = src_ref.at[3 * (1 - p) + 1], 4 + p
        return remote(src, dst_ref.at[where], send.at[n], recv.at[where], (item, s * 4 + g))

    def came(where):
        block = dst_ref.at[where]
        return remote(block, block, send.at[0], recv.at[where], (item, far(z) * 4 + g))

    moves.remotes = [lambda n=n: out(n) for n in range(4)]
    moves.locals = [
        lambda: pltpu.make_async_copy(src_ref.at[3 * p + 2 * r], dst_ref.at[z], own_sem.at[0]),
        lambda: pltpu.make_async_copy(src_ref.at[3 * p + 1], dst_ref.at[4 + p], own_sem.at[1]),
    ]
    moves.arrivals = [lambda w=w: came(w) for w in zs[1:] + (4 + (1 - p),)]
    return moves


def from_slots(item, z, g, src_ref, dst_ref, send, recv, own_sem):
    zs = (z, flip(z), far(z), far(flip(z)))
    p, r = z // 2, z % 2
    mine = 3 * p + 2 * r
    moves = Moves()

    def out(n):
        s = zs[n + 1] if n < 3 else far(z)
        src, where = (src_ref.at[s], mine) if n < 3 else (src_ref.at[4 + (1 - p)], 3 * p + 1)
        return remote(src, dst_ref.at[where], send.at[n], recv.at[where], (item, s * 4 + g))

    def came(where):
        block = dst_ref.at[where]
        return remote(block, block, send.at[0], recv.at[where], (item, far(z) * 4 + g))

    moves.remotes = [lambda n=n: out(n) for n in range(4)]
    moves.locals = [
        lambda: pltpu.make_async_copy(src_ref.at[z], dst_ref.at[mine], own_sem.at[0]),
        lambda: pltpu.make_async_copy(src_ref.at[4 + p], dst_ref.at[3 * p + 1], own_sem.at[1]),
    ]
    theirs = [3 * (s // 2) + 2 * (s % 2) for s in zs[1:]] + [3 * (1 - p) + 1]
    moves.arrivals = [lambda w=w: came(w) for w in theirs]
    return moves


def z_peers(item, z, g):
    return [(item, s * 4 + g) for s in (flip(z), far(z), far(flip(z)))]


def g_peers(item, z, g):
    return [(item, z * 4 + h) for h in (flip(g), far(g), far(flip(g)))]


def swap_heads(item, z, g, src_ref, dst_ref, send, recv, own_sem):
    moves = Moves()

    def out(n, h):
        return remote(src_ref.at[h], dst_ref.at[g], send.at[n], recv.at[g], (item, z * 4 + h))

    def came(h):
        return remote(dst_ref.at[h], dst_ref.at[h], send.at[0], recv.at[h], (item, z * 4 + h))

    moves.remotes = [lambda n=n, h=h: out(n, h) for n, h in enumerate((far(g), far(flip(g)), flip(g)))]
    moves.locals = [lambda: pltpu.make_async_copy(src_ref.at[g], dst_ref.at[g], own_sem)]
    moves.arrivals = [lambda h=h: came(h) for h in (flip(g), far(g), far(flip(g)))]
    return moves


def nt(left, right):
    return lax.dot_general(left, right, (((1,), (1,)), ((), ())), preferred_element_type=F32)


def front_phase(ins, outs, landing, sems):
    x_ref, cot_ref, count_ref, gain_ref, wq_ref, wk_ref, wv_ref = ins
    q_out, k_out, v_out, kt_out, o01_out, o2_out, xn_out, wc_out = outs
    orecv_ref, dy_ref, hid_ref, xall_ref, osend_ref = landing
    (
        z_send, f_send, g_send, recv, own_sem, win_sem, o_send, o_recv, cot_send, cot_recv, cot_own,
        half_sem, tile_sem, last_sem,
    ) = sems
    item, z, g = place()
    p, r = z // 2, z % 2
    gc, gx = flip(g), far(g)
    gcx = far(gc)
    zs = (z, flip(z), far(z), far(flip(z)))
    core, across = (item, z * 4 + gc), (item, z * 4 + gx)
    lane = lanes_of(256)
    low = lane < 64

    def items_of(s):
        return (3 * (s // 2) + 2 * (s % 2), 3 * (s // 2) + 1)

    started = []

    def go(make):
        make().start()
        started.append(make)

    def forward(n, ab):
        def make(k, peer):
            where = zs[n] * 4 + g
            src = x_ref.at[items_of(z)[ab]] if n == 0 else xall_ref.at[ab, where]
            return remote(src, xall_ref.at[ab, where], f_send.at[n, ab, k], recv.at[ab, where], peer)

        go(lambda: make(0, across))
        go(lambda: make(1, core))

    def arrived(ab, where):
        block = xall_ref.at[ab, where]
        remote(block, block, z_send.at[0, 0], recv.at[ab, where], core).wait_recv()

    def send_z(ab):
        for n, s in enumerate(zs[1:]):
            go(
                lambda n=n, s=s: remote(
                    x_ref.at[items_of(s)[ab]],
                    xall_ref.at[ab, z * 4 + g],
                    z_send.at[n, ab],
                    recv.at[ab, z * 4 + g],
                    (item, s * 4 + g),
                )
            )

    def own_copy(ab):
        return pltpu.make_async_copy(x_ref.at[items_of(z)[ab]], xall_ref.at[ab, z * 4 + g], own_sem.at[ab])

    def forward_z(ab, n):
        arrived(ab, zs[n] * 4 + g)
        forward(n, ab)

    def forward_x(ab, n):
        def make():
            where = zs[n] * 4 + gx
            block = xall_ref.at[ab, where]
            return remote(block, block, g_send.at[n, ab], recv.at[ab, where], core)

        arrived(ab, zs[n] * 4 + gx)
        go(make)

    def o_copy(t, k):
        h = (gx, gcx, gc)[k]
        return remote(
            osend_ref.at[h, t], orecv_ref.at[g, t], o_send.at[t, k], o_recv.at[g, t], (item, z * 4 + h)
        )

    def self_copy(t):
        return pltpu.make_async_copy(osend_ref.at[g, t], orecv_ref.at[g, t], tile_sem.at[t, 3])

    def block_copy(j):
        src = xall_ref.at[0, j * 4 + g] if j < 4 else xall_ref.at[1, (r + 2 * (j - 4)) * 4 + g]
        return pltpu.make_async_copy(src, hid_ref.at[j], last_sem.at[j])

    moved = to_slots(item, z, g, cot_ref, dy_ref, cot_send, cot_recv, cot_own)

    def arrive():
        for t in range(6):
            for h in (gx, gcx, gc):
                block = orecv_ref.at[h, t]
                remote(block, block, o_send.at[0, 0], o_recv.at[h, t], core).wait_recv()
            self_copy(t).wait()
        moved.finish()

    def leave():
        for t in range(6):
            for k in range(3):
                o_copy(t, k).wait_send()
        for make in started:
            make().wait_send()

    def body(win_ref, q_ref, k_ref, v_ref, kt_ref, o01_ref, o2_ref, xn_ref, wc_ref):
        send_z(0)
        forward(0, 0)
        send_z(1)
        forward(0, 1)
        cut = pl.ds(pl.multiple_of(g * 3 // 2 * 128, 128), 256)
        windows = []
        for n, ref in enumerate((wq_ref, wk_ref, wv_ref)):
            windows.append(pltpu.make_async_copy(ref.at[:, cut], win_ref.at[n], win_sem.at[n]))

        for copy in windows + [own_copy(0), own_copy(1)]:
            copy.start()
        for copy in windows:
            copy.wait()
        odd = g % 2 == 1

        @pl.loop(0, 3)
        def _(i):
            rows = pl.ds(pl.multiple_of(i * 256, 256), 256)
            firsts, lasts = [], []
            for n in range(3):
                left = win_ref[n, rows, 0:128].astype(F32)
                right = win_ref[n, rows, 128:256].astype(F32)
                crossed = pltpu.roll(jnp.where(low, right, left), 64, 1)
                firsts.append(jnp.where(odd, crossed, left))
                lasts.append(jnp.where(odd, pltpu.roll(right, 64, 1), right))
            for n in range(3):
                wc_ref[rows, n * 128 : n * 128 + 128] = firsts[n].astype(BF)
            wc_ref[rows, 384:512] = jnp.where(low, lasts[1], pltpu.roll(lasts[2], 64, 1)).astype(BF)
            wc_ref[rows, 512:640] = jnp.where(low, lasts[0], 0.0).astype(BF)

        def project(ab, n):
            zz = zs[n]
            if n == 0:
                own_copy(ab).wait()
            for h in (gc, gcx):
                arrived(ab, zz * 4 + h)
            rows = pl.ds(pl.multiple_of(ab * 1024 + zz * 256, 256), 256)
            h = xall_ref[ab, pl.ds(zz * 4, 4)].reshape(256, 768).astype(F32)
            inv = lax.rsqrt(jnp.mean(h * h, axis=-1, keepdims=True) + EPS)
            xn = (h * inv * gain_ref[...].reshape(1, 768)).astype(BF)
            xn_ref[rows, :] = xn
            y = matmul(xn, wc_ref[:, 128:512])
            count = count_ref[p, (2 * r if ab == 0 else 1)]
            at = lax.broadcasted_iota(jnp.int32, (256, 128), 0) + zz * 256
            bias = jnp.where(at < count, 0.0, NEG)
            one = jnp.where((lane % 64) < 4, 1.0, 0.0)
            k_aug = jnp.where(lane % 64 == 0, bias, one)
            k01, v01, kv2 = y[:, :128], y[:, 128:256], y[:, 256:]
            keys = (jnp.where(low, k01, k_aug), jnp.where(low, k_aug, k01), jnp.where(low, kv2, k_aug))
            cols = pl.ds(pl.multiple_of(zz * 256, 256), 256)
            for head in range(3):
                key = keys[head].astype(BF)
                k_ref[head, rows, :] = key
                kt_ref[head, ab, :, cols] = key.T
            v_ref[0, rows, :] = jnp.where(low, v01, one).astype(BF)
            v_ref[1, rows, :] = jnp.where(low, one, v01).astype(BF)
            v_ref[2, rows, :] = jnp.where(low, one, kv2).astype(BF)

        def half_copy(ab, n):
            rows = pl.ds(ab * 1024, 1024)
            a, b = (
                (k_ref.at[:, rows], k_out.at[:, rows]), (v_ref.at[:, rows], v_out.at[:, rows]),
                (kt_ref.at[:, ab], kt_out.at[:, ab]), (xn_ref.at[rows], xn_out.at[rows]),
            )[n]
            return pltpu.make_async_copy(a, b, half_sem.at[ab, n])

        def tile(t):
            off = jnp.where(t < 4, t, 4 + r + 2 * (t - 4)) * 256
            xq = xn_ref[pl.ds(pl.multiple_of(off, 256), 256), :]
            q01 = matmul(xq, wc_ref[:, 0:128]).astype(BF).astype(F32) * 0.125
            q2 = matmul(xq, wc_ref[:, 512:640]).astype(BF).astype(F32) * 0.125
            flag = jnp.where(lane % 64 == 0, 1.0, 0.0)
            qs = (jnp.where(low, q01, flag), jnp.where(low, flag, q01), jnp.where(low, q2, flag))
            at = pl.ds(pl.multiple_of(t * 256, 256), 256)
            ab = t // 4
            keys = pl.ds(pl.multiple_of(ab * 1024, 1024), 1024)
            outs = []
            for head in range(3):
                s = matmul(qs[head].astype(BF), kt_ref[head, ab])
                top = jnp.max(s, axis=1, keepdims=True)
                e = jnp.exp(s - top).astype(BF)
                o = matmul(e, v_ref[head, keys, :])
                total = o[:, 64:65] if head == 0 else o[:, 0:1]
                outs.append(o / total)
                lse = -(top + jnp.log(total))
                hi = lse.astype(BF).astype(F32)
                mid = (lse - hi).astype(BF).astype(F32)
                lo = lse - hi - mid
                part = lane % 64
                aug = jnp.where(part == 1, hi, jnp.where(part == 2, mid, jnp.where(part == 3, lo, flag)))
                data = low if head != 1 else jnp.logical_not(low)
                q_ref[head, at, :] = jnp.where(data, qs[head], aug).astype(BF)
            o01 = jnp.where(low, outs[0], outs[1])
            o2 = outs[2]
            o01_ref[at, :] = o01
            o2_ref[at, :] = o2
            for h in range(4):
                osend_ref[h, t, 0:64, :] = o01[h * 64 : h * 64 + 64].astype(BF)
                first = o2[h * 64 : h * 64 + 32]
                second = o2[h * 64 + 32 : h * 64 + 64]
                folded = jnp.where(low[:32], pltpu.roll(first, 64, 1), second)
                osend_ref[h, t, 64:96, :] = folded.astype(BF)

        saved = []

        def keep(makes):
            for make in makes:
                make().start()
                saved.append(make)

        def tile_copy(t, k):
            rows = pl.ds(whole(t * 256, 256), 256)
            a, b = (
                (q_ref.at[:, rows], q_out.at[:, rows]), (o01_ref.at[rows], o01_out.at[rows]),
                (o2_ref.at[rows], o2_out.at[rows]),
            )[k]
            return pltpu.make_async_copy(a, b, tile_sem.at[t, k])

        keep([lambda: pltpu.make_async_copy(wc_ref, wc_out, last_sem.at[6])])
        forward_z(0, 1)
        forward_x(0, 0)
        project(0, 0)
        forward_z(0, 2)
        forward_x(0, 1)
        project(0, 1)
        forward_z(0, 3)
        forward_z(1, 1)
        forward_x(0, 2)
        project(0, 2)
        forward_x(0, 3)
        forward_x(1, 0)
        project(0, 3)
        keep([lambda n=n: half_copy(0, n) for n in range(4)])
        forward_z(1, 2)

        @pl.loop(0, 6)
        def _(t):
            tile(t)
            for k in range(3):
                o_copy(t, k).start()
            self_copy(t).start()
            for k in range(3):
                tile_copy(t, k).start()

            @pl.when(t == 0)
            def _():
                forward_z(1, 3)
                moved.start()
                forward_x(1, 1)

            @pl.when(t == 1)
            def _():
                project(1, 0)
                project(1, 1)

            @pl.when(t == 2)
            def _():
                forward_x(1, 2)
                project(1, 2)

            @pl.when(t == 3)
            def _():
                forward_x(1, 3)
                project(1, 3)
                keep([lambda n=n: half_copy(1, n) for n in range(4)])
                keep([lambda j=j: block_copy(j) for j in range(6)])

        for t in range(6):
            for k in range(3):
                tile_copy(t, k).wait()
        for make in saved:
            make().wait()

    return body, arrive, leave


GELU_A = 0.044715
GELU_C = math.sqrt(2.0 / math.pi)


def widen_kernel(
    qkv_ref, so_ref, sg_ref, su_ref, sd_ref, gains_ref, first_ref, second_ref,
    q_ref, k_ref, v_ref, o_ref, g_ref, u_ref, d_ref, gain1_ref, gain2_ref, first_out, second_out,
):
    first_out[...] = first_ref[...]
    second_out[...] = second_ref[...]

    @pl.when(pl.program_id(0) == 0)
    def _():
        gain1_ref[...] = gains_ref[0, :]
        gain2_ref[...] = gains_ref[1, :]

    low = lanes_of(qkv_ref.shape[1]) < 64

    def swap(v):
        return pltpu.roll(v, 64, 1)

    for out, first, last, high in ((q_ref, 0, 512, False), (k_ref, 128, 384, False), (v_ref, 256, 384, True)):
        a = [qkv_ref[n, :, first : first + 128].astype(F32) for n in range(4)]
        b = [qkv_ref[n, :, last : last + 128].astype(F32) for n in range(4)]
        low_b = [swap(x) if high else x for x in b]
        high_b = [x if high else swap(x) for x in b]
        tiles = (
            a[0], jnp.where(low, low_b[0], swap(a[1])), jnp.where(low, swap(a[1]), high_b[1]),
            a[2], jnp.where(low, low_b[2], swap(a[3])), jnp.where(low, swap(a[3]), high_b[3]),
        )
        for n, tile in enumerate(tiles):
            out[:, n * 128 : n * 128 + 128] = tile
    o_ref[...] = so_ref[...].astype(F32)
    g_ref[...] = sg_ref[...].astype(F32)
    u_ref[...] = su_ref[...].astype(F32)
    d_ref[...] = sd_ref[...].astype(F32)

def widen(qkv, s_out, s_gate, s_up, s_down, gains, first, second):
    s = jax.ShapeDtypeStruct
    steps = 4

    def spec(a):
        if len(a.shape) == 3:
            return pl.BlockSpec((a.shape[0], a.shape[1] // steps, a.shape[2]), lambda i: (0, i, 0))
        return pl.BlockSpec((a.shape[0] // steps, a.shape[1]), lambda i: (i, 0))

    outs = tuple(s(a.shape, F32) for a in (s_out, s_out, s_out, s_out, s_gate, s_up, s_down))
    ins = (qkv, s_out, s_gate, s_up, s_down)
    width = gains.shape[1]
    vector = pl.BlockSpec((width,), lambda i: (0,))
    moved = (s(first.shape, first.dtype), s(second.shape, second.dtype))
    return pl.pallas_call(
        widen_kernel,
        grid=(steps,),
        out_shape=outs + (s((width,), F32),) * 2 + moved,
        in_specs=[spec(a) for a in ins] + [pl.BlockSpec(gains.shape, lambda i: (0, 0)), spec(first), spec(second)],
        out_specs=tuple(spec(a) for a in outs) + (vector, vector, spec(first), spec(second)),
        compiler_params=pltpu.CompilerParams(vmem_limit_bytes=62 << 20),
        name="widen",
    )(*ins, gains, first, second)


class Stream:
    def __init__(self, spare, res, acc, first, rest, sems, order, coords, core, cut):
        self.spare, self.res, self.acc, self.first, self.rest = spare, res, acc, first, rest
        self.send, self.recv, self.own, self.back, self.got, self.fwd, self.fgot = sems
        row, col, half = cut
        self.rows, self.wide = acc.shape
        self.row = row
        self.order = [coords[name] for name in order]
        self.deep = len(order)
        bit, self.peer = core
        if half:
            self.mine = pl.ds(pl.multiple_of(bit * half + col, 128), self.wide)
            self.other = pl.ds(pl.multiple_of((1 - bit) * half + col, 128), self.wide)
        else:
            self.mine = pl.ds(col, self.wide)
        self.base, self.size = [0], [self.rows]
        for bit, _ in self.order:
            self.size.append(self.size[-1] // 2)
            self.base.append(self.base[-1] + bit * self.size[-1])

    def part(self, base, size):
        return pl.ds(whole(base, 16), size)

    def at(self, base, size, mine=True):
        cols = self.mine if mine else self.other
        return self.res.at[pl.ds(whole(self.row + base, 16), size), cols]

    def sibling(self, k):
        return self.base[k - 1] + (1 - self.order[k - 1][0]) * self.size[k]

    def own_out(self):
        here = self.base[self.deep], self.size[self.deep]
        return pltpu.make_async_copy(self.acc.at[self.part(*here)], self.at(*here), self.own.at[1])

    def c_push(self, k):
        if k == 0:
            return remote(self.spare, self.first, self.send.at[0], self.recv.at[0], self.peer)
        return remote(
            self.acc.at[self.part(self.sibling(k), self.size[k])],
            self.rest.at[pl.ds(self.rows - 2 * self.size[k], self.size[k])],
            self.send.at[k],
            self.recv.at[k],
            self.order[k - 1][1],
        )

    def c_back(self, k):
        here = self.base[k], self.size[k]
        src = self.acc.at[self.part(*here)] if k == self.deep else self.at(*here)
        return remote(
            src, self.at(*here), self.back.at[k - 1], self.got.at[k - 1], self.order[k - 1][1]
        )

    def c_forward(self, k):
        if k == 0:
            here = self.base[self.deep], self.size[self.deep]
            src = self.acc.at[self.part(*here)]
        else:
            here = self.sibling(k), self.size[k]
            src = self.at(*here)
        return remote(src, self.at(*here), self.fwd.at[k], self.fgot.at[k], self.peer)

    def open(self):
        self.c_push(0).start()

    def fold(self, k):
        self.c_push(k).wait_recv()
        base, size = self.base[k], self.size[k]
        other, at = (self.first, 0) if k == 0 else (self.rest, self.rows - 2 * size)
        step = 64 if size % 64 == 0 else 48 if size % 48 == 0 else 32

        @pl.loop(0, size // step)
        def _(n):
            rows = self.part(base + n * step, step)
            more = other[pl.ds(pl.multiple_of(at + n * step, 16), step), :]
            self.acc[rows, :] = (self.acc[rows, :].astype(F32) + more.astype(F32)).astype(BF)

        if k < self.deep:
            self.c_push(k + 1).start()
        else:
            self.c_back(k).start()
            self.c_forward(0).start()
            self.own_out().start()

    def collect(self, k):
        here = self.sibling(k), self.size[k]
        block = self.at(*here)
        remote(block, block, self.back.at[k - 1], self.got.at[k - 1], self.peer).wait_recv()
        if k == self.deep:
            self.own_out().wait()
        if k > 1:
            self.c_back(k - 1).start()
        self.c_forward(k).start()

    def close(self):
        for k in range(self.deep + 1):
            if k == 0:
                here = self.base[self.deep], self.size[self.deep]
            else:
                here = self.sibling(k), self.size[k]
            block = self.at(*here, mine=False)
            remote(block, block, self.fwd.at[k], self.fgot.at[k], self.peer).wait_recv()
            self.c_push(k).wait_send()
            self.c_forward(k).wait_send()
            if k > 0:
                self.c_back(k).wait_send()


class Grouped(Stream):
    def __init__(self, res, acc, rest, sems, order, coords, core, cut, group, across):
        super().__init__(None, res, acc, None, rest, sems, order, coords, core, cut)
        self.group, self.gx, self.across = group, far(group), across

    def at(self, base, size, n=0):
        h = (self.group, self.gx, flip(self.group), far(flip(self.group)))[n]
        return self.res.at[h, self.part(base, size), self.mine]

    def c_across(self):
        here = self.base[self.deep], self.size[self.deep]
        return remote(
            self.acc.at[self.part(*here)],
            self.at(*here),
            self.back.at[self.deep, 0],
            self.got.at[self.deep, 0],
            self.across,
        )

    def c_back(self, k, n):
        here = self.base[k], self.size[k]
        own = k == self.deep and n == 0
        src = self.acc.at[self.part(*here)] if own else self.at(*here, n)
        return remote(
            src, self.at(*here, n), self.back.at[k - 1, n], self.got.at[k - 1, n], self.order[k - 1][1]
        )

    def c_forward(self, k, n):
        if k == 0:
            here = self.base[self.deep], self.size[self.deep]
            src = self.acc.at[self.part(*here)] if n == 0 else self.at(*here, n)
        else:
            here = self.sibling(k), self.size[k]
            src = self.at(*here, n)
        return remote(src, self.at(*here, n), self.fwd.at[k, n], self.fgot.at[k, n], self.peer)

    def fold(self, k):
        if k == 0:
            self.c_push(1).start()
            return
        if k < self.deep:
            super().fold(k)
            return
        self.c_push(k).wait_recv()
        base, size = self.base[k], self.size[k]
        rows = self.part(base, size)
        more = self.rest[pl.ds(self.rows - 2 * size, size), :]
        self.acc[rows, :] = (self.acc[rows, :].astype(F32) + more.astype(F32)).astype(BF)
        self.c_across().start()
        self.c_back(k, 0).start()
        self.c_forward(0, 0).start()
        self.own_out().start()

    def extend(self):
        self.c_across().wait_recv()
        self.c_back(self.deep, 1).start()
        self.c_forward(0, 1).start()

    def collect(self, k):
        here = self.sibling(k), self.size[k]
        if k == self.deep:
            self.own_out().wait()
        for n in range(2):
            block = self.at(*here, n)
            remote(block, block, self.back.at[k - 1, n], self.got.at[k - 1, n], self.peer).wait_recv()
            if k > 1:
                if n == 1:
                    self.c_back(k - 1, 0).start()
                    self.c_back(k - 1, 1).start()
            self.c_forward(k, n).start()

    def close(self):
        self.c_across().wait_send()
        for k in range(self.deep + 1):
            if k == 0:
                here = self.base[self.deep], self.size[self.deep]
            else:
                here = self.sibling(k), self.size[k]
                self.c_push(k).wait_send()
            for n in range(2):
                block = self.at(*here, 2 + n)
                remote(block, block, self.fwd.at[k, n], self.fgot.at[k, n], self.peer).wait_recv()
                self.c_forward(k, n).wait_send()
                if k > 0:
                    self.c_back(k, n).wait_send()


PIECES = {
    "G0": (0, 0, 0, 0, 768, 256, 256, ("x", "zl", "y", "zh")),
    "G1": (0, 1, 0, 512, 768, 256, 256, ("x", "y", "zh", "zl")),
    "G2": (0, 2, 0, 1024, 768, 256, 256, ("y", "x", "zl", "zh")),
    "G3": (0, 3, 0, 1536, 768, 256, 256, ("x", "y", "zl", "zh")),
    "U0": (1, 0, 0, 0, 768, 256, 256, ("y", "x", "zl", "zh")),
    "U1": (1, 1, 0, 512, 768, 256, 256, ("zh", "x", "y", "zl")),
    "U2": (1, 2, 0, 1024, 768, 256, 256, ("zl", "y", "x", "zh")),
    "U3": (1, 3, 0, 1536, 768, 256, 256, ("y", "x", "zl", "zh")),
    "D0": (2, 0, 0, 0, 512, 384, 384, ("x", "y", "zl", "zh")),
    "D1": (2, 1, 512, 0, 512, 384, 384, ("y", "x", "zl", "zh")),
    "D2": (2, 2, 1024, 0, 512, 384, 384, ("y", "x", "zl", "zh")),
    "D3": (2, 3, 1536, 0, 512, 384, 384, ("zl", "x", "y", "zh")),
    "O": (3, 0, 0, 0, 768, 384, 384, ("x", "y", "zl", "zh")),
}
GROUPS = {
    "qA": (0, 256, ("zl", "y", "zh")),
    "qB": (256, 384, ("y", "zl", "zh")),
}
PLAN = (
    "ff", "open.G0", "open.U0", "open.D0", "ff", "open.G1", "open.U1", "open.D1", "fG0.0", "ff",
    "fU0.0", "open.G2", "open.D2", "open.U2", "fG1.0", "fU1.0", "fD0.0", "fD1.0", "ff", "open.D3",
    "open.U3", "open.G3", "fG0.1", "fG2.0", "fD2.0", "fU2.0", "fU0.1", "ffpost", "open.O", "fG0.2",
    "fG3.0", "fG1.1", "res", "fD1.1", "fU1.1", "fU3.0", "fD3.0", "fD0.1", "fU0.2", "fU2.1",
    "fO.0", "fG2.1", "fD2.1", "swap", "tile", "fG0.3", "tile", "fG3.1", "fG1.2", "tile",
    "fD1.2", "fU3.1", "fU0.3", "fU1.2", "fG0.4", "fD0.2", "fD3.1", "tile", "fG1.3", "fU0.4",
    "fD1.3", "fG3.2", "fU2.2", "gG0.4", "fD0.3", "fU1.3", "tile", "gU0.4", "fO.1", "fG1.4",
    "gG0.3", "fG3.3", "fD1.4", "fG2.2", "tile", "gU0.3", "fD2.2", "fU3.2", "gG1.4", "dxn",
    "gD1.4", "fO.2", "gG0.2", "fD3.2", "fU2.3", "fG2.3", "gw", "end", "xsB", "fqA.0",
    "gD1.3", "fqB.0", "gU0.2", "tB", "xsA", "tA", "fO.3", "fD2.3", "fU3.3", "gG0.1",
    "fD3.3", "fU2.4", "fG2.4", "gG1.3", "fqA.1", "fD0.4", "fO.4", "fU3.4", "fqB.1", "gU2.4",
    "zB", "gG2.4", "gD0.4", "fG3.4", "gD1.2", "fD2.4", "gU0.1", "gO.4", "fqB.2", "gU3.4",
    "gG1.2", "fqA.2", "nB", "gG2.3", "fU1.4", "nA", "gD1.1", "gG3.4", "gD0.3", "gO.3",
    "gain.0", "gU2.3", "gD2.4", "fqB.3", "gG1.1", "gU3.3", "gain.1", "fqA.3", "gG2.2", "gD0.2",
    "eqB", "gU1.4", "gU3.2", "gO.2", "gain.2", "eqA", "gU2.2", "fD3.4", "gG3.3", "gD0.1",
    "gG2.1", "gD2.3", "gU1.3", "gU3.1", "gO.1", "gain.3", "gqB.3", "gD2.2", "gG3.2", "gU2.1",
    "gU1.2", "gain.4", "gqA.3", "gD3.4", "gD2.1", "gG3.1", "gqB.2", "gqA.2", "gD3.3", "gU1.1",
    "gain.5", "gD3.2", "gqA.1", "gqB.1", "gD3.1",
)


def layer_kernel(*refs):
    take = iter(refs)

    def some(n):
        return [next(take) for _ in range(n)]

    x_ref, cot_ref, count_ref, gain_ref, wq_ref, wk_ref, wv_ref = some(7)
    gain2_ref, wo_hbm, wg_hbm, wu_hbm, wd_hbm = some(5)
    out_ref, res_out_ref = some(2)
    outs = some(5)
    (gains_out,) = some(1)
    loads_hbm = some(8)
    orecv_ref, dy_ref, xall_ref, osend_ref = some(4)
    front_sems = some(14)
    h_ref, dh_ref, res_ref, dsend_ref, dgain2_ref = some(5)
    both = some(4)
    dense_sem, w_sem, load_sem = some(3)
    (do_ref, p_ref) = some(2)
    (rc_ref, sx_ref, rx_ref, t_ref, zb_ref, rz_ref, ig_ref, dgain_ref) = some(8)
    (c_send, c_recv, x_send, x_recv, z_send, z_recv) = some(6)
    (rs_send, rs_recv, rs_own, h_send, h_recv, h_own, hs, hr, ho) = some(9)
    item, z, g = place()
    gc, gx = flip(g), far(g)
    gcx = far(gc)
    p, r = z // 2, z % 2
    side = g % 2
    coords = {
        "x": (g // 2, (item, z * 4 + gx)),
        "y": (item, (1 - item, z * 4 + g)),
        "zl": (z % 2, (item, flip(z) * 4 + g)),
        "zh": (z // 2, (item, far(z) * 4 + g)),
    }
    across, pair = coords["x"][1], coords["zl"][1]
    core = (item, z * 4 + gc)
    zs = (z, flip(z), far(z), far(flip(z)))
    streams = {}
    for name, (n, m, row, col, _, _, half, order) in PIECES.items():
        first, rest = some(2)
        streams[name] = Stream(
            both[n].at[m, 1 - side], outs[n], both[n].at[m, side], first, rest, some(7), order, coords,
            (side, core), (row, col, half),
        )
    (gw_ref,) = some(1)
    for name, (col, wide, order) in GROUPS.items():
        (rest,) = some(1)
        acc = gw_ref.at[:, pl.ds(col, wide)]
        streams[name] = Grouped(
            outs[4], acc, rest, some(7), order, coords, (side, core), (0, col, 0), g, across
        )
    buf, got, gain_send, gain_recv = some(4)

    greet(g_peers(item, z, g) + z_peers(item, z, g) + [coords["y"][1]])
    swapped = swap_heads(item, z, g, dsend_ref, do_ref, hs, hr, ho.at[0])
    lane = lanes_of(256)
    low = lane < 64
    part = lane % 64

    body, arrive, leave = front_phase(
        (x_ref, cot_ref, count_ref, gain_ref, wq_ref, wk_ref, wv_ref), loads_hbm,
        (orecv_ref, dy_ref, h_ref, xall_ref, osend_ref), front_sems,
    )

    def dense(emit, wo_ref, wg_ref, wu_ref, wd_ref, att_ref, sec_ref, xn_ref, xt_ref, dxn_ref):
        size = 512
        load_wo = pltpu.make_async_copy(wo_hbm, wo_ref, dense_sem.at[0])
        load_wo.start()

        def load(c, n):
            cut = pl.ds(whole(c * size, size), size)
            a, b = ((wg_hbm, wg_ref), (wu_hbm, wu_ref), (wd_hbm, wd_ref))[n]
            a, b = (a.at[:, cut], b.at[:, cut]) if n < 2 else (a.at[cut, :], b.at[cut, :])
            return pltpu.make_async_copy(a, b, w_sem.at[n, c])

        for c in range(4):
            for n in range(3):
                load(c, n).start()
        low = lanes_of(384) < 64

        def swap(v):
            return pltpu.roll(v, 64, 1)

        arrive()
        pairs = [orecv_ref[n, :, 0:64, :].astype(F32).reshape(384, 128) for n in range(4)]

        def unfold(n, high):
            f = orecv_ref[n, :, 64:96, :].astype(F32)
            s = swap(f.reshape(192, 128)).reshape(6, 32, 128)
            two = (s, f) if high else (f, s)
            return jnp.concatenate(two, axis=1).reshape(384, 128)

        tiles = (
            pairs[0],
            jnp.where(low, unfold(0, False), swap(pairs[1])),
            jnp.where(low, swap(pairs[1]), unfold(1, True)),
            pairs[2],
            jnp.where(low, unfold(2, False), swap(pairs[3])),
            jnp.where(low, swap(pairs[3]), unfold(3, True)),
        )
        for n, v in enumerate(tiles):
            att_ref[:, n * 128 : n * 128 + 128] = v.astype(BF)
        load_wo.wait()
        second = h_ref[...].reshape(384, 768).astype(F32) + matmul(att_ref[...], wo_ref[...])
        sec_ref[...] = second
        dh_ref[...] = second.reshape(6, 64, 768)
        inv = lax.rsqrt(jnp.mean(second * second, axis=-1, keepdims=True) + EPS)
        xn_ref[...] = (second * inv * gain2_ref[...].reshape(1, 768)).astype(BF)
        xt_ref[...] = xn_ref[...].T
        dxn_ref[...] = jnp.zeros_like(dxn_ref)

        def chunk(c):
            cut = pl.ds(pl.multiple_of(c * size, size), size)
            for n in range(3):
                load(c, n).wait()
            dy = dy_ref[...].reshape(384, 768)
            gate = matmul(xn_ref[...], wg_ref[:, cut])
            upper = matmul(xn_ref[...], wu_ref[:, cut])
            d_mixed = nt(dy, wd_ref[cut, :])
            square = gate * gate
            tan = jnp.tanh(GELU_C * (gate + GELU_A * square * gate))
            half = 0.5 * (1.0 + tan)
            act = gate * half
            slope = half + 0.5 * gate * (1.0 - tan * tan) * (GELU_C * (1.0 + 3.0 * GELU_A * square))
            mixed = (act * upper).astype(BF)
            d_gate = (d_mixed * upper * slope).astype(BF)
            d_upper = (d_mixed * act).astype(BF)
            for n, grad in enumerate((d_gate, d_upper)):
                full = matmul(xt_ref[...], grad).astype(BF)
                both[n][c, 0] = full[:, : size // 2]
                both[n][c, 1] = full[:, size // 2 :]
            down = outer(mixed, dy).astype(BF)
            both[2][c, 0] = down[:, :384]
            both[2][c, 1] = down[:, 384:]
            sec_ref[...] += matmul(mixed, wd_ref[cut, :])
            dxn_ref[...] += nt(d_gate, wg_ref[:, cut]) + nt(d_upper, wu_ref[:, cut])

        run_loop("ff", 4, chunk, emit)
        emit_between("ff", "ffpost")
        res_ref[...] = sec_ref[...].astype(BF).reshape(6, 64, 768)
        second = dh_ref[...].reshape(384, 768)
        inv = lax.rsqrt(jnp.mean(second * second, axis=-1, keepdims=True) + EPS)
        d_xn = dxn_ref[...]
        dgain2_ref[...] = jnp.sum(d_xn * second * inv, axis=0, keepdims=True)
        dyg = d_xn * gain2_ref[...].reshape(1, 768)
        dot = jnp.mean(dyg * second, axis=-1, keepdims=True)
        dy = dy_ref[...].reshape(384, 768)
        d_second = dy.astype(F32) + inv * dyg - second * (inv * inv * inv * dot)
        dh_ref[...] = d_second.reshape(6, 64, 768)
        d_branch = d_second.astype(BF)
        d_att = nt(d_branch, wo_ref[...]).astype(BF).astype(F32)
        d = [d_att[:, n * 128 : n * 128 + 128] for n in range(6)]
        firsts = (d[0], swap(jnp.where(low, d[2], d[1])), d[3], swap(jnp.where(low, d[5], d[4])))
        lasts = ((d[1], False), (d[2], True), (d[4], False), (d[5], True))
        low3 = lax.broadcasted_iota(jnp.int32, (6, 32, 128), 2) < 64
        for n in range(4):
            dsend_ref[n, :, 0:64, :] = firsts[n].astype(BF).reshape(6, 64, 128)
            v, high = lasts[n]
            v3, s3 = v.reshape(6, 64, 128), swap(v).reshape(6, 64, 128)
            top, bottom = v3[:, :32], v3[:, 32:]
            top_s, bottom_s = s3[:, :32], s3[:, 32:]
            f = jnp.where(low3, top_s, bottom) if high else jnp.where(low3, top, bottom_s)
            dsend_ref[n, :, 64:96, :] = f.astype(BF)
        swapped.start()
        g_out = outer(att_ref[...], d_branch).astype(BF)
        both[3][0, 0] = g_out[:, :384]
        both[3][0, 1] = g_out[:, 384:]

    def pieces(delta):
        neg = -delta
        hi = neg.astype(BF).astype(F32)
        mid = (neg - hi).astype(BF).astype(F32)
        lo = neg - hi - mid
        return jnp.where(part == 1, hi, jnp.where(part == 2, mid, jnp.where(part == 3, lo, 0.0)))

    loads = {}

    def tile(t):
        q_ref, k_ref, v_ref, kt_ref, o01_ref, o2_ref = (loads[n] for n in range(6))
        dk_ref, dv_ref, d5_ref = (loads[n] for n in ("dk", "dv", "d5"))
        at = pl.ds(pl.multiple_of(t * 256, 256), 256)
        ab = t // 4
        keys = pl.ds(pl.multiple_of(ab * 1024, 1024), 1024)
        do01 = do_ref[:, t, 0:64, :].astype(F32).reshape(256, 128)
        folded = do_ref[:, t, 64:96, :].astype(F32)
        two = []
        for h in range(4):
            two.append(pltpu.roll(folded[h], 64, 1))
            two.append(folded[h])
        do2 = jnp.concatenate(two, axis=0)
        prod = do01 * o01_ref[at, :]
        prod2 = do2 * o2_ref[at, :]
        delta0 = jnp.sum(jnp.where(low, prod, 0.0), axis=1, keepdims=True)
        delta1 = jnp.sum(jnp.where(low, 0.0, prod), axis=1, keepdims=True)
        delta2 = jnp.sum(jnp.where(low, 0.0, prod2), axis=1, keepdims=True)
        dos = (
            jnp.where(low, do01, pieces(delta0)).astype(BF),
            jnp.where(low, pieces(delta1), do01).astype(BF),
            jnp.where(low, pieces(delta2), do2).astype(BF),
        )
        dqs = []
        for head in range(3):
            q = q_ref[head, at, :]
            prob = jnp.exp(nt(k_ref[head, keys, :], q))
            d_prob = nt(v_ref[head, keys, :], dos[head])
            d_log = (prob * d_prob).astype(BF)
            dv_ref[head, keys, :] += matmul(prob.astype(BF), dos[head])
            dk_ref[head, keys, :] += matmul(d_log, q)
            dqs.append(matmul(kt_ref[head, ab], d_log).T * 0.125)
        off = jnp.where(t < 4, t, 4 + r + 2 * (t - 4)) * 256
        rows = pl.ds(pl.multiple_of(off, 256), 256)
        d5_ref[rows, 0:128] = jnp.where(low, dqs[0], dqs[1]).astype(BF)
        d5_ref[rows, 512:640] = jnp.where(low, dqs[2], 0.0).astype(BF)

    halves = ((0, slice(0, 4)), (1, slice(4, 8)))
    away = (gc, gcx)

    def c_copy(k, ab):
        cut = halves[ab][1]
        return remote(p_ref.at[away[k], cut], rc_ref.at[k, cut], c_send.at[k, ab], c_recv.at[k, ab], core)

    def x_copy(ab):
        cut = halves[ab][1]
        return remote(sx_ref.at[cut], rx_ref.at[cut], x_send.at[ab], x_recv.at[ab], across)

    z_copy = remote(zb_ref, rz_ref, z_send.at[0], z_recv.at[0], pair)
    mine = 3 * p + 2 * r

    def home(n):
        if n < 4:
            s = (zs[3], zs[2], zs[1], z)[n]
            src, dst = ig_ref.at[s], out_ref.at[mine]
        else:
            s = z if n == 5 else zs[2]
            src, dst = ig_ref.at[4 + (1 - p if n == 4 else p)], out_ref.at[3 * p + 1]
        if n in (3, 5):
            return pltpu.make_async_copy(src, dst, h_own.at[n // 4])
        where = mine if n < 4 else 3 * p + 1
        return remote(src, dst, h_send.at[min(n, 3)], h_recv.at[where], (item, s * 4 + g))

    gain = gain_ref[...].reshape(1, 768)

    def norm_back(d_xn, j):
        h = h_ref[j].astype(F32)
        inv = lax.rsqrt(jnp.mean(h * h, axis=-1, keepdims=True) + EPS)
        dgain_ref[...] += jnp.sum(d_xn * h * inv, axis=0, keepdims=True)
        dyg = d_xn * gain
        dot = jnp.mean(dyg * h, axis=-1, keepdims=True)
        ig_ref[j] = (dh_ref[j] + inv * dyg - h * (inv * inv * inv * dot)).astype(BF)

    def load_copy(n):
        return pltpu.make_async_copy(loads_hbm[n], loads[n], load_sem.at[n])

    def run_swap():
        for n in range(8):
            load_copy(n).wait()
        swapped.finish()

    def run_dxn():
        wc_ref, dk_ref, dv_ref, d5_ref = (loads[n] for n in (7, "dk", "dv", "d5"))

        @pl.loop(0, 8)
        def _(i):
            rows = pl.ds(pl.multiple_of(i * 256, 256), 256)
            d5_ref[rows, 128:256] = jnp.where(low, dk_ref[0, rows, :], dk_ref[1, rows, :]).astype(BF)
            d5_ref[rows, 256:384] = jnp.where(low, dv_ref[0, rows, :], dv_ref[1, rows, :]).astype(BF)
            d5_ref[rows, 384:512] = jnp.where(low, dk_ref[2, rows, :], dv_ref[2, rows, :]).astype(BF)
            d_xn = nt(d5_ref[rows, :], wc_ref[...]).astype(BF)
            for h in range(4):
                p_ref[h, i, :, :] = d_xn[h * 64 : h * 64 + 64]

        for k in (1, 0):
            for ab in (1, 0):
                c_copy(k, ab).start()

    def run_gw():
        for c in range(5):
            cols = slice(c * 128, c * 128 + 128)
            gw_ref[:, cols] = outer(loads[6][...], loads["d5"][:, cols]).astype(BF)

    def run_xs(ab):
        c_copy(1, ab).wait_recv()

        @pl.loop(0, 4)
        def _(j):
            n = ab * 4 + j
            sx_ref[n] = (p_ref[gx, n].astype(F32) + rc_ref[1, n].astype(F32)).astype(BF)

        x_copy(ab).start()

    def run_t(ab):
        c_copy(0, ab).wait_recv()

        @pl.loop(0, 4)
        def _(j):
            n = ab * 4 + j
            t_ref[n] = p_ref[g, n].astype(F32) + rc_ref[0, n].astype(F32)

    def run_z():
        x_copy(1).wait_recv()
        for q in range(2):
            n = 4 + (1 - r) + 2 * q
            zb_ref[q] = (t_ref[n] + rx_ref[n].astype(F32)).astype(BF)
        z_copy.start()

    def run_na():
        x_copy(0).wait_recv()
        for n, s in enumerate((zs[3], zs[2], zs[1], z)):
            norm_back(t_ref[s] + rx_ref[s].astype(F32), s)
            home(n).start()

    def run_nb():
        z_copy.wait_recv()
        for n, q in enumerate((1 - p, p)):
            k = 4 + r + 2 * q
            norm_back(t_ref[k] + rx_ref[k].astype(F32) + rz_ref[q].astype(F32), 4 + q)
            home(4 + n).start()

    gain_peers = [core] + [peer for _, peer in coords.values()]

    def gain_copy(k):
        return remote(buf.at[k], got.at[k], gain_send.at[k], gain_recv.at[k], gain_peers[k])

    def run_gain(k):
        if k == 0:
            buf[0] = jnp.zeros_like(buf[0])
            buf[0, 0:1, :] = dgain_ref[...]
            buf[0, 1:2, :] = dgain2_ref[...]
        else:
            gain_copy(k - 1).wait_recv()
            buf[k] = buf[k - 1] + got[k - 1]
        if k < 5:
            gain_copy(k).start()
        else:
            gains_out[...] = buf[5]

    homes = from_slots(item, z, g, res_ref, res_out_ref, rs_send, rs_recv, rs_own)

    single = {
        "swap": run_swap, "dxn": run_dxn, "gw": run_gw, "xsB": lambda: run_xs(1), "xsA": lambda: run_xs(0),
        "tB": lambda: run_t(1), "tA": lambda: run_t(0), "zB": run_z, "nA": run_na, "nB": run_nb, "res": homes.start,
    }

    def emit(task):
        if task in single:
            single[task]()
            return
        head, _, k = task.partition(".")
        if head == "gain":
            run_gain(int(k))
        elif head[0] == "f":
            streams[head[1:]].fold(int(k))
        elif head == "open":
            streams[k].open()
        elif head[0] == "g":
            streams[head[1:]].collect(int(k))
        else:
            streams[head[1:]].extend()

    def run_loop(name, count, body, emit):
        at = [n for n, task in enumerate(PLAN) if task == name]

        @pl.loop(0, count)
        def _(t):
            body(t)
            for n in range(count - 1):
                tasks = PLAN[at[n] + 1 : at[n + 1]]
                if tasks:

                    @pl.when(t == n)
                    def _():
                        for task in tasks:
                            emit(task)

    def emit_between(first, last):
        start = 0 if first is None else len(PLAN) - PLAN[::-1].index(first)
        stop = len(PLAN) if last is None else PLAN.index(last)
        for task in PLAN[start:stop]:
            emit(task)

    width, hidden = wg_hbm.shape
    v = pltpu.VMEM
    kept = [v(ref.shape, ref.dtype) for ref in loads_hbm]
    pl.run_scoped(body, v((3, width, 256), BF), *kept)
    pl.run_scoped(
        functools.partial(dense, emit),
        v((width, width), BF), v((width, hidden), BF), v((width, hidden), BF), v((hidden, width), BF),
        v((384, width), BF), v((384, width), F32), v((384, width), BF),
        v((width, 384), BF), v((384, width), F32),
    )

    def attend(*scoped):
        loads.update(enumerate(scoped[:8]))
        loads.update(zip(("dk", "dv", "d5"), scoped[8:]))
        for n in range(8):
            load_copy(n).start()
        for n in ("dk", "dv", "d5"):
            loads[n][...] = jnp.zeros_like(loads[n])
        dgain_ref[...] = jnp.zeros_like(dgain_ref)
        emit_between("ffpost", "tile")
        run_loop("tile", 6, tile, emit)
        emit_between("tile", "end")

    pl.run_scoped(
        attend,
        *kept,
        v((3, 2048, 128), F32), v((3, 2048, 128), F32), v((2048, 640), BF),
    )
    emit_between("end", None)

    for s in zs[1:]:
        where = 3 * (s // 2) + 2 * (s % 2)
        remote(ig_ref.at[0], out_ref.at[where], h_send.at[0], h_recv.at[where], pair).wait_recv()
    where = 3 * (1 - p) + 1
    remote(ig_ref.at[0], out_ref.at[where], h_send.at[0], h_recv.at[where], pair).wait_recv()
    homes.finish()
    leave()
    home(3).wait()
    home(5).wait()
    for stream in streams.values():
        stream.close()
    for n in (0, 1, 2, 4):
        home(n).wait_send()
    z_copy.wait_send()
    for ab in range(2):
        x_copy(ab).wait_send()
        for k in range(2):
            c_copy(k, ab).wait_send()
    for k in range(5):
        gain_copy(k).wait_send()


def layer(x6, cot6, counts, gain1, wq, wk, wv, gain2, w_out, w_gate, w_up, w_down):
    dma = pltpu.SemaphoreType.DMA
    s = jax.ShapeDtypeStruct
    v = pltpu.VMEM
    rows_shape = x6.shape
    _, rows, width = rows_shape
    heads = (4, 6, 96, 128)
    gains = (8, width)
    group = (width, 640)
    outs = (s(rows_shape, BF), s(rows_shape, BF)) + tuple(s(a.shape, BF) for a in (w_gate, w_up, w_down, w_out))
    outs += (s((4,) + group, BF), s(gains, F32))
    outs += (
        s((3, 1536, 128), BF), s((3, 2048, 128), BF), s((3, 2048, 128), BF), s((3, 2, 128, 1024), BF),
        s((1536, 128), F32), s((1536, 128), F32), s((2048, width), BF), s(group, BF),
    )
    scratch = [
        v(heads, BF), v(rows_shape, BF), v((2, 16, rows, width), BF), v(heads, BF),
        dma((3, 2)), dma((4, 2, 2)), dma((4, 2)), dma((2, 16)), dma((2,)), dma((3,)),
        dma((6, 3)), dma((4, 6)), dma((4,)), dma((6,)), dma((2,)), dma((2, 4)), dma((6, 4)), dma((7,)),
        v(rows_shape, BF), v(rows_shape, F32), v(rows_shape, BF), v(heads, BF), v((1, width), F32),
        v((4, 2, width, 256), BF), v((4, 2, width, 256), BF), v((4, 2, 512, width // 2), BF), v((1, 2, width, width // 2), BF),
        dma((4,)), dma((3, 4)), dma((8,)),
        v(heads, BF), v((4, 8, rows, width), BF),
        v((2, 8, rows, width), BF), v((8, rows, width), BF), v((8, rows, width), BF),
        v((8, rows, width), F32), v((2, rows, width), BF), v((2, rows, width), BF), v((6, rows, width), BF),
        v((1, width), F32),
        dma((2, 2)), dma((2, 2)), dma((2,)), dma((2,)), dma((1,)), dma((1,)), dma((4,)), dma((6,)), dma((2,)),
        dma((4,)), dma((6,)), dma((2,)), dma((3,)), dma((4,)), dma((1,)),
    ]
    for _, _, _, _, high, wide, _, _ in PIECES.values():
        scratch += [v((high, wide), BF)] * 2
        scratch += [dma((5,)), dma((5,)), dma((2,)), dma((4,)), dma((4,)), dma((5,)), dma((5,))]
    scratch += [v(group, BF)]
    for _, wide, _ in GROUPS.values():
        scratch += [v((width, wide), BF)]
        scratch += [dma((4,)), dma((4,)), dma((2,)), dma((4, 2)), dma((4, 2)), dma((4, 2)), dma((4, 2))]
    scratch += [v((6,) + gains, F32), v((5,) + gains, F32), dma((5,)), dma((5,))]
    return pl.pallas_call(
        layer_kernel,
        out_shape=outs,
        in_specs=[ANY, ANY, SMEM, VMEM, ANY, ANY, ANY, VMEM] + [ANY] * 4,
        out_specs=(ANY,) * 7 + (VMEM,) + (ANY,) * 8,
        scratch_shapes=scratch,
        compiler_params=params(1, 63),
        name="layer",
    )(x6, cot6, counts, gain1, wq, wk, wv, gain2, w_out, w_gate, w_up, w_down)


def fast(
    inputs, counts, norm_gain1, w_query, w_key, w_value, w_out, norm_gain2, w_gate, w_up, w_down, cotangent
):
    band_rows, width = inputs.shape[2:]
    input_grads, results, s_gate, s_up, s_down, s_out, s_qkv, s_gains, *_ = layer(
        inputs.reshape(6, band_rows, width), cotangent.reshape(6, band_rows, width), counts, norm_gain1,
        w_query, w_key, w_value, norm_gain2, w_out, w_gate, w_up, w_down,
    )
    *grads, gain1, gain2, results, input_grads = widen(
        s_qkv, s_out, s_gate, s_up, s_down, s_gains, results, input_grads
    )
    return (
        results.reshape(inputs.shape), input_grads.reshape(inputs.shape), gain1, *grads[:4], gain2, *grads[4:]
    )


def program(*args):
    micro, seqs, band_rows, width = args[0].shape
    small = lax.axis_size("band") == 16 and lax.axis_size("items") == 2
    if small and (micro, seqs, band_rows, width, HEADS, HEAD_DIM) == (2, 3, 64, 768, 12, 64):
        return fast(*args)
    return per_device(*args)


def solution(mesh):
    return jax.shard_map(
        program,
        mesh=mesh,
        in_specs=(
            P(None, "items", "band", None),
            P(None, "items"),
            P(),
            P(),
            P(),
            P(),
            P(),
            P(),
            P(),
            P(),
            P(),
            P(None, "items", "band", None),
        ),
        out_specs=(
            P(None, "items", "band", None),
            P(None, "items", "band", None),
            P(),
            P(),
            P(),
            P(),
            P(),
            P(),
            P(),
            P(),
            P(),
        ),
        check_vma=False,
    )
```

```python
import functools
import math

import jax
import jax.numpy as jnp
from jax import lax
from jax.experimental import pallas as pl
from jax.experimental.pallas import tpu as pltpu
from jax.sharding import PartitionSpec as P

HEADS = 12
HEAD_DIM = 64


EPS = 1e-06


def shortened(shard):

    def short(part):
        return part.astype(jnp.bfloat16) if part.dtype == jnp.float32 else part

    return jax.tree.map(short, shard)


def rms_scale(values, gain):
    return values * lax.rsqrt(jnp.mean(values * values, axis=-1, keepdims=True) + EPS) * gain


def gated(gate, upper):
    return jax.nn.gelu(gate, approximate=True) * upper


def outer(left, right):
    return lax.dot_general(
        left, right, (((0,), (0,)), ((), ())), preferred_element_type=jnp.float32
    )


def transposed(left, weight):
    return lax.dot_general(
        left, weight, (((1,), (1,)), ((), ())), preferred_element_type=jnp.float32
    )


def matmul(left, right):
    return jnp.dot(left, right, preferred_element_type=jnp.float32)


def scores(query, key, scale):
    return jnp.einsum("sqhd,skhd->shqk", query, key, preferred_element_type=jnp.float32) * scale


def per_device(
    inputs,
    counts,
    norm_gain1,
    w_query,
    w_key,
    w_value,
    w_out,
    norm_gain2,
    w_gate,
    w_up,
    w_down,
    cotangent,
):
    micro, seqs, band_rows, width = inputs.shape
    bands = lax.axis_size("band")
    length = band_rows * bands
    rows = seqs * band_rows
    heads = HEADS
    head_dim = HEAD_DIM
    scale = 1.0 / math.sqrt(head_dim)
    key_place = jnp.arange(length, dtype=jnp.int32)
    params = (norm_gain1, w_query, w_key, w_value, w_out, norm_gain2, w_gate, w_up, w_down)
    totals = [jnp.zeros(p.shape, jnp.float32) for p in params]
    results = []
    input_grads = []
    for number in range(micro):
        hidden = inputs[number].astype(jnp.float32).reshape(rows, width)
        lengths = counts[number]
        normed = rms_scale(hidden, norm_gain1).astype(jnp.bfloat16)
        query = matmul(normed, w_query).astype(jnp.bfloat16)
        key_local = matmul(normed, w_key).astype(jnp.bfloat16)
        value_local = matmul(normed, w_value).astype(jnp.bfloat16)
        query_four = query.reshape(seqs, band_rows, heads, head_dim)
        key_three = key_local.reshape(seqs, band_rows, width)
        value_three = value_local.reshape(seqs, band_rows, width)
        key_all, value_all = (
            lax.all_gather(key_three, "band", axis=1, tiled=True),
            lax.all_gather(value_three, "band", axis=1, tiled=True),
        )
        live = key_place[None, :] < lengths[:, None]
        key_four = key_all.reshape(seqs, length, heads, head_dim)
        value_four = value_all.reshape(seqs, length, heads, head_dim)
        logits = jnp.where(live[:, None, None, :], scores(query_four, key_four, scale), -jnp.inf)
        top = jnp.max(logits, axis=-1, keepdims=True)
        expo = jnp.exp(logits - top)
        summed = jnp.sum(expo, axis=-1, keepdims=True)
        log_total = top + jnp.log(summed)
        prob = (expo / summed).astype(jnp.bfloat16)
        attended = jnp.einsum(
            "shqk,skhd->sqhd", prob, value_four, preferred_element_type=jnp.float32
        )
        attended = attended.reshape(rows, width).astype(jnp.bfloat16)
        second = hidden + matmul(attended, w_out)
        normed_two = rms_scale(second, norm_gain2).astype(jnp.bfloat16)
        gate = matmul(normed_two, w_gate)
        upper = matmul(normed_two, w_up)
        mixed = gated(gate, upper).astype(jnp.bfloat16)
        results.append(
            (second + matmul(mixed, w_down)).astype(jnp.bfloat16).reshape(seqs, band_rows, width)
        )
        grad_rows = cotangent[number].reshape(rows, width)
        totals[8] = totals[8] + outer(mixed, grad_rows)
        d_mixed = transposed(grad_rows, w_down)
        pull_gate = jax.vjp(gated, gate, upper)[1]
        d_gate, d_upper = pull_gate(d_mixed)
        d_gate = d_gate.astype(jnp.bfloat16)
        d_upper = d_upper.astype(jnp.bfloat16)
        totals[6] = totals[6] + outer(normed_two, d_gate)
        totals[7] = totals[7] + outer(normed_two, d_upper)
        d_normed_two = transposed(d_gate, w_gate) + transposed(d_upper, w_up)
        pull_two = jax.vjp(rms_scale, second, norm_gain2)[1]
        d_second_norm, d_gain_two = pull_two(d_normed_two)
        totals[5] = totals[5] + d_gain_two
        d_second = grad_rows.astype(jnp.float32) + d_second_norm
        d_branch = d_second.astype(jnp.bfloat16)
        totals[4] = totals[4] + outer(attended, d_branch)
        d_attended = transposed(d_branch, w_out).astype(jnp.bfloat16)
        d_att_four = d_attended.reshape(seqs, band_rows, heads, head_dim)
        key_all, value_all = (
            lax.all_gather(key_three, "band", axis=1, tiled=True),
            lax.all_gather(value_three, "band", axis=1, tiled=True),
        )
        key_four = key_all.reshape(seqs, length, heads, head_dim)
        value_four = value_all.reshape(seqs, length, heads, head_dim)
        logits = jnp.where(live[:, None, None, :], scores(query_four, key_four, scale), -jnp.inf)
        prob_full = jnp.exp(logits - log_total)
        prob = prob_full.astype(jnp.bfloat16)
        d_prob = jnp.einsum(
            "sqhd,skhd->shqk", d_att_four, value_four, preferred_element_type=jnp.float32
        )
        delta = jnp.sum(d_prob * prob_full, axis=-1, keepdims=True)
        d_logits = (prob_full * (d_prob - delta)).astype(jnp.bfloat16)
        d_query = (
            jnp.einsum("shqk,skhd->sqhd", d_logits, key_four, preferred_element_type=jnp.float32)
            * scale
        )
        d_query = d_query.reshape(rows, width).astype(jnp.bfloat16)
        d_key_all = (
            jnp.einsum("shqk,sqhd->skhd", d_logits, query_four, preferred_element_type=jnp.float32)
            * scale
        )
        d_value_all = jnp.einsum(
            "shqk,sqhd->skhd", prob, d_att_four, preferred_element_type=jnp.float32
        )
        d_key_three, d_value_three = (
            lax.psum_scatter(
                d_key_all.reshape(seqs, length, width).astype(jnp.bfloat16),
                "band",
                scatter_dimension=1,
                tiled=True,
            ).astype(jnp.float32),
            lax.psum_scatter(
                d_value_all.reshape(seqs, length, width).astype(jnp.bfloat16),
                "band",
                scatter_dimension=1,
                tiled=True,
            ).astype(jnp.float32),
        )
        d_key = d_key_three.reshape(rows, width).astype(jnp.bfloat16)
        d_value = d_value_three.reshape(rows, width).astype(jnp.bfloat16)
        totals[1] = totals[1] + outer(normed, d_query)
        totals[2] = totals[2] + outer(normed, d_key)
        totals[3] = totals[3] + outer(normed, d_value)
        d_normed = (
            transposed(d_query, w_query) + transposed(d_key, w_key) + transposed(d_value, w_value)
        )
        pull_one = jax.vjp(rms_scale, hidden, norm_gain1)[1]
        d_hidden_norm, d_gain_one = pull_one(d_normed)
        totals[0] = totals[0] + d_gain_one
        input_grads.append(
            (d_second + d_hidden_norm).astype(jnp.bfloat16).reshape(seqs, band_rows, width)
        )
    shares = jax.tree.map(
        lambda part: part.astype(jnp.float32),
        lax.psum_scatter(shortened(tuple(totals)), "band", scatter_dimension=0, tiled=True),
    )
    summed_shares = jax.tree.map(
        lambda part: part.astype(jnp.float32), lax.psum(shortened(shares), "items")
    )
    whole = jax.tree.map(
        lambda part, own: part.astype(own.dtype),
        lax.all_gather(shortened(summed_shares), "band", axis=0, tiled=True),
        summed_shares,
    )
    return (jnp.stack(results), jnp.stack(input_grads)) + tuple(whole)


MESH_ID = pl.DeviceIdType.MESH
NEG = -1e30
BF = jnp.bfloat16
F32 = jnp.float32


def place():
    item = lax.axis_index("items")
    band = lax.axis_index("band")
    return item, band // 4, band % 4


def flip(value):
    return value + 1 - 2 * (value % 2)


def far(value):
    return (value + 2) % 4


def greet(peers):
    barrier = pltpu.get_barrier_semaphore()
    for peer in peers:
        pl.semaphore_signal(barrier, inc=1, device_id=peer, device_id_type=MESH_ID)
    pl.semaphore_wait(barrier, len(peers))


def remote(src, dst, send, recv, peer):
    return pltpu.make_async_remote_copy(
        src_ref=src, dst_ref=dst, send_sem=send, recv_sem=recv, device_id=peer, device_id_type=MESH_ID
    )


def params(number, vmem=62):
    return pltpu.CompilerParams(
        collective_id=number, has_side_effects=True, vmem_limit_bytes=vmem << 20
    )


def whole(value, unit):
    return value if isinstance(value, int) else pl.multiple_of(value, unit)


def lanes_of(rows):
    return lax.broadcasted_iota(jnp.int32, (rows, 128), 1)


ANY = pl.BlockSpec(memory_space=pl.ANY)
VMEM = pl.BlockSpec(memory_space=pltpu.VMEM)
SMEM = pl.BlockSpec(memory_space=pltpu.SMEM)


class Moves:
    def __init__(self):
        self.remotes, self.locals, self.arrivals = [], [], []

    def start(self):
        for make in self.remotes + self.locals:
            make().start()

    def finish(self):
        for make in self.arrivals:
            make().wait_recv()
        for make in self.locals:
            make().wait()
        for make in self.remotes:
            make().wait_send()


def to_slots(item, z, g, src_ref, dst_ref, send, recv, own_sem):
    zs = (z, flip(z), far(z), far(flip(z)))
    p, r = z // 2, z % 2
    moves = Moves()

    def out(n):
        if n < 3:
            s = zs[n + 1]
            src, where = src_ref.at[3 * (s // 2) + 2 * (s % 2)], z
        else:
            s = far(z)
            src, where = src_ref.at[3 * (1 - p) + 1], 4 + p
        return remote(src, dst_ref.at[where], send.at[n], recv.at[where], (item, s * 4 + g))

    def came(where):
        block = dst_ref.at[where]
        return remote(block, block, send.at[0], recv.at[where], (item, far(z) * 4 + g))

    moves.remotes = [lambda n=n: out(n) for n in range(4)]
    moves.locals = [
        lambda: pltpu.make_async_copy(src_ref.at[3 * p + 2 * r], dst_ref.at[z], own_sem.at[0]),
        lambda: pltpu.make_async_copy(src_ref.at[3 * p + 1], dst_ref.at[4 + p], own_sem.at[1]),
    ]
    moves.arrivals = [lambda w=w: came(w) for w in zs[1:] + (4 + (1 - p),)]
    return moves


def from_slots(item, z, g, src_ref, dst_ref, send, recv, own_sem):
    zs = (z, flip(z), far(z), far(flip(z)))
    p, r = z // 2, z % 2
    mine = 3 * p + 2 * r
    moves = Moves()

    def out(n):
        s = zs[n + 1] if n < 3 else far(z)
        src, where = (src_ref.at[s], mine) if n < 3 else (src_ref.at[4 + (1 - p)], 3 * p + 1)
        return remote(src, dst_ref.at[where], send.at[n], recv.at[where], (item, s * 4 + g))

    def came(where):
        block = dst_ref.at[where]
        return remote(block, block, send.at[0], recv.at[where], (item, far(z) * 4 + g))

    moves.remotes = [lambda n=n: out(n) for n in range(4)]
    moves.locals = [
        lambda: pltpu.make_async_copy(src_ref.at[z], dst_ref.at[mine], own_sem.at[0]),
        lambda: pltpu.make_async_copy(src_ref.at[4 + p], dst_ref.at[3 * p + 1], own_sem.at[1]),
    ]
    theirs = [3 * (s // 2) + 2 * (s % 2) for s in zs[1:]] + [3 * (1 - p) + 1]
    moves.arrivals = [lambda w=w: came(w) for w in theirs]
    return moves


def z_peers(item, z, g):
    return [(item, s * 4 + g) for s in (flip(z), far(z), far(flip(z)))]


def g_peers(item, z, g):
    return [(item, z * 4 + h) for h in (flip(g), far(g), far(flip(g)))]


def swap_heads(item, z, g, src_ref, dst_ref, send, recv, own_sem):
    moves = Moves()

    def out(n, h):
        return remote(src_ref.at[h], dst_ref.at[g], send.at[n], recv.at[g], (item, z * 4 + h))

    def came(h):
        return remote(dst_ref.at[h], dst_ref.at[h], send.at[0], recv.at[h], (item, z * 4 + h))

    moves.remotes = [lambda n=n, h=h: out(n, h) for n, h in enumerate((far(g), far(flip(g)), flip(g)))]
    moves.locals = [lambda: pltpu.make_async_copy(src_ref.at[g], dst_ref.at[g], own_sem)]
    moves.arrivals = [lambda h=h: came(h) for h in (flip(g), far(g), far(flip(g)))]
    return moves


def nt(left, right):
    return lax.dot_general(left, right, (((1,), (1,)), ((), ())), preferred_element_type=F32)


def front_phase(ins, outs, landing, sems):
    x_ref, cot_ref, count_ref, gain_ref, wq_ref, wk_ref, wv_ref = ins
    q_out, k_out, v_out, kt_out, o01_out, o2_out, xn_out, wc_out = outs
    orecv_ref, dy_ref, hid_ref, xall_ref, osend_ref = landing
    (
        z_send, f_send, g_send, recv, own_sem, win_sem, o_send, o_recv, cot_send, cot_recv, cot_own,
        half_sem, tile_sem, last_sem,
    ) = sems
    item, z, g = place()
    p, r = z // 2, z % 2
    gc, gx = flip(g), far(g)
    gcx = far(gc)
    zs = (z, flip(z), far(z), far(flip(z)))
    core, across = (item, z * 4 + gc), (item, z * 4 + gx)
    lane = lanes_of(256)
    low = lane < 64

    def items_of(s):
        return (3 * (s // 2) + 2 * (s % 2), 3 * (s // 2) + 1)

    started = []

    def go(make):
        make().start()
        started.append(make)

    def forward(n, ab):
        def make(k, peer):
            where = zs[n] * 4 + g
            src = x_ref.at[items_of(z)[ab]] if n == 0 else xall_ref.at[ab, where]
            return remote(src, xall_ref.at[ab, where], f_send.at[n, ab, k], recv.at[ab, where], peer)

        go(lambda: make(0, across))
        go(lambda: make(1, core))

    def arrived(ab, where):
        block = xall_ref.at[ab, where]
        remote(block, block, z_send.at[0, 0], recv.at[ab, where], core).wait_recv()

    def send_z(ab):
        for n, s in enumerate(zs[1:]):
            go(
                lambda n=n, s=s: remote(
                    x_ref.at[items_of(s)[ab]],
                    xall_ref.at[ab, z * 4 + g],
                    z_send.at[n, ab],
                    recv.at[ab, z * 4 + g],
                    (item, s * 4 + g),
                )
            )

    def own_copy(ab):
        return pltpu.make_async_copy(x_ref.at[items_of(z)[ab]], xall_ref.at[ab, z * 4 + g], own_sem.at[ab])

    def forward_z(ab, n):
        arrived(ab, zs[n] * 4 + g)
        forward(n, ab)

    def forward_x(ab, n):
        def make():
            where = zs[n] * 4 + gx
            block = xall_ref.at[ab, where]
            return remote(block, block, g_send.at[n, ab], recv.at[ab, where], core)

        arrived(ab, zs[n] * 4 + gx)
        go(make)

    def o_copy(t, k):
        h = (gx, gcx, gc)[k]
        return remote(
            osend_ref.at[h, t], orecv_ref.at[g, t], o_send.at[t, k], o_recv.at[g, t], (item, z * 4 + h)
        )

    def self_copy(t):
        return pltpu.make_async_copy(osend_ref.at[g, t], orecv_ref.at[g, t], tile_sem.at[t, 3])

    def block_copy(j):
        src = xall_ref.at[0, j * 4 + g] if j < 4 else xall_ref.at[1, (r + 2 * (j - 4)) * 4 + g]
        return pltpu.make_async_copy(src, hid_ref.at[j], last_sem.at[j])

    moved = to_slots(item, z, g, cot_ref, dy_ref, cot_send, cot_recv, cot_own)

    def arrive():
        for t in range(6):
            for h in (gx, gcx, gc):
                block = orecv_ref.at[h, t]
                remote(block, block, o_send.at[0, 0], o_recv.at[h, t], core).wait_recv()
            self_copy(t).wait()
        moved.finish()

    def leave():
        for t in range(6):
            for k in range(3):
                o_copy(t, k).wait_send()
        for make in started:
            make().wait_send()

    def body(win_ref, q_ref, k_ref, v_ref, kt_ref, o01_ref, o2_ref, xn_ref, wc_ref):
        send_z(0)
        forward(0, 0)
        send_z(1)
        forward(0, 1)
        cut = pl.ds(pl.multiple_of(g * 3 // 2 * 128, 128), 256)
        windows = []
        for n, ref in enumerate((wq_ref, wk_ref, wv_ref)):
            windows.append(pltpu.make_async_copy(ref.at[:, cut], win_ref.at[n], win_sem.at[n]))

        for copy in windows + [own_copy(0), own_copy(1)]:
            copy.start()
        for copy in windows:
            copy.wait()
        odd = g % 2 == 1

        @pl.loop(0, 3)
        def _(i):
            rows = pl.ds(pl.multiple_of(i * 256, 256), 256)
            firsts, lasts = [], []
            for n in range(3):
                left = win_ref[n, rows, 0:128].astype(F32)
                right = win_ref[n, rows, 128:256].astype(F32)
                crossed = pltpu.roll(jnp.where(low, right, left), 64, 1)
                firsts.append(jnp.where(odd, crossed, left))
                lasts.append(jnp.where(odd, pltpu.roll(right, 64, 1), right))
            for n in range(3):
                wc_ref[rows, n * 128 : n * 128 + 128] = firsts[n].astype(BF)
            wc_ref[rows, 384:512] = jnp.where(low, lasts[1], pltpu.roll(lasts[2], 64, 1)).astype(BF)
            wc_ref[rows, 512:640] = jnp.where(low, lasts[0], 0.0).astype(BF)

        def project(ab, n):
            zz = zs[n]
            if n == 0:
                own_copy(ab).wait()
            for h in (gc, gcx):
                arrived(ab, zz * 4 + h)
            rows = pl.ds(pl.multiple_of(ab * 1024 + zz * 256, 256), 256)
            h = xall_ref[ab, pl.ds(zz * 4, 4)].reshape(256, 768).astype(F32)
            inv = lax.rsqrt(jnp.mean(h * h, axis=-1, keepdims=True) + EPS)
            xn = (h * inv * gain_ref[...].reshape(1, 768)).astype(BF)
            xn_ref[rows, :] = xn
            y = matmul(xn, wc_ref[:, 128:512])
            count = count_ref[p, (2 * r if ab == 0 else 1)]
            at = lax.broadcasted_iota(jnp.int32, (256, 128), 0) + zz * 256
            bias = jnp.where(at < count, 0.0, NEG)
            one = jnp.where((lane % 64) < 4, 1.0, 0.0)
            k_aug = jnp.where(lane % 64 == 0, bias, one)
            k01, v01, kv2 = y[:, :128], y[:, 128:256], y[:, 256:]
            keys = (jnp.where(low, k01, k_aug), jnp.where(low, k_aug, k01), jnp.where(low, kv2, k_aug))
            cols = pl.ds(pl.multiple_of(zz * 256, 256), 256)
            for head in range(3):
                key = keys[head].astype(BF)
                k_ref[head, rows, :] = key
                kt_ref[head, ab, :, cols] = key.T
            v_ref[0, rows, :] = jnp.where(low, v01, one).astype(BF)
            v_ref[1, rows, :] = jnp.where(low, one, v01).astype(BF)
            v_ref[2, rows, :] = jnp.where(low, one, kv2).astype(BF)

        def half_copy(ab, n):
            rows = pl.ds(ab * 1024, 1024)
            a, b = (
                (k_ref.at[:, rows], k_out.at[:, rows]), (v_ref.at[:, rows], v_out.at[:, rows]),
                (kt_ref.at[:, ab], kt_out.at[:, ab]), (xn_ref.at[rows], xn_out.at[rows]),
            )[n]
            return pltpu.make_async_copy(a, b, half_sem.at[ab, n])

        def tile(t):
            off = jnp.where(t < 4, t, 4 + r + 2 * (t - 4)) * 256
            xq = xn_ref[pl.ds(pl.multiple_of(off, 256), 256), :]
            q01 = matmul(xq, wc_ref[:, 0:128]).astype(BF).astype(F32) * 0.125
            q2 = matmul(xq, wc_ref[:, 512:640]).astype(BF).astype(F32) * 0.125
            flag = jnp.where(lane % 64 == 0, 1.0, 0.0)
            qs = (jnp.where(low, q01, flag), jnp.where(low, flag, q01), jnp.where(low, q2, flag))
            at = pl.ds(pl.multiple_of(t * 256, 256), 256)
            ab = t // 4
            keys = pl.ds(pl.multiple_of(ab * 1024, 1024), 1024)
            outs = []
            for head in range(3):
                s = matmul(qs[head].astype(BF), kt_ref[head, ab])
                top = jnp.max(s, axis=1, keepdims=True)
                e = jnp.exp(s - top).astype(BF)
                o = matmul(e, v_ref[head, keys, :])
                total = o[:, 64:65] if head == 0 else o[:, 0:1]
                outs.append(o / total)
                lse = -(top + jnp.log(total))
                hi = lse.astype(BF).astype(F32)
                mid = (lse - hi).astype(BF).astype(F32)
                lo = lse - hi - mid
                part = lane % 64
                aug = jnp.where(part == 1, hi, jnp.where(part == 2, mid, jnp.where(part == 3, lo, flag)))
                data = low if head != 1 else jnp.logical_not(low)
                q_ref[head, at, :] = jnp.where(data, qs[head], aug).astype(BF)
            o01 = jnp.where(low, outs[0], outs[1])
            o2 = outs[2]
            o01_ref[at, :] = o01
            o2_ref[at, :] = o2
            for h in range(4):
                osend_ref[h, t, 0:64, :] = o01[h * 64 : h * 64 + 64].astype(BF)
                first = o2[h * 64 : h * 64 + 32]
                second = o2[h * 64 + 32 : h * 64 + 64]
                folded = jnp.where(low[:32], pltpu.roll(first, 64, 1), second)
                osend_ref[h, t, 64:96, :] = folded.astype(BF)

        saved = []

        def keep(makes):
            for make in makes:
                make().start()
                saved.append(make)

        def tile_copy(t, k):
            rows = pl.ds(whole(t * 256, 256), 256)
            a, b = (
                (q_ref.at[:, rows], q_out.at[:, rows]), (o01_ref.at[rows], o01_out.at[rows]),
                (o2_ref.at[rows], o2_out.at[rows]),
            )[k]
            return pltpu.make_async_copy(a, b, tile_sem.at[t, k])

        keep([lambda: pltpu.make_async_copy(wc_ref, wc_out, last_sem.at[6])])
        forward_z(0, 1)
        forward_x(0, 0)
        project(0, 0)
        forward_z(0, 2)
        forward_x(0, 1)
        project(0, 1)
        forward_z(0, 3)
        forward_z(1, 1)
        forward_x(0, 2)
        project(0, 2)
        forward_x(0, 3)
        forward_x(1, 0)
        project(0, 3)
        keep([lambda n=n: half_copy(0, n) for n in range(4)])
        forward_z(1, 2)

        @pl.loop(0, 6)
        def _(t):
            tile(t)
            for k in range(3):
                o_copy(t, k).start()
            self_copy(t).start()
            for k in range(3):
                tile_copy(t, k).start()

            @pl.when(t == 0)
            def _():
                forward_z(1, 3)
                moved.start()
                forward_x(1, 1)

            @pl.when(t == 1)
            def _():
                project(1, 0)
                project(1, 1)

            @pl.when(t == 2)
            def _():
                forward_x(1, 2)
                project(1, 2)

            @pl.when(t == 3)
            def _():
                forward_x(1, 3)
                project(1, 3)
                keep([lambda n=n: half_copy(1, n) for n in range(4)])
                keep([lambda j=j: block_copy(j) for j in range(6)])

        for t in range(6):
            for k in range(3):
                tile_copy(t, k).wait()
        for make in saved:
            make().wait()

    return body, arrive, leave


GELU_A = 0.044715
GELU_C = math.sqrt(2.0 / math.pi)


def widen_kernel(
    qkv_ref, last_ref, so_ref, sg_ref, su_ref, sd_ref, gains_ref, first_ref, second_ref,
    q_ref, k_ref, v_ref, o_ref, g_ref, u_ref, d_ref, gain1_ref, gain2_ref, first_out, second_out,
):
    first_out[...] = first_ref[...]
    second_out[...] = second_ref[...]

    @pl.when(pl.program_id(0) == 0)
    def _():
        gain1_ref[...] = gains_ref[0, :]
        gain2_ref[...] = gains_ref[1, :]

    low = lanes_of(qkv_ref.shape[1]) < 64

    def swap(v):
        return pltpu.roll(v, 64, 1)

    later = pl.program_id(0) * 2 >= pl.num_programs(0)
    for out, first, where in ((q_ref, 0, 0), (k_ref, 128, 1), (v_ref, 256, 2)):
        a = [qkv_ref[n, :, first : first + 128].astype(F32) for n in range(4)]
        if where == 0:
            b = [last_ref[n].astype(F32) for n in range(4)]
            low_b = [jnp.where(later, swap(x), x) for x in b]
            high_b = [swap(x) for x in low_b]
        else:
            b = [qkv_ref[n, :, 384:512].astype(F32) for n in range(4)]
            low_b = b if where == 1 else [swap(x) for x in b]
            high_b = [swap(x) for x in low_b]
        tiles = (
            a[0], jnp.where(low, low_b[0], swap(a[1])), jnp.where(low, swap(a[1]), high_b[1]),
            a[2], jnp.where(low, low_b[2], swap(a[3])), jnp.where(low, swap(a[3]), high_b[3]),
        )
        for n, tile in enumerate(tiles):
            out[:, n * 128 : n * 128 + 128] = tile
    o_ref[...] = so_ref[...].astype(F32)
    g_ref[...] = sg_ref[...].astype(F32)
    u_ref[...] = su_ref[...].astype(F32)
    d_ref[...] = sd_ref[...].astype(F32)

def widen(qkv, last, s_out, s_gate, s_up, s_down, gains, first, second):
    s = jax.ShapeDtypeStruct
    steps = 4

    def spec(a):
        if len(a.shape) == 3:
            return pl.BlockSpec((a.shape[0], a.shape[1] // steps, a.shape[2]), lambda i: (0, i, 0))
        return pl.BlockSpec((a.shape[0] // steps, a.shape[1]), lambda i: (i, 0))

    outs = tuple(s(a.shape, F32) for a in (s_out, s_out, s_out, s_out, s_gate, s_up, s_down))
    ins = (s_out, s_gate, s_up, s_down)
    folded = pl.BlockSpec((4, last.shape[1] // 2, 128), lambda i: (0, i % 2, 0))
    width = gains.shape[1]
    vector = pl.BlockSpec((width,), lambda i: (0,))
    moved = (s(first.shape, first.dtype), s(second.shape, second.dtype))
    return pl.pallas_call(
        widen_kernel,
        grid=(steps,),
        out_shape=outs + (s((width,), F32),) * 2 + moved,
        in_specs=[spec(qkv), folded] + [spec(a) for a in ins] + [pl.BlockSpec(gains.shape, lambda i: (0, 0)), spec(first), spec(second)],
        out_specs=tuple(spec(a) for a in outs) + (vector, vector, spec(first), spec(second)),
        compiler_params=pltpu.CompilerParams(vmem_limit_bytes=62 << 20),
        name="widen",
    )(qkv, last, *ins, gains, first, second)


class Stream:
    def __init__(self, spare, res, acc, first, rest, sems, order, coords, core, cut):
        self.spare, self.res, self.acc, self.first, self.rest = spare, res, acc, first, rest
        self.send, self.recv, self.own, self.back, self.got, self.fwd, self.fgot = sems
        row, col, half = cut
        self.rows, self.wide = acc.shape
        self.row = row
        self.order = [coords[name] for name in order]
        self.deep = len(order)
        bit, self.peer = core
        if half:
            self.mine = pl.ds(pl.multiple_of(bit * half + col, 128), self.wide)
            self.other = pl.ds(pl.multiple_of((1 - bit) * half + col, 128), self.wide)
        else:
            self.mine = pl.ds(col, self.wide)
        self.base, self.size = [0], [self.rows]
        for bit, _ in self.order:
            self.size.append(self.size[-1] // 2)
            self.base.append(self.base[-1] + bit * self.size[-1])

    def part(self, base, size):
        return pl.ds(whole(base, 16), size)

    def at(self, base, size, mine=True):
        cols = self.mine if mine else self.other
        return self.res.at[pl.ds(whole(self.row + base, 16), size), cols]

    def sibling(self, k):
        return self.base[k - 1] + (1 - self.order[k - 1][0]) * self.size[k]

    def own_out(self):
        here = self.base[self.deep], self.size[self.deep]
        return pltpu.make_async_copy(self.acc.at[self.part(*here)], self.at(*here), self.own.at[1])

    def c_push(self, k):
        if k == 0:
            return remote(self.spare, self.first, self.send.at[0], self.recv.at[0], self.peer)
        return remote(
            self.acc.at[self.part(self.sibling(k), self.size[k])],
            self.rest.at[pl.ds(self.rows - 2 * self.size[k], self.size[k])],
            self.send.at[k],
            self.recv.at[k],
            self.order[k - 1][1],
        )

    def c_back(self, k):
        here = self.base[k], self.size[k]
        src = self.acc.at[self.part(*here)] if k == self.deep else self.at(*here)
        return remote(
            src, self.at(*here), self.back.at[k - 1], self.got.at[k - 1], self.order[k - 1][1]
        )

    def c_forward(self, k):
        if k == 0:
            here = self.base[self.deep], self.size[self.deep]
            src = self.acc.at[self.part(*here)]
        else:
            here = self.sibling(k), self.size[k]
            src = self.at(*here)
        return remote(src, self.at(*here), self.fwd.at[k], self.fgot.at[k], self.peer)

    def open(self):
        self.c_push(0).start()

    def fold(self, k):
        self.c_push(k).wait_recv()
        base, size = self.base[k], self.size[k]
        other, at = (self.first, 0) if k == 0 else (self.rest, self.rows - 2 * size)
        step = 64 if size % 64 == 0 else 48 if size % 48 == 0 else 32

        @pl.loop(0, size // step)
        def _(n):
            rows = self.part(base + n * step, step)
            more = other[pl.ds(pl.multiple_of(at + n * step, 16), step), :]
            self.acc[rows, :] = (self.acc[rows, :].astype(F32) + more.astype(F32)).astype(BF)

        if k < self.deep:
            self.c_push(k + 1).start()
        else:
            self.c_back(k).start()
            self.c_forward(0).start()
            self.own_out().start()

    def collect(self, k):
        here = self.sibling(k), self.size[k]
        block = self.at(*here)
        remote(block, block, self.back.at[k - 1], self.got.at[k - 1], self.peer).wait_recv()
        if k == self.deep:
            self.own_out().wait()
        if k > 1:
            self.c_back(k - 1).start()
        self.c_forward(k).start()

    def close(self):
        for k in range(self.deep + 1):
            if k == 0:
                here = self.base[self.deep], self.size[self.deep]
            else:
                here = self.sibling(k), self.size[k]
            block = self.at(*here, mine=False)
            remote(block, block, self.fwd.at[k], self.fgot.at[k], self.peer).wait_recv()
            self.c_push(k).wait_send()
            self.c_forward(k).wait_send()
            if k > 0:
                self.c_back(k).wait_send()


class Grouped(Stream):
    def __init__(self, res, acc, rest, sems, order, coords, core, cut, group, across, late):
        super().__init__(None, res, acc, None, rest, sems, order, coords, core, cut)
        self.group, self.gx, self.across, self.late = group, far(group), across, late

    def at(self, base, size, n=0):
        h = (self.group, self.gx, flip(self.group), far(flip(self.group)))[n]
        return self.res.at[h, self.part(base, size), self.mine]

    def source(self, k, n):
        here = self.base[k], self.size[k]
        return self.acc.at[self.part(*here)] if k == self.deep and n == 0 else self.at(*here, n)

    def c_across(self):
        k = self.late
        return remote(
            self.source(k, 0),
            self.at(self.base[k], self.size[k]),
            self.back.at[self.deep, 0],
            self.got.at[self.deep, 0],
            self.across,
        )

    def c_back(self, k, n):
        there = self.at(self.base[k], self.size[k], n)
        return remote(
            self.source(k, n), there, self.back.at[k - 1, n], self.got.at[k - 1, n], self.order[k - 1][1]
        )

    def span(self, k, n):
        if k > 0:
            return self.sibling(k), self.size[k]
        k = self.deep if n == 0 else self.late
        return self.base[k], self.size[k]

    def c_forward(self, k, n):
        src = self.source(self.deep, 0) if k == n == 0 else self.at(*self.span(k, n), n)
        return remote(src, self.at(*self.span(k, n), n), self.fwd.at[k, n], self.fgot.at[k, n], self.peer)

    def fold(self, k):
        if k == 0:
            self.c_push(1).start()
            return
        if k < self.deep:
            super().fold(k)
            return
        self.c_push(k).wait_recv()
        base, size = self.base[k], self.size[k]
        rows = self.part(base, size)
        more = self.rest[pl.ds(self.rows - 2 * size, size), :]
        self.acc[rows, :] = (self.acc[rows, :].astype(F32) + more.astype(F32)).astype(BF)
        if self.late == k:
            self.c_across().start()
        self.c_back(k, 0).start()
        self.c_forward(0, 0).start()
        self.own_out().start()

    def extend(self):
        self.c_across().wait_recv()
        if self.late > 0:
            self.c_back(self.late, 1).start()
        self.c_forward(0, 1).start()

    def collect(self, k):
        if k == self.deep:
            self.own_out().wait()
        two = 2 if k <= self.late else 1
        for n in range(two):
            block = self.at(*self.span(k, n), n)
            remote(block, block, self.back.at[k - 1, n], self.got.at[k - 1, n], self.peer).wait_recv()
        if self.late == k - 1:
            self.c_across().start()
        if k > 1:
            for n in range(two):
                self.c_back(k - 1, n).start()
        for n in range(two):
            self.c_forward(k, n).start()

    def close(self):
        self.c_across().wait_send()
        for k in range(self.deep + 1):
            if k > 0:
                self.c_push(k).wait_send()
            for n in range(2 if k <= self.late else 1):
                block = self.at(*self.span(k, n), 2 + n)
                remote(block, block, self.fwd.at[k, n], self.fgot.at[k, n], self.peer).wait_recv()
                self.c_forward(k, n).wait_send()
                if k > 0:
                    self.c_back(k, n).wait_send()


X, Y, ZL, ZH = range(4)
(FF, FFPOST, RES, SWAP, TILE, DXN, GW, END, XSB, XSA, TB, TA, ZB, NA, NB) = range(100, 115)
OPEN, FOLD, COLLECT, EXTEND, GAIN = range(5)
PIECES = (
    (0, 0, 0, 0, 768, 256, 256, (ZL, Y, X, ZH)),
    (0, 1, 0, 512, 768, 256, 256, (Y, X, ZL, ZH)),
    (0, 2, 0, 1024, 768, 256, 256, (Y, X, ZL, ZH)),
    (0, 3, 0, 1536, 768, 256, 256, (ZL, X, Y, ZH)),
    (1, 0, 0, 0, 768, 256, 256, (ZL, Y, X, ZH)),
    (1, 1, 0, 512, 768, 256, 256, (Y, ZL, X, ZH)),
    (1, 2, 0, 1024, 768, 256, 256, (Y, X, ZH, ZL)),
    (1, 3, 0, 1536, 768, 256, 256, (ZL, Y, X, ZH)),
    (2, 0, 0, 0, 512, 384, 384, (X, ZH, Y, ZL)),
    (2, 1, 512, 0, 512, 384, 384, (X, Y, ZL, ZH)),
    (2, 2, 1024, 0, 512, 384, 384, (X, Y, ZL, ZH)),
    (2, 3, 1536, 0, 512, 384, 384, (X, Y, ZL, ZH)),
    (3, 0, 0, 0, 768, 384, 384, (X, Y, ZL, ZH)),
)
GROUPS = (
    (0, 384, 768, 128, (Y, ZH, ZL), 0),
    (0, 0, 768, 384, (Y, ZH, ZL), 1),
    (1, 0, 384, 128, (ZL, Y, ZH), 1),
)
PLAN = (
    FF, (OPEN, 8, 0), (OPEN, 0, 0), (OPEN, 4, 0), FF, (OPEN, 5, 0), (OPEN, 1, 0), (OPEN, 9, 0),
    (FOLD, 8, 0), FF, (FOLD, 4, 0), (FOLD, 5, 0), (OPEN, 6, 0), (OPEN, 10, 0), (OPEN, 2, 0), (FOLD, 1, 0),
    (FOLD, 0, 0), (FOLD, 9, 0), FF, (OPEN, 7, 0), (OPEN, 11, 0), (OPEN, 3, 0), (FOLD, 8, 1), (FOLD, 6, 0),
    (FOLD, 2, 0), (FOLD, 10, 0), (FOLD, 4, 1), (FOLD, 5, 1), FFPOST, (OPEN, 12, 0), (FOLD, 9, 1), (FOLD, 1, 1),
    (FOLD, 11, 0), (FOLD, 7, 0), (FOLD, 0, 1), RES, (FOLD, 8, 2), (FOLD, 3, 0), (FOLD, 10, 1), (FOLD, 5, 2),
    (FOLD, 12, 0), (FOLD, 6, 1), (FOLD, 7, 1), (FOLD, 2, 1), SWAP, TILE, (FOLD, 4, 2), (FOLD, 1, 2),
    TILE, (FOLD, 9, 2), TILE, (FOLD, 5, 3), (FOLD, 11, 1), (FOLD, 8, 3), (FOLD, 0, 2), TILE,
    (FOLD, 7, 2), (FOLD, 10, 2), TILE, (FOLD, 1, 3), (FOLD, 12, 1), (FOLD, 5, 4), (FOLD, 9, 3), (FOLD, 11, 2),
    (FOLD, 6, 2), (FOLD, 3, 1), (FOLD, 10, 3), TILE, (FOLD, 4, 3), (FOLD, 1, 4), (FOLD, 2, 2), (COLLECT, 5, 4),
    (FOLD, 11, 3), (FOLD, 9, 4), (FOLD, 0, 3), (FOLD, 12, 2), (FOLD, 7, 3), DXN, (FOLD, 6, 3), (FOLD, 2, 3),
    (COLLECT, 5, 3), (FOLD, 3, 2), (FOLD, 10, 4), GW, END, XSB, (FOLD, 12, 3), (FOLD, 15, 0),
    (FOLD, 14, 0), (FOLD, 0, 4), XSA, TB, TA, (FOLD, 11, 4), (FOLD, 2, 4), (FOLD, 13, 0),
    (COLLECT, 5, 2), (COLLECT, 10, 4), (FOLD, 6, 4), (COLLECT, 9, 4), (FOLD, 3, 3), (COLLECT, 1, 4), (FOLD, 12, 4), (FOLD, 15, 1),
    (COLLECT, 0, 4), (COLLECT, 11, 4), (COLLECT, 10, 3), (COLLECT, 2, 4), (COLLECT, 6, 4), (COLLECT, 9, 3), (FOLD, 14, 1), (FOLD, 3, 4),
    (COLLECT, 1, 3), ZB, (COLLECT, 12, 4), (FOLD, 13, 1), (COLLECT, 11, 3), (COLLECT, 2, 3), (COLLECT, 6, 3), (COLLECT, 5, 1),
    (FOLD, 7, 4), (FOLD, 15, 2), (FOLD, 4, 4), (COLLECT, 10, 2), (FOLD, 14, 2), NA, (COLLECT, 3, 4), (COLLECT, 9, 2),
    (COLLECT, 0, 3), NB, (COLLECT, 12, 3), (COLLECT, 11, 2), (COLLECT, 1, 2), (GAIN, 0, 0), (COLLECT, 2, 2), (FOLD, 13, 2),
    (COLLECT, 7, 4), (COLLECT, 3, 3), (FOLD, 8, 4), (COLLECT, 4, 4), (COLLECT, 6, 2), (GAIN, 0, 1), (FOLD, 14, 3), (COLLECT, 0, 2),
    (COLLECT, 10, 1), (COLLECT, 12, 2), (COLLECT, 9, 1), (COLLECT, 1, 1), (FOLD, 13, 3), (COLLECT, 8, 4), (COLLECT, 14, 3), (COLLECT, 11, 1),
    (COLLECT, 2, 1), (COLLECT, 7, 3), (FOLD, 15, 3), (COLLECT, 3, 2), (COLLECT, 0, 1), (COLLECT, 4, 3), (COLLECT, 6, 1), (COLLECT, 13, 3),
    (GAIN, 0, 2), (COLLECT, 8, 3), (COLLECT, 7, 2), (COLLECT, 14, 2), (COLLECT, 15, 3), (COLLECT, 4, 2), (GAIN, 0, 3), (COLLECT, 12, 1),
    (COLLECT, 3, 1), (COLLECT, 13, 2), (COLLECT, 8, 2), (EXTEND, 14, 0), (COLLECT, 15, 2), (COLLECT, 7, 1), (COLLECT, 13, 1), (COLLECT, 8, 1),
    (EXTEND, 15, 0), (COLLECT, 4, 1), (GAIN, 0, 4), (COLLECT, 14, 1), (COLLECT, 15, 1), (GAIN, 0, 5), (EXTEND, 13, 0),
)


def layer_kernel(*refs):
    take = iter(refs)

    def some(n):
        return [next(take) for _ in range(n)]

    x_ref, cot_ref, count_ref, gain_ref, wq_ref, wk_ref, wv_ref = some(7)
    gain2_ref, wo_hbm, wg_hbm, wu_hbm, wd_hbm = some(5)
    out_ref, res_out_ref = some(2)
    outs = some(6)
    (gains_out,) = some(1)
    loads_hbm = some(8)
    orecv_ref, dy_ref, xall_ref, osend_ref = some(4)
    front_sems = some(14)
    h_ref, dh_ref, res_ref, dsend_ref, dgain2_ref = some(5)
    both = some(4)
    dense_sem, w_sem, load_sem = some(3)
    (do_ref, p_ref) = some(2)
    (rc_ref, sx_ref, rx_ref, t_ref, zb_ref, rz_ref, ig_ref, dgain_ref) = some(8)
    (c_send, c_recv, x_send, x_recv, z_send, z_recv) = some(6)
    (rs_send, rs_recv, rs_own, h_send, h_recv, h_own, hs, hr, ho) = some(9)
    item, z, g = place()
    gc, gx = flip(g), far(g)
    gcx = far(gc)
    p, r = z // 2, z % 2
    side = g % 2
    coords = (
        (g // 2, (item, z * 4 + gx)),
        (item, (1 - item, z * 4 + g)),
        (z % 2, (item, flip(z) * 4 + g)),
        (z // 2, (item, far(z) * 4 + g)),
    )
    across, pair = coords[X][1], coords[ZL][1]
    core = (item, z * 4 + gc)
    zs = (z, flip(z), far(z), far(flip(z)))
    streams = []
    for n, m, row, col, _, _, half, order in PIECES:
        first, rest = some(2)
        stream = Stream(
            both[n].at[m, 1 - side], outs[n], both[n].at[m, side], first, rest, some(7), order, coords,
            (side, core), (row, col, half),
        )
        streams.append(stream)
    gw_refs = some(2)
    for n, col, _, wide, order, late in GROUPS:
        (rest,) = some(1)
        acc = gw_refs[n].at[:, pl.ds(col, wide)]
        stream = Grouped(
            outs[4 + n], acc, rest, some(7), order, coords, (side, core), (0, col, 0), g, across, late
        )
        streams.append(stream)
    buf, got, gain_send, gain_recv = some(4)

    greet(g_peers(item, z, g) + z_peers(item, z, g) + [coords[Y][1]])
    swapped = swap_heads(item, z, g, dsend_ref, do_ref, hs, hr, ho.at[0])
    lane = lanes_of(256)
    low = lane < 64
    part = lane % 64

    body, arrive, leave = front_phase(
        (x_ref, cot_ref, count_ref, gain_ref, wq_ref, wk_ref, wv_ref), loads_hbm,
        (orecv_ref, dy_ref, h_ref, xall_ref, osend_ref), front_sems,
    )

    def dense(emit, wo_ref, wg_ref, wu_ref, wd_ref, att_ref, sec_ref, xn_ref, xt_ref, dxn_ref):
        size = 512
        load_wo = pltpu.make_async_copy(wo_hbm, wo_ref, dense_sem.at[0])
        load_wo.start()

        def load(c, n):
            cut = pl.ds(whole(c * size, size), size)
            a, b = ((wg_hbm, wg_ref), (wu_hbm, wu_ref), (wd_hbm, wd_ref))[n]
            a, b = (a.at[:, cut], b.at[:, cut]) if n < 2 else (a.at[cut, :], b.at[cut, :])
            return pltpu.make_async_copy(a, b, w_sem.at[n, c])

        for c in range(4):
            for n in range(3):
                load(c, n).start()
        low = lanes_of(384) < 64

        def swap(v):
            return pltpu.roll(v, 64, 1)

        arrive()
        pairs = [orecv_ref[n, :, 0:64, :].astype(F32).reshape(384, 128) for n in range(4)]

        def unfold(n, high):
            f = orecv_ref[n, :, 64:96, :].astype(F32)
            s = swap(f.reshape(192, 128)).reshape(6, 32, 128)
            two = (s, f) if high else (f, s)
            return jnp.concatenate(two, axis=1).reshape(384, 128)

        tiles = (
            pairs[0],
            jnp.where(low, unfold(0, False), swap(pairs[1])),
            jnp.where(low, swap(pairs[1]), unfold(1, True)),
            pairs[2],
            jnp.where(low, unfold(2, False), swap(pairs[3])),
            jnp.where(low, swap(pairs[3]), unfold(3, True)),
        )
        for n, v in enumerate(tiles):
            att_ref[:, n * 128 : n * 128 + 128] = v.astype(BF)
        load_wo.wait()
        second = h_ref[...].reshape(384, 768).astype(F32) + matmul(att_ref[...], wo_ref[...])
        sec_ref[...] = second
        dh_ref[...] = second.reshape(6, 64, 768)
        inv = lax.rsqrt(jnp.mean(second * second, axis=-1, keepdims=True) + EPS)
        xn_ref[...] = (second * inv * gain2_ref[...].reshape(1, 768)).astype(BF)
        xt_ref[...] = xn_ref[...].T
        dxn_ref[...] = jnp.zeros_like(dxn_ref)

        def chunk(c):
            cut = pl.ds(pl.multiple_of(c * size, size), size)
            for n in range(3):
                load(c, n).wait()
            dy = dy_ref[...].reshape(384, 768)
            gate = matmul(xn_ref[...], wg_ref[:, cut])
            upper = matmul(xn_ref[...], wu_ref[:, cut])
            d_mixed = nt(dy, wd_ref[cut, :])
            square = gate * gate
            tan = jnp.tanh(GELU_C * (gate + GELU_A * square * gate))
            half = 0.5 * (1.0 + tan)
            act = gate * half
            slope = half + 0.5 * gate * (1.0 - tan * tan) * (GELU_C * (1.0 + 3.0 * GELU_A * square))
            mixed = (act * upper).astype(BF)
            d_gate = (d_mixed * upper * slope).astype(BF)
            d_upper = (d_mixed * act).astype(BF)
            for n, grad in enumerate((d_gate, d_upper)):
                full = matmul(xt_ref[...], grad).astype(BF)
                both[n][c, 0] = full[:, : size // 2]
                both[n][c, 1] = full[:, size // 2 :]
            down = outer(mixed, dy).astype(BF)
            both[2][c, 0] = down[:, :384]
            both[2][c, 1] = down[:, 384:]
            sec_ref[...] += matmul(mixed, wd_ref[cut, :])
            dxn_ref[...] += nt(d_gate, wg_ref[:, cut]) + nt(d_upper, wu_ref[:, cut])

        run_loop(FF, 4, chunk, emit)
        emit_between(FF, FFPOST)
        res_ref[...] = sec_ref[...].astype(BF).reshape(6, 64, 768)
        second = dh_ref[...].reshape(384, 768)
        inv = lax.rsqrt(jnp.mean(second * second, axis=-1, keepdims=True) + EPS)
        d_xn = dxn_ref[...]
        dgain2_ref[...] = jnp.sum(d_xn * second * inv, axis=0, keepdims=True)
        dyg = d_xn * gain2_ref[...].reshape(1, 768)
        dot = jnp.mean(dyg * second, axis=-1, keepdims=True)
        dy = dy_ref[...].reshape(384, 768)
        d_second = dy.astype(F32) + inv * dyg - second * (inv * inv * inv * dot)
        dh_ref[...] = d_second.reshape(6, 64, 768)
        d_branch = d_second.astype(BF)
        d_att = nt(d_branch, wo_ref[...]).astype(BF).astype(F32)
        d = [d_att[:, n * 128 : n * 128 + 128] for n in range(6)]
        firsts = (d[0], swap(jnp.where(low, d[2], d[1])), d[3], swap(jnp.where(low, d[5], d[4])))
        lasts = ((d[1], False), (d[2], True), (d[4], False), (d[5], True))
        low3 = lax.broadcasted_iota(jnp.int32, (6, 32, 128), 2) < 64
        for n in range(4):
            dsend_ref[n, :, 0:64, :] = firsts[n].astype(BF).reshape(6, 64, 128)
            v, high = lasts[n]
            v3, s3 = v.reshape(6, 64, 128), swap(v).reshape(6, 64, 128)
            top, bottom = v3[:, :32], v3[:, 32:]
            top_s, bottom_s = s3[:, :32], s3[:, 32:]
            f = jnp.where(low3, top_s, bottom) if high else jnp.where(low3, top, bottom_s)
            dsend_ref[n, :, 64:96, :] = f.astype(BF)
        swapped.start()
        g_out = outer(att_ref[...], d_branch).astype(BF)
        both[3][0, 0] = g_out[:, :384]
        both[3][0, 1] = g_out[:, 384:]

    def pieces(delta):
        neg = -delta
        hi = neg.astype(BF).astype(F32)
        mid = (neg - hi).astype(BF).astype(F32)
        lo = neg - hi - mid
        return jnp.where(part == 1, hi, jnp.where(part == 2, mid, jnp.where(part == 3, lo, 0.0)))

    loads = {}

    def tile(t):
        q_ref, k_ref, v_ref, kt_ref, o01_ref, o2_ref = (loads[n] for n in range(6))
        dk_ref, dv_ref, d5_ref = (loads[n] for n in ("dk", "dv", "d5"))
        at = pl.ds(pl.multiple_of(t * 256, 256), 256)
        ab = t // 4
        keys = pl.ds(pl.multiple_of(ab * 1024, 1024), 1024)
        do01 = do_ref[:, t, 0:64, :].astype(F32).reshape(256, 128)
        folded = do_ref[:, t, 64:96, :].astype(F32)
        two = []
        for h in range(4):
            two.append(pltpu.roll(folded[h], 64, 1))
            two.append(folded[h])
        do2 = jnp.concatenate(two, axis=0)
        prod = do01 * o01_ref[at, :]
        prod2 = do2 * o2_ref[at, :]
        delta0 = jnp.sum(jnp.where(low, prod, 0.0), axis=1, keepdims=True)
        delta1 = jnp.sum(jnp.where(low, 0.0, prod), axis=1, keepdims=True)
        delta2 = jnp.sum(jnp.where(low, 0.0, prod2), axis=1, keepdims=True)
        dos = (
            jnp.where(low, do01, pieces(delta0)).astype(BF),
            jnp.where(low, pieces(delta1), do01).astype(BF),
            jnp.where(low, pieces(delta2), do2).astype(BF),
        )
        dqs = []
        for head in range(3):
            q = q_ref[head, at, :]
            prob = jnp.exp(nt(k_ref[head, keys, :], q))
            d_prob = nt(v_ref[head, keys, :], dos[head])
            d_log = (prob * d_prob).astype(BF)
            dv_ref[head, keys, :] += matmul(prob.astype(BF), dos[head])
            dk_ref[head, keys, :] += matmul(d_log, q)
            dqs.append(matmul(kt_ref[head, ab], d_log).T * 0.125)
        off = jnp.where(t < 4, t, 4 + r + 2 * (t - 4)) * 256
        rows = pl.ds(pl.multiple_of(off, 256), 256)
        d5_ref[rows, 0:128] = jnp.where(low, dqs[0], dqs[1]).astype(BF)
        d5_ref[rows, 512:640] = jnp.where(low, dqs[2], 0.0).astype(BF)

    halves = ((0, slice(0, 4)), (1, slice(4, 8)))
    away = (gc, gcx)

    def c_copy(k, ab):
        cut = halves[ab][1]
        return remote(p_ref.at[away[k], cut], rc_ref.at[k, cut], c_send.at[k, ab], c_recv.at[k, ab], core)

    def x_copy(ab):
        cut = halves[ab][1]
        return remote(sx_ref.at[cut], rx_ref.at[cut], x_send.at[ab], x_recv.at[ab], across)

    z_copy = remote(zb_ref, rz_ref, z_send.at[0], z_recv.at[0], pair)
    mine = 3 * p + 2 * r

    def home(n):
        if n < 4:
            s = (zs[3], zs[2], zs[1], z)[n]
            src, dst = ig_ref.at[s], out_ref.at[mine]
        else:
            s = z if n == 5 else zs[2]
            src, dst = ig_ref.at[4 + (1 - p if n == 4 else p)], out_ref.at[3 * p + 1]
        if n in (3, 5):
            return pltpu.make_async_copy(src, dst, h_own.at[n // 4])
        where = mine if n < 4 else 3 * p + 1
        return remote(src, dst, h_send.at[min(n, 3)], h_recv.at[where], (item, s * 4 + g))

    gain = gain_ref[...].reshape(1, 768)

    def norm_back(d_xn, j):
        h = h_ref[j].astype(F32)
        inv = lax.rsqrt(jnp.mean(h * h, axis=-1, keepdims=True) + EPS)
        dgain_ref[...] += jnp.sum(d_xn * h * inv, axis=0, keepdims=True)
        dyg = d_xn * gain
        dot = jnp.mean(dyg * h, axis=-1, keepdims=True)
        ig_ref[j] = (dh_ref[j] + inv * dyg - h * (inv * inv * inv * dot)).astype(BF)

    def load_copy(n):
        return pltpu.make_async_copy(loads_hbm[n], loads[n], load_sem.at[n])

    def run_swap():
        for n in range(8):
            load_copy(n).wait()
        swapped.finish()

    def run_dxn():
        wc_ref, dk_ref, dv_ref, d5_ref = (loads[n] for n in (7, "dk", "dv", "d5"))

        @pl.loop(0, 8)
        def _(i):
            rows = pl.ds(pl.multiple_of(i * 256, 256), 256)
            d5_ref[rows, 128:256] = jnp.where(low, dk_ref[0, rows, :], dk_ref[1, rows, :]).astype(BF)
            d5_ref[rows, 256:384] = jnp.where(low, dv_ref[0, rows, :], dv_ref[1, rows, :]).astype(BF)
            d5_ref[rows, 384:512] = jnp.where(low, dk_ref[2, rows, :], dv_ref[2, rows, :]).astype(BF)
            d_xn = nt(d5_ref[rows, :], wc_ref[...]).astype(BF)
            for h in range(4):
                p_ref[h, i, :, :] = d_xn[h * 64 : h * 64 + 64]

        for k in (1, 0):
            for ab in (1, 0):
                c_copy(k, ab).start()

    def run_gw():
        for c in range(4):
            cols = slice(c * 128, c * 128 + 128)
            gw_refs[0][:, cols] = outer(loads[6][...], loads["d5"][:, cols]).astype(BF)
        last = outer(loads[6][...], loads["d5"][:, 512:640])
        folded = jnp.where(lanes_of(384) < 64, last[:384], pltpu.roll(last[384:], 64, 1))
        gw_refs[1][...] = folded.astype(BF)

    def run_xs(ab):
        c_copy(1, ab).wait_recv()

        @pl.loop(0, 4)
        def _(j):
            n = ab * 4 + j
            sx_ref[n] = (p_ref[gx, n].astype(F32) + rc_ref[1, n].astype(F32)).astype(BF)

        x_copy(ab).start()

    def run_t(ab):
        c_copy(0, ab).wait_recv()

        @pl.loop(0, 4)
        def _(j):
            n = ab * 4 + j
            t_ref[n] = p_ref[g, n].astype(F32) + rc_ref[0, n].astype(F32)

    def run_z():
        x_copy(1).wait_recv()
        for q in range(2):
            n = 4 + (1 - r) + 2 * q
            zb_ref[q] = (t_ref[n] + rx_ref[n].astype(F32)).astype(BF)
        z_copy.start()

    def run_na():
        x_copy(0).wait_recv()
        for n, s in enumerate((zs[3], zs[2], zs[1], z)):
            norm_back(t_ref[s] + rx_ref[s].astype(F32), s)
            home(n).start()

    def run_nb():
        z_copy.wait_recv()
        for n, q in enumerate((1 - p, p)):
            k = 4 + r + 2 * q
            norm_back(t_ref[k] + rx_ref[k].astype(F32) + rz_ref[q].astype(F32), 4 + q)
            home(4 + n).start()

    gain_peers = [core] + [peer for _, peer in coords]

    def gain_copy(k):
        return remote(buf.at[k], got.at[k], gain_send.at[k], gain_recv.at[k], gain_peers[k])

    def run_gain(k):
        if k == 0:
            buf[0] = jnp.zeros_like(buf[0])
            buf[0, 0:1, :] = dgain_ref[...]
            buf[0, 1:2, :] = dgain2_ref[...]
        else:
            gain_copy(k - 1).wait_recv()
            buf[k] = buf[k - 1] + got[k - 1]
        if k < 5:
            gain_copy(k).start()
        else:
            gains_out[...] = buf[5]

    homes = from_slots(item, z, g, res_ref, res_out_ref, rs_send, rs_recv, rs_own)

    single = {
        SWAP: run_swap, DXN: run_dxn, GW: run_gw, XSB: lambda: run_xs(1), XSA: lambda: run_xs(0),
        TB: lambda: run_t(1), TA: lambda: run_t(0), ZB: run_z, NA: run_na, NB: run_nb, RES: homes.start,
    }

    def emit(task):
        if task in single:
            single[task]()
        elif isinstance(task, tuple):
            kind, n, k = task
            if kind == GAIN:
                run_gain(k)
            elif kind == OPEN:
                streams[n].open()
            elif kind == FOLD:
                streams[n].fold(k)
            elif kind == COLLECT:
                streams[n].collect(k)
            else:
                streams[n].extend()

    def run_loop(name, count, body, emit):
        at = [n for n, task in enumerate(PLAN) if task == name]

        @pl.loop(0, count)
        def _(t):
            body(t)
            for n in range(count - 1):
                tasks = PLAN[at[n] + 1 : at[n + 1]]
                if tasks:

                    @pl.when(t == n)
                    def _():
                        for task in tasks:
                            emit(task)

    def emit_between(first, last):
        start = 0 if first is None else len(PLAN) - PLAN[::-1].index(first)
        stop = len(PLAN) if last is None else PLAN.index(last)
        for task in PLAN[start:stop]:
            emit(task)

    width, hidden = wg_hbm.shape
    v = pltpu.VMEM
    kept = [v(ref.shape, ref.dtype) for ref in loads_hbm]
    pl.run_scoped(body, v((3, width, 256), BF), *kept)
    pl.run_scoped(
        functools.partial(dense, emit),
        v((width, width), BF), v((width, hidden), BF), v((width, hidden), BF), v((hidden, width), BF),
        v((384, width), BF), v((384, width), F32), v((384, width), BF),
        v((width, 384), BF), v((384, width), F32),
    )

    def attend(*scoped):
        loads.update(enumerate(scoped[:8]))
        loads.update(zip(("dk", "dv", "d5"), scoped[8:]))
        for n in range(8):
            load_copy(n).start()
        for n in ("dk", "dv", "d5"):
            loads[n][...] = jnp.zeros_like(loads[n])
        dgain_ref[...] = jnp.zeros_like(dgain_ref)
        emit_between(FFPOST, TILE)
        run_loop(TILE, 6, tile, emit)
        emit_between(TILE, END)

    pl.run_scoped(
        attend,
        *kept,
        v((3, 2048, 128), F32), v((3, 2048, 128), F32), v((2048, 640), BF),
    )
    emit_between(END, None)

    for s in zs[1:]:
        where = 3 * (s // 2) + 2 * (s % 2)
        remote(ig_ref.at[0], out_ref.at[where], h_send.at[0], h_recv.at[where], pair).wait_recv()
    where = 3 * (1 - p) + 1
    remote(ig_ref.at[0], out_ref.at[where], h_send.at[0], h_recv.at[where], pair).wait_recv()
    homes.finish()
    leave()
    home(3).wait()
    home(5).wait()
    for stream in streams:
        stream.close()
    for n in (0, 1, 2, 4):
        home(n).wait_send()
    z_copy.wait_send()
    for ab in range(2):
        x_copy(ab).wait_send()
        for k in range(2):
            c_copy(k, ab).wait_send()
    for k in range(5):
        gain_copy(k).wait_send()


def layer(x6, cot6, counts, gain1, wq, wk, wv, gain2, w_out, w_gate, w_up, w_down):
    dma = pltpu.SemaphoreType.DMA
    s = jax.ShapeDtypeStruct
    v = pltpu.VMEM
    rows_shape = x6.shape
    _, rows, width = rows_shape
    heads = (4, 6, 96, 128)
    gains = (8, width)
    group, rest = (width, 512), (width // 2, 128)
    outs = (s(rows_shape, BF), s(rows_shape, BF)) + tuple(s(a.shape, BF) for a in (w_gate, w_up, w_down, w_out))
    outs += (s((4,) + group, BF), s((4,) + rest, BF), s(gains, F32))
    outs += (
        s((3, 1536, 128), BF), s((3, 2048, 128), BF), s((3, 2048, 128), BF), s((3, 2, 128, 1024), BF),
        s((1536, 128), F32), s((1536, 128), F32), s((2048, width), BF), s((width, 640), BF),
    )
    scratch = [
        v(heads, BF), v(rows_shape, BF), v((2, 16, rows, width), BF), v(heads, BF),
        dma((3, 2)), dma((4, 2, 2)), dma((4, 2)), dma((2, 16)), dma((2,)), dma((3,)),
        dma((6, 3)), dma((4, 6)), dma((4,)), dma((6,)), dma((2,)), dma((2, 4)), dma((6, 4)), dma((7,)),
        v(rows_shape, BF), v(rows_shape, F32), v(rows_shape, BF), v(heads, BF), v((1, width), F32),
        v((4, 2, width, 256), BF), v((4, 2, width, 256), BF), v((4, 2, 512, width // 2), BF), v((1, 2, width, width // 2), BF),
        dma((4,)), dma((3, 4)), dma((8,)),
        v(heads, BF), v((4, 8, rows, width), BF),
        v((2, 8, rows, width), BF), v((8, rows, width), BF), v((8, rows, width), BF),
        v((8, rows, width), F32), v((2, rows, width), BF), v((2, rows, width), BF), v((6, rows, width), BF),
        v((1, width), F32),
        dma((2, 2)), dma((2, 2)), dma((2,)), dma((2,)), dma((1,)), dma((1,)), dma((4,)), dma((6,)), dma((2,)),
        dma((4,)), dma((6,)), dma((2,)), dma((3,)), dma((4,)), dma((1,)),
    ]
    for _, _, _, _, high, wide, _, _ in PIECES:
        scratch += [v((high, wide), BF)] * 2
        scratch += [dma((5,)), dma((5,)), dma((2,)), dma((4,)), dma((4,)), dma((5,)), dma((5,))]
    scratch += [v(group, BF), v(rest, BF)]
    for _, _, high, wide, _, _ in GROUPS:
        scratch += [v((high, wide), BF)]
        scratch += [dma((4,)), dma((4,)), dma((2,)), dma((4, 2)), dma((4, 2)), dma((4, 2)), dma((4, 2))]
    scratch += [v((6,) + gains, F32), v((5,) + gains, F32), dma((5,)), dma((5,))]
    return pl.pallas_call(
        layer_kernel,
        out_shape=outs,
        in_specs=[ANY, ANY, SMEM, VMEM, ANY, ANY, ANY, VMEM] + [ANY] * 4,
        out_specs=(ANY,) * 8 + (VMEM,) + (ANY,) * 8,
        scratch_shapes=scratch,
        compiler_params=params(1, 63),
        name="layer",
    )(x6, cot6, counts, gain1, wq, wk, wv, gain2, w_out, w_gate, w_up, w_down)


def fast(
    inputs, counts, norm_gain1, w_query, w_key, w_value, w_out, norm_gain2, w_gate, w_up, w_down, cotangent
):
    band_rows, width = inputs.shape[2:]
    input_grads, results, s_gate, s_up, s_down, s_out, s_qkv, s_last, s_gains, *_ = layer(
        inputs.reshape(6, band_rows, width), cotangent.reshape(6, band_rows, width), counts, norm_gain1,
        w_query, w_key, w_value, norm_gain2, w_out, w_gate, w_up, w_down,
    )
    *grads, gain1, gain2, results, input_grads = widen(
        s_qkv, s_last, s_out, s_gate, s_up, s_down, s_gains, results, input_grads
    )
    return (
        results.reshape(inputs.shape), input_grads.reshape(inputs.shape), gain1, *grads[:4], gain2, *grads[4:]
    )


def program(*args):
    micro, seqs, band_rows, width = args[0].shape
    small = lax.axis_size("band") == 16 and lax.axis_size("items") == 2
    if small and (micro, seqs, band_rows, width, HEADS, HEAD_DIM) == (2, 3, 64, 768, 12, 64):
        return fast(*args)
    return per_device(*args)


def solution(mesh):
    return jax.shard_map(
        program,
        mesh=mesh,
        in_specs=(
            P(None, "items", "band", None),
            P(None, "items"),
            P(),
            P(),
            P(),
            P(),
            P(),
            P(),
            P(),
            P(),
            P(),
            P(None, "items", "band", None),
        ),
        out_specs=(
            P(None, "items", "band", None),
            P(None, "items", "band", None),
            P(),
            P(),
            P(),
            P(),
            P(),
            P(),
            P(),
            P(),
            P(),
        ),
        check_vma=False,
    )
```

```python
import functools
import math

import jax
import jax.numpy as jnp
from jax import lax
from jax.experimental import pallas as pl
from jax.experimental.pallas import tpu as pltpu
from jax.sharding import PartitionSpec as P

HEADS = 12
HEAD_DIM = 64


EPS = 1e-06


def shortened(shard):

    def short(part):
        return part.astype(jnp.bfloat16) if part.dtype == jnp.float32 else part

    return jax.tree.map(short, shard)


def rms_scale(values, gain):
    return values * lax.rsqrt(jnp.mean(values * values, axis=-1, keepdims=True) + EPS) * gain


def gated(gate, upper):
    return jax.nn.gelu(gate, approximate=True) * upper


def outer(left, right):
    return lax.dot_general(
        left, right, (((0,), (0,)), ((), ())), preferred_element_type=jnp.float32
    )


def transposed(left, weight):
    return lax.dot_general(
        left, weight, (((1,), (1,)), ((), ())), preferred_element_type=jnp.float32
    )


def matmul(left, right):
    return jnp.dot(left, right, preferred_element_type=jnp.float32)


def scores(query, key, scale):
    return jnp.einsum("sqhd,skhd->shqk", query, key, preferred_element_type=jnp.float32) * scale


def per_device(
    inputs,
    counts,
    norm_gain1,
    w_query,
    w_key,
    w_value,
    w_out,
    norm_gain2,
    w_gate,
    w_up,
    w_down,
    cotangent,
):
    micro, seqs, band_rows, width = inputs.shape
    bands = lax.axis_size("band")
    length = band_rows * bands
    rows = seqs * band_rows
    heads = HEADS
    head_dim = HEAD_DIM
    scale = 1.0 / math.sqrt(head_dim)
    key_place = jnp.arange(length, dtype=jnp.int32)
    params = (norm_gain1, w_query, w_key, w_value, w_out, norm_gain2, w_gate, w_up, w_down)
    totals = [jnp.zeros(p.shape, jnp.float32) for p in params]
    results = []
    input_grads = []
    for number in range(micro):
        hidden = inputs[number].astype(jnp.float32).reshape(rows, width)
        lengths = counts[number]
        normed = rms_scale(hidden, norm_gain1).astype(jnp.bfloat16)
        query = matmul(normed, w_query).astype(jnp.bfloat16)
        key_local = matmul(normed, w_key).astype(jnp.bfloat16)
        value_local = matmul(normed, w_value).astype(jnp.bfloat16)
        query_four = query.reshape(seqs, band_rows, heads, head_dim)
        key_three = key_local.reshape(seqs, band_rows, width)
        value_three = value_local.reshape(seqs, band_rows, width)
        key_all, value_all = (
            lax.all_gather(key_three, "band", axis=1, tiled=True),
            lax.all_gather(value_three, "band", axis=1, tiled=True),
        )
        live = key_place[None, :] < lengths[:, None]
        key_four = key_all.reshape(seqs, length, heads, head_dim)
        value_four = value_all.reshape(seqs, length, heads, head_dim)
        logits = jnp.where(live[:, None, None, :], scores(query_four, key_four, scale), -jnp.inf)
        top = jnp.max(logits, axis=-1, keepdims=True)
        expo = jnp.exp(logits - top)
        summed = jnp.sum(expo, axis=-1, keepdims=True)
        log_total = top + jnp.log(summed)
        prob = (expo / summed).astype(jnp.bfloat16)
        attended = jnp.einsum(
            "shqk,skhd->sqhd", prob, value_four, preferred_element_type=jnp.float32
        )
        attended = attended.reshape(rows, width).astype(jnp.bfloat16)
        second = hidden + matmul(attended, w_out)
        normed_two = rms_scale(second, norm_gain2).astype(jnp.bfloat16)
        gate = matmul(normed_two, w_gate)
        upper = matmul(normed_two, w_up)
        mixed = gated(gate, upper).astype(jnp.bfloat16)
        results.append(
            (second + matmul(mixed, w_down)).astype(jnp.bfloat16).reshape(seqs, band_rows, width)
        )
        grad_rows = cotangent[number].reshape(rows, width)
        totals[8] = totals[8] + outer(mixed, grad_rows)
        d_mixed = transposed(grad_rows, w_down)
        pull_gate = jax.vjp(gated, gate, upper)[1]
        d_gate, d_upper = pull_gate(d_mixed)
        d_gate = d_gate.astype(jnp.bfloat16)
        d_upper = d_upper.astype(jnp.bfloat16)
        totals[6] = totals[6] + outer(normed_two, d_gate)
        totals[7] = totals[7] + outer(normed_two, d_upper)
        d_normed_two = transposed(d_gate, w_gate) + transposed(d_upper, w_up)
        pull_two = jax.vjp(rms_scale, second, norm_gain2)[1]
        d_second_norm, d_gain_two = pull_two(d_normed_two)
        totals[5] = totals[5] + d_gain_two
        d_second = grad_rows.astype(jnp.float32) + d_second_norm
        d_branch = d_second.astype(jnp.bfloat16)
        totals[4] = totals[4] + outer(attended, d_branch)
        d_attended = transposed(d_branch, w_out).astype(jnp.bfloat16)
        d_att_four = d_attended.reshape(seqs, band_rows, heads, head_dim)
        key_all, value_all = (
            lax.all_gather(key_three, "band", axis=1, tiled=True),
            lax.all_gather(value_three, "band", axis=1, tiled=True),
        )
        key_four = key_all.reshape(seqs, length, heads, head_dim)
        value_four = value_all.reshape(seqs, length, heads, head_dim)
        logits = jnp.where(live[:, None, None, :], scores(query_four, key_four, scale), -jnp.inf)
        prob_full = jnp.exp(logits - log_total)
        prob = prob_full.astype(jnp.bfloat16)
        d_prob = jnp.einsum(
            "sqhd,skhd->shqk", d_att_four, value_four, preferred_element_type=jnp.float32
        )
        delta = jnp.sum(d_prob * prob_full, axis=-1, keepdims=True)
        d_logits = (prob_full * (d_prob - delta)).astype(jnp.bfloat16)
        d_query = (
            jnp.einsum("shqk,skhd->sqhd", d_logits, key_four, preferred_element_type=jnp.float32)
            * scale
        )
        d_query = d_query.reshape(rows, width).astype(jnp.bfloat16)
        d_key_all = (
            jnp.einsum("shqk,sqhd->skhd", d_logits, query_four, preferred_element_type=jnp.float32)
            * scale
        )
        d_value_all = jnp.einsum(
            "shqk,sqhd->skhd", prob, d_att_four, preferred_element_type=jnp.float32
        )
        d_key_three, d_value_three = (
            lax.psum_scatter(
                d_key_all.reshape(seqs, length, width).astype(jnp.bfloat16),
                "band",
                scatter_dimension=1,
                tiled=True,
            ).astype(jnp.float32),
            lax.psum_scatter(
                d_value_all.reshape(seqs, length, width).astype(jnp.bfloat16),
                "band",
                scatter_dimension=1,
                tiled=True,
            ).astype(jnp.float32),
        )
        d_key = d_key_three.reshape(rows, width).astype(jnp.bfloat16)
        d_value = d_value_three.reshape(rows, width).astype(jnp.bfloat16)
        totals[1] = totals[1] + outer(normed, d_query)
        totals[2] = totals[2] + outer(normed, d_key)
        totals[3] = totals[3] + outer(normed, d_value)
        d_normed = (
            transposed(d_query, w_query) + transposed(d_key, w_key) + transposed(d_value, w_value)
        )
        pull_one = jax.vjp(rms_scale, hidden, norm_gain1)[1]
        d_hidden_norm, d_gain_one = pull_one(d_normed)
        totals[0] = totals[0] + d_gain_one
        input_grads.append(
            (d_second + d_hidden_norm).astype(jnp.bfloat16).reshape(seqs, band_rows, width)
        )
    shares = jax.tree.map(
        lambda part: part.astype(jnp.float32),
        lax.psum_scatter(shortened(tuple(totals)), "band", scatter_dimension=0, tiled=True),
    )
    summed_shares = jax.tree.map(
        lambda part: part.astype(jnp.float32), lax.psum(shortened(shares), "items")
    )
    whole = jax.tree.map(
        lambda part, own: part.astype(own.dtype),
        lax.all_gather(shortened(summed_shares), "band", axis=0, tiled=True),
        summed_shares,
    )
    return (jnp.stack(results), jnp.stack(input_grads)) + tuple(whole)


MESH_ID = pl.DeviceIdType.MESH
NEG = -1e30
BF = jnp.bfloat16
F32 = jnp.float32


def place():
    item = lax.axis_index("items")
    band = lax.axis_index("band")
    return item, band // 4, band % 4


def flip(value):
    return value + 1 - 2 * (value % 2)


def far(value):
    return (value + 2) % 4


def greet(peers):
    barrier = pltpu.get_barrier_semaphore()
    for peer in peers:
        pl.semaphore_signal(barrier, inc=1, device_id=peer, device_id_type=MESH_ID)
    pl.semaphore_wait(barrier, len(peers))


def remote(src, dst, send, recv, peer):
    return pltpu.make_async_remote_copy(
        src_ref=src, dst_ref=dst, send_sem=send, recv_sem=recv, device_id=peer, device_id_type=MESH_ID
    )


def params(number, vmem=62):
    return pltpu.CompilerParams(
        collective_id=number, has_side_effects=True, vmem_limit_bytes=vmem << 20
    )


def whole(value, unit):
    return value if isinstance(value, int) else pl.multiple_of(value, unit)


def lanes_of(rows):
    return lax.broadcasted_iota(jnp.int32, (rows, 128), 1)


ANY = pl.BlockSpec(memory_space=pl.ANY)
VMEM = pl.BlockSpec(memory_space=pltpu.VMEM)
SMEM = pl.BlockSpec(memory_space=pltpu.SMEM)


class Moves:
    def __init__(self):
        self.remotes, self.locals, self.arrivals = [], [], []

    def start(self):
        for make in self.remotes + self.locals:
            make().start()

    def finish(self):
        for make in self.arrivals:
            make().wait_recv()
        for make in self.locals:
            make().wait()
        for make in self.remotes:
            make().wait_send()


def to_slots(item, z, g, src_ref, dst_ref, send, recv, own_sem):
    zs = (z, flip(z), far(z), far(flip(z)))
    p, r = z // 2, z % 2
    moves = Moves()

    def out(n):
        if n < 3:
            s = zs[n + 1]
            src, where = src_ref.at[3 * (s // 2) + 2 * (s % 2)], z
        else:
            s = far(z)
            src, where = src_ref.at[3 * (1 - p) + 1], 4 + p
        return remote(src, dst_ref.at[where], send.at[n], recv.at[where], (item, s * 4 + g))

    def came(where):
        block = dst_ref.at[where]
        return remote(block, block, send.at[0], recv.at[where], (item, far(z) * 4 + g))

    moves.remotes = [lambda n=n: out(n) for n in range(4)]
    moves.locals = [
        lambda: pltpu.make_async_copy(src_ref.at[3 * p + 2 * r], dst_ref.at[z], own_sem.at[0]),
        lambda: pltpu.make_async_copy(src_ref.at[3 * p + 1], dst_ref.at[4 + p], own_sem.at[1]),
    ]
    moves.arrivals = [lambda w=w: came(w) for w in zs[1:] + (4 + (1 - p),)]
    return moves


def from_slots(item, z, g, src_ref, dst_ref, send, recv, own_sem):
    zs = (z, flip(z), far(z), far(flip(z)))
    p, r = z // 2, z % 2
    mine = 3 * p + 2 * r
    moves = Moves()

    def out(n):
        s = zs[n + 1] if n < 3 else far(z)
        src, where = (src_ref.at[s], mine) if n < 3 else (src_ref.at[4 + (1 - p)], 3 * p + 1)
        return remote(src, dst_ref.at[where], send.at[n], recv.at[where], (item, s * 4 + g))

    def came(where):
        block = dst_ref.at[where]
        return remote(block, block, send.at[0], recv.at[where], (item, far(z) * 4 + g))

    moves.remotes = [lambda n=n: out(n) for n in range(4)]
    moves.locals = [
        lambda: pltpu.make_async_copy(src_ref.at[z], dst_ref.at[mine], own_sem.at[0]),
        lambda: pltpu.make_async_copy(src_ref.at[4 + p], dst_ref.at[3 * p + 1], own_sem.at[1]),
    ]
    theirs = [3 * (s // 2) + 2 * (s % 2) for s in zs[1:]] + [3 * (1 - p) + 1]
    moves.arrivals = [lambda w=w: came(w) for w in theirs]
    return moves


def z_peers(item, z, g):
    return [(item, s * 4 + g) for s in (flip(z), far(z), far(flip(z)))]


def g_peers(item, z, g):
    return [(item, z * 4 + h) for h in (flip(g), far(g), far(flip(g)))]


def swap_heads(item, z, g, src_ref, dst_ref, send, recv, own_sem):
    moves = Moves()

    def out(n, h):
        return remote(src_ref.at[h], dst_ref.at[g], send.at[n], recv.at[g], (item, z * 4 + h))

    def came(h):
        return remote(dst_ref.at[h], dst_ref.at[h], send.at[0], recv.at[h], (item, z * 4 + h))

    moves.remotes = [lambda n=n, h=h: out(n, h) for n, h in enumerate((far(g), far(flip(g)), flip(g)))]
    moves.locals = [lambda: pltpu.make_async_copy(src_ref.at[g], dst_ref.at[g], own_sem)]
    moves.arrivals = [lambda h=h: came(h) for h in (flip(g), far(g), far(flip(g)))]
    return moves


def nt(left, right):
    return lax.dot_general(left, right, (((1,), (1,)), ((), ())), preferred_element_type=F32)


def front_phase(ins, outs, landing, sems):
    x_ref, cot_ref, count_ref, gain_ref, wq_ref, wk_ref, wv_ref = ins
    q_out, k_out, v_out, kt_out, o01_out, o2_out, xn_out, wc_out = outs
    orecv_ref, dy_ref, hid_ref, xall_ref, osend_ref = landing
    (
        z_send, f_send, g_send, recv, own_sem, win_sem, o_send, o_recv, cot_send, cot_recv, cot_own,
        half_sem, tile_sem, last_sem,
    ) = sems
    item, z, g = place()
    p, r = z // 2, z % 2
    gc, gx = flip(g), far(g)
    gcx = far(gc)
    zs = (z, flip(z), far(z), far(flip(z)))
    core, across = (item, z * 4 + gc), (item, z * 4 + gx)
    lane = lanes_of(256)
    low = lane < 64

    def items_of(s):
        return (3 * (s // 2) + 2 * (s % 2), 3 * (s // 2) + 1)

    started = []

    def go(make):
        make().start()
        started.append(make)

    def forward(n, ab):
        def make(k, peer):
            where = zs[n] * 4 + g
            src = x_ref.at[items_of(z)[ab]] if n == 0 else xall_ref.at[ab, where]
            return remote(src, xall_ref.at[ab, where], f_send.at[n, ab, k], recv.at[ab, where], peer)

        go(lambda: make(0, across))
        go(lambda: make(1, core))

    def arrived(ab, where):
        block = xall_ref.at[ab, where]
        remote(block, block, z_send.at[0, 0], recv.at[ab, where], core).wait_recv()

    def send_z(ab):
        for n, s in enumerate(zs[1:]):
            go(
                lambda n=n, s=s: remote(
                    x_ref.at[items_of(s)[ab]],
                    xall_ref.at[ab, z * 4 + g],
                    z_send.at[n, ab],
                    recv.at[ab, z * 4 + g],
                    (item, s * 4 + g),
                )
            )

    def own_copy(ab):
        return pltpu.make_async_copy(x_ref.at[items_of(z)[ab]], xall_ref.at[ab, z * 4 + g], own_sem.at[ab])

    def forward_z(ab, n):
        arrived(ab, zs[n] * 4 + g)
        forward(n, ab)

    def forward_x(ab, n):
        def make():
            where = zs[n] * 4 + gx
            block = xall_ref.at[ab, where]
            return remote(block, block, g_send.at[n, ab], recv.at[ab, where], core)

        arrived(ab, zs[n] * 4 + gx)
        go(make)

    def o_copy(t, k):
        h = (gx, gcx, gc)[k]
        return remote(
            osend_ref.at[h, t], orecv_ref.at[g, t], o_send.at[t, k], o_recv.at[g, t], (item, z * 4 + h)
        )

    def self_copy(t):
        return pltpu.make_async_copy(osend_ref.at[g, t], orecv_ref.at[g, t], tile_sem.at[t, 3])

    def block_copy(j):
        src = xall_ref.at[0, j * 4 + g] if j < 4 else xall_ref.at[1, (r + 2 * (j - 4)) * 4 + g]
        return pltpu.make_async_copy(src, hid_ref.at[j], last_sem.at[j])

    moved = to_slots(item, z, g, cot_ref, dy_ref, cot_send, cot_recv, cot_own)

    def arrive():
        for t in range(6):
            for h in (gx, gcx, gc):
                block = orecv_ref.at[h, t]
                remote(block, block, o_send.at[0, 0], o_recv.at[h, t], core).wait_recv()
            self_copy(t).wait()
        moved.finish()

    def leave():
        for t in range(6):
            for k in range(3):
                o_copy(t, k).wait_send()
        for make in started:
            make().wait_send()

    def body(win_ref, q_ref, k_ref, v_ref, kt_ref, o01_ref, o2_ref, xn_ref, wc_ref):
        send_z(0)
        forward(0, 0)
        send_z(1)
        forward(0, 1)
        cut = pl.ds(pl.multiple_of(g * 3 // 2 * 128, 128), 256)
        windows = []
        for n, ref in enumerate((wq_ref, wk_ref, wv_ref)):
            windows.append(pltpu.make_async_copy(ref.at[:, cut], win_ref.at[n], win_sem.at[n]))

        for copy in windows + [own_copy(0), own_copy(1)]:
            copy.start()
        for copy in windows:
            copy.wait()
        odd = g % 2 == 1

        @pl.loop(0, 3)
        def _(i):
            rows = pl.ds(pl.multiple_of(i * 256, 256), 256)
            firsts, lasts = [], []
            for n in range(3):
                left = win_ref[n, rows, 0:128].astype(F32)
                right = win_ref[n, rows, 128:256].astype(F32)
                crossed = pltpu.roll(jnp.where(low, right, left), 64, 1)
                firsts.append(jnp.where(odd, crossed, left))
                lasts.append(jnp.where(odd, pltpu.roll(right, 64, 1), right))
            for n in range(3):
                wc_ref[rows, n * 128 : n * 128 + 128] = firsts[n].astype(BF)
            wc_ref[rows, 384:512] = jnp.where(low, lasts[1], pltpu.roll(lasts[2], 64, 1)).astype(BF)
            wc_ref[rows, 512:640] = jnp.where(low, lasts[0], 0.0).astype(BF)

        def project(ab, n):
            zz = zs[n]
            if n == 0:
                own_copy(ab).wait()
            for h in (gc, gcx):
                arrived(ab, zz * 4 + h)
            rows = pl.ds(pl.multiple_of(ab * 1024 + zz * 256, 256), 256)
            h = xall_ref[ab, pl.ds(zz * 4, 4)].reshape(256, 768).astype(F32)
            inv = lax.rsqrt(jnp.mean(h * h, axis=-1, keepdims=True) + EPS)
            xn = (h * inv * gain_ref[...].reshape(1, 768)).astype(BF)
            xn_ref[rows, :] = xn
            y = matmul(xn, wc_ref[:, 128:512])
            count = count_ref[p, (2 * r if ab == 0 else 1)]
            at = lax.broadcasted_iota(jnp.int32, (256, 128), 0) + zz * 256
            bias = jnp.where(at < count, 0.0, NEG)
            one = jnp.where((lane % 64) < 4, 1.0, 0.0)
            k_aug = jnp.where(lane % 64 == 0, bias, one)
            k01, v01, kv2 = y[:, :128], y[:, 128:256], y[:, 256:]
            keys = (jnp.where(low, k01, k_aug), jnp.where(low, k_aug, k01), jnp.where(low, kv2, k_aug))
            cols = pl.ds(pl.multiple_of(zz * 256, 256), 256)
            for head in range(3):
                key = keys[head].astype(BF)
                k_ref[head, rows, :] = key
                kt_ref[head, ab, :, cols] = key.T
            v_ref[0, rows, :] = jnp.where(low, v01, one).astype(BF)
            v_ref[1, rows, :] = jnp.where(low, one, v01).astype(BF)
            v_ref[2, rows, :] = jnp.where(low, one, kv2).astype(BF)

        def half_copy(ab, n):
            rows = pl.ds(ab * 1024, 1024)
            a, b = (
                (k_ref.at[:, rows], k_out.at[:, rows]), (v_ref.at[:, rows], v_out.at[:, rows]),
                (kt_ref.at[:, ab], kt_out.at[:, ab]), (xn_ref.at[rows], xn_out.at[rows]),
            )[n]
            return pltpu.make_async_copy(a, b, half_sem.at[ab, n])

        def tile(t):
            off = jnp.where(t < 4, t, 4 + r + 2 * (t - 4)) * 256
            xq = xn_ref[pl.ds(pl.multiple_of(off, 256), 256), :]
            q01 = matmul(xq, wc_ref[:, 0:128]).astype(BF).astype(F32) * 0.125
            q2 = matmul(xq, wc_ref[:, 512:640]).astype(BF).astype(F32) * 0.125
            flag = jnp.where(lane % 64 == 0, 1.0, 0.0)
            qs = (jnp.where(low, q01, flag), jnp.where(low, flag, q01), jnp.where(low, q2, flag))
            at = pl.ds(pl.multiple_of(t * 256, 256), 256)
            ab = t // 4
            keys = pl.ds(pl.multiple_of(ab * 1024, 1024), 1024)
            outs = []
            for head in range(3):
                s = matmul(qs[head].astype(BF), kt_ref[head, ab])
                top = jnp.max(s, axis=1, keepdims=True)
                e = jnp.exp(s - top).astype(BF)
                o = matmul(e, v_ref[head, keys, :])
                total = o[:, 64:65] if head == 0 else o[:, 0:1]
                outs.append(o / total)
                lse = -(top + jnp.log(total))
                hi = lse.astype(BF).astype(F32)
                mid = (lse - hi).astype(BF).astype(F32)
                lo = lse - hi - mid
                part = lane % 64
                aug = jnp.where(part == 1, hi, jnp.where(part == 2, mid, jnp.where(part == 3, lo, flag)))
                data = low if head != 1 else jnp.logical_not(low)
                q_ref[head, at, :] = jnp.where(data, qs[head], aug).astype(BF)
            o01 = jnp.where(low, outs[0], outs[1])
            o2 = outs[2]
            o01_ref[at, :] = o01
            o2_ref[at, :] = o2
            for h in range(4):
                osend_ref[h, t, 0:64, :] = o01[h * 64 : h * 64 + 64].astype(BF)
                first = o2[h * 64 : h * 64 + 32]
                second = o2[h * 64 + 32 : h * 64 + 64]
                folded = jnp.where(low[:32], pltpu.roll(first, 64, 1), second)
                osend_ref[h, t, 64:96, :] = folded.astype(BF)

        saved = []

        def keep(makes):
            for make in makes:
                make().start()
                saved.append(make)

        def tile_copy(t, k):
            rows = pl.ds(whole(t * 256, 256), 256)
            a, b = (
                (q_ref.at[:, rows], q_out.at[:, rows]), (o01_ref.at[rows], o01_out.at[rows]),
                (o2_ref.at[rows], o2_out.at[rows]),
            )[k]
            return pltpu.make_async_copy(a, b, tile_sem.at[t, k])

        keep([lambda: pltpu.make_async_copy(wc_ref, wc_out, last_sem.at[6])])
        forward_z(0, 1)
        forward_x(0, 0)
        project(0, 0)
        forward_z(0, 2)
        forward_x(0, 1)
        project(0, 1)
        forward_z(0, 3)
        forward_z(1, 1)
        forward_x(0, 2)
        project(0, 2)
        forward_x(0, 3)
        forward_x(1, 0)
        project(0, 3)
        keep([lambda n=n: half_copy(0, n) for n in range(4)])
        forward_z(1, 2)

        @pl.loop(0, 6)
        def _(t):
            tile(t)
            for k in range(3):
                o_copy(t, k).start()
            self_copy(t).start()
            for k in range(3):
                tile_copy(t, k).start()

            @pl.when(t == 0)
            def _():
                forward_z(1, 3)
                moved.start()
                forward_x(1, 1)

            @pl.when(t == 1)
            def _():
                project(1, 0)
                project(1, 1)

            @pl.when(t == 2)
            def _():
                forward_x(1, 2)
                project(1, 2)

            @pl.when(t == 3)
            def _():
                forward_x(1, 3)
                project(1, 3)
                keep([lambda n=n: half_copy(1, n) for n in range(4)])
                keep([lambda j=j: block_copy(j) for j in range(6)])

        for t in range(6):
            for k in range(3):
                tile_copy(t, k).wait()
        for make in saved:
            make().wait()

    return body, arrive, leave


GELU_A = 0.044715
GELU_C = math.sqrt(2.0 / math.pi)


def widen_kernel(
    qkv_ref, last_ref, so_ref, sg_ref, su_ref, sd_ref, gains_ref, first_ref, second_ref,
    q_ref, k_ref, v_ref, o_ref, g_ref, u_ref, d_ref, gain1_ref, gain2_ref, first_out, second_out,
):
    first_out[...] = first_ref[...]
    second_out[...] = second_ref[...]

    @pl.when(pl.program_id(0) == 0)
    def _():
        gain1_ref[...] = gains_ref[0, :]
        gain2_ref[...] = gains_ref[1, :]

    low = lanes_of(qkv_ref.shape[1]) < 64

    def swap(v):
        return pltpu.roll(v, 64, 1)

    later = pl.program_id(0) * 2 >= pl.num_programs(0)
    for out, first, where in ((q_ref, 0, 0), (k_ref, 128, 1), (v_ref, 256, 2)):
        a = [qkv_ref[n, :, first : first + 128].astype(F32) for n in range(4)]
        if where == 0:
            b = [last_ref[n].astype(F32) for n in range(4)]
            low_b = [jnp.where(later, swap(x), x) for x in b]
            high_b = [swap(x) for x in low_b]
        else:
            b = [qkv_ref[n, :, 384:512].astype(F32) for n in range(4)]
            low_b = b if where == 1 else [swap(x) for x in b]
            high_b = [swap(x) for x in low_b]
        tiles = (
            a[0], jnp.where(low, low_b[0], swap(a[1])), jnp.where(low, swap(a[1]), high_b[1]),
            a[2], jnp.where(low, low_b[2], swap(a[3])), jnp.where(low, swap(a[3]), high_b[3]),
        )
        for n, tile in enumerate(tiles):
            out[:, n * 128 : n * 128 + 128] = tile
    o_ref[...] = so_ref[...].astype(F32)
    g_ref[...] = sg_ref[...].astype(F32)
    u_ref[...] = su_ref[...].astype(F32)
    d_ref[...] = sd_ref[...].astype(F32)

def widen(qkv, last, s_out, s_gate, s_up, s_down, gains, first, second):
    s = jax.ShapeDtypeStruct
    steps = 4

    def spec(a):
        if len(a.shape) == 3:
            return pl.BlockSpec((a.shape[0], a.shape[1] // steps, a.shape[2]), lambda i: (0, i, 0))
        return pl.BlockSpec((a.shape[0] // steps, a.shape[1]), lambda i: (i, 0))

    outs = tuple(s(a.shape, F32) for a in (s_out, s_out, s_out, s_out, s_gate, s_up, s_down))
    ins = (s_out, s_gate, s_up, s_down)
    folded = pl.BlockSpec((4, last.shape[1] // 2, 128), lambda i: (0, i % 2, 0))
    width = gains.shape[1]
    vector = pl.BlockSpec((width,), lambda i: (0,))
    moved = (s(first.shape, first.dtype), s(second.shape, second.dtype))
    return pl.pallas_call(
        widen_kernel,
        grid=(steps,),
        out_shape=outs + (s((width,), F32),) * 2 + moved,
        in_specs=[spec(qkv), folded] + [spec(a) for a in ins] + [pl.BlockSpec(gains.shape, lambda i: (0, 0)), spec(first), spec(second)],
        out_specs=tuple(spec(a) for a in outs) + (vector, vector, spec(first), spec(second)),
        compiler_params=pltpu.CompilerParams(vmem_limit_bytes=62 << 20),
        name="widen",
    )(qkv, last, *ins, gains, first, second)


class Stream:
    def __init__(self, spare, res, acc, first, rest, sems, order, coords, core, cut):
        self.spare, self.res, self.acc, self.first, self.rest = spare, res, acc, first, rest
        self.send, self.recv, self.own, self.back, self.got, self.fwd, self.fgot = sems
        row, col, half = cut
        self.rows, self.wide = acc.shape
        self.row = row
        self.order = [coords[name] for name in order]
        self.deep = len(order)
        bit, self.peer = core
        if half:
            self.mine = pl.ds(pl.multiple_of(bit * half + col, 128), self.wide)
            self.other = pl.ds(pl.multiple_of((1 - bit) * half + col, 128), self.wide)
        else:
            self.mine = pl.ds(col, self.wide)
        self.base, self.size = [0], [self.rows]
        for bit, _ in self.order:
            self.size.append(self.size[-1] // 2)
            self.base.append(self.base[-1] + bit * self.size[-1])

    def part(self, base, size):
        return pl.ds(whole(base, 16), size)

    def at(self, base, size, mine=True):
        cols = self.mine if mine else self.other
        return self.res.at[pl.ds(whole(self.row + base, 16), size), cols]

    def sibling(self, k):
        return self.base[k - 1] + (1 - self.order[k - 1][0]) * self.size[k]

    def own_out(self):
        here = self.base[self.deep], self.size[self.deep]
        return pltpu.make_async_copy(self.acc.at[self.part(*here)], self.at(*here), self.own.at[1])

    def c_push(self, k):
        if k == 0:
            return remote(self.spare, self.first, self.send.at[0], self.recv.at[0], self.peer)
        return remote(
            self.acc.at[self.part(self.sibling(k), self.size[k])],
            self.rest.at[pl.ds(self.rows - 2 * self.size[k], self.size[k])],
            self.send.at[k],
            self.recv.at[k],
            self.order[k - 1][1],
        )

    def c_back(self, k):
        here = self.base[k], self.size[k]
        src = self.acc.at[self.part(*here)] if k == self.deep else self.at(*here)
        return remote(
            src, self.at(*here), self.back.at[k - 1], self.got.at[k - 1], self.order[k - 1][1]
        )

    def c_forward(self, k):
        if k == 0:
            here = self.base[self.deep], self.size[self.deep]
            src = self.acc.at[self.part(*here)]
        else:
            here = self.sibling(k), self.size[k]
            src = self.at(*here)
        return remote(src, self.at(*here), self.fwd.at[k], self.fgot.at[k], self.peer)

    def open(self):
        self.c_push(0).start()

    def fold(self, k):
        self.c_push(k).wait_recv()
        base, size = self.base[k], self.size[k]
        other, at = (self.first, 0) if k == 0 else (self.rest, self.rows - 2 * size)
        step = 64 if size % 64 == 0 else 48 if size % 48 == 0 else 32

        @pl.loop(0, size // step)
        def _(n):
            rows = self.part(base + n * step, step)
            more = other[pl.ds(pl.multiple_of(at + n * step, 16), step), :]
            self.acc[rows, :] = (self.acc[rows, :].astype(F32) + more.astype(F32)).astype(BF)

        if k < self.deep:
            self.c_push(k + 1).start()
        else:
            self.c_back(k).start()
            self.c_forward(0).start()
            self.own_out().start()

    def collect(self, k):
        here = self.sibling(k), self.size[k]
        block = self.at(*here)
        remote(block, block, self.back.at[k - 1], self.got.at[k - 1], self.peer).wait_recv()
        if k == self.deep:
            self.own_out().wait()
        if k > 1:
            self.c_back(k - 1).start()
        self.c_forward(k).start()

    def close(self):
        for k in range(self.deep + 1):
            if k == 0:
                here = self.base[self.deep], self.size[self.deep]
            else:
                here = self.sibling(k), self.size[k]
            block = self.at(*here, mine=False)
            remote(block, block, self.fwd.at[k], self.fgot.at[k], self.peer).wait_recv()
            self.c_push(k).wait_send()
            self.c_forward(k).wait_send()
            if k > 0:
                self.c_back(k).wait_send()


class Grouped(Stream):
    def __init__(self, res, acc, rest, sems, order, coords, core, cut, group, across, late):
        super().__init__(None, res, acc, None, rest, sems, order, coords, core, cut)
        self.group, self.gx, self.across, self.late = group, far(group), across, late

    def at(self, base, size, n=0):
        h = (self.group, self.gx, flip(self.group), far(flip(self.group)))[n]
        return self.res.at[h, self.part(base, size), self.mine]

    def source(self, k, n):
        here = self.base[k], self.size[k]
        return self.acc.at[self.part(*here)] if k == self.deep and n == 0 else self.at(*here, n)

    def c_across(self):
        k = self.late
        return remote(
            self.source(k, 0),
            self.at(self.base[k], self.size[k]),
            self.back.at[self.deep, 0],
            self.got.at[self.deep, 0],
            self.across,
        )

    def c_back(self, k, n):
        there = self.at(self.base[k], self.size[k], n)
        return remote(
            self.source(k, n), there, self.back.at[k - 1, n], self.got.at[k - 1, n], self.order[k - 1][1]
        )

    def span(self, k, n):
        if k > 0:
            return self.sibling(k), self.size[k]
        k = self.deep if n == 0 else self.late
        return self.base[k], self.size[k]

    def c_forward(self, k, n):
        src = self.source(self.deep, 0) if k == n == 0 else self.at(*self.span(k, n), n)
        return remote(src, self.at(*self.span(k, n), n), self.fwd.at[k, n], self.fgot.at[k, n], self.peer)

    def fold(self, k):
        if k == 0:
            self.c_push(1).start()
            return
        if k < self.deep:
            super().fold(k)
            return
        self.c_push(k).wait_recv()
        base, size = self.base[k], self.size[k]
        rows = self.part(base, size)
        more = self.rest[pl.ds(self.rows - 2 * size, size), :]
        self.acc[rows, :] = (self.acc[rows, :].astype(F32) + more.astype(F32)).astype(BF)
        if self.late == k:
            self.c_across().start()
        self.c_back(k, 0).start()
        self.c_forward(0, 0).start()
        self.own_out().start()

    def extend(self):
        self.c_across().wait_recv()
        if self.late > 0:
            self.c_back(self.late, 1).start()
        self.c_forward(0, 1).start()

    def collect(self, k):
        if k == self.deep:
            self.own_out().wait()
        two = 2 if k <= self.late else 1
        for n in range(two):
            block = self.at(*self.span(k, n), n)
            remote(block, block, self.back.at[k - 1, n], self.got.at[k - 1, n], self.peer).wait_recv()
        if self.late == k - 1:
            self.c_across().start()
        if k > 1:
            for n in range(two):
                self.c_back(k - 1, n).start()
        for n in range(two):
            self.c_forward(k, n).start()

    def close(self):
        self.c_across().wait_send()
        for k in range(self.deep + 1):
            if k > 0:
                self.c_push(k).wait_send()
            for n in range(2 if k <= self.late else 1):
                block = self.at(*self.span(k, n), 2 + n)
                remote(block, block, self.fwd.at[k, n], self.fgot.at[k, n], self.peer).wait_recv()
                self.c_forward(k, n).wait_send()
                if k > 0:
                    self.c_back(k, n).wait_send()


X, Y, ZL, ZH = range(4)
(FF, FFPOST, RES, SWAP, TILE, DXN, GW, END, XSB, XSA, TB, TA, ZB, NA, NB) = range(100, 115)
OPEN, FOLD, COLLECT, EXTEND, GAIN = range(5)
PIECES = (
    (0, 0, 0, 0, 768, 256, 256, (Y, X, ZL, ZH)),
    (0, 1, 0, 512, 768, 256, 256, (X, Y, ZL, ZH)),
    (0, 2, 0, 1024, 768, 256, 256, (X, Y, ZL, ZH)),
    (0, 3, 0, 1536, 768, 256, 256, (Y, ZL, X, ZH)),
    (1, 0, 0, 0, 768, 256, 256, (Y, X, ZL, ZH)),
    (1, 1, 0, 512, 768, 256, 256, (Y, X, ZL, ZH)),
    (1, 2, 0, 1024, 768, 256, 256, (ZH, Y, X, ZL)),
    (1, 3, 0, 1536, 768, 256, 256, (X, Y, ZH, ZL)),
    (2, 0, 0, 0, 512, 384, 384, (Y, X, ZL, ZH)),
    (2, 1, 512, 0, 512, 384, 384, (ZL, Y, ZH, X)),
    (2, 2, 1024, 0, 512, 384, 384, (ZL, X, Y, ZH)),
    (2, 3, 1536, 0, 512, 384, 384, (X, Y, ZH, ZL)),
    (3, 0, 0, 0, 768, 384, 384, (X, ZH, Y, ZL)),
)
GROUPS = (
    (0, 384, 768, 128, (ZL, Y, ZH), 2),
    (0, 0, 768, 384, (Y, ZL, ZH), 1),
    (1, 0, 384, 128, (Y, ZL, ZH), 0),
)
PLAN = (
    FF, (OPEN, 8, 0), (OPEN, 4, 0), (OPEN, 0, 0), FF, (OPEN, 1, 0), (OPEN, 5, 0), (OPEN, 9, 0),
    (FOLD, 8, 0), FF, (OPEN, 10, 0), (OPEN, 2, 0), (OPEN, 6, 0), (FOLD, 0, 0), (FOLD, 1, 0), (FOLD, 5, 0),
    (FOLD, 4, 0), (FOLD, 9, 0), FF, (OPEN, 3, 0), (OPEN, 7, 0), (OPEN, 11, 0), (FOLD, 8, 1), (FOLD, 6, 0),
    (FOLD, 10, 0), (FOLD, 2, 0), FFPOST, (OPEN, 12, 0), (FOLD, 0, 1), (FOLD, 8, 2), (FOLD, 9, 1), (FOLD, 1, 1),
    (FOLD, 3, 0), (FOLD, 11, 0), RES, (FOLD, 7, 0), (FOLD, 5, 1), (FOLD, 2, 1), (FOLD, 12, 0), (FOLD, 4, 1),
    (FOLD, 6, 1), (FOLD, 10, 1), (FOLD, 9, 2), (FOLD, 8, 3), (FOLD, 1, 2), SWAP, TILE, (FOLD, 0, 2),
    TILE, (FOLD, 3, 1), TILE, (FOLD, 6, 2), (FOLD, 11, 1), (FOLD, 2, 2), (FOLD, 1, 3), TILE,
    (FOLD, 0, 3), (FOLD, 9, 3), (FOLD, 3, 2), (FOLD, 7, 1), (FOLD, 8, 4), (FOLD, 2, 3), (FOLD, 5, 2), (FOLD, 1, 4),
    (FOLD, 11, 2), TILE, (FOLD, 0, 4), (COLLECT, 8, 4), TILE, (FOLD, 5, 3), (FOLD, 7, 2), (FOLD, 12, 1),
    (COLLECT, 1, 4), DXN, (FOLD, 11, 3), (COLLECT, 8, 3), (COLLECT, 0, 4), (FOLD, 10, 2), (FOLD, 4, 2), GW,
    END, XSB, (FOLD, 6, 3), (FOLD, 13, 0), (FOLD, 14, 0), (FOLD, 15, 0), XSA, TB,
    (FOLD, 3, 3), TA, (FOLD, 11, 4), (COLLECT, 8, 2), (COLLECT, 0, 3), (FOLD, 7, 3), (FOLD, 5, 4), (FOLD, 10, 3),
    (FOLD, 4, 3), (FOLD, 12, 2), (COLLECT, 1, 3), (FOLD, 13, 1), (FOLD, 3, 4), (COLLECT, 11, 4), (FOLD, 7, 4), (COLLECT, 5, 4),
    (FOLD, 10, 4), (FOLD, 4, 4), (FOLD, 14, 1), (COLLECT, 3, 4), (FOLD, 15, 1), (COLLECT, 7, 4), ZB, (COLLECT, 5, 3),
    (COLLECT, 11, 3), (COLLECT, 10, 4), (FOLD, 2, 4), (FOLD, 6, 4), (COLLECT, 4, 4), (COLLECT, 8, 1), (FOLD, 14, 2), (FOLD, 12, 3),
    (FOLD, 15, 2), (COLLECT, 7, 3), (COLLECT, 1, 2), (FOLD, 13, 2), NA, NB, (COLLECT, 2, 4), (COLLECT, 10, 3),
    (COLLECT, 0, 2), (COLLECT, 4, 3), (COLLECT, 11, 2), (GAIN, 0, 0), (COLLECT, 7, 2), (COLLECT, 5, 2), (COLLECT, 3, 3), (COLLECT, 6, 4),
    (FOLD, 14, 3), (FOLD, 12, 4), (FOLD, 15, 3), (FOLD, 13, 3), (GAIN, 0, 1), (COLLECT, 1, 1), (COLLECT, 10, 2), (COLLECT, 0, 1),
    (COLLECT, 4, 2), (COLLECT, 5, 1), (COLLECT, 2, 3), (COLLECT, 11, 1), (COLLECT, 3, 2), (COLLECT, 4, 1), (FOLD, 9, 4), (COLLECT, 12, 4),
    (COLLECT, 7, 1), (COLLECT, 2, 2), (COLLECT, 6, 3), (GAIN, 0, 2), (COLLECT, 9, 4), (COLLECT, 14, 3), (COLLECT, 15, 3), (COLLECT, 3, 1),
    (COLLECT, 10, 1), (COLLECT, 13, 3), (COLLECT, 12, 3), (COLLECT, 2, 1), (COLLECT, 9, 3), (COLLECT, 6, 2), (EXTEND, 13, 0), (GAIN, 0, 3),
    (COLLECT, 14, 2), (COLLECT, 15, 2), (COLLECT, 9, 2), (COLLECT, 13, 2), (COLLECT, 12, 2), (GAIN, 0, 4), (EXTEND, 14, 0), (COLLECT, 15, 1),
    (COLLECT, 9, 1), (COLLECT, 6, 1), (COLLECT, 12, 1), (COLLECT, 13, 1), (GAIN, 0, 5), (EXTEND, 15, 0), (COLLECT, 14, 1),
)


def layer_kernel(*refs):
    take = iter(refs)

    def some(n):
        return [next(take) for _ in range(n)]

    x_ref, cot_ref, count_ref, gain_ref, wq_ref, wk_ref, wv_ref = some(7)
    gain2_ref, wo_hbm, wg_hbm, wu_hbm, wd_hbm = some(5)
    out_ref, res_out_ref = some(2)
    outs = some(6)
    (gains_out,) = some(1)
    loads_hbm = some(8)
    orecv_ref, dy_ref, xall_ref, osend_ref = some(4)
    front_sems = some(14)
    h_ref, dh_ref, res_ref, dsend_ref, dgain2_ref = some(5)
    both = some(4)
    dense_sem, w_sem, load_sem = some(3)
    (do_ref, p_ref) = some(2)
    (rc_ref, sx_ref, rx_ref, t_ref, zb_ref, rz_ref, ig_ref, dgain_ref) = some(8)
    (c_send, c_recv, x_send, x_recv, z_send, z_recv) = some(6)
    (rs_send, rs_recv, rs_own, h_send, h_recv, h_own, hs, hr, ho) = some(9)
    item, z, g = place()
    gc, gx = flip(g), far(g)
    gcx = far(gc)
    p, r = z // 2, z % 2
    side = g % 2
    coords = (
        (g // 2, (item, z * 4 + gx)),
        (item, (1 - item, z * 4 + g)),
        (z % 2, (item, flip(z) * 4 + g)),
        (z // 2, (item, far(z) * 4 + g)),
    )
    across, pair = coords[X][1], coords[ZL][1]
    core = (item, z * 4 + gc)
    zs = (z, flip(z), far(z), far(flip(z)))
    streams = []
    for n, m, row, col, _, _, half, order in PIECES:
        first, rest = some(2)
        stream = Stream(
            both[n].at[m, 1 - side], outs[n], both[n].at[m, side], first, rest, some(7), order, coords,
            (side, core), (row, col, half),
        )
        streams.append(stream)
    gw_refs = some(2)
    for n, col, _, wide, order, late in GROUPS:
        (rest,) = some(1)
        acc = gw_refs[n].at[:, pl.ds(col, wide)]
        stream = Grouped(
            outs[4 + n], acc, rest, some(7), order, coords, (side, core), (0, col, 0), g, across, late
        )
        streams.append(stream)
    buf, got, gain_send, gain_recv = some(4)

    greet(g_peers(item, z, g) + z_peers(item, z, g) + [coords[Y][1]])
    swapped = swap_heads(item, z, g, dsend_ref, do_ref, hs, hr, ho.at[0])
    lane = lanes_of(256)
    low = lane < 64
    part = lane % 64

    body, arrive, leave = front_phase(
        (x_ref, cot_ref, count_ref, gain_ref, wq_ref, wk_ref, wv_ref), loads_hbm,
        (orecv_ref, dy_ref, h_ref, xall_ref, osend_ref), front_sems,
    )

    def dense(emit, wo_ref, wg_ref, wu_ref, wd_ref, att_ref, sec_ref, xn_ref, xt_ref, dxn_ref):
        size = 512
        load_wo = pltpu.make_async_copy(wo_hbm, wo_ref, dense_sem.at[0])
        load_wo.start()

        def load(c, n):
            cut = pl.ds(whole(c * size, size), size)
            a, b = ((wg_hbm, wg_ref), (wu_hbm, wu_ref), (wd_hbm, wd_ref))[n]
            a, b = (a.at[:, cut], b.at[:, cut]) if n < 2 else (a.at[cut, :], b.at[cut, :])
            return pltpu.make_async_copy(a, b, w_sem.at[n, c])

        for c in range(4):
            for n in range(3):
                load(c, n).start()
        low = lanes_of(384) < 64

        def swap(v):
            return pltpu.roll(v, 64, 1)

        arrive()
        pairs = [orecv_ref[n, :, 0:64, :].astype(F32).reshape(384, 128) for n in range(4)]

        def unfold(n, high):
            f = orecv_ref[n, :, 64:96, :].astype(F32)
            s = swap(f.reshape(192, 128)).reshape(6, 32, 128)
            two = (s, f) if high else (f, s)
            return jnp.concatenate(two, axis=1).reshape(384, 128)

        tiles = (
            pairs[0],
            jnp.where(low, unfold(0, False), swap(pairs[1])),
            jnp.where(low, swap(pairs[1]), unfold(1, True)),
            pairs[2],
            jnp.where(low, unfold(2, False), swap(pairs[3])),
            jnp.where(low, swap(pairs[3]), unfold(3, True)),
        )
        for n, v in enumerate(tiles):
            att_ref[:, n * 128 : n * 128 + 128] = v.astype(BF)
        load_wo.wait()
        second = h_ref[...].reshape(384, 768).astype(F32) + matmul(att_ref[...], wo_ref[...])
        sec_ref[...] = second
        dh_ref[...] = second.reshape(6, 64, 768)
        inv = lax.rsqrt(jnp.mean(second * second, axis=-1, keepdims=True) + EPS)
        xn_ref[...] = (second * inv * gain2_ref[...].reshape(1, 768)).astype(BF)
        xt_ref[...] = xn_ref[...].T
        dxn_ref[...] = jnp.zeros_like(dxn_ref)

        def chunk(c):
            cut = pl.ds(pl.multiple_of(c * size, size), size)
            for n in range(3):
                load(c, n).wait()
            dy = dy_ref[...].reshape(384, 768)
            gate = matmul(xn_ref[...], wg_ref[:, cut])
            upper = matmul(xn_ref[...], wu_ref[:, cut])
            d_mixed = nt(dy, wd_ref[cut, :])
            square = gate * gate
            tan = jnp.tanh(GELU_C * (gate + GELU_A * square * gate))
            half = 0.5 * (1.0 + tan)
            act = gate * half
            slope = half + 0.5 * gate * (1.0 - tan * tan) * (GELU_C * (1.0 + 3.0 * GELU_A * square))
            mixed = (act * upper).astype(BF)
            d_gate = (d_mixed * upper * slope).astype(BF)
            d_upper = (d_mixed * act).astype(BF)
            for n, grad in enumerate((d_gate, d_upper)):
                full = matmul(xt_ref[...], grad).astype(BF)
                both[n][c, 0] = full[:, : size // 2]
                both[n][c, 1] = full[:, size // 2 :]
            down = outer(mixed, dy).astype(BF)
            both[2][c, 0] = down[:, :384]
            both[2][c, 1] = down[:, 384:]
            sec_ref[...] += matmul(mixed, wd_ref[cut, :])
            dxn_ref[...] += nt(d_gate, wg_ref[:, cut]) + nt(d_upper, wu_ref[:, cut])

        run_loop(FF, 4, chunk, emit)
        emit_between(FF, FFPOST)
        res_ref[...] = sec_ref[...].astype(BF).reshape(6, 64, 768)
        second = dh_ref[...].reshape(384, 768)
        inv = lax.rsqrt(jnp.mean(second * second, axis=-1, keepdims=True) + EPS)
        d_xn = dxn_ref[...]
        dgain2_ref[...] = jnp.sum(d_xn * second * inv, axis=0, keepdims=True)
        dyg = d_xn * gain2_ref[...].reshape(1, 768)
        dot = jnp.mean(dyg * second, axis=-1, keepdims=True)
        dy = dy_ref[...].reshape(384, 768)
        d_second = dy.astype(F32) + inv * dyg - second * (inv * inv * inv * dot)
        dh_ref[...] = d_second.reshape(6, 64, 768)
        d_branch = d_second.astype(BF)
        d_att = nt(d_branch, wo_ref[...]).astype(BF).astype(F32)
        d = [d_att[:, n * 128 : n * 128 + 128] for n in range(6)]
        firsts = (d[0], swap(jnp.where(low, d[2], d[1])), d[3], swap(jnp.where(low, d[5], d[4])))
        lasts = ((d[1], False), (d[2], True), (d[4], False), (d[5], True))
        low3 = lax.broadcasted_iota(jnp.int32, (6, 32, 128), 2) < 64
        for n in range(4):
            dsend_ref[n, :, 0:64, :] = firsts[n].astype(BF).reshape(6, 64, 128)
            v, high = lasts[n]
            v3, s3 = v.reshape(6, 64, 128), swap(v).reshape(6, 64, 128)
            top, bottom = v3[:, :32], v3[:, 32:]
            top_s, bottom_s = s3[:, :32], s3[:, 32:]
            f = jnp.where(low3, top_s, bottom) if high else jnp.where(low3, top, bottom_s)
            dsend_ref[n, :, 64:96, :] = f.astype(BF)
        swapped.start()
        g_out = outer(att_ref[...], d_branch).astype(BF)
        both[3][0, 0] = g_out[:, :384]
        both[3][0, 1] = g_out[:, 384:]

    def pieces(delta):
        neg = -delta
        hi = neg.astype(BF).astype(F32)
        mid = (neg - hi).astype(BF).astype(F32)
        lo = neg - hi - mid
        return jnp.where(part == 1, hi, jnp.where(part == 2, mid, jnp.where(part == 3, lo, 0.0)))

    loads = {}

    def tile(t):
        q_ref, k_ref, v_ref, kt_ref, o01_ref, o2_ref = (loads[n] for n in range(6))
        dk_ref, dv_ref, d5_ref = (loads[n] for n in ("dk", "dv", "d5"))
        at = pl.ds(pl.multiple_of(t * 256, 256), 256)
        ab = t // 4
        keys = pl.ds(pl.multiple_of(ab * 1024, 1024), 1024)
        do01 = do_ref[:, t, 0:64, :].astype(F32).reshape(256, 128)
        folded = do_ref[:, t, 64:96, :].astype(F32)
        two = []
        for h in range(4):
            two.append(pltpu.roll(folded[h], 64, 1))
            two.append(folded[h])
        do2 = jnp.concatenate(two, axis=0)
        prod = do01 * o01_ref[at, :]
        prod2 = do2 * o2_ref[at, :]
        delta0 = jnp.sum(jnp.where(low, prod, 0.0), axis=1, keepdims=True)
        delta1 = jnp.sum(jnp.where(low, 0.0, prod), axis=1, keepdims=True)
        delta2 = jnp.sum(jnp.where(low, 0.0, prod2), axis=1, keepdims=True)
        dos = (
            jnp.where(low, do01, pieces(delta0)).astype(BF),
            jnp.where(low, pieces(delta1), do01).astype(BF),
            jnp.where(low, pieces(delta2), do2).astype(BF),
        )
        dqs = []
        for head in range(3):
            q = q_ref[head, at, :]
            prob = jnp.exp(nt(k_ref[head, keys, :], q))
            d_prob = nt(v_ref[head, keys, :], dos[head])
            d_log = (prob * d_prob).astype(BF)
            dv_ref[head, keys, :] += matmul(prob.astype(BF), dos[head])
            dk_ref[head, keys, :] += matmul(d_log, q)
            dqs.append(matmul(kt_ref[head, ab], d_log).T * 0.125)
        off = jnp.where(t < 4, t, 4 + r + 2 * (t - 4)) * 256
        rows = pl.ds(pl.multiple_of(off, 256), 256)
        d5_ref[rows, 0:128] = jnp.where(low, dqs[0], dqs[1]).astype(BF)
        d5_ref[rows, 512:640] = jnp.where(low, dqs[2], 0.0).astype(BF)

    halves = ((0, slice(0, 4)), (1, slice(4, 8)))
    away = (gc, gcx)

    def c_copy(k, ab):
        cut = halves[ab][1]
        return remote(p_ref.at[away[k], cut], rc_ref.at[k, cut], c_send.at[k, ab], c_recv.at[k, ab], core)

    def x_copy(ab):
        cut = halves[ab][1]
        return remote(sx_ref.at[cut], rx_ref.at[cut], x_send.at[ab], x_recv.at[ab], across)

    z_copy = remote(zb_ref, rz_ref, z_send.at[0], z_recv.at[0], pair)
    mine = 3 * p + 2 * r

    def home(n):
        if n < 4:
            s = (zs[3], zs[2], zs[1], z)[n]
            src, dst = ig_ref.at[s], out_ref.at[mine]
        else:
            s = z if n == 5 else zs[2]
            src, dst = ig_ref.at[4 + (1 - p if n == 4 else p)], out_ref.at[3 * p + 1]
        if n in (3, 5):
            return pltpu.make_async_copy(src, dst, h_own.at[n // 4])
        where = mine if n < 4 else 3 * p + 1
        return remote(src, dst, h_send.at[min(n, 3)], h_recv.at[where], (item, s * 4 + g))

    gain = gain_ref[...].reshape(1, 768)

    def norm_back(d_xn, j):
        h = h_ref[j].astype(F32)
        inv = lax.rsqrt(jnp.mean(h * h, axis=-1, keepdims=True) + EPS)
        dgain_ref[...] += jnp.sum(d_xn * h * inv, axis=0, keepdims=True)
        dyg = d_xn * gain
        dot = jnp.mean(dyg * h, axis=-1, keepdims=True)
        ig_ref[j] = (dh_ref[j] + inv * dyg - h * (inv * inv * inv * dot)).astype(BF)

    def load_copy(n):
        return pltpu.make_async_copy(loads_hbm[n], loads[n], load_sem.at[n])

    def run_swap():
        for n in range(8):
            load_copy(n).wait()
        swapped.finish()

    def run_dxn():
        wc_ref, dk_ref, dv_ref, d5_ref = (loads[n] for n in (7, "dk", "dv", "d5"))

        @pl.loop(0, 8)
        def _(i):
            rows = pl.ds(pl.multiple_of(i * 256, 256), 256)
            d5_ref[rows, 128:256] = jnp.where(low, dk_ref[0, rows, :], dk_ref[1, rows, :]).astype(BF)
            d5_ref[rows, 256:384] = jnp.where(low, dv_ref[0, rows, :], dv_ref[1, rows, :]).astype(BF)
            d5_ref[rows, 384:512] = jnp.where(low, dk_ref[2, rows, :], dv_ref[2, rows, :]).astype(BF)
            d_xn = nt(d5_ref[rows, :], wc_ref[...]).astype(BF)
            for h in range(4):
                p_ref[h, i, :, :] = d_xn[h * 64 : h * 64 + 64]

        for k in (1, 0):
            for ab in (1, 0):
                c_copy(k, ab).start()

    def run_gw():
        for c in range(4):
            cols = slice(c * 128, c * 128 + 128)
            gw_refs[0][:, cols] = outer(loads[6][...], loads["d5"][:, cols]).astype(BF)
        last = outer(loads[6][...], loads["d5"][:, 512:640])
        folded = jnp.where(lanes_of(384) < 64, last[:384], pltpu.roll(last[384:], 64, 1))
        gw_refs[1][...] = folded.astype(BF)

    def run_xs(ab):
        c_copy(1, ab).wait_recv()

        @pl.loop(0, 4)
        def _(j):
            n = ab * 4 + j
            sx_ref[n] = (p_ref[gx, n].astype(F32) + rc_ref[1, n].astype(F32)).astype(BF)

        x_copy(ab).start()

    def run_t(ab):
        c_copy(0, ab).wait_recv()

        @pl.loop(0, 4)
        def _(j):
            n = ab * 4 + j
            t_ref[n] = p_ref[g, n].astype(F32) + rc_ref[0, n].astype(F32)

    def run_z():
        x_copy(1).wait_recv()
        for q in range(2):
            n = 4 + (1 - r) + 2 * q
            zb_ref[q] = (t_ref[n] + rx_ref[n].astype(F32)).astype(BF)
        z_copy.start()

    def run_na():
        x_copy(0).wait_recv()
        for n, s in enumerate((zs[3], zs[2], zs[1], z)):
            norm_back(t_ref[s] + rx_ref[s].astype(F32), s)
            home(n).start()

    def run_nb():
        z_copy.wait_recv()
        for n, q in enumerate((1 - p, p)):
            k = 4 + r + 2 * q
            norm_back(t_ref[k] + rx_ref[k].astype(F32) + rz_ref[q].astype(F32), 4 + q)
            home(4 + n).start()

    gain_peers = [core] + [peer for _, peer in coords]

    def gain_copy(k):
        return remote(buf.at[k], got.at[k], gain_send.at[k], gain_recv.at[k], gain_peers[k])

    def run_gain(k):
        if k == 0:
            buf[0] = jnp.zeros_like(buf[0])
            buf[0, 0:1, :] = dgain_ref[...]
            buf[0, 1:2, :] = dgain2_ref[...]
        else:
            gain_copy(k - 1).wait_recv()
            buf[k] = buf[k - 1] + got[k - 1]
        if k < 5:
            gain_copy(k).start()
        else:
            gains_out[...] = buf[5]

    homes = from_slots(item, z, g, res_ref, res_out_ref, rs_send, rs_recv, rs_own)

    single = {
        SWAP: run_swap, DXN: run_dxn, GW: run_gw, XSB: lambda: run_xs(1), XSA: lambda: run_xs(0),
        TB: lambda: run_t(1), TA: lambda: run_t(0), ZB: run_z, NA: run_na, NB: run_nb, RES: homes.start,
    }

    def emit(task):
        if task in single:
            single[task]()
        elif isinstance(task, tuple):
            kind, n, k = task
            if kind == GAIN:
                run_gain(k)
            elif kind == OPEN:
                streams[n].open()
            elif kind == FOLD:
                streams[n].fold(k)
            elif kind == COLLECT:
                streams[n].collect(k)
            else:
                streams[n].extend()

    def run_loop(name, count, body, emit):
        at = [n for n, task in enumerate(PLAN) if task == name]

        @pl.loop(0, count)
        def _(t):
            body(t)
            for n in range(count - 1):
                tasks = PLAN[at[n] + 1 : at[n + 1]]
                if tasks:

                    @pl.when(t == n)
                    def _():
                        for task in tasks:
                            emit(task)

    def emit_between(first, last):
        start = 0 if first is None else len(PLAN) - PLAN[::-1].index(first)
        stop = len(PLAN) if last is None else PLAN.index(last)
        for task in PLAN[start:stop]:
            emit(task)

    width, hidden = wg_hbm.shape
    v = pltpu.VMEM
    kept = [v(ref.shape, ref.dtype) for ref in loads_hbm]
    pl.run_scoped(body, v((3, width, 256), BF), *kept)
    pl.run_scoped(
        functools.partial(dense, emit),
        v((width, width), BF), v((width, hidden), BF), v((width, hidden), BF), v((hidden, width), BF),
        v((384, width), BF), v((384, width), F32), v((384, width), BF),
        v((width, 384), BF), v((384, width), F32),
    )

    def attend(*scoped):
        loads.update(enumerate(scoped[:8]))
        loads.update(zip(("dk", "dv", "d5"), scoped[8:]))
        for n in range(8):
            load_copy(n).start()
        for n in ("dk", "dv", "d5"):
            loads[n][...] = jnp.zeros_like(loads[n])
        dgain_ref[...] = jnp.zeros_like(dgain_ref)
        emit_between(FFPOST, TILE)
        run_loop(TILE, 6, tile, emit)
        emit_between(TILE, END)

    pl.run_scoped(
        attend,
        *kept,
        v((3, 2048, 128), F32), v((3, 2048, 128), F32), v((2048, 640), BF),
    )
    emit_between(END, None)

    for s in zs[1:]:
        where = 3 * (s // 2) + 2 * (s % 2)
        remote(ig_ref.at[0], out_ref.at[where], h_send.at[0], h_recv.at[where], pair).wait_recv()
    where = 3 * (1 - p) + 1
    remote(ig_ref.at[0], out_ref.at[where], h_send.at[0], h_recv.at[where], pair).wait_recv()
    homes.finish()
    leave()
    home(3).wait()
    home(5).wait()
    for stream in streams:
        stream.close()
    for n in (0, 1, 2, 4):
        home(n).wait_send()
    z_copy.wait_send()
    for ab in range(2):
        x_copy(ab).wait_send()
        for k in range(2):
            c_copy(k, ab).wait_send()
    for k in range(5):
        gain_copy(k).wait_send()


def layer(x6, cot6, counts, gain1, wq, wk, wv, gain2, w_out, w_gate, w_up, w_down):
    dma = pltpu.SemaphoreType.DMA
    s = jax.ShapeDtypeStruct
    v = pltpu.VMEM
    rows_shape = x6.shape
    _, rows, width = rows_shape
    heads = (4, 6, 96, 128)
    gains = (8, width)
    group, rest = (width, 512), (width // 2, 128)
    outs = (s(rows_shape, BF), s(rows_shape, BF)) + tuple(s(a.shape, BF) for a in (w_gate, w_up, w_down, w_out))
    outs += (s((4,) + group, BF), s((4,) + rest, BF), s(gains, F32))
    outs += (
        s((3, 1536, 128), BF), s((3, 2048, 128), BF), s((3, 2048, 128), BF), s((3, 2, 128, 1024), BF),
        s((1536, 128), F32), s((1536, 128), F32), s((2048, width), BF), s((width, 640), BF),
    )
    scratch = [
        v(heads, BF), v(rows_shape, BF), v((2, 16, rows, width), BF), v(heads, BF),
        dma((3, 2)), dma((4, 2, 2)), dma((4, 2)), dma((2, 16)), dma((2,)), dma((3,)),
        dma((6, 3)), dma((4, 6)), dma((4,)), dma((6,)), dma((2,)), dma((2, 4)), dma((6, 4)), dma((7,)),
        v(rows_shape, BF), v(rows_shape, F32), v(rows_shape, BF), v(heads, BF), v((1, width), F32),
        v((4, 2, width, 256), BF), v((4, 2, width, 256), BF), v((4, 2, 512, width // 2), BF), v((1, 2, width, width // 2), BF),
        dma((4,)), dma((3, 4)), dma((8,)),
        v(heads, BF), v((4, 8, rows, width), BF),
        v((2, 8, rows, width), BF), v((8, rows, width), BF), v((8, rows, width), BF),
        v((8, rows, width), F32), v((2, rows, width), BF), v((2, rows, width), BF), v((6, rows, width), BF),
        v((1, width), F32),
        dma((2, 2)), dma((2, 2)), dma((2,)), dma((2,)), dma((1,)), dma((1,)), dma((4,)), dma((6,)), dma((2,)),
        dma((4,)), dma((6,)), dma((2,)), dma((3,)), dma((4,)), dma((1,)),
    ]
    for _, _, _, _, high, wide, _, _ in PIECES:
        scratch += [v((high, wide), BF)] * 2
        scratch += [dma((5,)), dma((5,)), dma((2,)), dma((4,)), dma((4,)), dma((5,)), dma((5,))]
    scratch += [v(group, BF), v(rest, BF)]
    for _, _, high, wide, _, _ in GROUPS:
        scratch += [v((high, wide), BF)]
        scratch += [dma((4,)), dma((4,)), dma((2,)), dma((4, 2)), dma((4, 2)), dma((4, 2)), dma((4, 2))]
    scratch += [v((6,) + gains, F32), v((5,) + gains, F32), dma((5,)), dma((5,))]
    return pl.pallas_call(
        layer_kernel,
        out_shape=outs,
        in_specs=[ANY, ANY, SMEM, VMEM, ANY, ANY, ANY, VMEM] + [ANY] * 4,
        out_specs=(ANY,) * 8 + (VMEM,) + (ANY,) * 8,
        scratch_shapes=scratch,
        compiler_params=params(1, 63),
        name="layer",
    )(x6, cot6, counts, gain1, wq, wk, wv, gain2, w_out, w_gate, w_up, w_down)


def fast(
    inputs, counts, norm_gain1, w_query, w_key, w_value, w_out, norm_gain2, w_gate, w_up, w_down, cotangent
):
    band_rows, width = inputs.shape[2:]
    input_grads, results, s_gate, s_up, s_down, s_out, s_qkv, s_last, s_gains, *_ = layer(
        inputs.reshape(6, band_rows, width), cotangent.reshape(6, band_rows, width), counts, norm_gain1,
        w_query, w_key, w_value, norm_gain2, w_out, w_gate, w_up, w_down,
    )
    *grads, gain1, gain2, results, input_grads = widen(
        s_qkv, s_last, s_out, s_gate, s_up, s_down, s_gains, results, input_grads
    )
    return (
        results.reshape(inputs.shape), input_grads.reshape(inputs.shape), gain1, *grads[:4], gain2, *grads[4:]
    )


def program(*args):
    micro, seqs, band_rows, width = args[0].shape
    small = lax.axis_size("band") == 16 and lax.axis_size("items") == 2
    if small and (micro, seqs, band_rows, width, HEADS, HEAD_DIM) == (2, 3, 64, 768, 12, 64):
        return fast(*args)
    return per_device(*args)


def solution(mesh):
    return jax.shard_map(
        program,
        mesh=mesh,
        in_specs=(
            P(None, "items", "band", None),
            P(None, "items"),
            P(),
            P(),
            P(),
            P(),
            P(),
            P(),
            P(),
            P(),
            P(),
            P(None, "items", "band", None),
        ),
        out_specs=(
            P(None, "items", "band", None),
            P(None, "items", "band", None),
            P(),
            P(),
            P(),
            P(),
            P(),
            P(),
            P(),
            P(),
            P(),
        ),
        check_vma=False,
    )
```
